32 devices in a mesh: groups: 2 (over y), seq: 8 (over z, x), dp: 2 (over core).
Axes of the slice: x: 2, y: 2, z: 4, core: 2. Of those that a mesh axis runs over, the one named last changes fastest.
Arguments:
- history_item_index: int32 [4, 8192], P(('groups', 'dp'), 'seq'), parts along dimension 0, may hold values from 0 to 4095
- log_head_retention: float32 [4, 8, 8192], P(('groups', 'dp'), None, 'seq'), parts along dimension 0, may hold values from -1.5 to 0
- user_history_length: int32 [4], P(('groups', 'dp')), parts along dimension 0, may hold values from 2048 to 8192, as said below
- candidate_item_index: int32 [4, 512], P(('groups', 'dp'), 'seq'), parts along dimension 0, may hold values from 0 to 4095
- item_stored_row: int32 [4096], replicated, may hold values from 0 to 4095, each once
- item_embedding_table: bfloat16 [4096, 512], P('dp'), may hold values from -6 to 6
- head_score_scale: float32 [8], replicated, may hold values from 0.2 to 4
- history_query_key_value_weight: bfloat16 [512, 1536], replicated, may hold values from -0.25 to 0.25
- history_output_weight: bfloat16 [512, 512], replicated, may hold values from -0.25 to 0.25
- candidate_key_value_weight: bfloat16 [512, 1024], replicated, may hold values from -0.25 to 0.25
- candidate_query_weight: bfloat16 [512, 512], replicated, may hold values from -0.25 to 0.25
- candidate_output_weight: bfloat16 [512, 512], replicated, may hold values from -0.25 to 0.25
Outputs:
- history_out: float32 [4, 8192, 512], P(('groups', 'dp'), 'seq'), parts along dimension 0
- cand_out: float32 [4, 512, 512], P(('groups', 'dp'), 'seq'), parts along dimension 0
The draws below stay inside these ranges and needn't reach their ends.
There are 2 independent parts, one for each index of `groups`. The reference program is written for one: setup_inputs(seed, part) draws one part's arguments, and reference() takes and returns one part's arrays. A program takes and returns all parts, laid end to end along the dimension named above; an argument that names none is the same for every part. Nothing has to cross between parts.
Inputs may be any that keep to these rules, and one draw needn't show every extreme that they name: `user_history_length`: at least one user has exactly 8192 events; positions at or past a user's length are padding. `item_stored_row`: each stored row holds exactly one item. `history_item_index`: items repeat within a history.
All inputs are finite; a program needn't handle non-finite values.
Results may differ from the reference program's by a relative error of at most 0.038.
Values may be sent and summed in bfloat16 or wider, within the bound.
No kernel may reach another device: no remote copies, remote signals or barrier semaphores. Data moves between devices by JAX's collectives and lax.ppermute only.
A program may use at most 128 MiB of HBM per device.

```python
import math
import jax
import jax.numpy as jnp
import numpy as np
from jax import lax

E = 512
HEAD_COUNT = 8
DH = 64
C = 512
SLAB = 1024
USER_COUNT = 2
HISTORY_LENGTH = 8192
V = 4096


def draw_log_head_retention(key, part):
    random_keys = jax.random.split(key, 5)
    fast_share = 0.5
    fast = jax.random.uniform(random_keys[0], (USER_COUNT, HEAD_COUNT, 1)) < fast_share
    slab_factor = jax.random.uniform(random_keys[1], (USER_COUNT, HEAD_COUNT, HISTORY_LENGTH // SLAB, 1), minval=0.5, maxval=1.5)
    slab_factor = jnp.broadcast_to(slab_factor, (USER_COUNT, HEAD_COUNT, HISTORY_LENGTH // SLAB, SLAB)).reshape(USER_COUNT, HEAD_COUNT, HISTORY_LENGTH)
    cell_factor = jax.random.uniform(random_keys[2], (USER_COUNT, HEAD_COUNT, HISTORY_LENGTH), minval=0.5, maxval=1.5)
    rate = jnp.where(fast, 1.0 / 40.0, math.log(2.0) / HISTORY_LENGTH)
    base = -rate * slab_factor * cell_factor
    event_positions = jnp.arange(HISTORY_LENGTH).astype(jnp.int32)
    spike_position = jax.random.randint(random_keys[3], (USER_COUNT, HEAD_COUNT, 2, 1), 0, HISTORY_LENGTH)
    spike_length = jax.random.uniform(random_keys[4], (USER_COUNT, HEAD_COUNT, 2, 1), minval=0.2, maxval=0.5)
    removed_events = jnp.sum(jnp.where(event_positions[None, None, None, :] == spike_position, jnp.log(1.0 - spike_length), 0.0), axis=2)
    return (base + removed_events).astype(jnp.float32)


def draw_user_history_length(key, part):
    first_key, second_key = jax.random.split(key)
    lengths = jax.random.randint(first_key, (USER_COUNT,), HISTORY_LENGTH // 4, HISTORY_LENGTH + 1)
    longest = jax.random.randint(second_key, (), 0, USER_COUNT)
    return jnp.where(jnp.arange(USER_COUNT) == longest, HISTORY_LENGTH, lengths).astype(jnp.int32)


def draw_head_score_scale(key, part):
    lower, upper = (0.2, 0.4)
    spread = jax.random.uniform(key, (HEAD_COUNT,))
    return jnp.exp(math.log(lower) + spread * (math.log(upper) - math.log(lower))).astype(jnp.float32)


def touch_ends(values, own_key, low, largest):
    dims = values.shape
    index_at = [jax.random.randint(jax.random.fold_in(own_key, axis), (), 0, dims[axis]) for axis in range(len(dims))]
    values = values.at[tuple(index_at)].set(low)
    longest = dims.index(max(dims))
    index_at[longest] = (index_at[longest] + 1) % dims[longest]
    return values.at[tuple(index_at)].set(largest)


def steps_of(key, extent, cuts, low, high):
    level, own = 1.0, jax.random.fold_in(key, 6)
    for position, parts in cuts:
        draws = jnp.exp(jax.random.uniform(jax.random.fold_in(own, position), (parts,), jnp.float32, low / len(cuts), high / len(cuts)))
        level = level * jnp.repeat(draws, extent[position] // parts).reshape([-1 if axis == position else 1 for axis in range(len(extent))])
    return level


def cumulative_ranks(number_of, slope):
    loads = [(1 << 20) // math.isqrt(rank ** slope) + 1 for rank in range(1, number_of + 1)]
    scale = 1 + sum(loads) // (1 << 30)
    return np.cumsum(np.array([max(1, weight // scale) for weight in loads]))


def skewed_ids(rng, dims, count, lean):
    grid = cumulative_ranks(count, lean)
    pick = jax.random.randint(jax.random.fold_in(rng, 1), dims, 0, int(grid[count - 1]))
    rank = jnp.searchsorted(jnp.asarray(grid, jnp.int32), pick, side="right")
    return jax.random.permutation(jax.random.fold_in(rng, 2), count)[rank].astype(jnp.int32)


def scatter_about(own_key, extent, scale, limit, pieces=(), kind=jnp.bfloat16):
    gain = steps_of(own_key, extent, pieces, -0.22, 0.18) if pieces else 1.0
    array = jax.random.normal(own_key, extent, jnp.float32) * scale * gain
    return jnp.minimum(jnp.maximum(array, -limit), limit).astype(kind)


def setup_inputs(seed: int = 0, part: int = 0) -> dict:
    key_of = jax.random.split(jax.random.key(seed), 13)
    part_keys = jax.random.split(jax.random.fold_in(key_of[12], part), 13)
    return {
        "history_item_index": touch_ends(skewed_ids(part_keys[0], (USER_COUNT, HISTORY_LENGTH), V, 2), jax.random.fold_in(part_keys[0], 3), 0, V - 1).astype(jnp.int32),
        "log_head_retention": draw_log_head_retention(jax.random.fold_in(jax.random.fold_in(key_of[12], part), 71), part),
        "user_history_length": draw_user_history_length(jax.random.fold_in(jax.random.fold_in(key_of[12], part), 71), part),
        "candidate_item_index": touch_ends(jax.random.randint(part_keys[3], (USER_COUNT, C), 0, V), jax.random.fold_in(part_keys[3], 1), 0, V - 1).astype(jnp.int32),
        "item_stored_row": jax.random.permutation(key_of[4], V).astype(jnp.int32),
        "item_embedding_table": scatter_about(key_of[5], (V, E), 1.0, 6.0, ((0, 2),)),
        "head_score_scale": draw_head_score_scale(jax.random.fold_in(key_of[12], 71), part),
        "history_query_key_value_weight": scatter_about(key_of[7], (E, 3 * E), E ** -0.5, 0.25),
        "history_output_weight": scatter_about(key_of[8], (E, E), E ** -0.5, 0.25),
        "candidate_key_value_weight": scatter_about(key_of[9], (E, 2 * E), E ** -0.5, 0.25),
        "candidate_query_weight": scatter_about(key_of[10], (E, E), E ** -0.5, 0.25),
        "candidate_output_weight": scatter_about(key_of[11], (E, E), E ** -0.5, 0.25),
    }


highest = lax.Precision.HIGHEST

def unit_rows(projected):
    scale = lax.rsqrt(lax.optimization_barrier(jnp.mean(projected * projected, axis=-1, keepdims=True)) + 1e-06)
    return projected * scale / math.sqrt(projected.shape[-1])

def block_terms(queries, key_rows, val_rows, decay):
    cumulative = jnp.cumsum(decay, axis=1)
    width = decay.shape[1]
    causal = jnp.arange(width)[:, None] >= jnp.arange(width)[None, :]
    attention_scores = jnp.einsum('shd,thd->hst', queries.astype(jnp.float32), key_rows.astype(jnp.float32))
    gap_log = jnp.where(causal[None], cumulative[:, :, None] - cumulative[:, None, :], 0.0)
    weights = jnp.where(causal[None], attention_scores * jnp.exp(gap_log), 0.0).astype(jnp.bfloat16)
    local_out = jnp.einsum('hst,thd->shd', weights.astype(jnp.float32), val_rows.astype(jnp.float32))
    tail_decay = jnp.exp(cumulative[:, -1:] - cumulative)
    keyed = key_rows.astype(jnp.float32) * jnp.transpose(tail_decay)[:, :, None]
    summary = jnp.einsum('thd,the->hde', keyed, val_rows.astype(jnp.float32), precision=highest)
    return (local_out, cumulative, summary, jnp.exp(cumulative[:, -1]))

def per_user_forward(input_arrays, item_stored_row, item_embedding_table, head_score_scale, history_query_key_value_weight, history_output_weight, candidate_key_value_weight, candidate_query_weight):
    history_item_index, log_head_retention, length, candidate_item_index = input_arrays
    blocks = HISTORY_LENGTH // SLAB
    embedded = item_embedding_table[item_stored_row[history_item_index]]
    rows_blocked = embedded.reshape(blocks, SLAB, E)
    decay_blocked = jnp.transpose(log_head_retention.reshape(HEAD_COUNT, blocks, SLAB), (1, 0, 2))
    starts = (jnp.arange(blocks) * SLAB).astype(jnp.int32)

    def step_block(state, items):
        rows, decay, first_pos = items
        alive = first_pos + jnp.arange(SLAB).astype(jnp.int32) < length
        projected = jnp.dot(rows, history_query_key_value_weight, preferred_element_type=jnp.float32).reshape(SLAB, 3, HEAD_COUNT, DH)
        queries = unit_rows(projected[:, 0]).astype(jnp.bfloat16)
        key_rows = jnp.where(alive[:, None, None], unit_rows(projected[:, 1]), 0.0).astype(jnp.bfloat16)
        val_rows = jnp.where(alive[:, None, None], projected[:, 2], 0.0).astype(jnp.bfloat16)
        local_out, cumulative, summary, total_decay = block_terms(queries, key_rows, val_rows, decay)
        carried = jnp.transpose(jnp.exp(cumulative))[:, :, None] * jnp.einsum('shd,hde->she', queries.astype(jnp.float32), state, precision=highest)
        mixed = local_out + carried
        normed = mixed * lax.rsqrt(lax.optimization_barrier(jnp.mean(mixed * mixed, axis=-1, keepdims=True)) + 1e-05)
        normed = normed.astype(jnp.bfloat16).reshape(SLAB, E)
        hidden_sum = rows.astype(jnp.float32) + jnp.dot(normed, history_output_weight, preferred_element_type=jnp.float32)
        hidden = hidden_sum.astype(jnp.bfloat16)
        pair = jnp.dot(hidden, candidate_key_value_weight, preferred_element_type=jnp.float32).astype(jnp.bfloat16)
        shown = jnp.where(alive[:, None], hidden_sum, jnp.zeros((), jnp.float32))
        new_state = total_decay[:, None, None] * state + summary
        return (new_state, (shown, pair, alive))
    zero_state = jnp.zeros((HEAD_COUNT, DH, DH), jnp.float32)
    final_state, outputs = lax.scan(step_block, zero_state, (rows_blocked, decay_blocked, starts))
    shown, pairs, alive_all = outputs
    cand_rows = item_embedding_table[item_stored_row[candidate_item_index]]
    candidate_query_rows = jnp.dot(cand_rows, candidate_query_weight, preferred_element_type=jnp.float32).astype(jnp.bfloat16).reshape(C, HEAD_COUNT, DH)

    def block_scores(pair, alive):
        second_key_random = pair[:, :E].reshape(SLAB, HEAD_COUNT, DH)
        attention_scores = head_score_scale[None, :, None] * jnp.einsum('mob,nob->mon', candidate_query_rows.astype(jnp.float32), second_key_random.astype(jnp.float32))
        return jnp.where(alive[None, None, :], attention_scores, -jnp.inf)

    def peak_step(peak, items):
        pair, alive = items
        return (jnp.maximum(peak, lax.optimization_barrier(jnp.max(block_scores(pair, alive), axis=-1))), None)
    peak_all, unused = lax.scan(peak_step, jnp.full((C, HEAD_COUNT), -jnp.inf, jnp.float32), (pairs, alive_all))

    def sum_step(carry, items):
        weighted, denominator = carry
        pair, alive = items
        attention_scores = block_scores(pair, alive)
        block_peak = lax.optimization_barrier(jnp.max(attention_scores, axis=-1))
        present = block_peak > -jnp.inf
        safe_peak = jnp.where(present, block_peak, 0.0)
        probs = jnp.where(alive[None, None, :], jnp.exp(attention_scores - safe_peak[:, :, None]), 0.0)
        probs = probs.astype(jnp.bfloat16)
        rescale = jnp.where(present, jnp.exp(safe_peak - peak_all), 0.0)
        val_two = pair[:, E:].reshape(SLAB, HEAD_COUNT, DH)
        block_weighted = jnp.einsum('cht,thd->chd', probs.astype(jnp.float32), val_two.astype(jnp.float32))
        weighted = weighted + rescale[:, :, None] * block_weighted
        denominator = denominator + rescale * lax.optimization_barrier(jnp.sum(probs.astype(jnp.float32), axis=-1))
        return ((weighted, denominator), None)
    start_sums = (jnp.zeros((C, HEAD_COUNT, DH), jnp.float32), jnp.zeros((C, HEAD_COUNT), jnp.float32))
    sums, unused_two = lax.scan(sum_step, start_sums, (pairs, alive_all))
    weighted, denominator = sums
    attended = (weighted / denominator[:, :, None]).astype(jnp.bfloat16).reshape(C, E)
    return (shown.reshape(HISTORY_LENGTH, E), attended)

def reference(history_item_index, log_head_retention, user_history_length, candidate_item_index, item_stored_row, item_embedding_table, head_score_scale, history_query_key_value_weight, history_output_weight, candidate_key_value_weight, candidate_query_weight, candidate_output_weight):

    def one_user(input_arrays):
        return per_user_forward(input_arrays, item_stored_row, item_embedding_table, head_score_scale, history_query_key_value_weight, history_output_weight, candidate_key_value_weight, candidate_query_weight)
    history_out, attended = lax.map(one_user, (history_item_index, log_head_retention, user_history_length, candidate_item_index))
    cand_out = jnp.dot(attended, candidate_output_weight, preferred_element_type=jnp.float32)
    return (history_out, cand_out)
```

```python
import math

import jax
import jax.numpy as jnp
from jax import lax
from jax.experimental import pallas as pl
from jax.experimental.pallas import tpu as pltpu
from jax.sharding import PartitionSpec as P

f32, bf16, i32 = jnp.float32, jnp.bfloat16, jnp.int32
CHUNK = 256
LANES = 128
LOG2E = math.log2(math.e)
DEAD = -1e30
VMEM_LIMIT = 40 << 20


def dot(a, b):
    return jnp.dot(a, b, preferred_element_type=f32)


def dot_nt(a, b):
    return lax.dot_general(a, b, (((1,), (1,)), ((), ())), preferred_element_type=f32)


def dot_tn(a, b):
    return lax.dot_general(a, b, (((0,), (0,)), ((), ())), preferred_element_type=f32)


def iota(shape, axis):
    return lax.broadcasted_iota(i32, shape, axis)


def thirds(value):
    high = value.astype(bf16).astype(f32)
    rest = value - high
    mid = rest.astype(bf16).astype(f32)
    return high, mid, rest - mid


def first_half(shape):
    return iota(shape, len(shape) - 1) % LANES < LANES // 2


def half_masks():
    low = first_half((1, LANES))
    return jnp.where(low, 1.0, 0.0).astype(bf16), jnp.where(low, 0.0, 1.0).astype(bf16)


def head_sums(width, heads):
    dims = (width, 2 * heads)
    same = iota(dims, 0) // (width // heads) == iota(dims, 1) % heads
    return jnp.where(same, 1.0, 0.0).astype(bf16)


def head_spread(width, heads):
    dims = (2 * heads, width)
    same = iota(dims, 1) // (width // heads) == iota(dims, 0) % heads
    return jnp.where(same, 1.0, 0.0).astype(bf16)


def spread(value, matrix):
    heads = value.shape[1] // 2
    high = value.astype(bf16).astype(f32)
    both = jnp.where(iota(value.shape, 1) < heads, high, value - high)
    return dot(both.astype(bf16), matrix)


def stored_slots(ids, stored):
    groups = stored.shape[0]
    n = ids.shape[1]
    pick = jnp.where(iota((groups, n), 0) == ids // LANES, 1.0, 0.0).astype(bf16)
    high = dot_tn((stored // 64).astype(f32).astype(bf16), pick)
    low = dot_tn((stored % 64).astype(f32).astype(bf16), pick)
    rows = jnp.where(iota((LANES, n), 0) == ids % LANES, high * 64.0 + low, 0.0)
    return jnp.sum(rows, axis=0, keepdims=True)


def as_column(row):
    return jnp.transpose(jnp.broadcast_to(row, (8, row.shape[1])))


def one_hot(column, first, count):
    local = column.astype(i32) - first
    return jnp.where(iota((column.shape[0], count), 1) == local, 1.0, 0.0).astype(bf16)


def own_rows_kernel(sc, ids, stored, decay, own, part_o, slot_o, crow_o, ccol_o, ctl_o):
    n, half, heads = ids.shape[1], own.shape[0], decay.shape[0]
    slot_o[...] = as_column(stored_slots(ids[...], stored[...]))
    upto = jnp.where(
        iota((CHUNK, CHUNK), 0) <= iota((CHUNK, CHUNK), 1), 1.0, 0.0
    ).astype(bf16)
    low = first_half((1, LANES))
    for i in range(n // CHUNK):
        pieces = jnp.concatenate(thirds(decay[:, i * CHUNK : (i + 1) * CHUNK]), axis=0)
        sums = dot(pieces.astype(bf16), upto)
        cum = sums[:heads] + sums[heads : 2 * heads] + sums[2 * heads :]
        crow_o[i] = cum
        ccol_o[i * CHUNK : (i + 1) * CHUNK, :] = jnp.transpose(jnp.concatenate([cum, cum], axis=0))
        for p in range(heads // 2):
            r = i * (heads // 2) + p
            ctl_o[r : r + 1, :] = jnp.where(
                low, cum[2 * p : 2 * p + 1, CHUNK - 1 :], cum[2 * p + 1 : 2 * p + 2, CHUNK - 1 :]
            )

    def step(i, carry):
        rows = pl.ds(pl.multiple_of(i * CHUNK, CHUNK), CHUNK)
        hot = one_hot(slot_o[rows, 0:1], sc[3] * half, half)
        part_o[rows, :] = dot(hot, own[...]).astype(bf16)
        return carry

    lax.fori_loop(0, n // CHUNK, step, 0)


def summary_kernel(
    sc, part, peer, slot, ccol, ctl, key_w, val_w, emb_o, key_o, val_o, enter_o, pay_o, total
):
    n, width = part.shape
    half, heads = peer.shape[0], ccol.shape[1] // 2
    pairs = heads // 2
    block = LANES // 2
    sums, lanes = head_sums(width, heads), head_spread(width, heads)
    total[...] = jnp.zeros_like(total)
    low = first_half((1, LANES))

    def step(i, carry):
        rows = pl.ds(pl.multiple_of(i * CHUNK, CHUNK), CHUNK)
        hot = one_hot(slot[rows, 0:1], (1 - sc[3]) * half, half)
        emb = (part[rows, :].astype(f32) + dot(hot, peer[...])).astype(bf16)
        emb_o[rows, :] = emb
        alive = sc[1] + i * CHUNK + iota((CHUNK, 1), 0) < sc[2]
        key = dot(emb, key_w[...])
        val = jnp.where(alive, dot(emb, val_w[...]), 0.0).astype(bf16)
        val_o[rows, :] = val
        square = dot((key * key).astype(bf16), sums)
        unit = lax.rsqrt(square * (heads / width) + 1e-06) * math.sqrt(heads / width)
        unit = jnp.where(alive, unit, 0.0)
        normed = key * spread(unit, lanes)
        key_o[rows, :] = normed.astype(bf16)
        cum = ccol[rows, :]
        tail = spread(jnp.exp(cum[CHUNK - 1 :, :] - cum), lanes)
        keyed = (normed * tail).astype(bf16)
        for p in range(pairs):
            cut = slice(p * LANES, (p + 1) * LANES)
            both = dot_tn(keyed[:, cut], val[:, cut])
            fresh = jnp.where(low, both[:block], both[block:])
            here = pl.ds(p * block, block)
            old = total[here, :]
            enter_o[i, here, :] = old
            keep = jnp.exp(ctl[pl.ds(i * pairs + p, 1), :])
            total[here, :] = old * keep + fresh
        return carry

    lax.fori_loop(0, n // CHUNK, step, 0)
    logs = ctl[0:pairs, :]
    for i in range(1, n // CHUNK):
        logs = logs + ctl[i * pairs : (i + 1) * pairs, :]
    pay_o[...] = pack_state(total[...], logs)


def pack_state(state, logs):
    pad = jnp.zeros((16 - 3 * logs.shape[0], LANES), f32)
    return jnp.concatenate([state, *thirds(logs), pad], axis=0).astype(bf16)


def unpack_state(packed):
    whole = packed.astype(f32)
    rows = whole.shape[0] - 16
    pairs = rows // (LANES // 2)
    tail = whole[rows:]
    return whole[:rows], tail[:pairs] + tail[pairs : 2 * pairs] + tail[2 * pairs : 3 * pairs]


def row_factors(logs):
    factors = jnp.exp(logs)
    return jnp.concatenate(
        [
            jnp.broadcast_to(factors[p : p + 1], (LANES // 2, LANES))
            for p in range(logs.shape[0])
        ],
        axis=0,
    )


def join_prefix(upper, prefix, prefix_logs, early, early_logs):
    joined = prefix + row_factors(prefix_logs) * early
    return (
        jnp.where(upper, joined, prefix),
        jnp.where(upper, prefix_logs + early_logs, prefix_logs),
    )


def first_join_kernel(bit, sc, mine, got, pay_o, prefix_o, logs_o):
    upper = (sc[0] >> bit) & 1 == 1
    state, logs = unpack_state(mine[...])
    other, other_logs = unpack_state(got[...])
    pay_o[...] = merged(upper, state, logs, other, other_logs)
    prefix_o[...] = jnp.where(upper, other, 0.0)
    logs_o[...] = jnp.where(upper, other_logs, 0.0)


def merged(upper, state, logs, other, other_logs):
    late_logs = jnp.where(upper, logs, other_logs)
    factor = row_factors(late_logs)
    early = jnp.where(upper, other, state)
    late = jnp.where(upper, state, other)
    return pack_state(early * factor + late, logs + other_logs)


def join_kernel(bit, sc, mine, got, prefix, prefix_logs, pay_o, prefix_o, logs_o):
    upper = (sc[0] >> bit) & 1 == 1
    state, logs = unpack_state(mine[...])
    other, other_logs = unpack_state(got[...])
    pay_o[...] = merged(upper, state, logs, other, other_logs)
    prefix_o[...], logs_o[...] = join_prefix(
        upper, prefix[...], prefix_logs[...], other, other_logs
    )


def local_kernel(emb, key, val, crow, ccol, query_w, query_o, intra_o):
    n, width = emb.shape
    heads = ccol.shape[1] // 2
    sums, lanes = head_sums(width, heads), head_spread(width, heads)
    mask_a, mask_b = half_masks()

    def step(i, carry):
        rows = pl.ds(pl.multiple_of(i * CHUNK, CHUNK), CHUNK)
        query = dot(emb[rows, :], query_w[...])
        square = dot((query * query).astype(bf16), sums)
        unit = lax.rsqrt(square * (heads / width) + 1e-06) * math.sqrt(heads / width)
        query = (query * spread(unit, lanes)).astype(bf16)
        query_o[rows, :] = query
        cum = ccol[rows, :]
        cum_row = crow[i]
        causal = iota((CHUNK, CHUNK), 0) >= iota((CHUNK, CHUNK), 1)
        for p in range(heads // 2):
            cut = slice(p * LANES, (p + 1) * LANES)
            key_p, val_p, query_p = key[rows, cut], val[rows, cut], query[:, cut]
            parts = []
            for b, mask in ((0, mask_a), (1, mask_b)):
                h = 2 * p + b
                scores = dot_nt(query_p * mask, key_p)
                gap = cum[:, h : h + 1] - cum_row[h : h + 1, :]
                parts.append(jnp.where(causal, scores * jnp.exp(gap), 0.0).astype(bf16))
            intra_o[rows, cut] = dot(parts[0], val_p * mask_a) + dot(parts[1], val_p * mask_b)
        return carry

    lax.fori_loop(0, n // CHUNK, step, 0)


def candidate_kernel(sc, ids, stored, own, peer, query_w, query_o):
    n, half = ids.shape[1], own.shape[0]
    column = as_column(stored_slots(ids[...], stored[...]))
    for i in range(n // CHUNK):
        slot = column[i * CHUNK : (i + 1) * CHUNK, 0:1]
        rows = dot(one_hot(slot, sc[3] * half, half), own[...])
        rows += dot(one_hot(slot, (1 - sc[3]) * half, half), peer[...])
        query_o[i * CHUNK : (i + 1) * CHUNK, :] = dot(rows.astype(bf16), query_w[...]).astype(bf16)


def attend(sc, scale, query, first_row, rows, key, val, emit):
    n, width = key.shape
    mask_a, mask_b = half_masks()
    alive = sc[1] + iota((1, n), 1) < sc[2]
    any_alive = sc[1] < sc[2]
    low = first_half((1, LANES))

    def pair(p, carry):
        cut = pl.ds(pl.multiple_of(p * LANES, LANES), LANES)
        key_p, val_p = key[:, cut], val[:, cut]
        query_p = query[first_row : first_row + rows, cut]
        peaks, sums = [], None
        for b, mask in ((0, mask_a), (1, mask_b)):
            factor = scale[2 * p + b] * LOG2E
            scores = jnp.where(alive, dot_nt(query_p * mask, key_p), DEAD)
            peak = jnp.max(scores, axis=1, keepdims=True)
            probs = jnp.exp2((scores - peak) * factor).astype(bf16)
            side = jnp.concatenate(
                [val_p * mask, jnp.broadcast_to(mask, (n, LANES))], axis=1
            )
            part = dot(probs, side)
            sums = part if sums is None else sums + part
            peaks.append(peak * factor)
        total = sums[:, LANES:]
        logs = jnp.where(low, peaks[0], peaks[1]) + jnp.log2(total)
        emit(p, cut, sums[:, :LANES] / total, jnp.where(any_alive, logs, DEAD))
        return carry

    lax.fori_loop(0, width // LANES, pair, 0)


def log_columns(p, pairs, logs, columns):
    lane = iota((1, LANES), 1) % (LANES // 2)
    for k, piece in enumerate(thirds(logs)):
        columns = jnp.where(lane == p + k * pairs, piece, columns)
    return columns


def log_spread(width):
    pairs = width // LANES
    dims = (LANES, width)
    lane, col = iota(dims, 0), iota(dims, 1)
    inner = lane % (LANES // 2)
    same = (lane // (LANES // 2) == (col // (LANES // 2)) % 2) & (inner % pairs == col // LANES)
    return jnp.where(same & (inner < 3 * pairs), 1.0, 0.0).astype(bf16)


def finish_kernel(
    sc, scale, emb, query, intra, enter, ccol, ctl, got, prefix, prefix_logs, out_w, pair_w,
    cand_q, hist_o, key_o, val_o, pay_o, columns, bit,
):
    n, width = emb.shape
    heads = ccol.shape[1] // 2
    pairs = heads // 2
    block = LANES // 2
    sums, lanes = head_sums(width, heads), head_spread(width, heads)
    upper = (sc[0] >> bit) & 1 == 1
    state, logs = unpack_state(got[...])
    entering = join_prefix(upper, prefix[...], prefix_logs[...], state, logs)[0]
    low = first_half((1, LANES))

    def step(i, gone):
        rows = pl.ds(pl.multiple_of(i * CHUNK, CHUNK), CHUNK)
        states = enter[i] + row_factors(gone) * entering
        parts = []
        for p in range(pairs):
            cut = slice(p * LANES, (p + 1) * LANES)
            one = states[p * block : (p + 1) * block]
            matrix = jnp.concatenate([jnp.where(low, one, 0.0), jnp.where(low, 0.0, one)], axis=0)
            parts.append(dot(query[rows, cut], matrix.astype(bf16)))
        carried = jnp.concatenate(parts, axis=1) * spread(jnp.exp(ccol[rows, :]), lanes)
        mixed = intra[rows, :] + carried
        square = dot((mixed * mixed).astype(bf16), sums)
        unit = lax.rsqrt(square * (heads / width) + 1e-05)
        normed = (mixed * spread(unit, lanes)).astype(bf16)
        hidden_sum = emb[rows, :].astype(f32) + dot(normed, out_w[...])
        alive = sc[1] + i * CHUNK + iota((CHUNK, 1), 0) < sc[2]
        hist_o[rows, :] = jnp.where(alive, hidden_sum, 0.0)
        both = dot(hidden_sum.astype(bf16), pair_w[...]).astype(bf16)
        key_o[rows, :] = both[:, :width]
        val_o[rows, :] = both[:, width:]
        return gone + ctl[pl.ds(pl.multiple_of(i * pairs, pairs), pairs), :]

    lax.fori_loop(0, n // CHUNK, step, jnp.zeros((pairs, LANES), f32))
    columns[...] = jnp.zeros_like(columns)
    count = pay_o.shape[0]

    def emit(p, cut, attended, logs):
        pay_o[:, cut] = attended.astype(bf16)
        columns[...] = log_columns(p, pairs, logs, columns[...])

    attend(sc, scale, cand_q, count, count, key_o, val_o, emit)
    pay_o[:, width:] = columns[...].astype(bf16)


def keep_kernel(sc, scale, cand_q, key, val, mean_o, logs_o):
    def emit(p, cut, attended, logs):
        mean_o[:, cut] = attended
        logs_o[:, cut] = logs

    attend(sc, scale, cand_q, 0, mean_o.shape[0], key, val, emit)


def weigh(mean, logs, got):
    width = mean.shape[1]
    other = got[:, :width].astype(f32)
    other_logs = dot(got[:, width:], log_spread(width))
    peak = jnp.maximum(logs, other_logs)
    mine, theirs = jnp.exp2(logs - peak), jnp.exp2(other_logs - peak)
    total = mine + theirs
    return (mine * mean + theirs * other) / total, peak + jnp.log2(total)


def fold_kernel(mean, logs, got, mean_o, logs_o, pay_o):
    new_mean, new_logs = weigh(mean[...], logs[...], got[...])
    keep, width = mean_o.shape
    mean_o[...] = new_mean[:keep]
    logs_o[...] = new_logs[:keep]
    sent = new_logs[keep:]
    columns = jnp.zeros((sent.shape[0], LANES), f32)
    pairs = width // LANES
    for p in range(pairs):
        columns = log_columns(p, pairs, sent[:, p * LANES : (p + 1) * LANES], columns)
    pay_o[...] = jnp.concatenate([new_mean[keep:], columns], axis=1).astype(bf16)


def last_kernel(mean, logs, got, out_w, cand_o):
    attended = weigh(mean[...], logs[...], got[...])[0]
    cand_o[...] = dot(attended.astype(bf16), out_w[...])


def shape(dims, dtype):
    return jax.ShapeDtypeStruct(dims, dtype)


VMEM = pl.BlockSpec(memory_space=pltpu.VMEM)
SMEM = pl.BlockSpec(memory_space=pltpu.SMEM)


def call(kernel, name, scalars, operands, outs, scratch=(), flops=0, moved=0):
    return pl.pallas_call(
        kernel,
        name=name,
        in_specs=[SMEM] * len(scalars) + [VMEM] * len(operands),
        out_specs=[VMEM] * len(outs),
        out_shape=outs,
        scratch_shapes=list(scratch),
        compiler_params=pltpu.CompilerParams(vmem_limit_bytes=VMEM_LIMIT),
        cost_estimate=pl.CostEstimate(flops=flops, transcendentals=0, bytes_accessed=moved),
    )(*scalars, *operands)


def shards(
    history_item_index,
    log_head_retention,
    user_history_length,
    candidate_item_index,
    item_stored_row,
    item_embedding_table,
    head_score_scale,
    history_query_key_value_weight,
    history_output_weight,
    candidate_key_value_weight,
    candidate_query_weight,
    candidate_output_weight,
):
    users, n = history_item_index.shape
    heads = log_head_retention.shape[1]
    half, width = item_embedding_table.shape
    owned = candidate_item_index.shape[1]
    seq = lax.axis_size("seq")
    assert users == 1 and lax.axis_size("dp") == 2 and seq & (seq - 1) == 0
    pairs = heads // 2
    rows = pairs * LANES // 2
    bits = seq.bit_length() - 1
    cands = owned * seq
    rank = lax.axis_index("seq")

    def swap(value, bit):
        return lax.ppermute(value, "seq", [(j, j ^ (1 << bit)) for j in range(seq)])

    peer = lax.ppermute(item_embedding_table, "dp", [(0, 1), (1, 0)])
    sc = jnp.stack(
        [rank, rank * n, user_history_length[0], lax.axis_index("dp")]
    ).astype(i32)
    stored = item_stored_row.reshape(-1, LANES)
    decay = log_head_retention.reshape(heads, n)
    ids = candidate_item_index
    for bit in reversed(range(bits)):
        ids = jnp.concatenate([ids, swap(ids, bit)], axis=1)

    part, slot, crow, ccol, ctl = call(
        own_rows_kernel, "own_rows", [sc],
        [history_item_index, stored, decay, item_embedding_table],
        [
            shape((n, width), bf16), shape((n, 8), f32), shape((n // CHUNK, heads, CHUNK), f32),
            shape((n, 2 * heads), f32), shape((n // CHUNK * pairs, LANES), f32),
        ],
        flops=2 * n * half * width,
    )
    query_w = history_query_key_value_weight[:, :width]
    key_w = history_query_key_value_weight[:, width : 2 * width]
    val_w = history_query_key_value_weight[:, 2 * width :]
    emb, key, val, enter, pay = call(
        summary_kernel, "summary", [sc],
        [part, peer, slot, ccol, ctl, key_w, val_w],
        [
            shape((n, width), bf16), shape((n, width), bf16), shape((n, width), bf16),
            shape((n // CHUNK, rows, LANES), f32), shape((rows + 16, LANES), bf16),
        ],
        [pltpu.VMEM((rows, LANES), f32)],
        flops=2 * n * half * width,
    )
    query, intra = call(
        local_kernel, "local", [], [emb, key, val, crow, ccol, query_w],
        [shape((n, width), bf16), shape((n, width), f32)],
        flops=2 * n * half * width,
    )
    (cand_q,) = call(
        candidate_kernel, "candidates", [sc],
        [ids, stored, item_embedding_table, peer, candidate_query_weight],
        [shape((cands, width), bf16)],
        flops=2 * cands * 2 * half * width,
    )
    prefix = logs = None
    for bit in range(bits - 1):
        got = swap(pay, bit)
        outs = [shape((rows + 16, LANES), bf16), shape((rows, LANES), f32), shape((pairs, LANES), f32)]
        if bit == 0:
            pay, prefix, logs = call(
                lambda *refs: first_join_kernel(0, *refs), "first_join", [sc], [pay, got], outs
            )
        else:
            pay, prefix, logs = call(
                lambda *refs, bit=bit: join_kernel(bit, *refs), "join", [sc],
                [pay, got, prefix, logs], outs,
            )
    got = swap(pay, bits - 1)
    send = cands // 2
    hist, key_two, val_two, pay = call(
        lambda *refs: finish_kernel(*refs, bit=bits - 1), "finish", [sc, head_score_scale],
        [
            emb, query, intra, enter, ccol, ctl, got, prefix, logs,
            history_output_weight, candidate_key_value_weight, cand_q,
        ],
        [
            shape((n, width), f32), shape((n, width), bf16), shape((n, width), bf16),
            shape((send, width + LANES), bf16),
        ],
        [pltpu.VMEM((send, LANES), f32)],
        flops=2 * n * half * width,
    )
    mean, logs = call(
        keep_kernel, "keep", [sc, head_score_scale], [cand_q, key_two, val_two],
        [shape((send, width), f32), shape((send, width), f32)],
        flops=2 * n * half * width,
    )
    for bit in range(bits - 1):
        got = swap(pay, bit)
        send //= 2
        mean, logs, pay = call(
            fold_kernel, "fold", [], [mean, logs, got],
            [shape((send, width), f32), shape((send, width), f32), shape((send, width + LANES), bf16)],
        )
    got = swap(pay, bits - 1)
    (cand_out,) = call(
        last_kernel, "last", [], [mean, logs, got, candidate_output_weight],
        [shape((owned, width), f32)],
    )
    return hist[None], cand_out[None]


def solution(mesh):
    in_specs = (
        P(("groups", "dp"), "seq"),
        P(("groups", "dp"), None, "seq"),
        P(("groups", "dp")),
        P(("groups", "dp"), "seq"),
        P(),
        P("dp", None),
        P(),
        P(),
        P(),
        P(),
        P(),
        P(),
    )
    out_specs = (P(("groups", "dp"), "seq", None), P(("groups", "dp"), "seq", None))
    return jax.shard_map(shards, mesh=mesh, in_specs=in_specs, out_specs=out_specs, check_vma=False)
```

```python
import math

import jax
import jax.numpy as jnp
from jax import lax
from jax.experimental import pallas as pl
from jax.experimental.pallas import tpu as pltpu
from jax.sharding import PartitionSpec as P

f32, bf16, i32 = jnp.float32, jnp.bfloat16, jnp.int32
CHUNK = 256
KEYS = 512
LANES = 128
LOG2E = math.log2(math.e)
DEAD = -1e30
VMEM_LIMIT = 40 << 20


def dot(a, b):
    return jnp.dot(a, b, preferred_element_type=f32)


def contract(a, b, left, right):
    return lax.dot_general(a, b, (((left,), (right,)), ((), ())), preferred_element_type=f32)


def iota(shape, axis):
    return lax.broadcasted_iota(i32, shape, axis)


def thirds(value):
    high = value.astype(bf16).astype(f32)
    rest = value - high
    mid = rest.astype(bf16).astype(f32)
    return high, mid, rest - mid


def first_half(shape):
    return iota(shape, len(shape) - 1) % LANES < LANES // 2


def half_masks():
    low = first_half((1, LANES))
    return jnp.where(low, 1.0, 0.0).astype(bf16), jnp.where(low, 0.0, 1.0).astype(bf16)


def same_head():
    dims = (2 * LANES, 2 * LANES)
    return jnp.where(iota(dims, 0) // 64 == iota(dims, 1) // 64, 1.0, 0.0).astype(bf16)


def head_means(value, ones):
    square = (value * value).astype(bf16)
    step = ones.shape[0]
    parts = [dot(square[:, c : c + step], ones) for c in range(0, value.shape[1], step)]
    return jnp.concatenate(parts, axis=1) * (1.0 / 64.0)


def head_spread(heads, first, count):
    dims = (2 * heads, 64 * count)
    return jnp.where(iota(dims, 1) // 64 + first == iota(dims, 0) % heads, 1.0, 0.0).astype(bf16)


def spread(value, matrix):
    heads = value.shape[1] // 2
    high = value.astype(bf16).astype(f32)
    both = jnp.where(iota(value.shape, 1) < heads, high, value - high)
    return dot(both.astype(bf16), matrix)


def stored_slots(ids, stored):
    groups = stored.shape[0]
    n = ids.shape[1]
    pick = jnp.where(iota((groups, n), 0) == ids // LANES, 1.0, 0.0).astype(bf16)
    high = contract((stored // 64).astype(f32).astype(bf16), pick, 0, 0)
    low = contract((stored % 64).astype(f32).astype(bf16), pick, 0, 0)
    rows = jnp.where(iota((LANES, n), 0) == ids % LANES, high * 64.0 + low, 0.0)
    return jnp.sum(rows, axis=0, keepdims=True)


def picked_rows(slots, first, table):
    count = table.shape[0]
    hot = jnp.where(iota((count, slots.shape[1]), 0) == slots.astype(i32) - first, 1.0, 0.0)
    return contract(hot.astype(bf16), table[...], 0, 0)


def chunk(i):
    return slice(i * CHUNK, (i + 1) * CHUNK)


def pair_cut(p):
    return slice(p * LANES, (p + 1) * LANES)


def own_rows_kernel(sc, ids, stored, decay, own, part_o, slot_o, crow_o, ccol_o, ctl_o):
    n, half, heads = ids.shape[1], own.shape[0], decay.shape[0]
    slots = stored_slots(ids[...], stored[...])
    slot_o[...] = slots
    upto = jnp.where(
        iota((CHUNK, CHUNK), 0) <= iota((CHUNK, CHUNK), 1), 1.0, 0.0
    ).astype(bf16)
    low = first_half((1, LANES))
    for i in range(n // CHUNK):
        part_o[chunk(i), :] = picked_rows(slots[:, chunk(i)], sc[3] * half, own).astype(bf16)
        pieces = jnp.concatenate(thirds(decay[:, chunk(i)]), axis=0)
        sums = dot(pieces.astype(bf16), upto)
        cum = sums[:heads] + sums[heads : 2 * heads] + sums[2 * heads :]
        crow_o[i] = cum
        ccol_o[chunk(i), :] = jnp.transpose(jnp.concatenate([cum, cum], axis=0))
        for p in range(heads // 2):
            r = i * (heads // 2) + p
            ctl_o[r : r + 1, :] = jnp.where(
                low, cum[2 * p : 2 * p + 1, CHUNK - 1 :], cum[2 * p + 1 : 2 * p + 2, CHUNK - 1 :]
            )


def summary_kernel(
    sc, part, peer, slot, ccol, ctl, id_rows, weight, emb_o, key_o, val_o, enter_o, pay_o
):
    n, width = part.shape
    half, heads = peer.shape[0], ccol.shape[1] // 2
    pairs = heads // 2
    block = LANES // 2
    ones, lanes = same_head(), head_spread(heads, 0, heads)
    low = first_half((1, LANES))
    chunks = n // CHUNK

    def project(i):
        other = picked_rows(slot[:, chunk(i)], (1 - sc[3]) * half, peer)
        emb = (part[chunk(i), :].astype(f32) + other).astype(bf16)
        emb_o[chunk(i), :] = emb
        return dot(emb, weight[:, width : 2 * width]), dot(emb, weight[:, 2 * width :])

    total = [jnp.zeros((block, LANES), f32)] * pairs
    ready = project(0)
    for i in range(chunks):
        key, val = ready
        if i + 1 < chunks:
            ready = project(i + 1)
        alive = sc[1] + i * CHUNK + iota((CHUNK, 1), 0) < sc[2]
        val = jnp.where(alive, val, 0.0).astype(bf16)
        val_o[chunk(i), :] = val
        unit = lax.rsqrt(head_means(key, ones) + 1e-06) * 0.125
        normed = jnp.where(alive, key * unit, 0.0)
        key_o[chunk(i), :] = normed.astype(bf16)
        cum = ccol[chunk(i), :]
        keyed = (normed * spread(jnp.exp(cum[CHUNK - 1 :, :] - cum), lanes)).astype(bf16)
        for p in range(pairs):
            both = contract(keyed[:, pair_cut(p)], val[:, pair_cut(p)], 0, 0)
            fresh = jnp.where(low, both[:block], both[block:])
            enter_o[i, p * block : (p + 1) * block, :] = total[p]
            total[p] = total[p] * jnp.exp(ctl[i * pairs + p : i * pairs + p + 1, :]) + fresh
    logs = ctl[0:pairs, :]
    for i in range(1, chunks):
        logs = logs + ctl[i * pairs : (i + 1) * pairs, :]
    pay_o[...] = pack_state(jnp.concatenate(total, axis=0), logs, id_rows[...])


def state_rows(pairs, ids):
    return pairs * 64 + -(-(3 * pairs + ids) // 16) * 16


def pack_state(state, logs, id_rows):
    pairs, ids = logs.shape[0], id_rows.shape[0]
    pad = state_rows(pairs, ids) - state.shape[0] - 3 * pairs - ids
    parts = [state, *thirds(logs), id_rows] + [jnp.zeros((pad, LANES), f32)] * (pad > 0)
    return jnp.concatenate(parts, axis=0).astype(bf16)


def unpack_state(packed, pairs):
    whole = packed.astype(f32)
    rows = pairs * 64
    logs = whole[rows : rows + pairs]
    for k in (1, 2):
        logs = logs + whole[rows + k * pairs : rows + (k + 1) * pairs]
    return whole[:rows], logs, whole[rows + 3 * pairs :]


def row_factors(logs):
    factors = jnp.exp(logs)
    return jnp.concatenate(
        [jnp.broadcast_to(factors[p : p + 1], (64, LANES)) for p in range(logs.shape[0])], axis=0
    )


def join_kernel(bit, ids, pairs, sc, mine, got, *refs):
    pay_o, prefix_o, logs_o, ids_o = refs[-4:]
    upper = (sc[0] >> bit) & 1 == 1
    state, logs, rows = unpack_state(mine[...], pairs)
    other, other_logs, other_rows = unpack_state(got[...], pairs)
    early = jnp.where(upper, other, state)
    late = jnp.where(upper, state, other)
    factor = row_factors(jnp.where(upper, logs, other_logs))
    id_rows = jnp.concatenate([rows[:ids], other_rows[:ids]], axis=0)
    ids_o[...] = id_rows
    sent = id_rows if pay_o.shape[0] >= state_rows(pairs, 2 * ids) else id_rows[:1]
    pay_o[...] = pack_state(early * factor + late, logs + other_logs, sent)
    if bit == 0:
        prefix_o[...] = jnp.where(upper, other, 0.0)
        logs_o[...] = jnp.where(upper, other_logs, 0.0)
    else:
        prefix, prefix_logs = refs[0][...], refs[1][...]
        prefix_o[...] = jnp.where(upper, prefix + row_factors(prefix_logs) * other, prefix)
        logs_o[...] = jnp.where(upper, prefix_logs + other_logs, prefix_logs)


def local_kernel(first, emb, key, val, crow, ccol, weight, query_o, intra_o):
    n, width = query_o.shape
    heads = ccol.shape[1] // 2
    ones, lanes = same_head(), head_spread(heads, first // 64, width // 64)
    mask_a, mask_b = half_masks()
    causal = iota((CHUNK, CHUNK), 0) >= iota((CHUNK, CHUNK), 1)

    def queries(i):
        query = dot(emb[chunk(i), :], weight[:, first : first + width])
        unit = lax.rsqrt(head_means(query, ones) + 1e-06) * 0.125
        query = query * unit
        decayed = query * spread(jnp.exp(ccol[chunk(i), :]), lanes)
        query_o[chunk(i), :] = decayed.astype(bf16)
        return query.astype(bf16)

    def scores(i, p, b, query):
        cut = pair_cut(p)
        wide = slice(first + p * LANES, first + (p + 1) * LANES)
        return contract(query[:, cut] * (mask_b if b else mask_a), key[chunk(i), wide], 1, 1)

    units = [(i, p, b) for i in range(n // CHUNK) for p in range(width // LANES) for b in (0, 1)]
    query = {0: queries(0)}
    ready = scores(*units[0], query[0])
    held = None
    for u, (i, p, b) in enumerate(units):
        current = ready
        if u + 1 < len(units):
            j = units[u + 1][0]
            if j not in query:
                query[j] = queries(j)
            ready = scores(*units[u + 1], query[j])
        h = first // 64 + 2 * p + b
        gap = ccol[chunk(i), h : h + 1] - crow[i, h : h + 1, :]
        weights = jnp.where(causal, current * jnp.exp(gap), 0.0).astype(bf16)
        wide = slice(first + p * LANES, first + (p + 1) * LANES)
        part = dot(weights, val[chunk(i), wide] * (mask_b if b else mask_a))
        if b == 0:
            held = part
        else:
            intra_o[chunk(i), pair_cut(p)] = held + part


def candidate_kernel(order, owned, sc, id_rows, stored, own, peer, query_w, pair_w, query_o, val_w_o):
    half, width = own.shape
    ids = id_rows[...]
    ids = (ids * float(LANES) + pltpu.roll(ids, LANES // 2, 1)).astype(i32)
    slots = [stored_slots(ids[j : j + 1], stored[...]) for j in order]
    step = max(1, LANES // owned)
    tiles = []
    for start in range(0, len(order), step):
        tile = slots[start]
        for k in range(1, min(step, len(order) - start)):
            moved = pltpu.roll(slots[start + k], k * owned, 1)
            tile = jnp.where(iota((1, LANES), 1) >= k * owned, moved, tile)
        tiles.append(tile)
    slots = jnp.concatenate(tiles, axis=1)
    for c in range(0, slots.shape[1], CHUNK):
        some = slots[:, c : c + CHUNK]
        rows = picked_rows(some, sc[3] * half, own) + picked_rows(some, (1 - sc[3]) * half, peer)
        query = dot(rows.astype(bf16), query_w[...])
        query_o[:, c : c + CHUNK] = jnp.transpose(query).astype(bf16)
    val_w_o[...] = jnp.transpose(pair_w[:, width:].astype(f32)).astype(bf16)


def attend(sc, scale, query, first, cols, key, val, emit):
    n, width = key.shape
    blocks = range(0, n, KEYS)

    def padded(h):
        rows = query[h * 64 : (h + 1) * 64, first : first + cols]
        zero = jnp.zeros_like(rows)
        return jnp.concatenate([zero, rows] if h % 2 else [rows, zero], axis=0)

    def scores(h, block, weights):
        rows = slice(block, block + KEYS)
        values = dot(key[rows, pair_cut(h // 2)], weights)
        alive = sc[1] + block + iota((KEYS, 1), 0) < sc[2]
        return jnp.where(alive, values, DEAD)

    def store(h, block, weights, buffer, peak):
        values = scores(h, block, weights)
        buffer[block : block + KEYS, :] = values
        top = jnp.max(values.reshape(KEYS // 8, 8, cols), axis=0)
        return top if peak is None else jnp.maximum(peak, top)

    def run(buffers):
        ones = jnp.ones((16, KEYS), bf16)
        peak, weights = None, padded(0)
        for block in blocks:
            peak = store(0, block, weights, buffers[0], peak)
        for h in range(width // 64):
            factor = scale[h] * LOG2E
            peak = jnp.max(peak, axis=0, keepdims=True)
            following = None
            more = h + 1 < width // 64
            weights = padded(h + 1) if more else None
            sums = None
            for block in blocks:
                if more:
                    following = store(h + 1, block, weights, buffers[(h + 1) % 2], following)
                gap = buffers[h % 2][block : block + KEYS, :] - peak
                probs = jnp.exp2(gap * factor).astype(bf16)
                side = jnp.concatenate(
                    [val[h * 64 : (h + 1) * 64, block : block + KEYS], ones], axis=0
                )
                part = dot(side, probs)
                sums = part if sums is None else sums + part
            total = sums[64:65]
            emit(h, sums[:64] / total, peak * factor + jnp.log2(total))
            peak = following

    return run


def finish_kernel(
    bit, sc, scale, emb, query_a, query_b, intra_a, intra_b, enter, ctl, got, prefix, prefix_logs,
    out_w, pair_w, val_w, cand_q, hist_o, key_o, val_o, pay_o, *buffers,
):
    n, width = emb.shape
    pairs = width // LANES
    ones = same_head()
    upper = (sc[0] >> bit) & 1 == 1
    state = unpack_state(got[...], pairs)[0]
    before, before_logs = prefix[...], prefix_logs[...]
    entering = jnp.where(upper, before + row_factors(before_logs) * state, before)
    lane = iota((1, 2 * LANES), 1) // 64
    chunks = n // CHUNK
    gone = [jnp.zeros((pairs, LANES), f32)]
    for i in range(chunks - 1):
        gone.append(gone[-1] + ctl[i * pairs : (i + 1) * pairs, :])

    def normed(i):
        states = enter[i] + row_factors(gone[i]) * entering
        parts = []
        for p in range(0, pairs, 2):
            wide = jnp.concatenate(
                [states[p * 64 : (p + 1) * 64], states[(p + 1) * 64 : (p + 2) * 64]], axis=1
            )
            matrix = jnp.concatenate([jnp.where(lane == k, wide, 0.0) for k in range(4)], axis=0)
            query, intra = (query_a, intra_a) if p < pairs // 2 else (query_b, intra_b)
            c = (p % (pairs // 2)) * LANES
            cut = slice(c, c + 2 * LANES)
            parts.append(dot(query[chunk(i), cut], matrix.astype(bf16)) + intra[chunk(i), cut])
        mixed = jnp.concatenate(parts, axis=1)
        return (mixed * lax.rsqrt(head_means(mixed, ones) + 1e-05)).astype(bf16)

    ready = normed(0)
    for i in range(chunks):
        current = ready
        if i + 1 < chunks:
            ready = normed(i + 1)
        hidden_sum = emb[chunk(i), :].astype(f32) + dot(current, out_w[...])
        alive = sc[1] + i * CHUNK + iota((CHUNK, 1), 0) < sc[2]
        hist_o[chunk(i), :] = jnp.where(alive, hidden_sum, 0.0)
        hidden = hidden_sum.astype(bf16)
        key_o[chunk(i), :] = dot(hidden, pair_w[:, :width]).astype(bf16)
        val_o[:, chunk(i)] = contract(val_w[...], hidden, 1, 1).astype(bf16)
    count = pay_o.shape[1]
    heads = width // 64
    any_alive = sc[1] < sc[2]
    log_rows = []

    def emit(h, attended, logs):
        pay_o[h * 64 : (h + 1) * 64, :] = attended.astype(bf16)
        log_rows.append(jnp.where(any_alive, logs, DEAD))

    attend(sc, scale, cand_q, count, count, key_o, val_o, emit)(buffers)
    pay_o[width:, :] = pack_logs(jnp.concatenate(log_rows, axis=0))


def pack_logs(logs):
    heads, cols = logs.shape
    return jnp.concatenate(
        [*thirds(logs), jnp.zeros((log_pad(heads) - 3 * heads, cols), f32)], axis=0
    ).astype(bf16)


def log_pad(heads):
    return -(-3 * heads // 16) * 16


def unpack_logs(rows, heads):
    rows = rows.astype(f32)
    return rows[:heads] + rows[heads : 2 * heads] + rows[2 * heads : 3 * heads]


def keep_kernel(sc, scale, cand_q, key, val, mean_o, logs_o, *buffers):
    any_alive = sc[1] < sc[2]

    def emit(h, attended, logs):
        mean_o[h * 64 : (h + 1) * 64, :] = attended
        logs_o[h : h + 1, :] = jnp.where(any_alive, logs, DEAD)

    attend(sc, scale, cand_q, 0, mean_o.shape[1], key, val, emit)(buffers)


def over_heads(rows):
    return jnp.concatenate(
        [jnp.broadcast_to(rows[h : h + 1], (64, rows.shape[1])) for h in range(rows.shape[0])],
        axis=0,
    )


def merge(parts):
    peak = parts[0][1]
    for _, logs in parts[1:]:
        peak = jnp.maximum(peak, logs)
    shares = [jnp.exp2(logs - peak) for _, logs in parts]
    total = sum(shares[1:], shares[0])
    mean = None
    for (value, _), share in zip(parts, shares):
        term = value * over_heads(share / total)
        mean = term if mean is None else mean + term
    return mean, peak + jnp.log2(total)


def received(got, heads):
    width = heads * 64
    return got[:width, :].astype(f32), unpack_logs(got[width:, :], heads)


def fold_kernel(mean, logs, got, mean_o, logs_o, pay_o):
    heads, keep = logs_o.shape
    width = heads * 64
    new_mean, new_logs = merge([(mean[...], logs[...]), received(got, heads)])
    mean_o[...] = new_mean[:, :keep]
    logs_o[...] = new_logs[:, :keep]
    pay_o[:width, :] = new_mean[:, keep:].astype(bf16)
    pay_o[width:, :] = pack_logs(new_logs[:, keep:])


def deal_kernel(mean, logs, got, mean_o, logs_o, *sends):
    heads, cols = logs_o.shape
    new_mean, new_logs = merge([(mean[...], logs[...]), received(got, heads)])
    mean_o[...] = new_mean[:, :cols]
    logs_o[...] = new_logs[:, :cols]
    whole = jnp.concatenate([new_mean, pack_logs(new_logs).astype(f32)], axis=0)
    owned = whole.shape[1] // 4
    half = whole.shape[0] // 2
    low = first_half((1, LANES))
    for k, send in enumerate(sends):
        start = (k + 1) * owned
        if 2 * owned == LANES:
            tile = whole[:, start // LANES * LANES : start // LANES * LANES + LANES]
            top, bottom = tile[:half], tile[half:]
            if start % LANES:
                top = pltpu.roll(top, owned, 1)
            else:
                bottom = pltpu.roll(bottom, owned, 1)
            send[...] = jnp.where(low, top, bottom).astype(bf16)
        else:
            send[...] = whole[:, start : start + owned].astype(bf16)


def last_kernel(owned, mean, logs, got_a, got_b, got_c, out_w, cand_o):
    heads = logs.shape[0]
    parts = [(mean[...], logs[...])]
    for got in (got_a, got_b, got_c):
        if 2 * owned == LANES:
            value = got[...].astype(f32)
            value = jnp.concatenate([value, pltpu.roll(value, owned, 1)], axis=0)
        else:
            value = got[...].astype(f32)
        parts.append((value[: heads * 64], unpack_logs(value[heads * 64 :], heads)))
    attended = merge(parts)[0].astype(bf16)
    cand_o[...] = contract(attended, out_w[...], 0, 0)[: cand_o.shape[0]]


def shape(dims, dtype):
    return jax.ShapeDtypeStruct(dims, dtype)


VMEM = pl.BlockSpec(memory_space=pltpu.VMEM)
SMEM = pl.BlockSpec(memory_space=pltpu.SMEM)
ANY = pl.BlockSpec(memory_space=pl.ANY)


def call(kernel, name, scalars, operands, outs, scratch=(), after=(), flops=0):
    count = len(scalars) + len(operands)

    def body(*refs):
        kernel(*refs[:count], *refs[count + len(after) :])

    return pl.pallas_call(
        body,
        name=name,
        in_specs=[SMEM] * len(scalars) + [VMEM] * len(operands) + [ANY] * len(after),
        out_specs=[VMEM] * len(outs),
        out_shape=outs,
        scratch_shapes=list(scratch),
        compiler_params=pltpu.CompilerParams(vmem_limit_bytes=VMEM_LIMIT),
        cost_estimate=pl.CostEstimate(flops=flops, transcendentals=0, bytes_accessed=0),
    )(*scalars, *operands, *after)


def reversed_bits(value, bits):
    return sum(((value >> b) & 1) << (bits - 1 - b) for b in range(bits))


def shards(
    history_item_index,
    log_head_retention,
    user_history_length,
    candidate_item_index,
    item_stored_row,
    item_embedding_table,
    head_score_scale,
    history_query_key_value_weight,
    history_output_weight,
    candidate_key_value_weight,
    candidate_query_weight,
    candidate_output_weight,
):
    users, n = history_item_index.shape
    heads = log_head_retention.shape[1]
    half, width = item_embedding_table.shape
    owned = candidate_item_index.shape[1]
    seq = lax.axis_size("seq")
    bits = seq.bit_length() - 1
    assert users == 1 and lax.axis_size("dp") == 2 and seq == 1 << bits and bits > 2
    assert width == heads * 64 and heads % 4 == 0 and owned <= 64
    pairs = heads // 2
    rows = pairs * 64
    cands = owned * seq
    rank = lax.axis_index("seq")

    def swap(value, mask):
        return lax.ppermute(value, "seq", [(j, j ^ mask) for j in range(seq)])

    peer = lax.ppermute(item_embedding_table, "dp", [(0, 1), (1, 0)])
    far_ids = swap(candidate_item_index, seq // 2)
    sc = jnp.stack(
        [rank, rank * n, user_history_length[0], lax.axis_index("dp")]
    ).astype(i32)
    stored = item_stored_row.reshape(-1, LANES)
    decay = log_head_retention.reshape(heads, n)
    ids = jnp.concatenate([candidate_item_index, far_ids], axis=0)
    ids = jnp.pad(ids, ((0, 0), (0, 64 - owned)))
    id_rows = jnp.concatenate([ids // LANES, ids % LANES], axis=1).astype(f32)

    part, slot, crow, ccol, ctl = call(
        own_rows_kernel, "own_rows", [sc],
        [history_item_index, stored, decay, item_embedding_table],
        [
            shape((n, width), bf16), shape((1, n), f32), shape((n // CHUNK, heads, CHUNK), f32),
            shape((n, 2 * heads), f32), shape((n // CHUNK * pairs, LANES), f32),
        ],
        flops=2 * n * half * width,
    )
    emb, key, val, enter, pay = call(
        summary_kernel, "summary", [sc],
        [part, peer, slot, ccol, ctl, id_rows, history_query_key_value_weight],
        [
            shape((n, width), bf16), shape((n, width), bf16), shape((n, width), bf16),
            shape((n // CHUNK, rows, LANES), f32), shape((state_rows(pairs, 2), LANES), bf16),
        ],
        flops=2 * n * half * width,
    )

    def local(first, name, after):
        return call(
            lambda *refs: local_kernel(first, *refs), name, [],
            [emb, key, val, crow, ccol, history_query_key_value_weight],
            [shape((n, width // 2), bf16), shape((n, width // 2), f32)],
            after=after, flops=2 * n * half * width // 2,
        )

    early = [local(0, "local_a", [])]
    prefix = logs = None
    for bit in range(bits - 1):
        got = swap(pay, 1 << bit)
        if bit == 1:
            early.append(local(width // 2, "local_b", [prefix]))
        count = 2 << bit
        sent = 2 * count if bit < bits - 2 else 1
        pay, prefix, logs, id_rows = call(
            lambda *refs, bit=bit, count=count: join_kernel(bit, count, pairs, *refs), "join", [sc],
            [pay, got] + ([prefix, logs] if bit else []),
            [
                shape((state_rows(pairs, sent), LANES), bf16), shape((rows, LANES), f32),
                shape((pairs, LANES), f32), shape((2 * count, LANES), f32),
            ],
            after=[early[-1][1]],
        )
    got = swap(pay, 1 << (bits - 1))
    half_seq = seq // 2
    places = {}
    for j in range(seq):
        places[(j & 1) * half_seq + (j >> 1)] = j
    order = [places[reversed_bits(j, bits)] for j in range(seq)]
    cand_q, val_w = call(
        lambda *refs: candidate_kernel(order, owned, *refs), "candidates", [sc],
        [
            id_rows, stored, item_embedding_table, peer, candidate_query_weight,
            candidate_key_value_weight,
        ],
        [shape((width, cands), bf16), shape((width, width), bf16)],
        flops=2 * cands * 2 * half * width,
    )
    (query_a, intra_a), (query_b, intra_b) = early
    send = cands // 2
    buffers = [pltpu.VMEM((n, send), f32)] * 2
    message = width + log_pad(heads)
    hist, key_two, val_two, pay = call(
        lambda *refs: finish_kernel(bits - 1, *refs), "finish", [sc, head_score_scale],
        [
            emb, query_a, query_b, intra_a, intra_b, enter, ctl, got, prefix, logs,
            history_output_weight, candidate_key_value_weight, val_w, cand_q,
        ],
        [
            shape((n, width), f32), shape((n, width), bf16), shape((width, n), bf16),
            shape((message, send), bf16),
        ],
        buffers,
        flops=2 * n * half * width,
    )
    mean, logs = call(
        keep_kernel, "keep", [sc, head_score_scale], [cand_q, key_two, val_two],
        [shape((width, send), f32), shape((heads, send), f32)],
        buffers,
        flops=2 * n * half * width,
    )
    for bit in range(bits - 3):
        got = swap(pay, 1 << bit)
        send //= 2
        mean, logs, pay = call(
            fold_kernel, "fold", [], [mean, logs, got],
            [shape((width, send), f32), shape((heads, send), f32), shape((message, send), bf16)],
        )
    got = swap(pay, 1 << (bits - 3))
    packed = 2 * owned == LANES
    cols = LANES if packed else owned
    mean, logs, *sends = call(
        deal_kernel, "deal", [], [mean, logs, got],
        [shape((width, cols), f32), shape((heads, cols), f32)]
        + [shape((message // 2, LANES) if packed else (message, owned), bf16)] * 3,
    )
    masks = [seq // 2, seq // 4, seq // 2 + seq // 4]
    gots = [swap(value, mask) for value, mask in zip(sends, masks)]
    (cand_out,) = call(
        lambda *refs: last_kernel(owned, *refs), "last", [],
        [mean, logs, *gots, candidate_output_weight],
        [shape((owned, width), f32)],
    )
    return hist[None], cand_out[None]


def solution(mesh):
    in_specs = (
        P(("groups", "dp"), "seq"),
        P(("groups", "dp"), None, "seq"),
        P(("groups", "dp")),
        P(("groups", "dp"), "seq"),
        P(),
        P("dp", None),
        P(),
        P(),
        P(),
        P(),
        P(),
        P(),
    )
    out_specs = (P(("groups", "dp"), "seq", None), P(("groups", "dp"), "seq", None))
    return jax.shard_map(shards, mesh=mesh, in_specs=in_specs, out_specs=out_specs, check_vma=False)
```

```python
import math

import jax
import jax.numpy as jnp
from jax import lax
from jax.experimental import pallas as pl
from jax.experimental.pallas import tpu as pltpu
from jax.sharding import PartitionSpec as P

f32, bf16, i32 = jnp.float32, jnp.bfloat16, jnp.int32
CHUNK = 256
KEYS = 512
LANES = 128
LOG2E = math.log2(math.e)
DEAD = -1e30
VMEM_LIMIT = 40 << 20


def dot(a, b):
    return jnp.dot(a, b, preferred_element_type=f32)


def contract(a, b, left, right):
    return lax.dot_general(a, b, (((left,), (right,)), ((), ())), preferred_element_type=f32)


def iota(shape, axis):
    return lax.broadcasted_iota(i32, shape, axis)


def thirds(value):
    high = value.astype(bf16).astype(f32)
    rest = value - high
    mid = rest.astype(bf16).astype(f32)
    return high, mid, rest - mid


def first_half(shape):
    return iota(shape, len(shape) - 1) % LANES < LANES // 2


def half_masks():
    low = first_half((1, LANES))
    return jnp.where(low, 1.0, 0.0).astype(bf16), jnp.where(low, 0.0, 1.0).astype(bf16)


def same_head():
    dims = (2 * LANES, 2 * LANES)
    return jnp.where(iota(dims, 0) // 64 == iota(dims, 1) // 64, 1.0, 0.0).astype(bf16)


def head_means(value, ones):
    square = (value * value).astype(bf16)
    step = ones.shape[0]
    parts = [dot(square[:, c : c + step], ones) for c in range(0, value.shape[1], step)]
    return jnp.concatenate(parts, axis=1) * (1.0 / 64.0)


def head_spread(heads, first, count):
    dims = (2 * heads, 64 * count)
    return jnp.where(iota(dims, 1) // 64 + first == iota(dims, 0) % heads, 1.0, 0.0).astype(bf16)


def spread(value, matrix):
    heads = value.shape[1] // 2
    high = value.astype(bf16).astype(f32)
    both = jnp.where(iota(value.shape, 1) < heads, high, value - high)
    return dot(both.astype(bf16), matrix)


def stored_slots(ids, stored):
    groups = stored.shape[0]
    n = ids.shape[1]
    pick = jnp.where(iota((groups, n), 0) == ids // LANES, 1.0, 0.0).astype(bf16)
    high = contract((stored // 64).astype(f32).astype(bf16), pick, 0, 0)
    low = contract((stored % 64).astype(f32).astype(bf16), pick, 0, 0)
    rows = jnp.where(iota((LANES, n), 0) == ids % LANES, high * 64.0 + low, 0.0)
    return jnp.sum(rows, axis=0, keepdims=True)


def picked_rows(slots, first, table):
    count = table.shape[0]
    hot = jnp.where(iota((count, slots.shape[1]), 0) == slots.astype(i32) - first, 1.0, 0.0)
    return contract(hot.astype(bf16), table[...], 0, 0)


def chunk(i):
    return slice(i * CHUNK, (i + 1) * CHUNK)


def pair_cut(p):
    return slice(p * LANES, (p + 1) * LANES)


def own_rows_kernel(
    ids_in, stored_in, decay_in, own_in, part_o, slot_o, crow_o, ccol_o, ctl_o,
    ids, stored, decay, own, sem,
):
    n, half, heads = ids.shape[1], own.shape[0], decay.shape[0]
    copies = [
        pltpu.make_async_copy(source, target, sem.at[k])
        for k, (source, target) in enumerate(
            ((ids_in, ids), (stored_in, stored), (decay_in, decay), (own_in, own))
        )
    ]
    for copy in copies:
        copy.start()
    copies[0].wait()
    copies[1].wait()
    slots = stored_slots(ids[...], stored[...])
    slot_o[...] = slots
    copies[2].wait()
    upto = jnp.where(
        iota((CHUNK, CHUNK), 0) <= iota((CHUNK, CHUNK), 1), 1.0, 0.0
    ).astype(bf16)
    low = first_half((1, LANES))
    for i in range(n // CHUNK):
        pieces = jnp.concatenate(thirds(decay[:, chunk(i)]), axis=0)
        sums = dot(pieces.astype(bf16), upto)
        cum = sums[:heads] + sums[heads : 2 * heads] + sums[2 * heads :]
        crow_o[i] = cum
        ccol_o[chunk(i), :] = jnp.transpose(jnp.concatenate([cum, cum], axis=0))
        for p in range(heads // 2):
            r = i * (heads // 2) + p
            ctl_o[r : r + 1, :] = jnp.where(
                low, cum[2 * p : 2 * p + 1, CHUNK - 1 :], cum[2 * p + 1 : 2 * p + 2, CHUNK - 1 :]
            )
    copies[3].wait()
    first = lax.axis_index("dp") * half
    for i in range(n // CHUNK):
        part_o[chunk(i), :] = picked_rows(slots[:, chunk(i)], first, own).astype(bf16)


def summary_kernel(
    length, part, peer, slot, ccol, ctl, id_rows, weight, emb_o, key_o, val_o, enter_o, pay_o
):
    n, width = part.shape
    half, heads = peer.shape[0], ccol.shape[1] // 2
    pairs = heads // 2
    block = LANES // 2
    ones, lanes = same_head(), head_spread(heads, 0, heads)
    low = first_half((1, LANES))
    chunks = n // CHUNK

    def project(i):
        other = picked_rows(slot[:, chunk(i)], (1 - lax.axis_index("dp")) * half, peer)
        emb = (part[chunk(i), :].astype(f32) + other).astype(bf16)
        emb_o[chunk(i), :] = emb
        return dot(emb, weight[:, width : 2 * width]), dot(emb, weight[:, 2 * width :])

    total = [jnp.zeros((block, LANES), f32)] * pairs
    ready = project(0)
    for i in range(chunks):
        key, val = ready
        if i + 1 < chunks:
            ready = project(i + 1)
        alive = iota((CHUNK, 1), 0) < length[0] - lax.axis_index("seq") * n - i * CHUNK
        val = jnp.where(alive, val, 0.0).astype(bf16)
        val_o[chunk(i), :] = val
        unit = lax.rsqrt(head_means(key, ones) + 1e-06) * 0.125
        normed = jnp.where(alive, key * unit, 0.0)
        key_o[chunk(i), :] = normed.astype(bf16)
        cum = ccol[chunk(i), :]
        keyed = (normed * spread(jnp.exp(cum[CHUNK - 1 :, :] - cum), lanes)).astype(bf16)
        for p in range(pairs):
            both = contract(keyed[:, pair_cut(p)], val[:, pair_cut(p)], 0, 0)
            fresh = jnp.where(low, both[:block], both[block:])
            enter_o[i, p * block : (p + 1) * block, :] = total[p]
            total[p] = total[p] * jnp.exp(ctl[i * pairs + p : i * pairs + p + 1, :]) + fresh
    logs = ctl[0:pairs, :]
    for i in range(1, chunks):
        logs = logs + ctl[i * pairs : (i + 1) * pairs, :]
    pay_o[...] = pack_state(jnp.concatenate(total, axis=0), logs, id_rows[...])


def state_rows(pairs, ids):
    return pairs * 64 + -(-(3 * pairs + ids) // 16) * 16


def pack_state(state, logs, id_rows):
    pairs, ids = logs.shape[0], id_rows.shape[0]
    pad = state_rows(pairs, ids) - state.shape[0] - 3 * pairs - ids
    parts = [state, *thirds(logs), id_rows] + [jnp.zeros((pad, LANES), f32)] * (pad > 0)
    return jnp.concatenate(parts, axis=0).astype(bf16)


def unpack_state(packed, pairs):
    whole = packed.astype(f32)
    rows = pairs * 64
    logs = whole[rows : rows + pairs]
    for k in (1, 2):
        logs = logs + whole[rows + k * pairs : rows + (k + 1) * pairs]
    return whole[:rows], logs, whole[rows + 3 * pairs :]


def row_factors(logs):
    factors = jnp.exp(logs)
    return jnp.concatenate(
        [jnp.broadcast_to(factors[p : p + 1], (64, LANES)) for p in range(logs.shape[0])], axis=0
    )


def join_kernel(bit, ids, pairs, mine, got, *refs):
    before = refs[: 2 if bit else 0]
    pay_o, prefix_o, logs_o, *ids_o = refs[len(before) :]
    upper = (lax.axis_index("seq") >> bit) & 1 == 1
    state, logs, rows = unpack_state(mine[...], pairs)
    other, other_logs, other_rows = unpack_state(got[...], pairs)
    early = jnp.where(upper, other, state)
    late = jnp.where(upper, state, other)
    factor = row_factors(jnp.where(upper, logs, other_logs))
    id_rows = jnp.concatenate([rows[:ids], other_rows[:ids]], axis=0)
    if ids_o:
        ids_o[0][...] = id_rows
    pay_o[...] = pack_state(
        early * factor + late, logs + other_logs, id_rows[:1] if ids_o else id_rows
    )
    if bit == 0:
        prefix_o[...] = jnp.where(upper, other, 0.0)
        logs_o[...] = jnp.where(upper, other_logs, 0.0)
    else:
        prefix, prefix_logs = before[0][...], before[1][...]
        prefix_o[...] = jnp.where(upper, prefix + row_factors(prefix_logs) * other, prefix)
        logs_o[...] = jnp.where(upper, prefix_logs + other_logs, prefix_logs)


def local_kernel(first, emb, key, val, crow, ccol, weight, query_o, intra_o):
    n, width = query_o.shape
    heads = ccol.shape[1] // 2
    ones, lanes = same_head(), head_spread(heads, first // 64, width // 64)
    mask_a, mask_b = half_masks()
    causal = iota((CHUNK, CHUNK), 0) >= iota((CHUNK, CHUNK), 1)

    def queries(i):
        query = dot(emb[chunk(i), :], weight[:, first : first + width])
        unit = lax.rsqrt(head_means(query, ones) + 1e-06) * 0.125
        query = query * unit
        decayed = query * spread(jnp.exp(ccol[chunk(i), :]), lanes)
        query_o[chunk(i), :] = decayed.astype(bf16)
        return query.astype(bf16)

    def scores(i, p, b, query):
        cut = pair_cut(p)
        wide = slice(first + p * LANES, first + (p + 1) * LANES)
        return contract(query[:, cut] * (mask_b if b else mask_a), key[chunk(i), wide], 1, 1)

    units = [(i, p, b) for i in range(n // CHUNK) for p in range(width // LANES) for b in (0, 1)]
    query = {0: queries(0)}
    ready = scores(*units[0], query[0])
    held = None
    for u, (i, p, b) in enumerate(units):
        current = ready
        if u + 1 < len(units):
            j = units[u + 1][0]
            if j not in query:
                query[j] = queries(j)
            ready = scores(*units[u + 1], query[j])
        h = first // 64 + 2 * p + b
        gap = ccol[chunk(i), h : h + 1] - crow[i, h : h + 1, :]
        weights = jnp.where(causal, current * jnp.exp(gap), 0.0).astype(bf16)
        wide = slice(first + p * LANES, first + (p + 1) * LANES)
        part = dot(weights, val[chunk(i), wide] * (mask_b if b else mask_a))
        if b == 0:
            held = part
        else:
            intra_o[chunk(i), pair_cut(p)] = held + part


def candidate_kernel(order, owned, id_rows, stored, own, peer, query_w, pair_w, query_o, val_w_o):
    half, width = own.shape
    ids = id_rows[...]
    ids = (ids * float(LANES) + pltpu.roll(ids, LANES // 2, 1)).astype(i32)
    slots = [stored_slots(ids[j : j + 1], stored[...]) for j in order]
    step = max(1, LANES // owned)
    tiles = []
    for start in range(0, len(order), step):
        tile = slots[start]
        for k in range(1, min(step, len(order) - start)):
            moved = pltpu.roll(slots[start + k], k * owned, 1)
            tile = jnp.where(iota((1, LANES), 1) >= k * owned, moved, tile)
        tiles.append(tile)
    slots = jnp.concatenate(tiles, axis=1)
    for c in range(0, slots.shape[1], CHUNK):
        some = slots[:, c : c + CHUNK]
        dp = lax.axis_index("dp")
        rows = picked_rows(some, dp * half, own) + picked_rows(some, (1 - dp) * half, peer)
        query = dot(rows.astype(bf16), query_w[...])
        query_o[:, c : c + CHUNK] = jnp.transpose(query).astype(bf16)
    val_w_o[...] = jnp.transpose(pair_w[:, width:].astype(f32)).astype(bf16)


def attend(alive_count, scale, query, first, cols, key, val, emit):
    n, width = key.shape
    blocks = range(0, n, KEYS)

    def padded(h):
        rows = query[h * 64 : (h + 1) * 64, first : first + cols]
        zero = jnp.zeros_like(rows)
        return jnp.concatenate([zero, rows] if h % 2 else [rows, zero], axis=0)

    def scores(h, block, weights):
        rows = slice(block, block + KEYS)
        values = dot(key[rows, pair_cut(h // 2)], weights)
        alive = iota((KEYS, 1), 0) < alive_count - block
        return jnp.where(alive, values, DEAD)

    def store(h, block, weights, buffer, peak):
        values = scores(h, block, weights)
        buffer[block : block + KEYS, :] = values
        top = jnp.max(values.reshape(KEYS // 8, 8, cols), axis=0)
        return top if peak is None else jnp.maximum(peak, top)

    def run(buffers):
        ones = jnp.ones((16, KEYS), bf16)
        peak, weights = None, padded(0)
        for block in blocks:
            peak = store(0, block, weights, buffers[0], peak)
        for h in range(width // 64):
            factor = scale[h] * LOG2E
            peak = jnp.max(peak, axis=0, keepdims=True)
            following = None
            more = h + 1 < width // 64
            weights = padded(h + 1) if more else None
            sums = None
            for block in blocks:
                if more:
                    following = store(h + 1, block, weights, buffers[(h + 1) % 2], following)
                gap = buffers[h % 2][block : block + KEYS, :] - peak
                probs = jnp.exp2(gap * factor).astype(bf16)
                side = jnp.concatenate(
                    [val[h * 64 : (h + 1) * 64, block : block + KEYS], ones], axis=0
                )
                part = dot(side, probs)
                sums = part if sums is None else sums + part
            total = sums[64:65]
            emit(h, sums[:64] / total, peak * factor + jnp.log2(total))
            peak = following

    return run


def finish_kernel(
    bit, length, scale, emb, query_a, query_b, intra_a, intra_b, enter, ctl, got, prefix, prefix_logs,
    out_w, pair_w, val_w, cand_q, hist_o, key_o, val_o, pay_o, *buffers,
):
    n, width = emb.shape
    pairs = width // LANES
    ones = same_head()
    upper = (lax.axis_index("seq") >> bit) & 1 == 1
    state = unpack_state(got[...], pairs)[0]
    before, before_logs = prefix[...], prefix_logs[...]
    entering = jnp.where(upper, before + row_factors(before_logs) * state, before)
    lane = iota((1, 2 * LANES), 1) // 64
    chunks = n // CHUNK
    gone = [jnp.zeros((pairs, LANES), f32)]
    for i in range(chunks - 1):
        gone.append(gone[-1] + ctl[i * pairs : (i + 1) * pairs, :])

    def normed(i):
        states = enter[i] + row_factors(gone[i]) * entering
        parts = []
        for p in range(0, pairs, 2):
            wide = jnp.concatenate(
                [states[p * 64 : (p + 1) * 64], states[(p + 1) * 64 : (p + 2) * 64]], axis=1
            )
            matrix = jnp.concatenate([jnp.where(lane == k, wide, 0.0) for k in range(4)], axis=0)
            query, intra = (query_a, intra_a) if p < pairs // 2 else (query_b, intra_b)
            c = (p % (pairs // 2)) * LANES
            cut = slice(c, c + 2 * LANES)
            parts.append(dot(query[chunk(i), cut], matrix.astype(bf16)) + intra[chunk(i), cut])
        mixed = jnp.concatenate(parts, axis=1)
        return (mixed * lax.rsqrt(head_means(mixed, ones) + 1e-05)).astype(bf16)

    ready = normed(0)
    for i in range(chunks):
        current = ready
        if i + 1 < chunks:
            ready = normed(i + 1)
        hidden_sum = emb[chunk(i), :].astype(f32) + dot(current, out_w[...])
        alive = iota((CHUNK, 1), 0) < length[0] - lax.axis_index("seq") * n - i * CHUNK
        hist_o[chunk(i), :] = jnp.where(alive, hidden_sum, 0.0)
        hidden = hidden_sum.astype(bf16)
        key_o[chunk(i), :] = dot(hidden, pair_w[:, :width]).astype(bf16)
        val_o[:, chunk(i)] = contract(val_w[...], hidden, 1, 1).astype(bf16)
    count = pay_o.shape[1]
    heads = width // 64
    alive_count = length[0] - lax.axis_index("seq") * n
    log_rows = []

    def emit(h, attended, logs):
        pay_o[h * 64 : (h + 1) * 64, :] = attended.astype(bf16)
        log_rows.append(jnp.where(alive_count > 0, logs, DEAD))

    attend(alive_count, scale, cand_q, count, count, key_o, val_o, emit)(buffers)
    pay_o[width:, :] = pack_logs(jnp.concatenate(log_rows, axis=0))


def pack_logs(logs):
    heads, cols = logs.shape
    return jnp.concatenate(
        [*thirds(logs), jnp.zeros((log_pad(heads) - 3 * heads, cols), f32)], axis=0
    ).astype(bf16)


def log_pad(heads):
    return -(-3 * heads // 16) * 16


def unpack_logs(rows, heads):
    rows = rows.astype(f32)
    return rows[:heads] + rows[heads : 2 * heads] + rows[2 * heads : 3 * heads]


def keep_kernel(length, scale, cand_q, key, val, mean_o, logs_o, *buffers):
    alive_count = length[0] - lax.axis_index("seq") * key.shape[0]

    def emit(h, attended, logs):
        mean_o[h * 64 : (h + 1) * 64, :] = attended
        logs_o[h : h + 1, :] = jnp.where(alive_count > 0, logs, DEAD)

    attend(alive_count, scale, cand_q, 0, mean_o.shape[1], key, val, emit)(buffers)


def over_heads(rows):
    return jnp.concatenate(
        [jnp.broadcast_to(rows[h : h + 1], (64, rows.shape[1])) for h in range(rows.shape[0])],
        axis=0,
    )


def merge(parts):
    peak = parts[0][1]
    for _, logs in parts[1:]:
        peak = jnp.maximum(peak, logs)
    shares = [jnp.exp2(logs - peak) for _, logs in parts]
    total = sum(shares[1:], shares[0])
    mean = None
    for (value, _), share in zip(parts, shares):
        term = value * over_heads(share / total)
        mean = term if mean is None else mean + term
    return mean, peak + jnp.log2(total)


def received(got, heads):
    width = heads * 64
    return got[:width, :].astype(f32), unpack_logs(got[width:, :], heads)


def fold_kernel(mean, logs, got, mean_o, logs_o, pay_o):
    heads, keep = logs_o.shape
    width = heads * 64
    new_mean, new_logs = merge([(mean[...], logs[...]), received(got, heads)])
    mean_o[...] = new_mean[:, :keep]
    logs_o[...] = new_logs[:, :keep]
    pay_o[:width, :] = new_mean[:, keep:].astype(bf16)
    pay_o[width:, :] = pack_logs(new_logs[:, keep:])


def deal_kernel(mean, logs, got, mean_o, logs_o, *sends):
    heads, cols = logs_o.shape
    new_mean, new_logs = merge([(mean[...], logs[...]), received(got, heads)])
    mean_o[...] = new_mean[:, :cols]
    logs_o[...] = new_logs[:, :cols]
    whole = jnp.concatenate([new_mean, pack_logs(new_logs).astype(f32)], axis=0)
    owned = whole.shape[1] // 4
    half = whole.shape[0] // 2
    low = first_half((1, LANES))
    for k, send in enumerate(sends):
        start = (k + 1) * owned
        if 2 * owned == LANES:
            tile = whole[:, start // LANES * LANES : start // LANES * LANES + LANES]
            top, bottom = tile[:half], tile[half:]
            if start % LANES:
                top = pltpu.roll(top, owned, 1)
            else:
                bottom = pltpu.roll(bottom, owned, 1)
            send[...] = jnp.where(low, top, bottom).astype(bf16)
        else:
            send[...] = whole[:, start : start + owned].astype(bf16)


def last_kernel(owned, mean, logs, got_a, got_b, got_c, out_w, cand_o):
    heads = logs.shape[0]
    parts = [(mean[...], logs[...])]
    for got in (got_a, got_b, got_c):
        if 2 * owned == LANES:
            value = got[...].astype(f32)
            value = jnp.concatenate([value, pltpu.roll(value, owned, 1)], axis=0)
        else:
            value = got[...].astype(f32)
        parts.append((value[: heads * 64], unpack_logs(value[heads * 64 :], heads)))
    attended = merge(parts)[0].astype(bf16)
    cand_o[...] = contract(attended, out_w[...], 0, 0)[: cand_o.shape[0]]


def shape(dims, dtype):
    return jax.ShapeDtypeStruct(dims, dtype)


VMEM = pl.BlockSpec(memory_space=pltpu.VMEM)
SMEM = pl.BlockSpec(memory_space=pltpu.SMEM)
ANY = pl.BlockSpec(memory_space=pl.ANY)


def call(kernel, name, scalars, operands, outs, scratch=(), after=(), flops=0, space=VMEM):
    count = len(scalars) + len(operands)

    def body(*refs):
        kernel(*refs[:count], *refs[count + len(after) :])

    return pl.pallas_call(
        body,
        name=name,
        in_specs=[SMEM] * len(scalars) + [space] * len(operands) + [ANY] * len(after),
        out_specs=[VMEM] * len(outs),
        out_shape=outs,
        scratch_shapes=list(scratch),
        compiler_params=pltpu.CompilerParams(vmem_limit_bytes=VMEM_LIMIT),
        cost_estimate=pl.CostEstimate(flops=flops, transcendentals=0, bytes_accessed=0),
    )(*scalars, *operands, *after)


def reversed_bits(value, bits):
    return sum(((value >> b) & 1) << (bits - 1 - b) for b in range(bits))


def shards(
    history_item_index,
    log_head_retention,
    user_history_length,
    candidate_item_index,
    item_stored_row,
    item_embedding_table,
    head_score_scale,
    history_query_key_value_weight,
    history_output_weight,
    candidate_key_value_weight,
    candidate_query_weight,
    candidate_output_weight,
):
    users, n = history_item_index.shape
    heads = log_head_retention.shape[1]
    half, width = item_embedding_table.shape
    owned = candidate_item_index.shape[1]
    seq = lax.axis_size("seq")
    bits = seq.bit_length() - 1
    assert users == 1 and lax.axis_size("dp") == 2 and seq == 1 << bits and bits > 2
    assert width == heads * 64 and heads % 4 == 0 and owned <= 64
    pairs = heads // 2
    rows = pairs * 64
    cands = owned * seq

    def swap(value, mask):
        return lax.ppermute(value, "seq", [(j, j ^ mask) for j in range(seq)])

    peer = lax.ppermute(item_embedding_table, "dp", [(0, 1), (1, 0)])
    far_ids = swap(candidate_item_index, seq // 2)
    stored = item_stored_row.reshape(-1, LANES)
    decay = log_head_retention.reshape(heads, n)
    ids = jnp.concatenate([candidate_item_index, far_ids], axis=0)
    ids = jnp.pad(ids, ((0, 0), (0, 64 - owned)))
    id_rows = jnp.concatenate([ids // LANES, ids % LANES], axis=1).astype(f32)

    part, slot, crow, ccol, ctl = call(
        own_rows_kernel, "own_rows", [],
        [history_item_index, stored, decay, item_embedding_table],
        [
            shape((n, width), bf16), shape((1, n), f32), shape((n // CHUNK, heads, CHUNK), f32),
            shape((n, 2 * heads), f32), shape((n // CHUNK * pairs, LANES), f32),
        ],
        [
            pltpu.VMEM((1, n), i32), pltpu.VMEM(stored.shape, i32), pltpu.VMEM((heads, n), f32),
            pltpu.VMEM((half, width), bf16), pltpu.SemaphoreType.DMA((4,)),
        ],
        space=ANY,
        flops=2 * n * half * width,
    )
    emb, key, val, enter, pay = call(
        summary_kernel, "summary", [user_history_length],
        [part, peer, slot, ccol, ctl, id_rows, history_query_key_value_weight],
        [
            shape((n, width), bf16), shape((n, width), bf16), shape((n, width), bf16),
            shape((n // CHUNK, rows, LANES), f32), shape((state_rows(pairs, 2), LANES), bf16),
        ],
        flops=2 * n * half * width,
    )

    def local(first, name, after):
        return call(
            lambda *refs: local_kernel(first, *refs), name, [],
            [emb, key, val, crow, ccol, history_query_key_value_weight],
            [shape((n, width // 2), bf16), shape((n, width // 2), f32)],
            after=after, flops=2 * n * half * width // 2,
        )

    early = [local(0, "local_a", [])]
    prefix = logs = None
    for bit in range(bits - 1):
        got = swap(pay, 1 << bit)
        if bit == 1:
            early.append(local(width // 2, "local_b", [prefix]))
        count = 2 << bit
        final = bit == bits - 2
        sent = 1 if final else 2 * count
        pay, prefix, logs, *id_rows = call(
            lambda *refs, bit=bit, count=count: join_kernel(bit, count, pairs, *refs), "join", [],
            [pay, got] + ([prefix, logs] if bit else []),
            [
                shape((state_rows(pairs, sent), LANES), bf16), shape((rows, LANES), f32),
                shape((pairs, LANES), f32),
            ] + [shape((2 * count, LANES), f32)] * final,
            after=[early[-1][1]],
        )
    got = swap(pay, 1 << (bits - 1))
    half_seq = seq // 2
    places = {}
    for j in range(seq):
        places[(j & 1) * half_seq + (j >> 1)] = j
    order = [places[reversed_bits(j, bits)] for j in range(seq)]
    cand_q, val_w = call(
        lambda *refs: candidate_kernel(order, owned, *refs), "candidates", [],
        [
            id_rows[0], stored, item_embedding_table, peer, candidate_query_weight,
            candidate_key_value_weight,
        ],
        [shape((width, cands), bf16), shape((width, width), bf16)],
        flops=2 * cands * 2 * half * width,
    )
    (query_a, intra_a), (query_b, intra_b) = early
    send = cands // 2
    buffers = [pltpu.VMEM((n, send), f32)] * 2
    message = width + log_pad(heads)
    hist, key_two, val_two, pay = call(
        lambda *refs: finish_kernel(bits - 1, *refs), "finish", [user_history_length, head_score_scale],
        [
            emb, query_a, query_b, intra_a, intra_b, enter, ctl, got, prefix, logs,
            history_output_weight, candidate_key_value_weight, val_w, cand_q,
        ],
        [
            shape((n, width), f32), shape((n, width), bf16), shape((width, n), bf16),
            shape((message, send), bf16),
        ],
        buffers,
        flops=2 * n * half * width,
    )
    mean, logs = call(
        keep_kernel, "keep", [user_history_length, head_score_scale], [cand_q, key_two, val_two],
        [shape((width, send), f32), shape((heads, send), f32)],
        buffers,
        flops=2 * n * half * width,
    )
    for bit in range(bits - 3):
        got = swap(pay, 1 << bit)
        send //= 2
        mean, logs, pay = call(
            fold_kernel, "fold", [], [mean, logs, got],
            [shape((width, send), f32), shape((heads, send), f32), shape((message, send), bf16)],
        )
    got = swap(pay, 1 << (bits - 3))
    packed = 2 * owned == LANES
    cols = LANES if packed else owned
    mean, logs, *sends = call(
        deal_kernel, "deal", [], [mean, logs, got],
        [shape((width, cols), f32), shape((heads, cols), f32)]
        + [shape((message // 2, LANES) if packed else (message, owned), bf16)] * 3,
    )
    masks = [seq // 2, seq // 4, seq // 2 + seq // 4]
    gots = [swap(value, mask) for value, mask in zip(sends, masks)]
    (cand_out,) = call(
        lambda *refs: last_kernel(owned, *refs), "last", [],
        [mean, logs, *gots, candidate_output_weight],
        [shape((owned, width), f32)],
    )
    return hist[None], cand_out[None]


def solution(mesh):
    in_specs = (
        P(("groups", "dp"), "seq"),
        P(("groups", "dp"), None, "seq"),
        P(("groups", "dp")),
        P(("groups", "dp"), "seq"),
        P(),
        P("dp", None),
        P(),
        P(),
        P(),
        P(),
        P(),
        P(),
    )
    out_specs = (P(("groups", "dp"), "seq", None), P(("groups", "dp"), "seq", None))
    return jax.shard_map(shards, mesh=mesh, in_specs=in_specs, out_specs=out_specs, check_vma=False)
```

```python
import math

import jax
import jax.numpy as jnp
from jax import lax
from jax.experimental import pallas as pl
from jax.experimental.pallas import tpu as pltpu
from jax.sharding import PartitionSpec as P

f32, bf16, i32 = jnp.float32, jnp.bfloat16, jnp.int32
CHUNK = 256
KEYS = 512
LANES = 128
LOG2E = math.log2(math.e)
DEAD = -1e30
VMEM_LIMIT = 40 << 20


def dot(a, b):
    return jnp.dot(a, b, preferred_element_type=f32)


def contract(a, b, left, right):
    return lax.dot_general(a, b, (((left,), (right,)), ((), ())), preferred_element_type=f32)


def iota(shape, axis):
    return lax.broadcasted_iota(i32, shape, axis)


def thirds(value):
    high = value.astype(bf16).astype(f32)
    rest = value - high
    mid = rest.astype(bf16).astype(f32)
    return high, mid, rest - mid


def first_half(shape):
    return iota(shape, len(shape) - 1) % LANES < LANES // 2


def half_masks():
    low = first_half((1, LANES))
    return jnp.where(low, 1.0, 0.0).astype(bf16), jnp.where(low, 0.0, 1.0).astype(bf16)


def same_head():
    dims = (2 * LANES, 2 * LANES)
    return jnp.where(iota(dims, 0) // 64 == iota(dims, 1) // 64, 1.0, 0.0).astype(bf16)


def head_means(value, ones):
    square = (value * value).astype(bf16)
    step = ones.shape[0]
    parts = [dot(square[:, c : c + step], ones) for c in range(0, value.shape[1], step)]
    return jnp.concatenate(parts, axis=1) * (1.0 / 64.0)


def head_spread(heads, first, count):
    dims = (2 * heads, 64 * count)
    return jnp.where(iota(dims, 1) // 64 + first == iota(dims, 0) % heads, 1.0, 0.0).astype(bf16)


def spread(value, matrix):
    heads = value.shape[1] // 2
    high = value.astype(bf16).astype(f32)
    both = jnp.where(iota(value.shape, 1) < heads, high, value - high)
    return dot(both.astype(bf16), matrix)


def stored_slots(ids, stored):
    groups = stored.shape[0]
    n = ids.shape[1]
    pick = jnp.where(iota((groups, n), 0) == ids // LANES, 1.0, 0.0).astype(bf16)
    high = contract((stored // 64).astype(f32).astype(bf16), pick, 0, 0)
    low = contract((stored % 64).astype(f32).astype(bf16), pick, 0, 0)
    rows = jnp.where(iota((LANES, n), 0) == ids % LANES, high * 64.0 + low, 0.0)
    return jnp.sum(rows, axis=0, keepdims=True)


def picked_rows(slots, first, table):
    count = table.shape[0]
    hot = jnp.where(iota((count, slots.shape[1]), 0) == slots.astype(i32) - first, 1.0, 0.0)
    return contract(hot.astype(bf16), table[...], 0, 0)


def chunk(i):
    return slice(i * CHUNK, (i + 1) * CHUNK)


def pair_cut(p):
    return slice(p * LANES, (p + 1) * LANES)


def own_rows_kernel(
    ids_in, stored_in, decay_in, own_in, part_o, slot_o, crow_o, ccol_o, ctl_o,
    ids, stored, decay, own, sem,
):
    n, half, heads = ids.shape[1], own.shape[0], decay.shape[0]
    copies = [
        pltpu.make_async_copy(source, target, sem.at[k])
        for k, (source, target) in enumerate(
            ((ids_in, ids), (stored_in, stored), (decay_in, decay), (own_in, own))
        )
    ]
    for copy in copies:
        copy.start()
    copies[0].wait()
    copies[1].wait()
    slots = stored_slots(ids[...], stored[...])
    slot_o[...] = slots
    copies[2].wait()
    upto = jnp.where(
        iota((CHUNK, CHUNK), 0) <= iota((CHUNK, CHUNK), 1), 1.0, 0.0
    ).astype(bf16)
    low = first_half((1, LANES))
    for i in range(n // CHUNK):
        pieces = jnp.concatenate(thirds(decay[:, chunk(i)]), axis=0)
        sums = dot(pieces.astype(bf16), upto)
        cum = sums[:heads] + sums[heads : 2 * heads] + sums[2 * heads :]
        crow_o[i] = cum
        ccol_o[chunk(i), :] = jnp.transpose(jnp.concatenate([cum, cum], axis=0))
        for p in range(heads // 2):
            r = i * (heads // 2) + p
            ctl_o[r : r + 1, :] = jnp.where(
                low, cum[2 * p : 2 * p + 1, CHUNK - 1 :], cum[2 * p + 1 : 2 * p + 2, CHUNK - 1 :]
            )
    copies[3].wait()
    first = lax.axis_index("dp") * half
    for i in range(n // CHUNK):
        part_o[chunk(i), :] = picked_rows(slots[:, chunk(i)], first, own).astype(bf16)


def summary_kernel(
    length, part, peer, slot, ccol, ctl, id_rows, weight, emb_o, key_o, val_o, enter_o, pay_o
):
    n, width = part.shape
    half, heads = peer.shape[0], ccol.shape[1] // 2
    pairs = heads // 2
    block = LANES // 2
    ones, lanes = same_head(), head_spread(heads, 0, heads)
    low = first_half((1, LANES))
    chunks = n // CHUNK

    def project(i):
        other = picked_rows(slot[:, chunk(i)], (1 - lax.axis_index("dp")) * half, peer)
        emb = (part[chunk(i), :].astype(f32) + other).astype(bf16)
        emb_o[chunk(i), :] = emb
        return dot(emb, weight[:, width : 2 * width]), dot(emb, weight[:, 2 * width :])

    total = [jnp.zeros((block, LANES), f32)] * pairs
    ready = project(0)
    for i in range(chunks):
        key, val = ready
        if i + 1 < chunks:
            ready = project(i + 1)
        alive = iota((CHUNK, 1), 0) < length[0] - lax.axis_index("seq") * n - i * CHUNK
        val = jnp.where(alive, val, 0.0).astype(bf16)
        val_o[chunk(i), :] = val
        unit = lax.rsqrt(head_means(key, ones) + 1e-06) * 0.125
        normed = jnp.where(alive, key * unit, 0.0)
        key_o[chunk(i), :] = normed.astype(bf16)
        cum = ccol[chunk(i), :]
        keyed = (normed * spread(jnp.exp(cum[CHUNK - 1 :, :] - cum), lanes)).astype(bf16)
        for p in range(pairs):
            both = contract(keyed[:, pair_cut(p)], val[:, pair_cut(p)], 0, 0)
            fresh = jnp.where(low, both[:block], both[block:])
            enter_o[i, p * block : (p + 1) * block, :] = total[p]
            total[p] = total[p] * jnp.exp(ctl[i * pairs + p : i * pairs + p + 1, :]) + fresh
    logs = ctl[0:pairs, :]
    for i in range(1, chunks):
        logs = logs + ctl[i * pairs : (i + 1) * pairs, :]
    pay_o[...] = pack_state(jnp.concatenate(total, axis=0), logs, id_rows[...])


def state_rows(pairs, ids):
    return pairs * 64 + -(-(3 * pairs + ids) // 16) * 16


def pack_state(state, logs, id_rows):
    pairs, ids = logs.shape[0], id_rows.shape[0]
    pad = state_rows(pairs, ids) - state.shape[0] - 3 * pairs - ids
    parts = [state, *thirds(logs), id_rows] + [jnp.zeros((pad, LANES), f32)] * (pad > 0)
    return jnp.concatenate(parts, axis=0).astype(bf16)


def unpack_state(packed, pairs):
    whole = packed.astype(f32)
    rows = pairs * 64
    logs = whole[rows : rows + pairs]
    for k in (1, 2):
        logs = logs + whole[rows + k * pairs : rows + (k + 1) * pairs]
    return whole[:rows], logs, whole[rows + 3 * pairs :]


def row_factors(logs):
    factors = jnp.exp(logs)
    return jnp.concatenate(
        [jnp.broadcast_to(factors[p : p + 1], (64, LANES)) for p in range(logs.shape[0])], axis=0
    )


def join_kernel(bit, ids, pairs, mine, got, *refs):
    before = refs[: 2 if bit else 0]
    pay_o, prefix_o, logs_o, *ids_o = refs[len(before) :]
    upper = (lax.axis_index("seq") >> bit) & 1 == 1
    state, logs, rows = unpack_state(mine[...], pairs)
    other, other_logs, other_rows = unpack_state(got[...], pairs)
    early = jnp.where(upper, other, state)
    late = jnp.where(upper, state, other)
    factor = row_factors(jnp.where(upper, logs, other_logs))
    id_rows = jnp.concatenate([rows[:ids], other_rows[:ids]], axis=0)
    if ids_o:
        ids_o[0][...] = id_rows
    pay_o[...] = pack_state(
        early * factor + late, logs + other_logs, id_rows[:1] if ids_o else id_rows
    )
    if bit == 0:
        prefix_o[...] = jnp.where(upper, other, 0.0)
        logs_o[...] = jnp.where(upper, other_logs, 0.0)
    else:
        prefix, prefix_logs = before[0][...], before[1][...]
        prefix_o[...] = jnp.where(upper, prefix + row_factors(prefix_logs) * other, prefix)
        logs_o[...] = jnp.where(upper, prefix_logs + other_logs, prefix_logs)


def local_kernel(first, emb, key, val, crow, ccol, weight, query_o, intra_o):
    n, width = query_o.shape
    heads = ccol.shape[1] // 2
    ones, lanes = same_head(), head_spread(heads, first // 64, width // 64)
    mask_a, mask_b = half_masks()
    causal = iota((CHUNK, CHUNK), 0) >= iota((CHUNK, CHUNK), 1)

    def queries(i):
        query = dot(emb[chunk(i), :], weight[:, first : first + width])
        unit = lax.rsqrt(head_means(query, ones) + 1e-06) * 0.125
        query = query * unit
        decayed = query * spread(jnp.exp(ccol[chunk(i), :]), lanes)
        query_o[chunk(i), :] = decayed.astype(bf16)
        return query.astype(bf16)

    def scores(i, p, b, query):
        cut = pair_cut(p)
        wide = slice(first + p * LANES, first + (p + 1) * LANES)
        return contract(query[:, cut] * (mask_b if b else mask_a), key[chunk(i), wide], 1, 1)

    units = [(i, p, b) for i in range(n // CHUNK) for p in range(width // LANES) for b in (0, 1)]
    query = {0: queries(0)}
    ready = scores(*units[0], query[0])
    held = None
    for u, (i, p, b) in enumerate(units):
        current = ready
        if u + 1 < len(units):
            j = units[u + 1][0]
            if j not in query:
                query[j] = queries(j)
            ready = scores(*units[u + 1], query[j])
        h = first // 64 + 2 * p + b
        gap = ccol[chunk(i), h : h + 1] - crow[i, h : h + 1, :]
        weights = jnp.where(causal, current * jnp.exp(gap), 0.0).astype(bf16)
        wide = slice(first + p * LANES, first + (p + 1) * LANES)
        part = dot(weights, val[chunk(i), wide] * (mask_b if b else mask_a))
        if b == 0:
            held = part
        else:
            intra_o[chunk(i), pair_cut(p)] = held + part


def candidate_kernel(order, owned, id_rows, stored, own, peer, query_w, pair_w, query_o, val_w_o):
    half, width = own.shape
    ids = id_rows[...]
    ids = (ids * float(LANES) + pltpu.roll(ids, LANES // 2, 1)).astype(i32)
    slots = [stored_slots(ids[j : j + 1], stored[...]) for j in order]
    step = max(1, LANES // owned)
    tiles = []
    for start in range(0, len(order), step):
        tile = slots[start]
        for k in range(1, min(step, len(order) - start)):
            moved = pltpu.roll(slots[start + k], k * owned, 1)
            tile = jnp.where(iota((1, LANES), 1) >= k * owned, moved, tile)
        tiles.append(tile)
    slots = jnp.concatenate(tiles, axis=1)
    for c in range(0, slots.shape[1], CHUNK):
        some = slots[:, c : c + CHUNK]
        dp = lax.axis_index("dp")
        rows = picked_rows(some, dp * half, own) + picked_rows(some, (1 - dp) * half, peer)
        query = dot(rows.astype(bf16), query_w[...])
        query_o[:, c : c + CHUNK] = jnp.transpose(query).astype(bf16)
    val_w_o[...] = jnp.transpose(pair_w[:, width:].astype(f32)).astype(bf16)


def attend(alive_count, scale, query, first, cols, key, val, emit):
    n, width = key.shape
    blocks = range(0, n, KEYS)

    def padded(h):
        rows = query[h * 64 : (h + 1) * 64, first : first + cols]
        zero = jnp.zeros_like(rows)
        return jnp.concatenate([zero, rows] if h % 2 else [rows, zero], axis=0)

    def scores(h, block, weights):
        rows = slice(block, block + KEYS)
        values = dot(key[rows, pair_cut(h // 2)], weights)
        alive = iota((KEYS, 1), 0) < alive_count - block
        return jnp.where(alive, values, DEAD)

    def store(h, block, weights, buffer, peak):
        values = scores(h, block, weights)
        buffer[block : block + KEYS, :] = values
        top = jnp.max(values.reshape(KEYS // 8, 8, cols), axis=0)
        return top if peak is None else jnp.maximum(peak, top)

    def run(buffers):
        ones = jnp.ones((16, KEYS), bf16)
        peak, weights = None, padded(0)
        for block in blocks:
            peak = store(0, block, weights, buffers[0], peak)
        for h in range(width // 64):
            factor = scale[h] * LOG2E
            peak = jnp.max(peak, axis=0, keepdims=True)
            following = None
            more = h + 1 < width // 64
            weights = padded(h + 1) if more else None
            sums = None
            for block in blocks:
                if more:
                    following = store(h + 1, block, weights, buffers[(h + 1) % 2], following)
                gap = buffers[h % 2][block : block + KEYS, :] - peak
                probs = jnp.exp2(gap * factor).astype(bf16)
                side = jnp.concatenate(
                    [val[h * 64 : (h + 1) * 64, block : block + KEYS], ones], axis=0
                )
                part = dot(side, probs)
                sums = part if sums is None else sums + part
            total = sums[64:65]
            emit(h, sums[:64] / total, peak * factor + jnp.log2(total))
            peak = following

    return run


def finish_kernel(
    bit, length, scale, emb, query_a, query_b, intra_a, intra_b, enter, ctl, got, prefix, prefix_logs,
    out_w, pair_w, val_w, cand_q, hist_o, key_o, val_o, pay_o, *buffers,
):
    n, width = emb.shape
    pairs = width // LANES
    ones = same_head()
    upper = (lax.axis_index("seq") >> bit) & 1 == 1
    state = unpack_state(got[...], pairs)[0]
    before, before_logs = prefix[...], prefix_logs[...]
    entering = jnp.where(upper, before + row_factors(before_logs) * state, before)
    lane = iota((1, 2 * LANES), 1) // 64
    chunks = n // CHUNK
    gone = [jnp.zeros((pairs, LANES), f32)]
    for i in range(chunks - 1):
        gone.append(gone[-1] + ctl[i * pairs : (i + 1) * pairs, :])

    def normed(i):
        states = enter[i] + row_factors(gone[i]) * entering
        parts = []
        for p in range(0, pairs, 2):
            wide = jnp.concatenate(
                [states[p * 64 : (p + 1) * 64], states[(p + 1) * 64 : (p + 2) * 64]], axis=1
            )
            matrix = jnp.concatenate([jnp.where(lane == k, wide, 0.0) for k in range(4)], axis=0)
            query, intra = (query_a, intra_a) if p < pairs // 2 else (query_b, intra_b)
            c = (p % (pairs // 2)) * LANES
            cut = slice(c, c + 2 * LANES)
            parts.append(dot(query[chunk(i), cut], matrix.astype(bf16)) + intra[chunk(i), cut])
        mixed = jnp.concatenate(parts, axis=1)
        return (mixed * lax.rsqrt(head_means(mixed, ones) + 1e-05)).astype(bf16)

    ready = normed(0)
    for i in range(chunks):
        current = ready
        if i + 1 < chunks:
            ready = normed(i + 1)
        hidden_sum = emb[chunk(i), :].astype(f32) + dot(current, out_w[...])
        alive = iota((CHUNK, 1), 0) < length[0] - lax.axis_index("seq") * n - i * CHUNK
        hist_o[chunk(i), :] = jnp.where(alive, hidden_sum, 0.0)
        hidden = hidden_sum.astype(bf16)
        key_o[chunk(i), :] = dot(hidden, pair_w[:, :width]).astype(bf16)
        val_o[:, chunk(i)] = contract(val_w[...], hidden, 1, 1).astype(bf16)
    count = pay_o.shape[1]
    heads = width // 64
    alive_count = length[0] - lax.axis_index("seq") * n
    log_rows = []

    def emit(h, attended, logs):
        pay_o[h * 64 : (h + 1) * 64, :] = attended.astype(bf16)
        log_rows.append(jnp.where(alive_count > 0, logs, DEAD))

    attend(alive_count, scale, cand_q, count, count, key_o, val_o, emit)(buffers)
    pay_o[width:, :] = pack_logs(jnp.concatenate(log_rows, axis=0))


def pack_logs(logs):
    heads, cols = logs.shape
    return jnp.concatenate(
        [*thirds(logs), jnp.zeros((log_pad(heads) - 3 * heads, cols), f32)], axis=0
    ).astype(bf16)


def log_pad(heads):
    return -(-3 * heads // 16) * 16


def unpack_logs(rows, heads):
    rows = rows.astype(f32)
    return rows[:heads] + rows[heads : 2 * heads] + rows[2 * heads : 3 * heads]


def keep_kernel(length, scale, cand_q, key, val, mean_o, logs_o, *buffers):
    alive_count = length[0] - lax.axis_index("seq") * key.shape[0]

    def emit(h, attended, logs):
        mean_o[h * 64 : (h + 1) * 64, :] = attended
        logs_o[h : h + 1, :] = jnp.where(alive_count > 0, logs, DEAD)

    attend(alive_count, scale, cand_q, 0, mean_o.shape[1], key, val, emit)(buffers)


def over_heads(rows):
    return jnp.concatenate(
        [jnp.broadcast_to(rows[h : h + 1], (64, rows.shape[1])) for h in range(rows.shape[0])],
        axis=0,
    )


def merge(parts):
    peak = parts[0][1]
    for _, logs in parts[1:]:
        peak = jnp.maximum(peak, logs)
    shares = [jnp.exp2(logs - peak) for _, logs in parts]
    total = sum(shares[1:], shares[0])
    mean = None
    for (value, _), share in zip(parts, shares):
        term = value * over_heads(share / total)
        mean = term if mean is None else mean + term
    return mean, peak + jnp.log2(total)


def received(got, heads):
    width = heads * 64
    return got[:width, :].astype(f32), unpack_logs(got[width:, :], heads)


def fold_kernel(mean, logs, got, mean_o, logs_o, pay_o):
    heads, keep = logs_o.shape
    width = heads * 64
    new_mean, new_logs = merge([(mean[...], logs[...]), received(got, heads)])
    mean_o[...] = new_mean[:, :keep]
    logs_o[...] = new_logs[:, :keep]
    pay_o[:width, :] = new_mean[:, keep:].astype(bf16)
    pay_o[width:, :] = pack_logs(new_logs[:, keep:])


def deal_kernel(mean, logs, got, mean_o, logs_o, *sends):
    heads, cols = logs_o.shape
    new_mean, new_logs = merge([(mean[...], logs[...]), received(got, heads)])
    mean_o[...] = new_mean[:, :cols]
    logs_o[...] = new_logs[:, :cols]
    whole = jnp.concatenate([new_mean, pack_logs(new_logs).astype(f32)], axis=0)
    owned = whole.shape[1] // 4
    half = whole.shape[0] // 2
    low = first_half((1, LANES))
    for k, send in enumerate(sends):
        start = (k + 1) * owned
        if 2 * owned == LANES:
            tile = whole[:, start // LANES * LANES : start // LANES * LANES + LANES]
            top, bottom = tile[:half], tile[half:]
            if start % LANES:
                top = pltpu.roll(top, owned, 1)
            else:
                bottom = pltpu.roll(bottom, owned, 1)
            send[...] = jnp.where(low, top, bottom).astype(bf16)
        else:
            send[...] = whole[:, start : start + owned].astype(bf16)


def last_kernel(owned, mean, logs, got_a, got_b, got_c, out_w, cand_o):
    heads = logs.shape[0]
    parts = [(mean[...], logs[...])]
    for got in (got_a, got_b, got_c):
        if 2 * owned == LANES:
            value = got[...].astype(f32)
            value = jnp.concatenate([value, pltpu.roll(value, owned, 1)], axis=0)
        else:
            value = got[...].astype(f32)
        parts.append((value[: heads * 64], unpack_logs(value[heads * 64 :], heads)))
    attended = merge(parts)[0].astype(bf16)
    cand_o[...] = contract(attended, out_w[...], 0, 0)[: cand_o.shape[0]]


def shape(dims, dtype):
    return jax.ShapeDtypeStruct(dims, dtype)


VMEM = pl.BlockSpec(memory_space=pltpu.VMEM)
SMEM = pl.BlockSpec(memory_space=pltpu.SMEM)
ANY = pl.BlockSpec(memory_space=pl.ANY)
HBM = pl.BlockSpec(memory_space=pltpu.HBM)


def call(kernel, name, scalars, operands, outs, scratch=(), after=(), flops=0, space=VMEM):
    count = len(scalars) + len(operands)

    if space is HBM:
        operands = [pltpu.with_memory_space_constraint(value, pltpu.HBM) for value in operands]

    def body(*refs):
        kernel(*refs[:count], *refs[count + len(after) :])

    return pl.pallas_call(
        body,
        name=name,
        in_specs=[SMEM] * len(scalars) + [space] * len(operands) + [ANY] * len(after),
        out_specs=[VMEM] * len(outs),
        out_shape=outs,
        scratch_shapes=list(scratch),
        compiler_params=pltpu.CompilerParams(vmem_limit_bytes=VMEM_LIMIT),
        cost_estimate=pl.CostEstimate(flops=flops, transcendentals=0, bytes_accessed=0),
    )(*scalars, *operands, *after)


def reversed_bits(value, bits):
    return sum(((value >> b) & 1) << (bits - 1 - b) for b in range(bits))


def shards(
    history_item_index,
    log_head_retention,
    user_history_length,
    candidate_item_index,
    item_stored_row,
    item_embedding_table,
    head_score_scale,
    history_query_key_value_weight,
    history_output_weight,
    candidate_key_value_weight,
    candidate_query_weight,
    candidate_output_weight,
):
    users, n = history_item_index.shape
    heads = log_head_retention.shape[1]
    half, width = item_embedding_table.shape
    owned = candidate_item_index.shape[1]
    seq = lax.axis_size("seq")
    bits = seq.bit_length() - 1
    assert users == 1 and lax.axis_size("dp") == 2 and seq == 1 << bits and bits > 2
    assert width == heads * 64 and heads % 4 == 0 and owned <= 64
    pairs = heads // 2
    rows = pairs * 64
    cands = owned * seq

    def swap(value, mask):
        return lax.ppermute(value, "seq", [(j, j ^ mask) for j in range(seq)])

    peer = lax.ppermute(item_embedding_table, "dp", [(0, 1), (1, 0)])
    far_ids = swap(candidate_item_index, seq // 2)
    stored = item_stored_row.reshape(-1, LANES)
    decay = log_head_retention.reshape(heads, n)
    ids = jnp.concatenate([candidate_item_index, far_ids], axis=0)
    ids = jnp.pad(ids, ((0, 0), (0, 64 - owned)))
    id_rows = jnp.concatenate([ids // LANES, ids % LANES], axis=1).astype(f32)

    part, slot, crow, ccol, ctl = call(
        own_rows_kernel, "own_rows", [],
        [history_item_index, stored, decay, item_embedding_table],
        [
            shape((n, width), bf16), shape((1, n), f32), shape((n // CHUNK, heads, CHUNK), f32),
            shape((n, 2 * heads), f32), shape((n // CHUNK * pairs, LANES), f32),
        ],
        [
            pltpu.VMEM((1, n), i32), pltpu.VMEM(stored.shape, i32), pltpu.VMEM((heads, n), f32),
            pltpu.VMEM((half, width), bf16), pltpu.SemaphoreType.DMA((4,)),
        ],
        space=HBM,
        flops=2 * n * half * width,
    )
    emb, key, val, enter, pay = call(
        summary_kernel, "summary", [user_history_length],
        [part, peer, slot, ccol, ctl, id_rows, history_query_key_value_weight],
        [
            shape((n, width), bf16), shape((n, width), bf16), shape((n, width), bf16),
            shape((n // CHUNK, rows, LANES), f32), shape((state_rows(pairs, 2), LANES), bf16),
        ],
        flops=2 * n * half * width,
    )

    def local(first, name, after):
        return call(
            lambda *refs: local_kernel(first, *refs), name, [],
            [emb, key, val, crow, ccol, history_query_key_value_weight],
            [shape((n, width // 2), bf16), shape((n, width // 2), f32)],
            after=after, flops=2 * n * half * width // 2,
        )

    early = [local(0, "local_a", [])]
    prefix = logs = None
    for bit in range(bits - 1):
        got = swap(pay, 1 << bit)
        if bit == 1:
            early.append(local(width // 2, "local_b", [prefix]))
        count = 2 << bit
        final = bit == bits - 2
        sent = 1 if final else 2 * count
        pay, prefix, logs, *id_rows = call(
            lambda *refs, bit=bit, count=count: join_kernel(bit, count, pairs, *refs), "join", [],
            [pay, got] + ([prefix, logs] if bit else []),
            [
                shape((state_rows(pairs, sent), LANES), bf16), shape((rows, LANES), f32),
                shape((pairs, LANES), f32),
            ] + [shape((2 * count, LANES), f32)] * final,
            after=[early[-1][1]],
        )
    got = swap(pay, 1 << (bits - 1))
    half_seq = seq // 2
    places = {}
    for j in range(seq):
        places[(j & 1) * half_seq + (j >> 1)] = j
    order = [places[reversed_bits(j, bits)] for j in range(seq)]
    cand_q, val_w = call(
        lambda *refs: candidate_kernel(order, owned, *refs), "candidates", [],
        [
            id_rows[0], stored, item_embedding_table, peer, candidate_query_weight,
            candidate_key_value_weight,
        ],
        [shape((width, cands), bf16), shape((width, width), bf16)],
        flops=2 * cands * 2 * half * width,
    )
    (query_a, intra_a), (query_b, intra_b) = early
    send = cands // 2
    buffers = [pltpu.VMEM((n, send), f32)] * 2
    message = width + log_pad(heads)
    hist, key_two, val_two, pay = call(
        lambda *refs: finish_kernel(bits - 1, *refs), "finish", [user_history_length, head_score_scale],
        [
            emb, query_a, query_b, intra_a, intra_b, enter, ctl, got, prefix, logs,
            history_output_weight, candidate_key_value_weight, val_w, cand_q,
        ],
        [
            shape((n, width), f32), shape((n, width), bf16), shape((width, n), bf16),
            shape((message, send), bf16),
        ],
        buffers,
        flops=2 * n * half * width,
    )
    mean, logs = call(
        keep_kernel, "keep", [user_history_length, head_score_scale], [cand_q, key_two, val_two],
        [shape((width, send), f32), shape((heads, send), f32)],
        buffers,
        flops=2 * n * half * width,
    )
    for bit in range(bits - 3):
        got = swap(pay, 1 << bit)
        send //= 2
        mean, logs, pay = call(
            fold_kernel, "fold", [], [mean, logs, got],
            [shape((width, send), f32), shape((heads, send), f32), shape((message, send), bf16)],
        )
    got = swap(pay, 1 << (bits - 3))
    packed = 2 * owned == LANES
    cols = LANES if packed else owned
    mean, logs, *sends = call(
        deal_kernel, "deal", [], [mean, logs, got],
        [shape((width, cols), f32), shape((heads, cols), f32)]
        + [shape((message // 2, LANES) if packed else (message, owned), bf16)] * 3,
    )
    masks = [seq // 2, seq // 4, seq // 2 + seq // 4]
    gots = [swap(value, mask) for value, mask in zip(sends, masks)]
    (cand_out,) = call(
        lambda *refs: last_kernel(owned, *refs), "last", [],
        [mean, logs, *gots, candidate_output_weight],
        [shape((owned, width), f32)],
    )
    return hist[None], cand_out[None]


def solution(mesh):
    in_specs = (
        P(("groups", "dp"), "seq"),
        P(("groups", "dp"), None, "seq"),
        P(("groups", "dp")),
        P(("groups", "dp"), "seq"),
        P(),
        P("dp", None),
        P(),
        P(),
        P(),
        P(),
        P(),
        P(),
    )
    out_specs = (P(("groups", "dp"), "seq", None), P(("groups", "dp"), "seq", None))
    return jax.shard_map(shards, mesh=mesh, in_specs=in_specs, out_specs=out_specs, check_vma=False)
```

```python
import math

import jax
import jax.numpy as jnp
from jax import lax
from jax.experimental import pallas as pl
from jax.experimental.pallas import tpu as pltpu
from jax.sharding import PartitionSpec as P

f32, bf16, i32 = jnp.float32, jnp.bfloat16, jnp.int32
CHUNK = 256
KEYS = 512
LANES = 128
LOG2E = math.log2(math.e)
DEAD = -1e30
VMEM_LIMIT = 40 << 20


def dot(a, b):
    return jnp.dot(a, b, preferred_element_type=f32)


def contract(a, b, left, right):
    return lax.dot_general(a, b, (((left,), (right,)), ((), ())), preferred_element_type=f32)


def iota(shape, axis):
    return lax.broadcasted_iota(i32, shape, axis)


def thirds(value):
    high = value.astype(bf16).astype(f32)
    rest = value - high
    mid = rest.astype(bf16).astype(f32)
    return high, mid, rest - mid


def first_half(shape):
    return iota(shape, len(shape) - 1) % LANES < LANES // 2


def half_masks():
    low = first_half((1, LANES))
    return jnp.where(low, 1.0, 0.0).astype(bf16), jnp.where(low, 0.0, 1.0).astype(bf16)


def same_head():
    dims = (2 * LANES, 2 * LANES)
    return jnp.where(iota(dims, 0) // 64 == iota(dims, 1) // 64, 1.0, 0.0).astype(bf16)


def head_means(value, ones):
    square = (value * value).astype(bf16)
    step = ones.shape[0]
    parts = [dot(square[:, c : c + step], ones) for c in range(0, value.shape[1], step)]
    return jnp.concatenate(parts, axis=1) * (1.0 / 64.0)


def head_spread(heads, first, count):
    dims = (2 * heads, 64 * count)
    return jnp.where(iota(dims, 1) // 64 + first == iota(dims, 0) % heads, 1.0, 0.0).astype(bf16)


def spread(value, matrix):
    heads = value.shape[1] // 2
    high = value.astype(bf16).astype(f32)
    both = jnp.where(iota(value.shape, 1) < heads, high, value - high)
    return dot(both.astype(bf16), matrix)


def stored_slots(ids, stored):
    groups = stored.shape[0]
    n = ids.shape[1]
    pick = jnp.where(iota((groups, n), 0) == ids // LANES, 1.0, 0.0).astype(bf16)
    high = contract((stored // 64).astype(f32).astype(bf16), pick, 0, 0)
    low = contract((stored % 64).astype(f32).astype(bf16), pick, 0, 0)
    rows = jnp.where(iota((LANES, n), 0) == ids % LANES, high * 64.0 + low, 0.0)
    return jnp.sum(rows, axis=0, keepdims=True)


def picked_rows(slots, first, table):
    count = table.shape[0]
    hot = jnp.where(iota((count, slots.shape[1]), 0) == slots.astype(i32) - first, 1.0, 0.0)
    return contract(hot.astype(bf16), table[...], 0, 0)


def chunk(i):
    return slice(i * CHUNK, (i + 1) * CHUNK)


def pair_cut(p):
    return slice(p * LANES, (p + 1) * LANES)


def own_rows_kernel(
    ids_in, stored_in, decay_in, own_in, weight_in, part_o, slot_o, crow_o, ccol_o, ctl_o, key_w_o,
    ids, stored, decay, own, key_w, sem,
):
    n, half, heads = ids.shape[1], own.shape[0], decay.shape[0]
    width = own.shape[1]
    middle = weight_in.at[:, width : 2 * width]
    copies = [
        pltpu.make_async_copy(source, target, sem.at[k])
        for k, (source, target) in enumerate(
            ((ids_in, ids), (stored_in, stored), (decay_in, decay), (middle, key_w), (own_in, own))
        )
    ]
    for copy in copies:
        copy.start()
    copies[0].wait()
    copies[1].wait()
    slots = stored_slots(ids[...], stored[...])
    slot_o[...] = slots
    copies[2].wait()
    upto = jnp.where(
        iota((CHUNK, CHUNK), 0) <= iota((CHUNK, CHUNK), 1), 1.0, 0.0
    ).astype(bf16)
    low = first_half((1, LANES))
    for i in range(n // CHUNK):
        pieces = jnp.concatenate(thirds(decay[:, chunk(i)]), axis=0)
        sums = dot(pieces.astype(bf16), upto)
        cum = sums[:heads] + sums[heads : 2 * heads] + sums[2 * heads :]
        crow_o[i] = cum
        ccol_o[chunk(i), :] = jnp.transpose(jnp.concatenate([cum, cum], axis=0))
        for p in range(heads // 2):
            r = i * (heads // 2) + p
            ctl_o[r : r + 1, :] = jnp.where(
                low, cum[2 * p : 2 * p + 1, CHUNK - 1 :], cum[2 * p + 1 : 2 * p + 2, CHUNK - 1 :]
            )
    copies[3].wait()
    key_w_o[...] = jnp.transpose(key_w[...].astype(f32)).astype(bf16)
    copies[4].wait()
    first = lax.axis_index("dp") * half
    for i in range(n // CHUNK):
        part_o[chunk(i), :] = picked_rows(slots[:, chunk(i)], first, own).astype(bf16)


def summary_kernel(
    length, part, peer, slot, crow, ctl, id_rows, key_w, weight, emb_o, key_o, val_o, enter_o, pay_o
):
    n, width = part.shape
    half, heads = peer.shape[0], crow.shape[1]
    pairs = heads // 2
    block = LANES // 2
    low = first_half((1, LANES))
    chunks = n // CHUNK
    here = length[...] - lax.axis_index("seq") * n

    def project(i):
        other = picked_rows(slot[:, chunk(i)], (1 - lax.axis_index("dp")) * half, peer)
        emb = (part[chunk(i), :].astype(f32) + other).astype(bf16)
        emb_o[chunk(i), :] = emb
        return contract(key_w[...], emb, 1, 1), dot(emb, weight[:, 2 * width :])

    total = [jnp.zeros((block, LANES), f32)] * pairs
    ready = project(0)
    for i in range(chunks):
        key, val = ready
        if i + 1 < chunks:
            ready = project(i + 1)
        val = jnp.where(iota((CHUNK, 1), 0) < here - i * CHUNK, val, 0.0).astype(bf16)
        val_o[chunk(i), :] = val
        alive = iota((1, CHUNK), 1) < here - i * CHUNK
        cum = crow[i]
        tail = jnp.exp(cum[:, CHUNK - 1 :] - cum)
        for p in range(pairs):
            keyed = []
            for h in (2 * p, 2 * p + 1):
                rows = key[h * 64 : (h + 1) * 64]
                mean = jnp.sum(rows * rows, axis=0, keepdims=True) * (1.0 / 64.0)
                unit = jnp.where(alive, lax.rsqrt(mean + 1e-06) * 0.125, 0.0)
                normed = rows * unit
                key_o[h * 64 : (h + 1) * 64, chunk(i)] = normed.astype(bf16)
                keyed.append(normed * tail[h : h + 1])
            keyed = jnp.concatenate(keyed, axis=0).astype(bf16)
            both = dot(keyed, val[:, pair_cut(p)])
            fresh = jnp.where(low, both[:block], both[block:])
            enter_o[i, p * block : (p + 1) * block, :] = total[p]
            total[p] = total[p] * jnp.exp(ctl[i * pairs + p : i * pairs + p + 1, :]) + fresh
    logs = ctl[0:pairs, :]
    for i in range(1, chunks):
        logs = logs + ctl[i * pairs : (i + 1) * pairs, :]
    pay_o[...] = pack_state(jnp.concatenate(total, axis=0), logs, id_rows[...])


def state_rows(pairs, ids):
    return pairs * 64 + -(-(3 * pairs + ids) // 16) * 16


def pack_state(state, logs, id_rows):
    pairs, ids = logs.shape[0], id_rows.shape[0]
    pad = state_rows(pairs, ids) - state.shape[0] - 3 * pairs - ids
    parts = [state, *thirds(logs), id_rows] + [jnp.zeros((pad, LANES), f32)] * (pad > 0)
    return jnp.concatenate(parts, axis=0).astype(bf16)


def unpack_state(packed, pairs):
    whole = packed.astype(f32)
    rows = pairs * 64
    logs = whole[rows : rows + pairs]
    for k in (1, 2):
        logs = logs + whole[rows + k * pairs : rows + (k + 1) * pairs]
    return whole[:rows], logs, whole[rows + 3 * pairs :]


def row_factors(logs):
    factors = jnp.exp(logs)
    return jnp.concatenate(
        [jnp.broadcast_to(factors[p : p + 1], (64, LANES)) for p in range(logs.shape[0])], axis=0
    )


def join_kernel(bit, ids, pairs, mine, got, *refs):
    before = refs[: 2 if bit else 0]
    pay_o, prefix_o, logs_o, *ids_o = refs[len(before) :]
    upper = (lax.axis_index("seq") >> bit) & 1 == 1
    state, logs, rows = unpack_state(mine[...], pairs)
    other, other_logs, other_rows = unpack_state(got[...], pairs)
    early = jnp.where(upper, other, state)
    late = jnp.where(upper, state, other)
    factor = row_factors(jnp.where(upper, logs, other_logs))
    id_rows = jnp.concatenate([rows[:ids], other_rows[:ids]], axis=0)
    if ids_o:
        ids_o[0][...] = id_rows
    pay_o[...] = pack_state(
        early * factor + late, logs + other_logs, id_rows[:1] if ids_o else id_rows
    )
    if bit == 0:
        prefix_o[...] = jnp.where(upper, other, 0.0)
        logs_o[...] = jnp.where(upper, other_logs, 0.0)
    else:
        prefix, prefix_logs = before[0][...], before[1][...]
        prefix_o[...] = jnp.where(upper, prefix + row_factors(prefix_logs) * other, prefix)
        logs_o[...] = jnp.where(upper, prefix_logs + other_logs, prefix_logs)


def local_kernel(first, emb, key, val, crow, ccol, weight, query_o, intra_o):
    n, width = query_o.shape
    heads = ccol.shape[1] // 2
    ones, lanes = same_head(), head_spread(heads, first // 64, width // 64)
    mask_a, mask_b = half_masks()
    causal = iota((CHUNK, CHUNK), 0) >= iota((CHUNK, CHUNK), 1)

    def queries(i):
        query = dot(emb[chunk(i), :], weight[:, first : first + width])
        unit = lax.rsqrt(head_means(query, ones) + 1e-06) * 0.125
        query = query * unit
        decayed = query * spread(jnp.exp(ccol[chunk(i), :]), lanes)
        query_o[chunk(i), :] = decayed.astype(bf16)
        return query.astype(bf16)

    def scores(i, p, b, query):
        cut = pair_cut(p)
        wide = slice(first + p * LANES, first + (p + 1) * LANES)
        return dot(query[:, cut] * (mask_b if b else mask_a), key[wide, chunk(i)])

    units = [(i, p, b) for i in range(n // CHUNK) for p in range(width // LANES) for b in (0, 1)]
    query = {0: queries(0)}
    ready = scores(*units[0], query[0])
    held = None
    for u, (i, p, b) in enumerate(units):
        current = ready
        if u + 1 < len(units):
            j = units[u + 1][0]
            if j not in query:
                query[j] = queries(j)
            ready = scores(*units[u + 1], query[j])
        h = first // 64 + 2 * p + b
        gap = ccol[chunk(i), h : h + 1] - crow[i, h : h + 1, :]
        weights = jnp.where(causal, current * jnp.exp(gap), 0.0).astype(bf16)
        wide = slice(first + p * LANES, first + (p + 1) * LANES)
        part = dot(weights, val[chunk(i), wide] * (mask_b if b else mask_a))
        if b == 0:
            held = part
        else:
            intra_o[chunk(i), pair_cut(p)] = held + part


def candidate_kernel(order, owned, id_rows, stored, own, peer, query_w, pair_w, query_o, val_w_o):
    half, width = own.shape
    ids = id_rows[...]
    ids = (ids * float(LANES) + pltpu.roll(ids, LANES // 2, 1)).astype(i32)
    slots = [stored_slots(ids[j : j + 1], stored[...]) for j in order]
    step = max(1, LANES // owned)
    tiles = []
    for start in range(0, len(order), step):
        tile = slots[start]
        for k in range(1, min(step, len(order) - start)):
            moved = pltpu.roll(slots[start + k], k * owned, 1)
            tile = jnp.where(iota((1, LANES), 1) >= k * owned, moved, tile)
        tiles.append(tile)
    slots = jnp.concatenate(tiles, axis=1)
    for c in range(0, slots.shape[1], CHUNK):
        some = slots[:, c : c + CHUNK]
        dp = lax.axis_index("dp")
        rows = picked_rows(some, dp * half, own) + picked_rows(some, (1 - dp) * half, peer)
        query = dot(rows.astype(bf16), query_w[...])
        query_o[:, c : c + CHUNK] = jnp.transpose(query).astype(bf16)
    val_w_o[...] = jnp.transpose(pair_w[:, width:].astype(f32)).astype(bf16)


def attend(alive_count, scale, query, first, cols, key, val, emit):
    n, width = key.shape
    blocks = range(0, n, KEYS)

    def padded(h):
        rows = query[h * 64 : (h + 1) * 64, first : first + cols]
        zero = jnp.zeros_like(rows)
        return jnp.concatenate([zero, rows] if h % 2 else [rows, zero], axis=0)

    def scores(h, block, weights):
        rows = slice(block, block + KEYS)
        values = dot(key[rows, pair_cut(h // 2)], weights)
        alive = iota((KEYS, 1), 0) < alive_count - block
        return jnp.where(alive, values, DEAD)

    def store(h, block, weights, buffer, peak):
        values = scores(h, block, weights)
        buffer[block : block + KEYS, :] = values
        top = jnp.max(values.reshape(KEYS // 8, 8, cols), axis=0)
        return top if peak is None else jnp.maximum(peak, top)

    def run(buffers):
        ones = jnp.ones((16, KEYS), bf16)
        peak, weights = None, padded(0)
        for block in blocks:
            peak = store(0, block, weights, buffers[0], peak)
        for h in range(width // 64):
            factor = scale[0:1, h : h + 1] * LOG2E
            peak = jnp.max(peak, axis=0, keepdims=True)
            following = None
            more = h + 1 < width // 64
            weights = padded(h + 1) if more else None
            sums = None
            for block in blocks:
                if more:
                    following = store(h + 1, block, weights, buffers[(h + 1) % 2], following)
                gap = buffers[h % 2][block : block + KEYS, :] - peak
                probs = jnp.exp2(gap * factor).astype(bf16)
                side = jnp.concatenate(
                    [val[h * 64 : (h + 1) * 64, block : block + KEYS], ones], axis=0
                )
                part = dot(side, probs)
                sums = part if sums is None else sums + part
            total = sums[64:65]
            emit(h, sums[:64] / total, peak * factor + jnp.log2(total))
            peak = following

    return run


def finish_kernel(
    bit, length, scale, emb, query_a, query_b, intra_a, intra_b, enter, ctl, got, prefix, prefix_logs,
    out_w, pair_w, val_w, cand_q, hist_o, key_o, val_o, pay_o,
    shown, sem, *buffers,
):
    n, width = emb.shape
    pairs = width // LANES
    ones = same_head()
    upper = (lax.axis_index("seq") >> bit) & 1 == 1
    state = unpack_state(got[...], pairs)[0]
    before, before_logs = prefix[...], prefix_logs[...]
    entering = jnp.where(upper, before + row_factors(before_logs) * state, before)
    lane = iota((1, 2 * LANES), 1) // 64
    chunks = n // CHUNK
    gone = [jnp.zeros((pairs, LANES), f32)]
    for i in range(chunks - 1):
        gone.append(gone[-1] + ctl[i * pairs : (i + 1) * pairs, :])

    def normed(i):
        states = enter[i] + row_factors(gone[i]) * entering
        parts = []
        for p in range(0, pairs, 2):
            wide = jnp.concatenate(
                [states[p * 64 : (p + 1) * 64], states[(p + 1) * 64 : (p + 2) * 64]], axis=1
            )
            matrix = jnp.concatenate([jnp.where(lane == k, wide, 0.0) for k in range(4)], axis=0)
            query, intra = (query_a, intra_a) if p < pairs // 2 else (query_b, intra_b)
            c = (p % (pairs // 2)) * LANES
            cut = slice(c, c + 2 * LANES)
            parts.append(dot(query[chunk(i), cut], matrix.astype(bf16)) + intra[chunk(i), cut])
        mixed = jnp.concatenate(parts, axis=1)
        return (mixed * lax.rsqrt(head_means(mixed, ones) + 1e-05)).astype(bf16)

    alive_count = length[...] - lax.axis_index("seq") * n
    copies = [
        pltpu.make_async_copy(shown.at[chunk(i), :], hist_o.at[chunk(i), :], sem.at[i])
        for i in range(chunks)
    ]
    ready = normed(0)
    for i in range(chunks):
        current = ready
        if i + 1 < chunks:
            ready = normed(i + 1)
        hidden_sum = emb[chunk(i), :].astype(f32) + dot(current, out_w[...])
        alive = iota((CHUNK, 1), 0) < alive_count - i * CHUNK
        shown[chunk(i), :] = jnp.where(alive, hidden_sum, 0.0)
        copies[i].start()
        hidden = hidden_sum.astype(bf16)
        key_o[chunk(i), :] = dot(hidden, pair_w[:, :width]).astype(bf16)
        val_o[:, chunk(i)] = contract(val_w[...], hidden, 1, 1).astype(bf16)
    count = pay_o.shape[1]
    heads = width // 64
    log_rows = []

    def emit(h, attended, logs):
        pay_o[h * 64 : (h + 1) * 64, :] = attended.astype(bf16)
        log_rows.append(live(alive_count, logs))

    attend(alive_count, scale, cand_q, count, count, key_o, val_o, emit)(buffers)
    pay_o[width:, :] = pack_logs(jnp.concatenate(log_rows, axis=0))
    for copy in copies:
        copy.wait()


def live(alive_count, logs):
    return jnp.where(jnp.broadcast_to(alive_count, logs.shape) > 0, logs, DEAD)


def pack_logs(logs):
    heads, cols = logs.shape
    return jnp.concatenate(
        [*thirds(logs), jnp.zeros((log_pad(heads) - 3 * heads, cols), f32)], axis=0
    ).astype(bf16)


def log_pad(heads):
    return -(-3 * heads // 16) * 16


def unpack_logs(rows, heads):
    rows = rows.astype(f32)
    return rows[:heads] + rows[heads : 2 * heads] + rows[2 * heads : 3 * heads]


def keep_kernel(length, scale, cand_q, key, val, mean_o, logs_o, *buffers):
    alive_count = length[...] - lax.axis_index("seq") * key.shape[0]

    def emit(h, attended, logs):
        mean_o[h * 64 : (h + 1) * 64, :] = attended
        logs_o[h : h + 1, :] = live(alive_count, logs)

    attend(alive_count, scale, cand_q, 0, mean_o.shape[1], key, val, emit)(buffers)


def over_heads(rows):
    return jnp.concatenate(
        [jnp.broadcast_to(rows[h : h + 1], (64, rows.shape[1])) for h in range(rows.shape[0])],
        axis=0,
    )


def merge(parts):
    peak = parts[0][1]
    for _, logs in parts[1:]:
        peak = jnp.maximum(peak, logs)
    shares = [jnp.exp2(logs - peak) for _, logs in parts]
    total = sum(shares[1:], shares[0])
    mean = None
    for (value, _), share in zip(parts, shares):
        term = value * over_heads(share / total)
        mean = term if mean is None else mean + term
    return mean, peak + jnp.log2(total)


def received(got, heads):
    width = heads * 64
    return got[:width, :].astype(f32), unpack_logs(got[width:, :], heads)


def fold_kernel(mean, logs, got, mean_o, logs_o, pay_o):
    heads, keep = logs_o.shape
    width = heads * 64
    new_mean, new_logs = merge([(mean[...], logs[...]), received(got, heads)])
    mean_o[...] = new_mean[:, :keep]
    logs_o[...] = new_logs[:, :keep]
    pay_o[:width, :] = new_mean[:, keep:].astype(bf16)
    pay_o[width:, :] = pack_logs(new_logs[:, keep:])


def deal_kernel(mean, logs, got, mean_o, logs_o, *sends):
    heads, cols = logs_o.shape
    new_mean, new_logs = merge([(mean[...], logs[...]), received(got, heads)])
    mean_o[...] = new_mean[:, :cols]
    logs_o[...] = new_logs[:, :cols]
    whole = jnp.concatenate([new_mean, pack_logs(new_logs).astype(f32)], axis=0)
    owned = whole.shape[1] // 4
    half = whole.shape[0] // 2
    low = first_half((1, LANES))
    for k, send in enumerate(sends):
        start = (k + 1) * owned
        if 2 * owned == LANES:
            tile = whole[:, start // LANES * LANES : start // LANES * LANES + LANES]
            top, bottom = tile[:half], tile[half:]
            if start % LANES:
                top = pltpu.roll(top, owned, 1)
            else:
                bottom = pltpu.roll(bottom, owned, 1)
            send[...] = jnp.where(low, top, bottom).astype(bf16)
        else:
            send[...] = whole[:, start : start + owned].astype(bf16)


def last_kernel(owned, mean, logs, got_a, got_b, got_c, out_w, cand_o):
    heads = logs.shape[0]
    parts = [(mean[...], logs[...])]
    for got in (got_a, got_b, got_c):
        if 2 * owned == LANES:
            value = got[...].astype(f32)
            value = jnp.concatenate([value, pltpu.roll(value, owned, 1)], axis=0)
        else:
            value = got[...].astype(f32)
        parts.append((value[: heads * 64], unpack_logs(value[heads * 64 :], heads)))
    attended = merge(parts)[0].astype(bf16)
    cand_o[...] = contract(attended, out_w[...], 0, 0)[: cand_o.shape[0]]


def shape(dims, dtype):
    return jax.ShapeDtypeStruct(dims, dtype)


VMEM = pl.BlockSpec(memory_space=pltpu.VMEM)
ANY = pl.BlockSpec(memory_space=pl.ANY)
HBM = pl.BlockSpec(memory_space=pltpu.HBM)


def call(kernel, name, operands, outs, scratch=(), after=(), flops=0, space=VMEM, spaces=None):
    count = len(operands)
    if space is HBM:
        operands = [pltpu.with_memory_space_constraint(value, pltpu.HBM) for value in operands]

    def body(*refs):
        kernel(*refs[:count], *refs[count + len(after) :])

    return pl.pallas_call(
        body,
        name=name,
        in_specs=[space] * count + [ANY] * len(after),
        out_specs=spaces or [VMEM] * len(outs),
        out_shape=outs,
        scratch_shapes=list(scratch),
        compiler_params=pltpu.CompilerParams(vmem_limit_bytes=VMEM_LIMIT),
        cost_estimate=pl.CostEstimate(flops=flops, transcendentals=0, bytes_accessed=0),
    )(*operands, *after)


def reversed_bits(value, bits):
    return sum(((value >> b) & 1) << (bits - 1 - b) for b in range(bits))


def shards(
    history_item_index,
    log_head_retention,
    user_history_length,
    candidate_item_index,
    item_stored_row,
    item_embedding_table,
    head_score_scale,
    history_query_key_value_weight,
    history_output_weight,
    candidate_key_value_weight,
    candidate_query_weight,
    candidate_output_weight,
):
    users, n = history_item_index.shape
    heads = log_head_retention.shape[1]
    half, width = item_embedding_table.shape
    owned = candidate_item_index.shape[1]
    seq = lax.axis_size("seq")
    bits = seq.bit_length() - 1
    assert users == 1 and lax.axis_size("dp") == 2 and seq == 1 << bits and bits > 2
    assert width == heads * 64 and heads % 4 == 0 and owned <= 64
    pairs = heads // 2
    rows = pairs * 64
    cands = owned * seq

    def swap(value, mask):
        return lax.ppermute(value, "seq", [(j, j ^ mask) for j in range(seq)])

    peer = lax.ppermute(item_embedding_table, "dp", [(0, 1), (1, 0)])
    far_ids = swap(candidate_item_index, seq // 2)
    length = user_history_length.reshape(1, 1)
    scale = head_score_scale.reshape(1, heads)
    stored = item_stored_row.reshape(-1, LANES)
    decay = log_head_retention.reshape(heads, n)
    ids = jnp.concatenate([candidate_item_index, far_ids], axis=0)
    ids = jnp.pad(ids, ((0, 0), (0, 64 - owned)))
    id_rows = jnp.concatenate([ids // LANES, ids % LANES], axis=1).astype(f32)

    part, slot, crow, ccol, ctl, key_w = call(
        own_rows_kernel, "own_rows",
        [
            history_item_index, stored, decay, item_embedding_table,
            history_query_key_value_weight,
        ],
        [
            shape((n, width), bf16), shape((1, n), f32), shape((n // CHUNK, heads, CHUNK), f32),
            shape((n, 2 * heads), f32), shape((n // CHUNK * pairs, LANES), f32),
            shape((width, width), bf16),
        ],
        [
            pltpu.VMEM((1, n), i32), pltpu.VMEM(stored.shape, i32), pltpu.VMEM((heads, n), f32),
            pltpu.VMEM((half, width), bf16), pltpu.VMEM((width, width), bf16),
            pltpu.SemaphoreType.DMA((5,)),
        ],
        space=HBM,
        flops=2 * n * half * width,
    )
    emb, key, val, enter, pay = call(
        summary_kernel, "summary",
        [length, part, peer, slot, crow, ctl, id_rows, key_w, history_query_key_value_weight],
        [
            shape((n, width), bf16), shape((width, n), bf16), shape((n, width), bf16),
            shape((n // CHUNK, rows, LANES), f32), shape((state_rows(pairs, 2), LANES), bf16),
        ],
        flops=2 * n * half * width,
    )

    def local(first, name, after):
        return call(
            lambda *refs: local_kernel(first, *refs), name,
            [emb, key, val, crow, ccol, history_query_key_value_weight],
            [shape((n, width // 2), bf16), shape((n, width // 2), f32)],
            after=after, flops=2 * n * half * width // 2,
        )

    early = [local(0, "local_a", [])]
    prefix = logs = None
    for bit in range(bits - 1):
        got = swap(pay, 1 << bit)
        if bit == 1:
            early.append(local(width // 2, "local_b", [prefix]))
        count = 2 << bit
        final = bit == bits - 2
        sent = 1 if final else 2 * count
        pay, prefix, logs, *id_rows = call(
            lambda *refs, bit=bit, count=count: join_kernel(bit, count, pairs, *refs), "join",
            [pay, got] + ([prefix, logs] if bit else []),
            [
                shape((state_rows(pairs, sent), LANES), bf16), shape((rows, LANES), f32),
                shape((pairs, LANES), f32),
            ] + [shape((2 * count, LANES), f32)] * final,
            after=[early[-1][1]],
        )
    got = swap(pay, 1 << (bits - 1))
    half_seq = seq // 2
    places = {}
    for j in range(seq):
        places[(j & 1) * half_seq + (j >> 1)] = j
    order = [places[reversed_bits(j, bits)] for j in range(seq)]
    cand_q, val_w = call(
        lambda *refs: candidate_kernel(order, owned, *refs), "candidates",
        [
            id_rows[0], stored, item_embedding_table, peer, candidate_query_weight,
            candidate_key_value_weight,
        ],
        [shape((width, cands), bf16), shape((width, width), bf16)],
        flops=2 * cands * 2 * half * width,
    )
    (query_a, intra_a), (query_b, intra_b) = early
    send = cands // 2
    buffers = [pltpu.VMEM((n, send), f32)] * 2
    message = width + log_pad(heads)
    hist, key_two, val_two, pay = call(
        lambda *refs: finish_kernel(bits - 1, *refs), "finish",
        [
            length, scale, emb, query_a, query_b, intra_a, intra_b, enter, ctl, got, prefix, logs,
            history_output_weight, candidate_key_value_weight, val_w, cand_q,
        ],
        [
            shape((n, width), f32), shape((n, width), bf16), shape((width, n), bf16),
            shape((message, send), bf16),
        ],
        [pltpu.VMEM((n, width), f32), pltpu.SemaphoreType.DMA((n // CHUNK,))] + buffers,
        spaces=[ANY, VMEM, VMEM, VMEM],
        flops=2 * n * half * width,
    )
    mean, logs = call(
        keep_kernel, "keep", [length, scale, cand_q, key_two, val_two],
        [shape((width, send), f32), shape((heads, send), f32)],
        buffers,
        flops=2 * n * half * width,
    )
    for bit in range(bits - 3):
        got = swap(pay, 1 << bit)
        send //= 2
        mean, logs, pay = call(
            fold_kernel, "fold", [mean, logs, got],
            [shape((width, send), f32), shape((heads, send), f32), shape((message, send), bf16)],
        )
    got = swap(pay, 1 << (bits - 3))
    packed = 2 * owned == LANES
    cols = LANES if packed else owned
    mean, logs, *sends = call(
        deal_kernel, "deal", [mean, logs, got],
        [shape((width, cols), f32), shape((heads, cols), f32)]
        + [shape((message // 2, LANES) if packed else (message, owned), bf16)] * 3,
    )
    masks = [seq // 2, seq // 4, seq // 2 + seq // 4]
    gots = [None] * 3
    for k in (0, 2, 1):
        gots[k] = swap(sends[k], masks[k])
    (cand_out,) = call(
        lambda *refs: last_kernel(owned, *refs), "last",
        [mean, logs, *gots, candidate_output_weight],
        [shape((owned, width), f32)],
    )
    return hist[None], cand_out[None]


def solution(mesh):
    in_specs = (
        P(("groups", "dp"), "seq"),
        P(("groups", "dp"), None, "seq"),
        P(("groups", "dp")),
        P(("groups", "dp"), "seq"),
        P(),
        P("dp", None),
        P(),
        P(),
        P(),
        P(),
        P(),
        P(),
    )
    out_specs = (P(("groups", "dp"), "seq", None), P(("groups", "dp"), "seq", None))
    return jax.shard_map(shards, mesh=mesh, in_specs=in_specs, out_specs=out_specs, check_vma=False)
```

```python
import math

import jax
import jax.numpy as jnp
from jax import lax
from jax.experimental import pallas as pl
from jax.experimental.pallas import tpu as pltpu
from jax.sharding import PartitionSpec as P

f32, bf16, i32 = jnp.float32, jnp.bfloat16, jnp.int32
CHUNK = 256
KEYS = 512
LANES = 128
LOG2E = math.log2(math.e)
DEAD = -1e30
VMEM_LIMIT = 40 << 20


def dot(a, b):
    return jnp.dot(a, b, preferred_element_type=f32)


def contract(a, b, left, right):
    return lax.dot_general(a, b, (((left,), (right,)), ((), ())), preferred_element_type=f32)


def iota(shape, axis):
    return lax.broadcasted_iota(i32, shape, axis)


def thirds(value):
    high = value.astype(bf16).astype(f32)
    rest = value - high
    mid = rest.astype(bf16).astype(f32)
    return high, mid, rest - mid


def first_half(shape):
    return iota(shape, len(shape) - 1) % LANES < LANES // 2


def half_masks():
    low = first_half((1, LANES))
    return jnp.where(low, 1.0, 0.0).astype(bf16), jnp.where(low, 0.0, 1.0).astype(bf16)


def same_head():
    dims = (2 * LANES, 2 * LANES)
    return jnp.where(iota(dims, 0) // 64 == iota(dims, 1) // 64, 1.0, 0.0).astype(bf16)


def head_means(value, ones):
    square = (value * value).astype(bf16)
    step = ones.shape[0]
    parts = [dot(square[:, c : c + step], ones) for c in range(0, value.shape[1], step)]
    return jnp.concatenate(parts, axis=1) * (1.0 / 64.0)


def head_spread(heads, first, count):
    dims = (2 * heads, 64 * count)
    return jnp.where(iota(dims, 1) // 64 + first == iota(dims, 0) % heads, 1.0, 0.0).astype(bf16)


def spread(value, matrix):
    heads = value.shape[1] // 2
    high = value.astype(bf16).astype(f32)
    both = jnp.where(iota(value.shape, 1) < heads, high, value - high)
    return dot(both.astype(bf16), matrix)


def stored_slots(ids, stored):
    groups = stored.shape[0]
    n = ids.shape[1]
    pick = jnp.where(iota((groups, n), 0) == ids // LANES, 1.0, 0.0).astype(bf16)
    high = contract((stored // 64).astype(f32).astype(bf16), pick, 0, 0)
    low = contract((stored % 64).astype(f32).astype(bf16), pick, 0, 0)
    rows = jnp.where(iota((LANES, n), 0) == ids % LANES, high * 64.0 + low, 0.0)
    return jnp.sum(rows, axis=0, keepdims=True)


def picked_rows(slots, first, table):
    count = table.shape[0]
    hot = jnp.where(iota((count, slots.shape[1]), 0) == slots.astype(i32) - first, 1.0, 0.0)
    return contract(hot.astype(bf16), table[...], 0, 0)


def chunk(i):
    return slice(i * CHUNK, (i + 1) * CHUNK)


def pair_cut(p):
    return slice(p * LANES, (p + 1) * LANES)


def own_rows_kernel(
    ids_in, stored_in, decay_in, own_in, weight_in, part_o, slot_o, crow_o, ccol_o, ctl_o, key_w_o,
    ids, stored, decay, own, key_w, sem,
):
    n, half, heads = ids.shape[1], own.shape[0], decay.shape[0]
    width = own.shape[1]
    middle = weight_in.at[:, width : 2 * width]
    copies = [
        pltpu.make_async_copy(source, target, sem.at[k])
        for k, (source, target) in enumerate(
            (
                (ids_in, ids), (stored_in, stored), (decay_in, decay), (middle, key_w),
                (own_in.at[: half // 2], own.at[: half // 2]),
                (own_in.at[half // 2 :], own.at[half // 2 :]),
            )
        )
    ]
    for copy in copies:
        copy.start()
    copies[0].wait()
    copies[1].wait()
    slots = stored_slots(ids[...], stored[...])
    slot_o[...] = slots
    copies[2].wait()
    upto = jnp.where(
        iota((CHUNK, CHUNK), 0) <= iota((CHUNK, CHUNK), 1), 1.0, 0.0
    ).astype(bf16)
    low = first_half((1, LANES))
    for i in range(n // CHUNK):
        pieces = jnp.concatenate(thirds(decay[:, chunk(i)]), axis=0)
        sums = dot(pieces.astype(bf16), upto)
        cum = sums[:heads] + sums[heads : 2 * heads] + sums[2 * heads :]
        crow_o[i] = cum
        ccol_o[chunk(i), :] = jnp.transpose(jnp.concatenate([cum, cum], axis=0))
        for p in range(heads // 2):
            r = i * (heads // 2) + p
            ctl_o[r : r + 1, :] = jnp.where(
                low, cum[2 * p : 2 * p + 1, CHUNK - 1 :], cum[2 * p + 1 : 2 * p + 2, CHUNK - 1 :]
            )
    copies[3].wait()
    key_w_o[...] = jnp.transpose(key_w[...].astype(f32)).astype(bf16)
    first = lax.axis_index("dp") * half
    for k in range(2):
        copies[4 + k].wait()
        piece = own.at[k * half // 2 : (k + 1) * half // 2]
        for i in range(n // CHUNK):
            rows = picked_rows(slots[:, chunk(i)], first + k * half // 2, piece)
            if k:
                rows += part_o[chunk(i), :].astype(f32)
            part_o[chunk(i), :] = rows.astype(bf16)


def summary_kernel(
    length, part, peer, slot, crow, ctl, id_rows, key_w, weight,
    emb_o, key_o, val_o, enter_o, pay_o, here_o,
):
    n, width = part.shape
    half, heads = peer.shape[0], crow.shape[1]
    pairs = heads // 2
    block = LANES // 2
    low = first_half((1, LANES))
    chunks = n // CHUNK
    here = length[0] - lax.axis_index("seq") * n
    here_o[...] = jnp.full(here_o.shape, here, i32)

    def project(i):
        other = picked_rows(slot[:, chunk(i)], (1 - lax.axis_index("dp")) * half, peer)
        emb = (part[chunk(i), :].astype(f32) + other).astype(bf16)
        emb_o[chunk(i), :] = emb
        return contract(key_w[...], emb, 1, 1), dot(emb, weight[:, 2 * width :])

    total = [jnp.zeros((block, LANES), f32)] * pairs
    ready = project(0)
    for i in range(chunks):
        key, val = ready
        if i + 1 < chunks:
            ready = project(i + 1)
        val = jnp.where(iota((CHUNK, 1), 0) < here - i * CHUNK, val, 0.0).astype(bf16)
        val_o[chunk(i), :] = val
        alive = iota((1, CHUNK), 1) < here - i * CHUNK
        cum = crow[i]
        tail = jnp.exp(cum[:, CHUNK - 1 :] - cum)
        for p in range(pairs):
            keyed = []
            for h in (2 * p, 2 * p + 1):
                rows = key[h * 64 : (h + 1) * 64]
                mean = jnp.sum(rows * rows, axis=0, keepdims=True) * (1.0 / 64.0)
                unit = jnp.where(alive, lax.rsqrt(mean + 1e-06) * 0.125, 0.0)
                normed = rows * unit
                key_o[h * 64 : (h + 1) * 64, chunk(i)] = normed.astype(bf16)
                keyed.append(normed * tail[h : h + 1])
            keyed = jnp.concatenate(keyed, axis=0).astype(bf16)
            both = dot(keyed, val[:, pair_cut(p)])
            fresh = jnp.where(low, both[:block], both[block:])
            enter_o[i, p * block : (p + 1) * block, :] = total[p]
            total[p] = total[p] * jnp.exp(ctl[i * pairs + p : i * pairs + p + 1, :]) + fresh
    logs = ctl[0:pairs, :]
    for i in range(1, chunks):
        logs = logs + ctl[i * pairs : (i + 1) * pairs, :]
    pay_o[...] = pack_state(jnp.concatenate(total, axis=0), logs, id_rows[...])


def state_rows(pairs, ids):
    return pairs * 64 + -(-(3 * pairs + ids) // 16) * 16


def pack_state(state, logs, id_rows):
    pairs, ids = logs.shape[0], id_rows.shape[0]
    pad = state_rows(pairs, ids) - state.shape[0] - 3 * pairs - ids
    parts = [state, *thirds(logs), id_rows] + [jnp.zeros((pad, LANES), f32)] * (pad > 0)
    return jnp.concatenate(parts, axis=0).astype(bf16)


def unpack_state(packed, pairs):
    whole = packed.astype(f32)
    rows = pairs * 64
    logs = whole[rows : rows + pairs]
    for k in (1, 2):
        logs = logs + whole[rows + k * pairs : rows + (k + 1) * pairs]
    return whole[:rows], logs, whole[rows + 3 * pairs :]


def row_factors(logs):
    factors = jnp.exp(logs)
    return jnp.concatenate(
        [jnp.broadcast_to(factors[p : p + 1], (64, LANES)) for p in range(logs.shape[0])], axis=0
    )


def join_kernel(bit, ids, pairs, mine, got, *refs):
    before = refs[: 2 if bit else 0]
    pay_o, prefix_o, logs_o = refs[len(before) :]
    upper = (lax.axis_index("seq") >> bit) & 1 == 1
    state, logs, rows = unpack_state(mine[...], pairs)
    other, other_logs, other_rows = unpack_state(got[...], pairs)
    early = jnp.where(upper, other, state)
    late = jnp.where(upper, state, other)
    factor = row_factors(jnp.where(upper, logs, other_logs))
    id_rows = jnp.concatenate([rows[:ids], other_rows[:ids]], axis=0)
    pay_o[...] = pack_state(early * factor + late, logs + other_logs, id_rows)
    if bit == 0:
        prefix_o[...] = jnp.where(upper, other, 0.0)
        logs_o[...] = jnp.where(upper, other_logs, 0.0)
    else:
        prefix, prefix_logs = before[0][...], before[1][...]
        prefix_o[...] = jnp.where(upper, prefix + row_factors(prefix_logs) * other, prefix)
        logs_o[...] = jnp.where(upper, prefix_logs + other_logs, prefix_logs)


def local_kernel(first, emb, key, val, crow, ccol, weight, query_o, intra_o):
    n, width = query_o.shape
    heads = ccol.shape[1] // 2
    ones, lanes = same_head(), head_spread(heads, first // 64, width // 64)
    mask_a, mask_b = half_masks()
    causal = iota((CHUNK, CHUNK), 0) >= iota((CHUNK, CHUNK), 1)

    def queries(i):
        query = dot(emb[chunk(i), :], weight[:, first : first + width])
        unit = lax.rsqrt(head_means(query, ones) + 1e-06) * 0.125
        query = query * unit
        decayed = query * spread(jnp.exp(ccol[chunk(i), :]), lanes)
        query_o[chunk(i), :] = decayed.astype(bf16)
        return query.astype(bf16)

    def scores(i, p, b, query):
        cut = pair_cut(p)
        wide = slice(first + p * LANES, first + (p + 1) * LANES)
        return dot(query[:, cut] * (mask_b if b else mask_a), key[wide, chunk(i)])

    units = [(i, p, b) for i in range(n // CHUNK) for p in range(width // LANES) for b in (0, 1)]
    query = {0: queries(0)}
    ready = scores(*units[0], query[0])
    held = None
    for u, (i, p, b) in enumerate(units):
        current = ready
        if u + 1 < len(units):
            j = units[u + 1][0]
            if j not in query:
                query[j] = queries(j)
            ready = scores(*units[u + 1], query[j])
        h = first // 64 + 2 * p + b
        gap = ccol[chunk(i), h : h + 1] - crow[i, h : h + 1, :]
        weights = jnp.where(causal, current * jnp.exp(gap), 0.0).astype(bf16)
        wide = slice(first + p * LANES, first + (p + 1) * LANES)
        part = dot(weights, val[chunk(i), wide] * (mask_b if b else mask_a))
        if b == 0:
            held = part
        else:
            intra_o[chunk(i), pair_cut(p)] = held + part


def candidate_kernel(order, owned, message, stored, own, peer, query_w, *refs):
    half, width = own.shape
    pairs = width // LANES
    ids = message[pairs * 64 :, :].astype(f32)
    ids = (ids * float(LANES) + pltpu.roll(ids, LANES // 2, 1)).astype(i32)
    slots = [stored_slots(ids[3 * pairs + j : 3 * pairs + j + 1], stored[...]) for j in order]
    step = LANES // owned
    tiles = []
    for start in range(0, len(order), step):
        tile = slots[start]
        for k in range(1, step):
            moved = pltpu.roll(slots[start + k], k * owned, 1)
            tile = jnp.where(iota((1, LANES), 1) >= k * owned, moved, tile)
        tiles.append(tile)
    slots = jnp.concatenate(tiles, axis=1)
    dp = lax.axis_index("dp")
    rows = picked_rows(slots, dp * half, own) + picked_rows(slots, (1 - dp) * half, peer)
    query = jnp.transpose(dot(rows.astype(bf16), query_w[...])).astype(bf16)
    if len(refs) > 2:
        pair_w, *refs, val_w_o = refs
        val_w_o[...] = jnp.transpose(pair_w[:, width:].astype(f32)).astype(bf16)
    part = query.shape[1] // 2
    refs[0][...] = query[:, :part]
    refs[1][...] = query[:, part:]


def attend(alive_count, scale, heads, queries, key, val, emit):
    n = key.shape[0]
    cols = sum(query.shape[1] for query in queries)
    blocks = range(0, n, KEYS)

    def padded(h):
        cut = slice(h * 64, (h + 1) * 64)
        rows = jnp.concatenate([query[cut, :] for query in queries], axis=1)
        zero = jnp.zeros_like(rows)
        return jnp.concatenate([zero, rows] if h % 2 else [rows, zero], axis=0)

    def scores(h, block, weights):
        rows = slice(block, block + KEYS)
        values = dot(key[rows, pair_cut(h // 2)], weights)
        alive = iota((KEYS, 1), 0) < alive_count - block
        return jnp.where(alive, values, DEAD)

    def store(h, block, weights, buffer, peak):
        values = scores(h, block, weights)
        buffer[block : block + KEYS, :] = values
        top = jnp.max(values.reshape(KEYS // 8, 8, cols), axis=0)
        return top if peak is None else jnp.maximum(peak, top)

    def run(buffers):
        ones = jnp.ones((16, KEYS), bf16)
        peak, weights = None, padded(heads[0])
        for block in blocks:
            peak = store(heads[0], block, weights, buffers[heads[0] % 2], peak)
        for h in heads:
            factor = scale[0:1, h : h + 1] * LOG2E
            peak = jnp.max(peak, axis=0, keepdims=True)
            following = None
            more = h + 1 in heads
            weights = padded(h + 1) if more else None
            sums = None
            for block in blocks:
                if more:
                    following = store(h + 1, block, weights, buffers[(h + 1) % 2], following)
                gap = buffers[h % 2][block : block + KEYS, :] - peak
                probs = jnp.exp2(gap * factor).astype(bf16)
                side = jnp.concatenate(
                    [val[h * 64 : (h + 1) * 64, block : block + KEYS], ones], axis=0
                )
                part = dot(side, probs)
                sums = part if sums is None else sums + part
            total = sums[64:65]
            emit(h, sums[:64] / total, peak * factor + jnp.log2(total))
            peak = following

    return run


def finish_kernel(
    bit, here, scale, emb, query_a, query_b, intra_a, intra_b, enter, ctl, got, prefix, prefix_logs,
    out_w, pair_w, val_w, cand_a, cand_b, hist_o, key_o, val_o, pay_o,
    shown, sem, *buffers,
):
    n, width = emb.shape
    pairs = width // LANES
    ones = same_head()
    upper = (lax.axis_index("seq") >> bit) & 1 == 1
    state = unpack_state(got[...], pairs)[0]
    before, before_logs = prefix[...], prefix_logs[...]
    entering = jnp.where(upper, before + row_factors(before_logs) * state, before)
    lane = iota((1, 2 * LANES), 1) // 64
    chunks = n // CHUNK
    gone = [jnp.zeros((pairs, LANES), f32)]
    for i in range(chunks - 1):
        gone.append(gone[-1] + ctl[i * pairs : (i + 1) * pairs, :])

    def normed(i):
        states = enter[i] + row_factors(gone[i]) * entering
        parts = []
        for p in range(0, pairs, 2):
            wide = jnp.concatenate(
                [states[p * 64 : (p + 1) * 64], states[(p + 1) * 64 : (p + 2) * 64]], axis=1
            )
            matrix = jnp.concatenate([jnp.where(lane == k, wide, 0.0) for k in range(4)], axis=0)
            query, intra = (query_a, intra_a) if p < pairs // 2 else (query_b, intra_b)
            c = (p % (pairs // 2)) * LANES
            cut = slice(c, c + 2 * LANES)
            parts.append(dot(query[chunk(i), cut], matrix.astype(bf16)) + intra[chunk(i), cut])
        mixed = jnp.concatenate(parts, axis=1)
        return (mixed * lax.rsqrt(head_means(mixed, ones) + 1e-05)).astype(bf16)

    alive_count = here[0:1, 0:1]
    copies = [
        pltpu.make_async_copy(shown.at[chunk(i), :], hist_o.at[chunk(i), :], sem.at[i])
        for i in range(chunks)
    ]
    ready = normed(0)
    for i in range(chunks):
        current = ready
        if i + 1 < chunks:
            ready = normed(i + 1)
        hidden_sum = emb[chunk(i), :].astype(f32) + dot(current, out_w[...])
        alive = iota((CHUNK, 1), 0) < alive_count - i * CHUNK
        shown[chunk(i), :] = jnp.where(alive, hidden_sum, 0.0)
        copies[i].start()
        hidden = hidden_sum.astype(bf16)
        key_o[chunk(i), :] = dot(hidden, pair_w[:, :width]).astype(bf16)
        val_o[:, chunk(i)] = contract(val_w[...], hidden, 1, 1).astype(bf16)
    send_part(alive_count, scale, 0, (cand_a, cand_b), key_o, val_o, pay_o, buffers)
    for copy in copies:
        copy.wait()


def send_part(alive_count, scale, first, queries, key, val, pay_o, buffers):
    heads = range(first, first + val.shape[0] // 128)
    count = len(heads) * 64
    log_rows = []

    def emit(h, attended, logs):
        h -= first
        pay_o[h * 64 : (h + 1) * 64, :] = attended.astype(bf16)
        log_rows.append(live(alive_count, logs))

    attend(alive_count, scale, heads, queries, key, val, emit)(buffers)
    pay_o[count:, :] = pack_logs(jnp.concatenate(log_rows, axis=0))


def send_kernel(here, scale, cand_a, cand_b, key, val, pay_o, *buffers):
    first = val.shape[0] // 128
    send_part(here[0:1, 0:1], scale, first, (cand_a, cand_b), key, val, pay_o, buffers)


def live(alive_count, logs):
    return jnp.where(jnp.broadcast_to(alive_count, logs.shape) > 0, logs, DEAD)


def pack_logs(logs):
    heads, cols = logs.shape
    return jnp.concatenate(
        [*thirds(logs), jnp.zeros((log_pad(heads) - 3 * heads, cols), f32)], axis=0
    ).astype(bf16)


def log_pad(heads):
    return -(-3 * heads // 16) * 16


def unpack_logs(rows, heads):
    rows = rows.astype(f32)
    return rows[:heads] + rows[heads : 2 * heads] + rows[2 * heads : 3 * heads]


def keep_kernel(here, scale, cand_a, cand_b, key, val, mean_o, logs_o, *buffers):
    alive_count = here[0:1, 0:1]

    def emit(h, attended, logs):
        mean_o[h * 64 : (h + 1) * 64, :] = attended
        logs_o[h : h + 1, :] = live(alive_count, logs)

    heads = range(val.shape[0] // 64)
    attend(alive_count, scale, heads, (cand_a, cand_b), key, val, emit)(buffers)


def over_heads(rows):
    return jnp.concatenate(
        [jnp.broadcast_to(rows[h : h + 1], (64, rows.shape[1])) for h in range(rows.shape[0])],
        axis=0,
    )


def merge(parts):
    peak = parts[0][1]
    for _, logs in parts[1:]:
        peak = jnp.maximum(peak, logs)
    shares = [jnp.exp2(logs - peak) for _, logs in parts]
    total = sum(shares[1:], shares[0])
    mean = None
    for (value, _), share in zip(parts, shares):
        term = value * over_heads(share / total)
        mean = term if mean is None else mean + term
    return mean, peak + jnp.log2(total)


def received(gots, heads):
    share = heads // len(gots)
    means = [got[: share * 64, :].astype(f32) for got in gots]
    logs = [unpack_logs(got[share * 64 :, :], share) for got in gots]
    return jnp.concatenate(means, axis=0), jnp.concatenate(logs, axis=0)


def fold_kernel(mean, logs, *refs):
    gots, (mean_o, logs_o, pay_o) = refs[:-3], refs[-3:]
    heads, keep = logs_o.shape
    width = heads * 64
    new_mean, new_logs = merge([(mean[...], logs[...]), received(gots, heads)])
    mean_o[...] = new_mean[:, :keep]
    logs_o[...] = new_logs[:, :keep]
    pay_o[:width, :] = new_mean[:, keep:].astype(bf16)
    pay_o[width:, :] = pack_logs(new_logs[:, keep:])


def deal_kernel(blocks, mean, logs, *refs):
    gots, mean_o, logs_o, sends = refs[:-5], refs[-5], refs[-4], refs[-3:]
    heads, cols = logs_o.shape
    new_mean, new_logs = merge([(mean[...], logs[...]), received(gots, heads)])
    mean_o[...] = new_mean[:, :cols]
    logs_o[...] = new_logs[:, :cols]
    whole = jnp.concatenate([new_mean, pack_logs(new_logs).astype(f32)], axis=0)
    owned = whole.shape[1] // 4
    half = whole.shape[0] // 2
    low = first_half((1, LANES))
    for block, send in zip(blocks, sends):
        start = block * owned
        if 2 * owned == LANES:
            tile = whole[:, start // LANES * LANES : start // LANES * LANES + LANES]
            top, bottom = tile[:half], tile[half:]
            if start % LANES:
                top = pltpu.roll(top, owned, 1)
            else:
                bottom = pltpu.roll(bottom, owned, 1)
            send[...] = jnp.where(low, top, bottom).astype(bf16)
        else:
            send[...] = whole[:, start : start + owned].astype(bf16)


def last_kernel(owned, mean, logs, got_a, got_b, got_c, out_w, cand_o):
    heads = logs.shape[0]
    parts = [(mean[...], logs[...])]
    for got in (got_a, got_b, got_c):
        if 2 * owned == LANES:
            value = got[...].astype(f32)
            value = jnp.concatenate([value, pltpu.roll(value, owned, 1)], axis=0)
        else:
            value = got[...].astype(f32)
        parts.append((value[: heads * 64], unpack_logs(value[heads * 64 :], heads)))
    attended = merge(parts)[0].astype(bf16)
    cand_o[...] = contract(attended, out_w[...], 0, 0)[: cand_o.shape[0]]


def shape(dims, dtype):
    return jax.ShapeDtypeStruct(dims, dtype)


VMEM = pl.BlockSpec(memory_space=pltpu.VMEM)
SMEM = pl.BlockSpec(memory_space=pltpu.SMEM)
ANY = pl.BlockSpec(memory_space=pl.ANY)
HBM = pl.BlockSpec(memory_space=pltpu.HBM)


def call(kernel, name, operands, outs, scratch=(), after=(), flops=0, space=VMEM, spaces=None, scalars=()):
    count = len(scalars) + len(operands)
    if space is HBM:
        operands = [pltpu.with_memory_space_constraint(value, pltpu.HBM) for value in operands]

    def body(*refs):
        kernel(*refs[:count], *refs[count + len(after) :])

    return pl.pallas_call(
        body,
        name=name,
        in_specs=[SMEM] * len(scalars) + [space] * len(operands) + [ANY] * len(after),
        out_specs=spaces or [VMEM] * len(outs),
        out_shape=outs,
        scratch_shapes=list(scratch),
        compiler_params=pltpu.CompilerParams(vmem_limit_bytes=VMEM_LIMIT),
        cost_estimate=pl.CostEstimate(flops=flops, transcendentals=0, bytes_accessed=0),
    )(*scalars, *operands, *after)


def reversed_bits(value, bits):
    return sum(((value >> b) & 1) << (bits - 1 - b) for b in range(bits))


def shards(
    history_item_index,
    log_head_retention,
    user_history_length,
    candidate_item_index,
    item_stored_row,
    item_embedding_table,
    head_score_scale,
    history_query_key_value_weight,
    history_output_weight,
    candidate_key_value_weight,
    candidate_query_weight,
    candidate_output_weight,
):
    users, n = history_item_index.shape
    heads = log_head_retention.shape[1]
    half, width = item_embedding_table.shape
    owned = candidate_item_index.shape[1]
    seq = lax.axis_size("seq")
    bits = seq.bit_length() - 1
    assert users == 1 and lax.axis_size("dp") == 2 and seq == 1 << bits and bits > 2
    assert width == heads * 64 and heads % 4 == 0 and LANES % owned == 0 and owned <= 64
    pairs = heads // 2
    rows = pairs * 64
    cands = owned * seq

    def swap(value, mask):
        return lax.ppermute(value, "seq", [(j, j ^ mask) for j in range(seq)])

    peer = lax.ppermute(item_embedding_table, "dp", [(0, 1), (1, 0)])
    scale = head_score_scale.reshape(1, heads)
    stored = item_stored_row.reshape(-1, LANES)
    decay = log_head_retention.reshape(heads, n)
    ids = jnp.pad(candidate_item_index, ((0, 0), (0, 64 - owned)))
    id_rows = jnp.concatenate([ids // LANES, ids % LANES], axis=1).astype(f32)

    part, slot, crow, ccol, ctl, key_w = call(
        own_rows_kernel, "own_rows",
        [
            history_item_index, stored, decay, item_embedding_table,
            history_query_key_value_weight,
        ],
        [
            shape((n, width), bf16), shape((1, n), f32), shape((n // CHUNK, heads, CHUNK), f32),
            shape((n, 2 * heads), f32), shape((n // CHUNK * pairs, LANES), f32),
            shape((width, width), bf16),
        ],
        [
            pltpu.VMEM((1, n), i32), pltpu.VMEM(stored.shape, i32), pltpu.VMEM((heads, n), f32),
            pltpu.VMEM((half, width), bf16), pltpu.VMEM((width, width), bf16),
            pltpu.SemaphoreType.DMA((6,)),
        ],
        space=HBM,
        flops=2 * n * half * width,
    )
    emb, key, val, enter, pay, here = call(
        summary_kernel, "summary",
        [part, peer, slot, crow, ctl, id_rows, key_w, history_query_key_value_weight],
        [
            shape((n, width), bf16), shape((width, n), bf16), shape((n, width), bf16),
            shape((n // CHUNK, rows, LANES), f32), shape((state_rows(pairs, 1), LANES), bf16),
            shape((8, LANES), i32),
        ],
        scalars=[user_history_length],
        flops=2 * n * half * width,
    )

    def local(first, name, after):
        return call(
            lambda *refs: local_kernel(first, *refs), name,
            [emb, key, val, crow, ccol, history_query_key_value_weight],
            [shape((n, width // 2), bf16), shape((n, width // 2), f32)],
            after=after, flops=2 * n * half * width // 2,
        )

    early = [local(0, "local_a", [])]
    prefix = logs = None
    for bit in range(bits - 1):
        got = swap(pay, 1 << bit)
        if bit == 1:
            early.append(local(width // 2, "local_b", [prefix]))
        count = 1 << bit
        pay, prefix, logs = call(
            lambda *refs, bit=bit, count=count: join_kernel(bit, count, pairs, *refs), "join",
            [pay, got] + ([prefix, logs] if bit else []),
            [
                shape((state_rows(pairs, 2 * count), LANES), bf16), shape((rows, LANES), f32),
                shape((pairs, LANES), f32),
            ],
            after=[early[-1][1]],
        )
    got = swap(pay, 1 << (bits - 1))
    order = [reversed_bits(j, bits) for j in range(seq)]
    half_order = list(range(seq // 2))
    if seq == 8:
        half_order = [0, 2, 1, 3]
        order = [0, 2, 4, 6, 1, 3, 5, 7]
    quarter = cands // 4

    def candidates(message, name, pair_w):
        return call(
            lambda *refs: candidate_kernel(half_order, owned, *refs), name,
            [message, stored, item_embedding_table, peer, candidate_query_weight, *pair_w],
            [shape((width, quarter), bf16)] * 2 + [shape((width, width), bf16)] * len(pair_w),
            flops=cands * 2 * half * width,
        )

    keep_a, send_a, val_w = candidates(pay, "near", [candidate_key_value_weight])
    keep_b, send_b = candidates(got, "far", [])
    if seq != 8:
        every = jnp.concatenate([keep_a, send_a, keep_b, send_b], axis=1)
        every = every.reshape(width, seq, owned)[:, jnp.array(order)].reshape(width, cands)
        keep_a, keep_b, send_a, send_b = (
            every[:, k * quarter : (k + 1) * quarter] for k in range(4)
        )
    (query_a, intra_a), (query_b, intra_b) = early
    send = cands // 2
    buffers = [pltpu.VMEM((n, send), f32)] * 2
    message = width + log_pad(heads)
    share = width // 2 + log_pad(heads // 2)
    hist, key_two, val_two, pay_a = call(
        lambda *refs: finish_kernel(bits - 1, *refs), "finish",
        [
            here, scale, emb, query_a, query_b, intra_a, intra_b, enter, ctl, got, prefix, logs,
            history_output_weight, candidate_key_value_weight, val_w, send_a, send_b,
        ],
        [
            shape((n, width), f32), shape((n, width), bf16), shape((width, n), bf16),
            shape((share, send), bf16),
        ],
        [pltpu.VMEM((n, width), f32), pltpu.SemaphoreType.DMA((n // CHUNK,))] + buffers,
        spaces=[ANY, VMEM, VMEM, VMEM],
        flops=2 * n * half * width,
    )
    (pay_b,) = call(
        send_kernel, "send", [here, scale, send_a, send_b, key_two, val_two],
        [shape((share, send), bf16)], buffers, flops=n * half * width,
    )
    gots = [swap(pay_a, 1), swap(pay_b, 1)]
    mean, logs = call(
        keep_kernel, "keep", [here, scale, keep_a, keep_b, key_two, val_two],
        [shape((width, send), f32), shape((heads, send), f32)], buffers, after=[pay_b],
        flops=2 * n * half * width,
    )
    for bit in range(1, bits - 2):
        send //= 2
        mean, logs, pay = call(
            fold_kernel, "fold", [mean, logs, *gots],
            [shape((width, send), f32), shape((heads, send), f32), shape((message, send), bf16)],
        )
        gots = [swap(pay, 1 << bit)]
    packed = 2 * owned == LANES
    cols = LANES if packed else owned
    blocks = [2, 3, 1] if seq == 8 else [1, 3, 2]
    mean, logs, *sends = call(
        lambda *refs: deal_kernel(blocks, *refs), "deal", [mean, logs, *gots],
        [shape((width, cols), f32), shape((heads, cols), f32)]
        + [shape((message // 2, LANES) if packed else (message, owned), bf16)] * 3,
    )
    gots = [swap(value, order[block]) for value, block in zip(sends, blocks)]
    (cand_out,) = call(
        lambda *refs: last_kernel(owned, *refs), "last",
        [mean, logs, *gots, candidate_output_weight],
        [shape((owned, width), f32)],
    )
    return hist[None], cand_out[None]


def solution(mesh):
    in_specs = (
        P(("groups", "dp"), "seq"),
        P(("groups", "dp"), None, "seq"),
        P(("groups", "dp")),
        P(("groups", "dp"), "seq"),
        P(),
        P("dp", None),
        P(),
        P(),
        P(),
        P(),
        P(),
        P(),
    )
    out_specs = (P(("groups", "dp"), "seq", None), P(("groups", "dp"), "seq", None))
    return jax.shard_map(shards, mesh=mesh, in_specs=in_specs, out_specs=out_specs, check_vma=False)
```

```python
import math

import jax
import jax.numpy as jnp
from jax import lax
from jax.experimental import pallas as pl
from jax.experimental.pallas import tpu as pltpu
from jax.sharding import PartitionSpec as P

f32, bf16, i32 = jnp.float32, jnp.bfloat16, jnp.int32
CHUNK = 256
KEYS = 512
LANES = 128
LOG2E = math.log2(math.e)
DEAD = -1e30
VMEM_LIMIT = 40 << 20


def dot(a, b):
    return jnp.dot(a, b, preferred_element_type=f32)


def contract(a, b, left, right):
    return lax.dot_general(a, b, (((left,), (right,)), ((), ())), preferred_element_type=f32)


def iota(shape, axis):
    return lax.broadcasted_iota(i32, shape, axis)


def thirds(value):
    high = value.astype(bf16).astype(f32)
    rest = value - high
    mid = rest.astype(bf16).astype(f32)
    return high, mid, rest - mid


def first_half(shape):
    return iota(shape, len(shape) - 1) % LANES < LANES // 2


def half_masks():
    low = first_half((1, LANES))
    return jnp.where(low, 1.0, 0.0).astype(bf16), jnp.where(low, 0.0, 1.0).astype(bf16)


def same_head():
    dims = (2 * LANES, 2 * LANES)
    return jnp.where(iota(dims, 0) // 64 == iota(dims, 1) // 64, 1.0, 0.0).astype(bf16)


def head_means(value, ones):
    square = (value * value).astype(bf16)
    step = ones.shape[0]
    parts = [dot(square[:, c : c + step], ones) for c in range(0, value.shape[1], step)]
    return jnp.concatenate(parts, axis=1) * (1.0 / 64.0)


def head_spread(heads, first, count):
    dims = (2 * heads, 64 * count)
    return jnp.where(iota(dims, 1) // 64 + first == iota(dims, 0) % heads, 1.0, 0.0).astype(bf16)


def spread(value, matrix):
    heads = value.shape[1] // 2
    high = value.astype(bf16).astype(f32)
    both = jnp.where(iota(value.shape, 1) < heads, high, value - high)
    return dot(both.astype(bf16), matrix)


def stored_slots(ids, stored):
    groups = stored.shape[0]
    n = ids.shape[1]
    pick = jnp.where(iota((groups, n), 0) == ids // LANES, 1.0, 0.0).astype(bf16)
    high = contract((stored // 64).astype(f32).astype(bf16), pick, 0, 0)
    low = contract((stored % 64).astype(f32).astype(bf16), pick, 0, 0)
    rows = jnp.where(iota((LANES, n), 0) == ids % LANES, high * 64.0 + low, 0.0)
    return jnp.sum(rows, axis=0, keepdims=True)


def picked_rows(slots, first, table):
    count = table.shape[0]
    hot = jnp.where(iota((count, slots.shape[1]), 0) == slots.astype(i32) - first, 1.0, 0.0)
    return contract(hot.astype(bf16), table[...], 0, 0)


def chunk(i):
    return slice(i * CHUNK, (i + 1) * CHUNK)


def pair_cut(p):
    return slice(p * LANES, (p + 1) * LANES)


def own_rows_kernel(
    ids_in, stored_in, decay_in, own_in, weight_in, cand_in,
    part_o, slot_o, crow_o, ccol_o, ctl_o, key_w_o, id_rows_o,
    ids, stored, decay, own, key_w, cand, sem,
):
    n, half, heads = ids.shape[1], own.shape[0], decay.shape[0]
    width = own.shape[1]
    middle = weight_in.at[:, width : 2 * width]
    copies = [
        pltpu.make_async_copy(source, target, sem.at[k])
        for k, (source, target) in enumerate(
            (
                (ids_in, ids), (stored_in, stored), (decay_in, decay), (middle, key_w),
                (own_in.at[: half // 2], own.at[: half // 2]),
                (own_in.at[half // 2 :], own.at[half // 2 :]), (cand_in, cand),
            )
        )
    ]
    for copy in copies:
        copy.start()
    copies[0].wait()
    copies[1].wait()
    slots = stored_slots(ids[...], stored[...])
    slot_o[...] = slots
    copies[6].wait()
    wide = jnp.concatenate([cand[...], jnp.zeros((1, LANES - cand.shape[1]), i32)], axis=1).astype(f32)
    high = jnp.floor(wide * (1.0 / LANES))
    low = pltpu.roll(jnp.broadcast_to(wide - high * LANES, (8, LANES)), LANES // 2, 1)[:1]
    id_rows_o[...] = jnp.where(first_half((1, LANES)), high, low)
    copies[2].wait()
    upto = jnp.where(
        iota((CHUNK, CHUNK), 0) <= iota((CHUNK, CHUNK), 1), 1.0, 0.0
    ).astype(bf16)
    low = first_half((1, LANES))
    for i in range(n // CHUNK):
        pieces = jnp.concatenate(thirds(decay[:, chunk(i)]), axis=0)
        sums = dot(pieces.astype(bf16), upto)
        cum = sums[:heads] + sums[heads : 2 * heads] + sums[2 * heads :]
        crow_o[i] = cum
        ccol_o[chunk(i), :] = jnp.transpose(jnp.concatenate([cum, cum], axis=0))
        for p in range(heads // 2):
            r = i * (heads // 2) + p
            ctl_o[r : r + 1, :] = jnp.where(
                low, cum[2 * p : 2 * p + 1, CHUNK - 1 :], cum[2 * p + 1 : 2 * p + 2, CHUNK - 1 :]
            )
    copies[3].wait()
    key_w_o[...] = jnp.transpose(key_w[...].astype(f32)).astype(bf16)
    first = lax.axis_index("dp") * half
    for k in range(2):
        copies[4 + k].wait()
        piece = own.at[k * half // 2 : (k + 1) * half // 2]
        for i in range(n // CHUNK):
            rows = picked_rows(slots[:, chunk(i)], first + k * half // 2, piece)
            if k:
                rows += part_o[chunk(i), :].astype(f32)
            part_o[chunk(i), :] = rows.astype(bf16)


def summary_kernel(
    length, part, peer, slot, crow, ctl, id_rows, key_w, weight,
    emb_o, key_o, val_o, enter_o, pay_o, here_o,
):
    n, width = part.shape
    half, heads = peer.shape[0], crow.shape[1]
    pairs = heads // 2
    block = LANES // 2
    low = first_half((1, LANES))
    chunks = n // CHUNK
    here = length[0] - lax.axis_index("seq") * n
    here_o[...] = jnp.full(here_o.shape, here, i32)

    def project(i):
        other = picked_rows(slot[:, chunk(i)], (1 - lax.axis_index("dp")) * half, peer)
        emb = (part[chunk(i), :].astype(f32) + other).astype(bf16)
        emb_o[chunk(i), :] = emb
        return contract(key_w[...], emb, 1, 1), dot(emb, weight[:, 2 * width :])

    total = [jnp.zeros((block, LANES), f32)] * pairs
    ready = project(0)
    for i in range(chunks):
        key, val = ready
        if i + 1 < chunks:
            ready = project(i + 1)
        val = jnp.where(iota((CHUNK, 1), 0) < here - i * CHUNK, val, 0.0).astype(bf16)
        val_o[chunk(i), :] = val
        alive = iota((1, CHUNK), 1) < here - i * CHUNK
        cum = crow[i]
        tail = jnp.exp(cum[:, CHUNK - 1 :] - cum)
        for p in range(pairs):
            keyed = []
            for h in (2 * p, 2 * p + 1):
                rows = key[h * 64 : (h + 1) * 64]
                mean = jnp.sum(rows * rows, axis=0, keepdims=True) * (1.0 / 64.0)
                unit = jnp.where(alive, lax.rsqrt(mean + 1e-06) * 0.125, 0.0)
                normed = rows * unit
                key_o[h * 64 : (h + 1) * 64, chunk(i)] = normed.astype(bf16)
                keyed.append(normed * tail[h : h + 1])
            keyed = jnp.concatenate(keyed, axis=0).astype(bf16)
            both = dot(keyed, val[:, pair_cut(p)])
            fresh = jnp.where(low, both[:block], both[block:])
            enter_o[i, p * block : (p + 1) * block, :] = total[p]
            total[p] = total[p] * jnp.exp(ctl[i * pairs + p : i * pairs + p + 1, :]) + fresh
    logs = ctl[0:pairs, :]
    for i in range(1, chunks):
        logs = logs + ctl[i * pairs : (i + 1) * pairs, :]
    pay_o[...] = pack_state(jnp.concatenate(total, axis=0), logs, id_rows[...])


def state_rows(pairs, ids):
    return pairs * 64 + -(-(3 * pairs + ids) // 16) * 16


def pack_state(state, logs, id_rows):
    pairs, ids = logs.shape[0], id_rows.shape[0]
    pad = state_rows(pairs, ids) - state.shape[0] - 3 * pairs - ids
    parts = [state, *thirds(logs), id_rows] + [jnp.zeros((pad, LANES), f32)] * (pad > 0)
    return jnp.concatenate(parts, axis=0).astype(bf16)


def unpack_state(packed, pairs):
    whole = packed.astype(f32)
    rows = pairs * 64
    logs = whole[rows : rows + pairs]
    for k in (1, 2):
        logs = logs + whole[rows + k * pairs : rows + (k + 1) * pairs]
    return whole[:rows], logs, whole[rows + 3 * pairs :]


def row_factors(logs):
    factors = jnp.exp(logs)
    return jnp.concatenate(
        [jnp.broadcast_to(factors[p : p + 1], (64, LANES)) for p in range(logs.shape[0])], axis=0
    )


def join_kernel(bit, ids, pairs, mine, got, *refs):
    before = refs[: 2 if bit else 0]
    pay_o, prefix_o, logs_o = refs[len(before) :]
    upper = (lax.axis_index("seq") >> bit) & 1 == 1
    state, logs, rows = unpack_state(mine[...], pairs)
    other, other_logs, other_rows = unpack_state(got[...], pairs)
    early = jnp.where(upper, other, state)
    late = jnp.where(upper, state, other)
    factor = row_factors(jnp.where(upper, logs, other_logs))
    id_rows = jnp.concatenate([rows[:ids], other_rows[:ids]], axis=0)
    pay_o[...] = pack_state(early * factor + late, logs + other_logs, id_rows)
    if bit == 0:
        prefix_o[...] = jnp.where(upper, other, 0.0)
        logs_o[...] = jnp.where(upper, other_logs, 0.0)
    else:
        prefix, prefix_logs = before[0][...], before[1][...]
        prefix_o[...] = jnp.where(upper, prefix + row_factors(prefix_logs) * other, prefix)
        logs_o[...] = jnp.where(upper, prefix_logs + other_logs, prefix_logs)


def local_kernel(first, emb, key, val, crow, ccol, weight, query_o, intra_o):
    n, width = query_o.shape
    heads = ccol.shape[1] // 2
    ones, lanes = same_head(), head_spread(heads, first // 64, width // 64)
    mask_a, mask_b = half_masks()
    causal = iota((CHUNK, CHUNK), 0) >= iota((CHUNK, CHUNK), 1)

    def queries(i):
        query = dot(emb[chunk(i), :], weight[:, first : first + width])
        unit = lax.rsqrt(head_means(query, ones) + 1e-06) * 0.125
        query = query * unit
        decayed = query * spread(jnp.exp(ccol[chunk(i), :]), lanes)
        query_o[chunk(i), :] = decayed.astype(bf16)
        return query.astype(bf16)

    def scores(i, p, b, query):
        cut = pair_cut(p)
        wide = slice(first + p * LANES, first + (p + 1) * LANES)
        return dot(query[:, cut] * (mask_b if b else mask_a), key[wide, chunk(i)])

    units = [(i, p, b) for i in range(n // CHUNK) for p in range(width // LANES) for b in (0, 1)]
    query = {0: queries(0)}
    ready = scores(*units[0], query[0])
    held = None
    for u, (i, p, b) in enumerate(units):
        current = ready
        if u + 1 < len(units):
            j = units[u + 1][0]
            if j not in query:
                query[j] = queries(j)
            ready = scores(*units[u + 1], query[j])
        h = first // 64 + 2 * p + b
        gap = ccol[chunk(i), h : h + 1] - crow[i, h : h + 1, :]
        weights = jnp.where(causal, current * jnp.exp(gap), 0.0).astype(bf16)
        wide = slice(first + p * LANES, first + (p + 1) * LANES)
        part = dot(weights, val[chunk(i), wide] * (mask_b if b else mask_a))
        if b == 0:
            held = part
        else:
            intra_o[chunk(i), pair_cut(p)] = held + part


def candidate_queries(ids, owned, message, stored, own, peer, query_w):
    half, width = own.shape
    pairs = width // LANES
    rows = message[pairs * 64 :, :].astype(f32)
    rows = (rows * float(LANES) + pltpu.roll(rows, LANES // 2, 1)).astype(i32)[3 * pairs :]
    slots = [stored_slots(rows[j : j + 1], stored[...]) for j in range(ids)]
    step = LANES // owned
    tiles = []
    for start in range(0, ids, step):
        tile = slots[start]
        for k in range(1, step):
            moved = pltpu.roll(slots[start + k], k * owned, 1)
            tile = jnp.where(iota((1, LANES), 1) >= k * owned, moved, tile)
        tiles.append(tile)
    slots = jnp.concatenate(tiles, axis=1)
    dp = lax.axis_index("dp")
    found = picked_rows(slots, dp * half, own) + picked_rows(slots, (1 - dp) * half, peer)
    return jnp.transpose(dot(found.astype(bf16), query_w[...]))


def near_kernel(ids, owned, message, stored, own, peer, query_w, pair_w, query_o, val_w_o):
    query = candidate_queries(ids, owned, message, stored, own, peer, query_w)
    query_o[...] = query.astype(bf16)
    val_w_o[...] = jnp.transpose(pair_w[:, own.shape[1] :].astype(f32)).astype(bf16)


def far_kernel(ids, owned, message, stored, own, peer, query_w, *refs):
    far = candidate_queries(ids, owned, message, stored, own, peer, query_w)
    if len(refs) == 1:
        refs[0][...] = far.astype(bf16)
        return
    near, outs = refs[0][...].astype(f32), refs[1:]
    low = first_half((1, LANES))
    for k, out in enumerate(outs):
        cut = pair_cut(k // 2)
        left, right = near[:, cut], far[:, cut]
        if k % 2:
            left = pltpu.roll(left, LANES // 2, 1)
        else:
            right = pltpu.roll(right, LANES // 2, 1)
        out[...] = jnp.where(low, left, right).astype(bf16)


def attend(alive_count, scale, query, key, val, buffers, emit):
    n, width = key.shape
    blocks = range(0, n, KEYS)
    pairs = width // LANES
    ones = jnp.ones((16, KEYS), bf16)

    def weights_of(p):
        rows = query[pair_cut(p), :]
        zero = jnp.zeros((64, LANES), bf16)
        top = jnp.concatenate([rows[:64], zero], axis=1)
        return jnp.concatenate([top, jnp.concatenate([zero, rows[64:]], axis=1)], axis=0)

    def store(p, block, weights, peak):
        values = dot(key[block : block + KEYS, pair_cut(p)], weights)
        values = jnp.where(iota((KEYS, 1), 0) < alive_count - block, values, DEAD)
        buffers[p % 2][block : block + KEYS, :] = values
        top = jnp.max(values.reshape(KEYS // 8, 8, 2 * LANES), axis=0)
        return top if peak is None else jnp.maximum(peak, top)

    peak, weights = None, weights_of(0)
    for block in blocks:
        peak = store(0, block, weights, peak)
    for p in range(pairs):
        factor = [
            jnp.broadcast_to(scale[0:1, h : h + 1], (1, LANES)) for h in (2 * p, 2 * p + 1)
        ]
        factor = jnp.concatenate(factor, axis=1) * LOG2E
        peak = jnp.max(peak, axis=0, keepdims=True)
        following = sums = None
        more = p + 1 < pairs
        if more:
            weights = weights_of(p + 1)
        for block in blocks:
            if more:
                following = store(p + 1, block, weights, following)
            gap = buffers[p % 2][block : block + KEYS, :] - peak
            probs = jnp.exp2(gap * factor).astype(bf16)
            side = jnp.concatenate([val[pair_cut(p), block : block + KEYS], ones], axis=0)
            part = dot(side, probs)
            sums = part if sums is None else sums + part
        total = sums[LANES : LANES + 1]
        logs = live(alive_count, peak * factor + jnp.log2(total))
        for b in (0, 1):
            cut = pair_cut(b)
            mean = sums[b * 64 : (b + 1) * 64, cut] / total[:, cut]
            emit(2 * p + b, mean, logs[:, cut])
        peak = following


def finish_kernel(
    bit, here, scale, emb, query_a, query_b, intra_a, intra_b, enter, ctl, got, prefix, prefix_logs,
    out_w, pair_w, val_w, cand_q, hist_o, key_o, val_o, pay_o,
    shown, sem, *buffers,
):
    n, width = emb.shape
    pairs = width // LANES
    ones = same_head()
    upper = (lax.axis_index("seq") >> bit) & 1 == 1
    state = unpack_state(got[...], pairs)[0]
    before, before_logs = prefix[...], prefix_logs[...]
    entering = jnp.where(upper, before + row_factors(before_logs) * state, before)
    lane = iota((1, 2 * LANES), 1) // 64
    chunks = n // CHUNK
    gone = [jnp.zeros((pairs, LANES), f32)]
    for i in range(chunks - 1):
        gone.append(gone[-1] + ctl[i * pairs : (i + 1) * pairs, :])

    def normed(i):
        states = enter[i] + row_factors(gone[i]) * entering
        parts = []
        for p in range(0, pairs, 2):
            wide = jnp.concatenate(
                [states[p * 64 : (p + 1) * 64], states[(p + 1) * 64 : (p + 2) * 64]], axis=1
            )
            matrix = jnp.concatenate([jnp.where(lane == k, wide, 0.0) for k in range(4)], axis=0)
            query, intra = (query_a, intra_a) if p < pairs // 2 else (query_b, intra_b)
            c = (p % (pairs // 2)) * LANES
            cut = slice(c, c + 2 * LANES)
            parts.append(dot(query[chunk(i), cut], matrix.astype(bf16)) + intra[chunk(i), cut])
        mixed = jnp.concatenate(parts, axis=1)
        return (mixed * lax.rsqrt(head_means(mixed, ones) + 1e-05)).astype(bf16)

    alive_count = here[0:1, 0:1]
    copies = [
        pltpu.make_async_copy(shown.at[chunk(i), :], hist_o.at[chunk(i), :], sem.at[i])
        for i in range(chunks)
    ]
    ready = normed(0)
    for i in range(chunks):
        current = ready
        if i + 1 < chunks:
            ready = normed(i + 1)
        hidden_sum = emb[chunk(i), :].astype(f32) + dot(current, out_w[...])
        alive = iota((CHUNK, 1), 0) < alive_count - i * CHUNK
        shown[chunk(i), :] = jnp.where(alive, hidden_sum, 0.0)
        copies[i].start()
        hidden = hidden_sum.astype(bf16)
        key_o[chunk(i), :] = dot(hidden, pair_w[:, :width]).astype(bf16)
        val_o[:, chunk(i)] = contract(val_w[...], hidden, 1, 1).astype(bf16)
    send_part(alive_count, scale, cand_q, key_o, val_o, pay_o, buffers)
    for copy in copies:
        copy.wait()


def send_part(alive_count, scale, query, key, val, pay_o, buffers):
    log_rows = []

    def emit(h, mean, logs):
        pay_o[h * 64 : (h + 1) * 64, :] = mean.astype(bf16)
        log_rows.append(logs)

    attend(alive_count, scale, query, key, val, buffers, emit)
    pay_o[val.shape[0] :, :] = pack_logs(jnp.concatenate(log_rows, axis=0))


def send_kernel(here, scale, query, key, val, pay_o, *buffers):
    send_part(here[0:1, 0:1], scale, query, key, val, pay_o, buffers)


def live(alive_count, logs):
    return jnp.where(jnp.broadcast_to(alive_count, logs.shape) > 0, logs, DEAD)


def pack_logs(logs):
    heads, cols = logs.shape
    return jnp.concatenate(
        [*thirds(logs), jnp.zeros((log_pad(heads) - 3 * heads, cols), f32)], axis=0
    ).astype(bf16)


def log_pad(heads):
    return -(-3 * heads // 16) * 16


def unpack_logs(rows, heads):
    rows = rows.astype(f32)
    return rows[:heads] + rows[heads : 2 * heads] + rows[2 * heads : 3 * heads]


def keep_kernel(here, scale, query, key, val, mean_o, logs_o, *buffers):
    def emit(h, mean, logs):
        mean_o[h * 64 : (h + 1) * 64, :] = mean
        logs_o[h : h + 1, :] = logs

    attend(here[0:1, 0:1], scale, query, key, val, buffers, emit)


def over_heads(rows):
    return jnp.concatenate(
        [jnp.broadcast_to(rows[h : h + 1], (64, rows.shape[1])) for h in range(rows.shape[0])],
        axis=0,
    )


def merge(parts):
    peak = parts[0][1]
    for _, logs in parts[1:]:
        peak = jnp.maximum(peak, logs)
    shares = [jnp.exp2(logs - peak) for _, logs in parts]
    total = sum(shares[1:], shares[0])
    mean = None
    for (value, _), share in zip(parts, shares):
        term = value * over_heads(share / total)
        mean = term if mean is None else mean + term
    return mean, peak + jnp.log2(total)


def received(got, heads):
    value = got[...].astype(f32)
    if value.shape[0] < heads * 64:
        value = jnp.concatenate([value, pltpu.roll(value, LANES // 2, 1)], axis=0)
    return value[: heads * 64], unpack_logs(value[heads * 64 :], heads)


def fold_kernel(mean, logs, *refs):
    gots, (mean_o, logs_o, pay_o) = refs[:-3], refs[-3:]
    heads, keep = logs_o.shape
    parts = [(mean[...], logs[...])] + [received(got, heads) for got in gots]
    new_mean, new_logs = merge(parts)
    mean_o[...] = new_mean[:, :keep]
    logs_o[...] = new_logs[:, :keep]
    whole = jnp.concatenate([new_mean, pack_logs(new_logs).astype(f32)], axis=0)
    if 2 * keep == LANES:
        half = whole.shape[0] // 2
        top = pltpu.roll(whole[:half], keep, 1)
        pay_o[...] = jnp.where(first_half((1, LANES)), top, whole[half:]).astype(bf16)
    else:
        pay_o[...] = whole[:, keep:].astype(bf16)


def last_kernel(mean, logs, got, out_w, cand_o):
    heads, cols = logs.shape
    other_mean, other_logs = received(got, heads)
    parts = [(mean[...], logs[...]), (other_mean[:, :cols], other_logs[:, :cols])]
    attended = merge(parts)[0].astype(bf16)
    cand_o[...] = contract(attended, out_w[...], 0, 0)


def shape(dims, dtype):
    return jax.ShapeDtypeStruct(dims, dtype)


VMEM = pl.BlockSpec(memory_space=pltpu.VMEM)
SMEM = pl.BlockSpec(memory_space=pltpu.SMEM)
ANY = pl.BlockSpec(memory_space=pl.ANY)
HBM = pl.BlockSpec(memory_space=pltpu.HBM)


def call(kernel, name, operands, outs, scratch=(), after=(), flops=0, space=VMEM, spaces=None, scalars=()):
    count = len(scalars) + len(operands)
    if space is HBM:
        operands = [pltpu.with_memory_space_constraint(value, pltpu.HBM) for value in operands]

    def body(*refs):
        kernel(*refs[:count], *refs[count + len(after) :])

    return pl.pallas_call(
        body,
        name=name,
        in_specs=[SMEM] * len(scalars) + [space] * len(operands) + [ANY] * len(after),
        out_specs=spaces or [VMEM] * len(outs),
        out_shape=outs,
        scratch_shapes=list(scratch),
        compiler_params=pltpu.CompilerParams(vmem_limit_bytes=VMEM_LIMIT),
        cost_estimate=pl.CostEstimate(flops=flops, transcendentals=0, bytes_accessed=0),
    )(*scalars, *operands, *after)


def reversed_bits(value, bits):
    return sum(((value >> b) & 1) << (bits - 1 - b) for b in range(bits))


def shards(
    history_item_index,
    log_head_retention,
    user_history_length,
    candidate_item_index,
    item_stored_row,
    item_embedding_table,
    head_score_scale,
    history_query_key_value_weight,
    history_output_weight,
    candidate_key_value_weight,
    candidate_query_weight,
    candidate_output_weight,
):
    users, n = history_item_index.shape
    heads = log_head_retention.shape[1]
    half, width = item_embedding_table.shape
    owned = candidate_item_index.shape[1]
    seq = lax.axis_size("seq")
    bits = seq.bit_length() - 1
    cands = owned * seq
    assert users == 1 and lax.axis_size("dp") == 2 and seq == 1 << bits and bits > 2
    assert width == heads * 64 and heads % 4 == 0 and LANES % owned == 0 and owned <= 64
    assert cands == 4 * LANES
    pairs = heads // 2
    rows = pairs * 64

    def swap(value, mask):
        return lax.ppermute(value, "seq", [(j, j ^ mask) for j in range(seq)])

    peer = lax.ppermute(item_embedding_table, "dp", [(0, 1), (1, 0)])
    scale = head_score_scale.reshape(1, heads)
    stored = item_stored_row.reshape(-1, LANES)
    decay = log_head_retention.reshape(heads, n)

    part, slot, crow, ccol, ctl, key_w, id_rows = call(
        own_rows_kernel, "own_rows",
        [
            history_item_index, stored, decay, item_embedding_table,
            history_query_key_value_weight, candidate_item_index,
        ],
        [
            shape((n, width), bf16), shape((1, n), f32), shape((n // CHUNK, heads, CHUNK), f32),
            shape((n, 2 * heads), f32), shape((n // CHUNK * pairs, LANES), f32),
            shape((width, width), bf16), shape((1, LANES), f32),
        ],
        [
            pltpu.VMEM((1, n), i32), pltpu.VMEM(stored.shape, i32), pltpu.VMEM((heads, n), f32),
            pltpu.VMEM((half, width), bf16), pltpu.VMEM((width, width), bf16),
            pltpu.VMEM((1, owned), i32), pltpu.SemaphoreType.DMA((7,)),
        ],
        space=HBM,
        flops=2 * n * half * width,
    )
    emb, key, val, enter, pay, here = call(
        summary_kernel, "summary",
        [part, peer, slot, crow, ctl, id_rows, key_w, history_query_key_value_weight],
        [
            shape((n, width), bf16), shape((width, n), bf16), shape((n, width), bf16),
            shape((n // CHUNK, rows, LANES), f32), shape((state_rows(pairs, 1), LANES), bf16),
            shape((8, LANES), i32),
        ],
        scalars=[user_history_length],
        flops=2 * n * half * width,
    )

    def local(first, name, after):
        return call(
            lambda *refs: local_kernel(first, *refs), name,
            [emb, key, val, crow, ccol, history_query_key_value_weight],
            [shape((n, width // 2), bf16), shape((n, width // 2), f32)],
            after=after, flops=2 * n * half * width // 2,
        )

    early = [local(0, "local_a", [])]
    prefix = logs = None
    for bit in range(bits - 1):
        got = swap(pay, 1 << bit)
        if bit == 1:
            early.append(local(width // 2, "local_b", [prefix]))
        count = 1 << bit
        pay, prefix, logs = call(
            lambda *refs, bit=bit, count=count: join_kernel(bit, count, pairs, *refs), "join",
            [pay, got] + ([prefix, logs] if bit else []),
            [
                shape((state_rows(pairs, 2 * count), LANES), bf16), shape((rows, LANES), f32),
                shape((pairs, LANES), f32),
            ],
            after=[early[-1][1]],
        )
    got = swap(pay, 1 << (bits - 1))
    half_seq = seq // 2
    tables = [stored, item_embedding_table, peer, candidate_query_weight]
    work = cands * 2 * half * width
    near, val_w = call(
        lambda *refs: near_kernel(half_seq, owned, *refs), "near",
        [pay, *tables, candidate_key_value_weight],
        [shape((width, cands // 2), bf16), shape((width, width), bf16)], flops=work,
    )
    if 2 * owned == LANES:
        quarters = call(
            lambda *refs: far_kernel(half_seq, owned, *refs), "far", [got, *tables, near],
            [shape((width, LANES), bf16)] * 4, flops=work,
        )
    else:
        (far,) = call(
            lambda *refs: far_kernel(half_seq, owned, *refs), "far", [got, *tables],
            [shape((width, cands // 2), bf16)], flops=work,
        )
        order = [t + 4 * reversed_bits(k, bits - 2) for t in range(4) for k in range(seq // 4)]
        every = jnp.concatenate([near, far], axis=1).reshape(width, seq, owned)
        every = every[:, jnp.array(order)].reshape(width, cands)
        quarters = [every[:, t * LANES : (t + 1) * LANES] for t in range(4)]
    (query_a, intra_a), (query_b, intra_b) = early
    buffers = [pltpu.VMEM((n, 2 * LANES), f32)] * 2
    message = width + log_pad(heads)
    hist, key_two, val_two, pay = call(
        lambda *refs: finish_kernel(bits - 1, *refs), "finish",
        [
            here, scale, emb, query_a, query_b, intra_a, intra_b, enter, ctl, got, prefix, logs,
            history_output_weight, candidate_key_value_weight, val_w, quarters[3],
        ],
        [
            shape((n, width), f32), shape((n, width), bf16), shape((width, n), bf16),
            shape((message, LANES), bf16),
        ],
        [pltpu.VMEM((n, width), f32), pltpu.SemaphoreType.DMA((n // CHUNK,))] + buffers,
        spaces=[ANY, VMEM, VMEM, VMEM],
        flops=2 * n * half * width,
    )
    gots = [swap(pay, 3)]
    for t in (2, 1):
        (pay,) = call(
            send_kernel, "send", [here, scale, quarters[t], key_two, val_two],
            [shape((message, LANES), bf16)], buffers, after=[pay], flops=work,
        )
        gots.append(swap(pay, t))
    mean, logs = call(
        keep_kernel, "keep", [here, scale, quarters[0], key_two, val_two],
        [shape((width, LANES), f32), shape((heads, LANES), f32)], buffers, after=[pay], flops=work,
    )
    cols = LANES
    for bit in range(2, bits):
        cols //= 2
        packed = 2 * cols == LANES
        mean, logs, pay = call(
            fold_kernel, "fold", [mean, logs, *gots],
            [
                shape((width, cols), f32), shape((heads, cols), f32),
                shape((message // 2, LANES) if packed else (message, cols), bf16),
            ],
        )
        if packed and bit < bits - 1:
            pay = jnp.concatenate([pay[:, :cols], pay[:, cols:]], axis=0)
        gots = [swap(pay, 1 << bit)]
    (cand_out,) = call(
        last_kernel, "last", [mean, logs, *gots, candidate_output_weight],
        [shape((owned, width), f32)],
    )
    return hist[None], cand_out[None]


def solution(mesh):
    in_specs = (
        P(("groups", "dp"), "seq"),
        P(("groups", "dp"), None, "seq"),
        P(("groups", "dp")),
        P(("groups", "dp"), "seq"),
        P(),
        P("dp", None),
        P(),
        P(),
        P(),
        P(),
        P(),
        P(),
    )
    out_specs = (P(("groups", "dp"), "seq", None), P(("groups", "dp"), "seq", None))
    return jax.shard_map(shards, mesh=mesh, in_specs=in_specs, out_specs=out_specs, check_vma=False)
```

```python
import math

import jax
import jax.numpy as jnp
from jax import lax
from jax.experimental import pallas as pl
from jax.experimental.pallas import tpu as pltpu
from jax.sharding import PartitionSpec as P

f32, bf16, i32 = jnp.float32, jnp.bfloat16, jnp.int32
CHUNK = 256
KEYS = 512
LANES = 128
LOG2E = math.log2(math.e)
DEAD = -1e30
VMEM_LIMIT = 40 << 20


def dot(a, b):
    return jnp.dot(a, b, preferred_element_type=f32)


def contract(a, b, left, right):
    return lax.dot_general(a, b, (((left,), (right,)), ((), ())), preferred_element_type=f32)


def iota(shape, axis):
    return lax.broadcasted_iota(i32, shape, axis)


def thirds(value):
    high = value.astype(bf16).astype(f32)
    rest = value - high
    mid = rest.astype(bf16).astype(f32)
    return high, mid, rest - mid


def first_half(shape):
    return iota(shape, len(shape) - 1) % LANES < LANES // 2


def half_masks():
    low = first_half((1, LANES))
    return jnp.where(low, 1.0, 0.0).astype(bf16), jnp.where(low, 0.0, 1.0).astype(bf16)


def same_head():
    dims = (2 * LANES, 2 * LANES)
    return jnp.where(iota(dims, 0) // 64 == iota(dims, 1) // 64, 1.0, 0.0).astype(bf16)


def head_means(value, ones):
    square = (value * value).astype(bf16)
    step = ones.shape[0]
    parts = [dot(square[:, c : c + step], ones) for c in range(0, value.shape[1], step)]
    return jnp.concatenate(parts, axis=1) * (1.0 / 64.0)


def head_spread(heads, first, count):
    dims = (2 * heads, 64 * count)
    return jnp.where(iota(dims, 1) // 64 + first == iota(dims, 0) % heads, 1.0, 0.0).astype(bf16)


def spread(value, matrix):
    heads = value.shape[1] // 2
    high = value.astype(bf16).astype(f32)
    both = jnp.where(iota(value.shape, 1) < heads, high, value - high)
    return dot(both.astype(bf16), matrix)


def stored_slots(ids, stored):
    groups = stored.shape[0]
    n = ids.shape[1]
    pick = jnp.where(iota((groups, n), 0) == ids // LANES, 1.0, 0.0).astype(bf16)
    high = contract((stored // 64).astype(f32).astype(bf16), pick, 0, 0)
    low = contract((stored % 64).astype(f32).astype(bf16), pick, 0, 0)
    rows = jnp.where(iota((LANES, n), 0) == ids % LANES, high * 64.0 + low, 0.0)
    return jnp.sum(rows, axis=0, keepdims=True)


def picked_rows(slots, first, table):
    count = table.shape[0]
    hot = jnp.where(iota((count, slots.shape[1]), 0) == slots.astype(i32) - first, 1.0, 0.0)
    return contract(hot.astype(bf16), table[...], 0, 0)


def chunk(i):
    return slice(i * CHUNK, (i + 1) * CHUNK)


def pair_cut(p):
    return slice(p * LANES, (p + 1) * LANES)


def own_rows_kernel(
    ids_in, stored_in, decay_in, own_in, weight_in, cand_in,
    part_o, slot_o, crow_o, ccol_o, ctl_o, key_w_o, id_rows_o,
    ids, stored, decay, own, key_w, cand, sem,
):
    n, half, heads = ids.shape[1], own.shape[0], decay.shape[0]
    width = own.shape[1]
    middle = weight_in.at[:, width : 2 * width]
    copies = [
        pltpu.make_async_copy(source, target, sem.at[k])
        for k, (source, target) in enumerate(
            (
                (ids_in, ids), (stored_in, stored), (cand_in, cand), (decay_in, decay),
                (own_in.at[: half // 2], own.at[: half // 2]),
                (own_in.at[half // 2 :], own.at[half // 2 :]), (middle, key_w),
            )
        )
    ]
    for copy in copies:
        copy.start()
    copies[0].wait()
    copies[1].wait()
    slots = stored_slots(ids[...], stored[...])
    slot_o[...] = slots
    copies[2].wait()
    wide = jnp.concatenate([cand[...], jnp.zeros((1, LANES - cand.shape[1]), i32)], axis=1).astype(f32)
    high = jnp.floor(wide * (1.0 / LANES))
    low = pltpu.roll(jnp.broadcast_to(wide - high * LANES, (8, LANES)), LANES // 2, 1)[:1]
    id_rows_o[...] = jnp.where(first_half((1, LANES)), high, low)
    copies[3].wait()
    upto = jnp.where(
        iota((CHUNK, CHUNK), 0) <= iota((CHUNK, CHUNK), 1), 1.0, 0.0
    ).astype(bf16)
    low = first_half((1, LANES))
    for i in range(n // CHUNK):
        pieces = jnp.concatenate(thirds(decay[:, chunk(i)]), axis=0)
        sums = dot(pieces.astype(bf16), upto)
        cum = sums[:heads] + sums[heads : 2 * heads] + sums[2 * heads :]
        crow_o[i] = cum
        ccol_o[chunk(i), :] = jnp.transpose(jnp.concatenate([cum, cum], axis=0))
        for p in range(heads // 2):
            r = i * (heads // 2) + p
            ctl_o[r : r + 1, :] = jnp.where(
                low, cum[2 * p : 2 * p + 1, CHUNK - 1 :], cum[2 * p + 1 : 2 * p + 2, CHUNK - 1 :]
            )
    first = lax.axis_index("dp") * half
    for k in range(2):
        copies[4 + k].wait()
        piece = own.at[k * half // 2 : (k + 1) * half // 2]
        for i in range(n // CHUNK):
            rows = picked_rows(slots[:, chunk(i)], first + k * half // 2, piece)
            if k:
                rows += part_o[chunk(i), :].astype(f32)
            part_o[chunk(i), :] = rows.astype(bf16)
    copies[6].wait()
    key_w_o[...] = jnp.transpose(key_w[...].astype(f32)).astype(bf16)


def summary_kernel(
    length, part, peer, slot, crow, ctl, id_rows, key_w, weight,
    emb_o, key_o, val_o, enter_o, pay_o, here_o,
):
    n, width = part.shape
    half, heads = peer.shape[0], crow.shape[1]
    pairs = heads // 2
    block = LANES // 2
    low = first_half((1, LANES))
    chunks = n // CHUNK
    here = length[0] - lax.axis_index("seq") * n
    here_o[...] = jnp.full(here_o.shape, here, i32)

    def project(i):
        other = picked_rows(slot[:, chunk(i)], (1 - lax.axis_index("dp")) * half, peer)
        emb = (part[chunk(i), :].astype(f32) + other).astype(bf16)
        emb_o[chunk(i), :] = emb
        return contract(key_w[...], emb, 1, 1), dot(emb, weight[:, 2 * width :])

    total = [jnp.zeros((block, LANES), f32)] * pairs
    ready = project(0)
    for i in range(chunks):
        key, val = ready
        if i + 1 < chunks:
            ready = project(i + 1)
        val = jnp.where(iota((CHUNK, 1), 0) < here - i * CHUNK, val, 0.0).astype(bf16)
        val_o[chunk(i), :] = val
        alive = iota((1, CHUNK), 1) < here - i * CHUNK
        cum = crow[i]
        tail = jnp.exp(cum[:, CHUNK - 1 :] - cum)
        for p in range(pairs):
            keyed = []
            for h in (2 * p, 2 * p + 1):
                rows = key[h * 64 : (h + 1) * 64]
                mean = jnp.sum(rows * rows, axis=0, keepdims=True) * (1.0 / 64.0)
                unit = jnp.where(alive, lax.rsqrt(mean + 1e-06) * 0.125, 0.0)
                normed = rows * unit
                key_o[h * 64 : (h + 1) * 64, chunk(i)] = normed.astype(bf16)
                keyed.append(normed * tail[h : h + 1])
            keyed = jnp.concatenate(keyed, axis=0).astype(bf16)
            both = dot(keyed, val[:, pair_cut(p)])
            fresh = jnp.where(low, both[:block], both[block:])
            enter_o[i, p * block : (p + 1) * block, :] = total[p]
            total[p] = total[p] * jnp.exp(ctl[i * pairs + p : i * pairs + p + 1, :]) + fresh
    logs = ctl[0:pairs, :]
    for i in range(1, chunks):
        logs = logs + ctl[i * pairs : (i + 1) * pairs, :]
    pay_o[...] = pack_state(jnp.concatenate(total, axis=0), logs, id_rows[...])


def state_rows(pairs, ids):
    return pairs * 64 + -(-(3 * pairs + ids) // 16) * 16


def pack_state(state, logs, id_rows):
    pairs, ids = logs.shape[0], id_rows.shape[0]
    pad = state_rows(pairs, ids) - state.shape[0] - 3 * pairs - ids
    parts = [state, *thirds(logs), id_rows] + [jnp.zeros((pad, LANES), f32)] * (pad > 0)
    return jnp.concatenate(parts, axis=0).astype(bf16)


def unpack_state(packed, pairs):
    whole = packed.astype(f32)
    rows = pairs * 64
    logs = whole[rows : rows + pairs]
    for k in (1, 2):
        logs = logs + whole[rows + k * pairs : rows + (k + 1) * pairs]
    return whole[:rows], logs, whole[rows + 3 * pairs :]


def row_factors(logs):
    factors = jnp.exp(logs)
    return jnp.concatenate(
        [jnp.broadcast_to(factors[p : p + 1], (64, LANES)) for p in range(logs.shape[0])], axis=0
    )


def join_kernel(bit, ids, pairs, mine, got, *refs):
    before = refs[: 2 if bit else 0]
    pay_o, prefix_o, logs_o = refs[len(before) :]
    upper = (lax.axis_index("seq") >> bit) & 1 == 1
    state, logs, rows = unpack_state(mine[...], pairs)
    other, other_logs, other_rows = unpack_state(got[...], pairs)
    early = jnp.where(upper, other, state)
    late = jnp.where(upper, state, other)
    factor = row_factors(jnp.where(upper, logs, other_logs))
    id_rows = jnp.concatenate([rows[:ids], other_rows[:ids]], axis=0)
    pay_o[...] = pack_state(early * factor + late, logs + other_logs, id_rows)
    if bit == 0:
        prefix_o[...] = jnp.where(upper, other, 0.0)
        logs_o[...] = jnp.where(upper, other_logs, 0.0)
    else:
        prefix, prefix_logs = before[0][...], before[1][...]
        prefix_o[...] = jnp.where(upper, prefix + row_factors(prefix_logs) * other, prefix)
        logs_o[...] = jnp.where(upper, prefix_logs + other_logs, prefix_logs)


def local_kernel(first, emb, key, val, crow, ccol, weight, query_o, intra_o):
    n, width = query_o.shape
    heads = ccol.shape[1] // 2
    ones, lanes = same_head(), head_spread(heads, first // 64, width // 64)
    mask_a, mask_b = half_masks()
    causal = iota((CHUNK, CHUNK), 0) >= iota((CHUNK, CHUNK), 1)

    def queries(i):
        query = dot(emb[chunk(i), :], weight[:, first : first + width])
        unit = lax.rsqrt(head_means(query, ones) + 1e-06) * 0.125
        query = query * unit
        decayed = query * spread(jnp.exp(ccol[chunk(i), :]), lanes)
        query_o[chunk(i), :] = decayed.astype(bf16)
        return query.astype(bf16)

    def scores(i, p, b, query):
        cut = pair_cut(p)
        wide = slice(first + p * LANES, first + (p + 1) * LANES)
        return dot(query[:, cut] * (mask_b if b else mask_a), key[wide, chunk(i)])

    units = [(i, p, b) for i in range(n // CHUNK) for p in range(width // LANES) for b in (0, 1)]
    query = {0: queries(0)}
    ready = scores(*units[0], query[0])
    held = None
    for u, (i, p, b) in enumerate(units):
        current = ready
        if u + 1 < len(units):
            j = units[u + 1][0]
            if j not in query:
                query[j] = queries(j)
            ready = scores(*units[u + 1], query[j])
        h = first // 64 + 2 * p + b
        gap = ccol[chunk(i), h : h + 1] - crow[i, h : h + 1, :]
        weights = jnp.where(causal, current * jnp.exp(gap), 0.0).astype(bf16)
        wide = slice(first + p * LANES, first + (p + 1) * LANES)
        part = dot(weights, val[chunk(i), wide] * (mask_b if b else mask_a))
        if b == 0:
            held = part
        else:
            intra_o[chunk(i), pair_cut(p)] = held + part


def candidate_queries(ids, owned, message, stored, own, peer, query_w):
    half, width = own.shape
    pairs = width // LANES
    rows = message[pairs * 64 :, :].astype(f32)
    rows = (rows * float(LANES) + pltpu.roll(rows, LANES // 2, 1)).astype(i32)[3 * pairs :]
    slots = [stored_slots(rows[j : j + 1], stored[...]) for j in range(ids)]
    step = LANES // owned
    tiles = []
    for start in range(0, ids, step):
        tile = slots[start]
        for k in range(1, step):
            moved = pltpu.roll(slots[start + k], k * owned, 1)
            tile = jnp.where(iota((1, LANES), 1) >= k * owned, moved, tile)
        tiles.append(tile)
    slots = jnp.concatenate(tiles, axis=1)
    dp = lax.axis_index("dp")
    found = picked_rows(slots, dp * half, own) + picked_rows(slots, (1 - dp) * half, peer)
    return jnp.transpose(dot(found.astype(bf16), query_w[...]))


def near_kernel(ids, owned, message, stored, own, peer, query_w, pair_w, query_o, val_w_o):
    query = candidate_queries(ids, owned, message, stored, own, peer, query_w)
    query_o[...] = query.astype(bf16)
    val_w_o[...] = jnp.transpose(pair_w[:, own.shape[1] :].astype(f32)).astype(bf16)


def far_kernel(ids, owned, message, stored, own, peer, query_w, *refs):
    far = candidate_queries(ids, owned, message, stored, own, peer, query_w)
    if len(refs) == 1:
        refs[0][...] = far.astype(bf16)
        return
    near, outs = refs[0][...].astype(f32), refs[1:]
    low = first_half((1, LANES))
    for k, out in enumerate(outs):
        cut = pair_cut(k // 2)
        left, right = near[:, cut], far[:, cut]
        if k % 2:
            left = pltpu.roll(left, LANES // 2, 1)
        else:
            right = pltpu.roll(right, LANES // 2, 1)
        out[...] = jnp.where(low, left, right).astype(bf16)


def attend(alive_count, scale, query, key, val, buffers, emit):
    n, width = key.shape
    blocks = range(0, n, KEYS)
    pairs = width // LANES
    ones = jnp.ones((16, KEYS), bf16)

    def weights_of(p):
        rows = query[pair_cut(p), :]
        zero = jnp.zeros((64, LANES), bf16)
        top = jnp.concatenate([rows[:64], zero], axis=1)
        return jnp.concatenate([top, jnp.concatenate([zero, rows[64:]], axis=1)], axis=0)

    def store(p, block, weights, peak):
        values = dot(key[block : block + KEYS, pair_cut(p)], weights)
        values = jnp.where(iota((KEYS, 1), 0) < alive_count - block, values, DEAD)
        buffers[p % 2][block : block + KEYS, :] = values
        top = jnp.max(values.reshape(KEYS // 8, 8, 2 * LANES), axis=0)
        return top if peak is None else jnp.maximum(peak, top)

    peak, weights = None, weights_of(0)
    for block in blocks:
        peak = store(0, block, weights, peak)
    for p in range(pairs):
        factor = [
            jnp.broadcast_to(scale[0:1, h : h + 1], (1, LANES)) for h in (2 * p, 2 * p + 1)
        ]
        factor = jnp.concatenate(factor, axis=1) * LOG2E
        peak = jnp.max(peak, axis=0, keepdims=True)
        following = sums = None
        more = p + 1 < pairs
        if more:
            weights = weights_of(p + 1)
        for block in blocks:
            if more:
                following = store(p + 1, block, weights, following)
            gap = buffers[p % 2][block : block + KEYS, :] - peak
            probs = jnp.exp2(gap * factor).astype(bf16)
            side = jnp.concatenate([val[pair_cut(p), block : block + KEYS], ones], axis=0)
            part = dot(side, probs)
            sums = part if sums is None else sums + part
        total = sums[LANES : LANES + 1]
        logs = live(alive_count, peak * factor + jnp.log2(total))
        for b in (0, 1):
            cut = pair_cut(b)
            mean = sums[b * 64 : (b + 1) * 64, cut] / total[:, cut]
            emit(2 * p + b, mean, logs[:, cut])
        peak = following


def finish_kernel(
    bit, here, scale, emb, query_a, query_b, intra_a, intra_b, enter, ctl, got, prefix, prefix_logs,
    out_w, pair_w, val_w, cand_q, hist_o, key_o, val_o, pay_o,
    shown, sem, *buffers,
):
    n, width = emb.shape
    pairs = width // LANES
    ones = same_head()
    upper = (lax.axis_index("seq") >> bit) & 1 == 1
    state = unpack_state(got[...], pairs)[0]
    before, before_logs = prefix[...], prefix_logs[...]
    entering = jnp.where(upper, before + row_factors(before_logs) * state, before)
    lane = iota((1, 2 * LANES), 1) // 64
    chunks = n // CHUNK
    gone = [jnp.zeros((pairs, LANES), f32)]
    for i in range(chunks - 1):
        gone.append(gone[-1] + ctl[i * pairs : (i + 1) * pairs, :])

    def normed(i):
        states = enter[i] + row_factors(gone[i]) * entering
        parts = []
        for p in range(0, pairs, 2):
            wide = jnp.concatenate(
                [states[p * 64 : (p + 1) * 64], states[(p + 1) * 64 : (p + 2) * 64]], axis=1
            )
            matrix = jnp.concatenate([jnp.where(lane == k, wide, 0.0) for k in range(4)], axis=0)
            query, intra = (query_a, intra_a) if p < pairs // 2 else (query_b, intra_b)
            c = (p % (pairs // 2)) * LANES
            cut = slice(c, c + 2 * LANES)
            parts.append(dot(query[chunk(i), cut], matrix.astype(bf16)) + intra[chunk(i), cut])
        mixed = jnp.concatenate(parts, axis=1)
        return (mixed * lax.rsqrt(head_means(mixed, ones) + 1e-05)).astype(bf16)

    alive_count = here[0:1, 0:1]
    copies = [
        pltpu.make_async_copy(shown.at[chunk(i), :], hist_o.at[chunk(i), :], sem.at[i])
        for i in range(chunks)
    ]
    ready = normed(0)
    for i in range(chunks):
        current = ready
        if i + 1 < chunks:
            ready = normed(i + 1)
        hidden_sum = emb[chunk(i), :].astype(f32) + dot(current, out_w[...])
        alive = iota((CHUNK, 1), 0) < alive_count - i * CHUNK
        shown[chunk(i), :] = jnp.where(alive, hidden_sum, 0.0)
        copies[i].start()
        hidden = hidden_sum.astype(bf16)
        key_o[chunk(i), :] = dot(hidden, pair_w[:, :width]).astype(bf16)
        val_o[:, chunk(i)] = contract(val_w[...], hidden, 1, 1).astype(bf16)
    send_part(alive_count, scale, cand_q, key_o, val_o, pay_o, buffers)
    for copy in copies:
        copy.wait()


def send_part(alive_count, scale, query, key, val, pay_o, buffers):
    log_rows = []

    def emit(h, mean, logs):
        pay_o[h * 64 : (h + 1) * 64, :] = mean.astype(bf16)
        log_rows.append(logs)

    attend(alive_count, scale, query, key, val, buffers, emit)
    pay_o[val.shape[0] :, :] = pack_logs(jnp.concatenate(log_rows, axis=0))


def send_kernel(here, scale, query, key, val, pay_o, *buffers):
    send_part(here[0:1, 0:1], scale, query, key, val, pay_o, buffers)


def live(alive_count, logs):
    return jnp.where(jnp.broadcast_to(alive_count, logs.shape) > 0, logs, DEAD)


def pack_logs(logs):
    heads, cols = logs.shape
    return jnp.concatenate(
        [*thirds(logs), jnp.zeros((log_pad(heads) - 3 * heads, cols), f32)], axis=0
    ).astype(bf16)


def log_pad(heads):
    return -(-3 * heads // 16) * 16


def unpack_logs(rows, heads):
    rows = rows.astype(f32)
    return rows[:heads] + rows[heads : 2 * heads] + rows[2 * heads : 3 * heads]


def keep_kernel(here, scale, query, key, val, mean_o, logs_o, *buffers):
    def emit(h, mean, logs):
        mean_o[h * 64 : (h + 1) * 64, :] = mean
        logs_o[h : h + 1, :] = logs

    attend(here[0:1, 0:1], scale, query, key, val, buffers, emit)


def over_heads(rows):
    return jnp.concatenate(
        [jnp.broadcast_to(rows[h : h + 1], (64, rows.shape[1])) for h in range(rows.shape[0])],
        axis=0,
    )


def merge(parts):
    peak = parts[0][1]
    for _, logs in parts[1:]:
        peak = jnp.maximum(peak, logs)
    shares = [jnp.exp2(logs - peak) for _, logs in parts]
    total = sum(shares[1:], shares[0])
    mean = None
    for (value, _), share in zip(parts, shares):
        term = value * over_heads(share / total)
        mean = term if mean is None else mean + term
    return mean, peak + jnp.log2(total)


def received(got, heads):
    value = got[...].astype(f32)
    if value.shape[0] < heads * 64:
        value = jnp.concatenate([value, pltpu.roll(value, LANES // 2, 1)], axis=0)
    return value[: heads * 64], unpack_logs(value[heads * 64 :], heads)


def fold_kernel(mean, logs, *refs):
    gots, (mean_o, logs_o, pay_o) = refs[:-3], refs[-3:]
    heads, keep = logs_o.shape
    parts = [(mean[...], logs[...])] + [received(got, heads) for got in gots]
    new_mean, new_logs = merge(parts)
    mean_o[...] = new_mean[:, :keep]
    logs_o[...] = new_logs[:, :keep]
    whole = jnp.concatenate([new_mean, pack_logs(new_logs).astype(f32)], axis=0)
    if 2 * keep == LANES:
        half = whole.shape[0] // 2
        top = pltpu.roll(whole[:half], keep, 1)
        pay_o[...] = jnp.where(first_half((1, LANES)), top, whole[half:]).astype(bf16)
    else:
        pay_o[...] = whole[:, keep:].astype(bf16)


def last_kernel(mean, logs, got, out_w, cand_o):
    heads, cols = logs.shape
    other_mean, other_logs = received(got, heads)
    parts = [(mean[...], logs[...]), (other_mean[:, :cols], other_logs[:, :cols])]
    attended = merge(parts)[0].astype(bf16)
    cand_o[...] = contract(attended, out_w[...], 0, 0)


def shape(dims, dtype):
    return jax.ShapeDtypeStruct(dims, dtype)


VMEM = pl.BlockSpec(memory_space=pltpu.VMEM)
SMEM = pl.BlockSpec(memory_space=pltpu.SMEM)
ANY = pl.BlockSpec(memory_space=pl.ANY)
HBM = pl.BlockSpec(memory_space=pltpu.HBM)


def call(kernel, name, operands, outs, scratch=(), after=(), flops=0, space=VMEM, spaces=None, scalars=()):
    count = len(scalars) + len(operands)
    if space is HBM:
        operands = [pltpu.with_memory_space_constraint(value, pltpu.HBM) for value in operands]

    def body(*refs):
        kernel(*refs[:count], *refs[count + len(after) :])

    return pl.pallas_call(
        body,
        name=name,
        in_specs=[SMEM] * len(scalars) + [space] * len(operands) + [ANY] * len(after),
        out_specs=spaces or [VMEM] * len(outs),
        out_shape=outs,
        scratch_shapes=list(scratch),
        compiler_params=pltpu.CompilerParams(vmem_limit_bytes=VMEM_LIMIT),
        cost_estimate=pl.CostEstimate(flops=flops, transcendentals=0, bytes_accessed=0),
    )(*scalars, *operands, *after)


def reversed_bits(value, bits):
    return sum(((value >> b) & 1) << (bits - 1 - b) for b in range(bits))


def shards(
    history_item_index,
    log_head_retention,
    user_history_length,
    candidate_item_index,
    item_stored_row,
    item_embedding_table,
    head_score_scale,
    history_query_key_value_weight,
    history_output_weight,
    candidate_key_value_weight,
    candidate_query_weight,
    candidate_output_weight,
):
    users, n = history_item_index.shape
    heads = log_head_retention.shape[1]
    half, width = item_embedding_table.shape
    owned = candidate_item_index.shape[1]
    seq = lax.axis_size("seq")
    bits = seq.bit_length() - 1
    cands = owned * seq
    assert users == 1 and lax.axis_size("dp") == 2 and seq == 1 << bits and bits > 2
    assert width == heads * 64 and heads % 4 == 0 and LANES % owned == 0 and owned <= 64
    assert cands == 4 * LANES
    pairs = heads // 2
    rows = pairs * 64

    def swap(value, mask):
        return lax.ppermute(value, "seq", [(j, j ^ mask) for j in range(seq)])

    peer = lax.ppermute(item_embedding_table, "dp", [(0, 1), (1, 0)])
    scale = head_score_scale.reshape(1, heads)
    stored = item_stored_row.reshape(-1, LANES)
    decay = log_head_retention.reshape(heads, n)

    part, slot, crow, ccol, ctl, key_w, id_rows = call(
        own_rows_kernel, "own_rows",
        [
            history_item_index, stored, decay, item_embedding_table,
            history_query_key_value_weight, candidate_item_index,
        ],
        [
            shape((n, width), bf16), shape((1, n), f32), shape((n // CHUNK, heads, CHUNK), f32),
            shape((n, 2 * heads), f32), shape((n // CHUNK * pairs, LANES), f32),
            shape((width, width), bf16), shape((1, LANES), f32),
        ],
        [
            pltpu.VMEM((1, n), i32), pltpu.VMEM(stored.shape, i32), pltpu.VMEM((heads, n), f32),
            pltpu.VMEM((half, width), bf16), pltpu.VMEM((width, width), bf16),
            pltpu.VMEM((1, owned), i32), pltpu.SemaphoreType.DMA((7,)),
        ],
        space=HBM,
        flops=2 * n * half * width,
    )
    emb, key, val, enter, pay, here = call(
        summary_kernel, "summary",
        [part, peer, slot, crow, ctl, id_rows, key_w, history_query_key_value_weight],
        [
            shape((n, width), bf16), shape((width, n), bf16), shape((n, width), bf16),
            shape((n // CHUNK, rows, LANES), f32), shape((state_rows(pairs, 1), LANES), bf16),
            shape((8, LANES), i32),
        ],
        scalars=[user_history_length],
        flops=2 * n * half * width,
    )

    def local(first, name, after):
        return call(
            lambda *refs: local_kernel(first, *refs), name,
            [emb, key, val, crow, ccol, history_query_key_value_weight],
            [shape((n, width // 2), bf16), shape((n, width // 2), f32)],
            after=after, flops=2 * n * half * width // 2,
        )

    early = [local(0, "local_a", [])]
    prefix = logs = None
    for bit in range(bits - 1):
        got = swap(pay, 1 << bit)
        if bit == 1:
            early.append(local(width // 2, "local_b", [prefix]))
        count = 1 << bit
        pay, prefix, logs = call(
            lambda *refs, bit=bit, count=count: join_kernel(bit, count, pairs, *refs), "join",
            [pay, got] + ([prefix, logs] if bit else []),
            [
                shape((state_rows(pairs, 2 * count), LANES), bf16), shape((rows, LANES), f32),
                shape((pairs, LANES), f32),
            ],
            after=[early[-1][1]],
        )
    got = swap(pay, 1 << (bits - 1))
    half_seq = seq // 2
    tables = [stored, item_embedding_table, peer, candidate_query_weight]
    work = cands * 2 * half * width
    near, val_w = call(
        lambda *refs: near_kernel(half_seq, owned, *refs), "near",
        [pay, *tables, candidate_key_value_weight],
        [shape((width, cands // 2), bf16), shape((width, width), bf16)], flops=work,
    )
    if 2 * owned == LANES:
        quarters = call(
            lambda *refs: far_kernel(half_seq, owned, *refs), "far", [got, *tables, near],
            [shape((width, LANES), bf16)] * 4, flops=work,
        )
    else:
        (far,) = call(
            lambda *refs: far_kernel(half_seq, owned, *refs), "far", [got, *tables],
            [shape((width, cands // 2), bf16)], flops=work,
        )
        order = [t + 4 * reversed_bits(k, bits - 2) for t in range(4) for k in range(seq // 4)]
        every = jnp.concatenate([near, far], axis=1).reshape(width, seq, owned)
        every = every[:, jnp.array(order)].reshape(width, cands)
        quarters = [every[:, t * LANES : (t + 1) * LANES] for t in range(4)]
    (query_a, intra_a), (query_b, intra_b) = early
    buffers = [pltpu.VMEM((n, 2 * LANES), f32)] * 2
    message = width + log_pad(heads)
    hist, key_two, val_two, pay = call(
        lambda *refs: finish_kernel(bits - 1, *refs), "finish",
        [
            here, scale, emb, query_a, query_b, intra_a, intra_b, enter, ctl, got, prefix, logs,
            history_output_weight, candidate_key_value_weight, val_w, quarters[3],
        ],
        [
            shape((n, width), f32), shape((n, width), bf16), shape((width, n), bf16),
            shape((message, LANES), bf16),
        ],
        [pltpu.VMEM((n, width), f32), pltpu.SemaphoreType.DMA((n // CHUNK,))] + buffers,
        spaces=[ANY, VMEM, VMEM, VMEM],
        flops=2 * n * half * width,
    )
    gots = [swap(pay, 3)]
    for t in (2, 1):
        (pay,) = call(
            send_kernel, "send", [here, scale, quarters[t], key_two, val_two],
            [shape((message, LANES), bf16)], buffers, after=[pay], flops=8 * work,
        )
        gots.append(swap(pay, t))
    mean, logs = call(
        keep_kernel, "keep", [here, scale, quarters[0], key_two, val_two],
        [shape((width, LANES), f32), shape((heads, LANES), f32)], buffers, after=[pay], flops=8 * work,
    )
    cols = LANES
    for bit in range(2, bits):
        cols //= 2
        packed = 2 * cols == LANES
        mean, logs, pay = call(
            fold_kernel, "fold", [mean, logs, *gots],
            [
                shape((width, cols), f32), shape((heads, cols), f32),
                shape((message // 2, LANES) if packed else (message, cols), bf16),
            ],
        )
        if packed and bit < bits - 1:
            pay = jnp.concatenate([pay[:, :cols], pay[:, cols:]], axis=0)
        gots = [swap(pay, 1 << bit)]
    (cand_out,) = call(
        last_kernel, "last", [mean, logs, *gots, candidate_output_weight],
        [shape((owned, width), f32)],
    )
    return hist[None], cand_out[None]


def solution(mesh):
    in_specs = (
        P(("groups", "dp"), "seq"),
        P(("groups", "dp"), None, "seq"),
        P(("groups", "dp")),
        P(("groups", "dp"), "seq"),
        P(),
        P("dp", None),
        P(),
        P(),
        P(),
        P(),
        P(),
        P(),
    )
    out_specs = (P(("groups", "dp"), "seq", None), P(("groups", "dp"), "seq", None))
    return jax.shard_map(shards, mesh=mesh, in_specs=in_specs, out_specs=out_specs, check_vma=False)
```

```python
import math

import jax
import jax.numpy as jnp
from jax import lax
from jax.experimental import pallas as pl
from jax.experimental.pallas import tpu as pltpu
from jax.sharding import PartitionSpec as P

f32, bf16, i32 = jnp.float32, jnp.bfloat16, jnp.int32
CHUNK = 256
KEYS = 512
LANES = 128
LOG2E = math.log2(math.e)
DEAD = -1e30
VMEM_LIMIT = 40 << 20


def dot(a, b):
    return jnp.dot(a, b, preferred_element_type=f32)


def contract(a, b, left, right):
    return lax.dot_general(a, b, (((left,), (right,)), ((), ())), preferred_element_type=f32)


def iota(shape, axis):
    return lax.broadcasted_iota(i32, shape, axis)


def thirds(value):
    high = value.astype(bf16).astype(f32)
    rest = value - high
    mid = rest.astype(bf16).astype(f32)
    return high, mid, rest - mid


def first_half(shape):
    return iota(shape, len(shape) - 1) % LANES < LANES // 2


def half_masks():
    low = first_half((1, LANES))
    return jnp.where(low, 1.0, 0.0).astype(bf16), jnp.where(low, 0.0, 1.0).astype(bf16)


def same_head():
    dims = (2 * LANES, 2 * LANES)
    return jnp.where(iota(dims, 0) // 64 == iota(dims, 1) // 64, 1.0, 0.0).astype(bf16)


def head_means(value, ones):
    square = (value * value).astype(bf16)
    step = ones.shape[0]
    parts = [dot(square[:, c : c + step], ones) for c in range(0, value.shape[1], step)]
    return jnp.concatenate(parts, axis=1) * (1.0 / 64.0)


def head_spread(heads, first, count):
    dims = (2 * heads, 64 * count)
    return jnp.where(iota(dims, 1) // 64 + first == iota(dims, 0) % heads, 1.0, 0.0).astype(bf16)


def spread(value, matrix):
    heads = value.shape[1] // 2
    high = value.astype(bf16).astype(f32)
    both = jnp.where(iota(value.shape, 1) < heads, high, value - high)
    return dot(both.astype(bf16), matrix)


def stored_slots(ids, stored):
    groups = stored.shape[0]
    n = ids.shape[1]
    pick = jnp.where(iota((groups, n), 0) == ids // LANES, 1.0, 0.0).astype(bf16)
    high = contract((stored // 64).astype(f32).astype(bf16), pick, 0, 0)
    low = contract((stored % 64).astype(f32).astype(bf16), pick, 0, 0)
    rows = jnp.where(iota((LANES, n), 0) == ids % LANES, high * 64.0 + low, 0.0)
    return jnp.sum(rows, axis=0, keepdims=True)


def picked_rows(slots, first, table):
    count = table.shape[0]
    hot = jnp.where(iota((count, slots.shape[1]), 0) == slots.astype(i32) - first, 1.0, 0.0)
    return contract(hot.astype(bf16), table[...], 0, 0)


def chunk(i):
    return slice(i * CHUNK, (i + 1) * CHUNK)


def pair_cut(p):
    return slice(p * LANES, (p + 1) * LANES)


def own_rows_kernel(
    ids_in, stored_in, decay_in, own_in, weight_in, part_o, slot_o, crow_o, ccol_o, ctl_o, key_w_o,
    ids, stored, decay, own, key_w, sem,
):
    n, half, heads = ids.shape[1], own.shape[0], decay.shape[0]
    width = own.shape[1]
    middle = weight_in.at[:, width : 2 * width]
    copies = [
        pltpu.make_async_copy(source, target, sem.at[k])
        for k, (source, target) in enumerate(
            (
                (ids_in, ids), (stored_in, stored), (decay_in, decay),
                (own_in.at[: half // 2], own.at[: half // 2]),
                (own_in.at[half // 2 :], own.at[half // 2 :]), (middle, key_w),
            )
        )
    ]
    for copy in copies:
        copy.start()
    copies[0].wait()
    copies[1].wait()
    slots = stored_slots(ids[...], stored[...])
    slot_o[...] = slots
    copies[2].wait()
    upto = jnp.where(
        iota((CHUNK, CHUNK), 0) <= iota((CHUNK, CHUNK), 1), 1.0, 0.0
    ).astype(bf16)
    low = first_half((1, LANES))
    for i in range(n // CHUNK):
        pieces = jnp.concatenate(thirds(decay[:, chunk(i)]), axis=0)
        sums = dot(pieces.astype(bf16), upto)
        cum = sums[:heads] + sums[heads : 2 * heads] + sums[2 * heads :]
        crow_o[i] = cum
        ccol_o[chunk(i), :] = jnp.transpose(jnp.concatenate([cum, cum], axis=0))
        for p in range(heads // 2):
            r = i * (heads // 2) + p
            ctl_o[r : r + 1, :] = jnp.where(
                low, cum[2 * p : 2 * p + 1, CHUNK - 1 :], cum[2 * p + 1 : 2 * p + 2, CHUNK - 1 :]
            )
    first = lax.axis_index("dp") * half
    for k in range(2):
        copies[3 + k].wait()
        piece = own.at[k * half // 2 : (k + 1) * half // 2]
        for i in range(n // CHUNK):
            rows = picked_rows(slots[:, chunk(i)], first + k * half // 2, piece)
            if k:
                rows += part_o[chunk(i), :].astype(f32)
            part_o[chunk(i), :] = rows.astype(bf16)
    copies[5].wait()
    key_w_o[...] = jnp.transpose(key_w[...].astype(f32)).astype(bf16)


def summary_kernel(
    length, part, peer, slot, crow, ctl, id_rows, key_w, weight,
    emb_o, key_o, val_o, enter_o, pay_o, here_o,
):
    n, width = part.shape
    half, heads = peer.shape[0], crow.shape[1]
    pairs = heads // 2
    block = LANES // 2
    low = first_half((1, LANES))
    chunks = n // CHUNK
    here = length[0] - lax.axis_index("seq") * n
    here_o[...] = jnp.full(here_o.shape, here, i32)

    def project(i):
        other = picked_rows(slot[:, chunk(i)], (1 - lax.axis_index("dp")) * half, peer)
        emb = (part[chunk(i), :].astype(f32) + other).astype(bf16)
        emb_o[chunk(i), :] = emb
        return contract(key_w[...], emb, 1, 1), dot(emb, weight[:, 2 * width :])

    total = [jnp.zeros((block, LANES), f32)] * pairs
    ready = project(0)
    for i in range(chunks):
        key, val = ready
        if i + 1 < chunks:
            ready = project(i + 1)
        val = jnp.where(iota((CHUNK, 1), 0) < here - i * CHUNK, val, 0.0).astype(bf16)
        val_o[chunk(i), :] = val
        alive = iota((1, CHUNK), 1) < here - i * CHUNK
        cum = crow[i]
        tail = jnp.exp(cum[:, CHUNK - 1 :] - cum)
        for p in range(pairs):
            keyed = []
            for h in (2 * p, 2 * p + 1):
                rows = key[h * 64 : (h + 1) * 64]
                mean = jnp.sum(rows * rows, axis=0, keepdims=True) * (1.0 / 64.0)
                unit = jnp.where(alive, lax.rsqrt(mean + 1e-06) * 0.125, 0.0)
                normed = rows * unit
                key_o[h * 64 : (h + 1) * 64, chunk(i)] = normed.astype(bf16)
                keyed.append(normed * tail[h : h + 1])
            keyed = jnp.concatenate(keyed, axis=0).astype(bf16)
            both = dot(keyed, val[:, pair_cut(p)])
            fresh = jnp.where(low, both[:block], both[block:])
            enter_o[i, p * block : (p + 1) * block, :] = total[p]
            total[p] = total[p] * jnp.exp(ctl[i * pairs + p : i * pairs + p + 1, :]) + fresh
    logs = ctl[0:pairs, :]
    for i in range(1, chunks):
        logs = logs + ctl[i * pairs : (i + 1) * pairs, :]
    pay_o[...] = pack_state(jnp.concatenate(total, axis=0), logs, id_rows[...])


def state_rows(pairs, ids):
    return pairs * 64 + -(-(3 * pairs + ids) // 16) * 16


def pack_state(state, logs, id_rows):
    pairs, ids = logs.shape[0], id_rows.shape[0]
    pad = state_rows(pairs, ids) - state.shape[0] - 3 * pairs - ids
    parts = [state, *thirds(logs), id_rows] + [jnp.zeros((pad, LANES), f32)] * (pad > 0)
    return jnp.concatenate(parts, axis=0).astype(bf16)


def unpack_state(packed, pairs):
    whole = packed.astype(f32)
    rows = pairs * 64
    logs = whole[rows : rows + pairs]
    for k in (1, 2):
        logs = logs + whole[rows + k * pairs : rows + (k + 1) * pairs]
    return whole[:rows], logs, whole[rows + 3 * pairs :]


def row_factors(logs):
    factors = jnp.exp(logs)
    return jnp.concatenate(
        [jnp.broadcast_to(factors[p : p + 1], (64, LANES)) for p in range(logs.shape[0])], axis=0
    )


def join_kernel(bit, ids, pairs, mine, got, *refs):
    before = refs[: 2 if bit else 0]
    pay_o, prefix_o, logs_o, *ids_o = refs[len(before) :]
    upper = (lax.axis_index("seq") >> bit) & 1 == 1
    state, logs, rows = unpack_state(mine[...], pairs)
    other, other_logs, other_rows = unpack_state(got[...], pairs)
    early = jnp.where(upper, other, state)
    late = jnp.where(upper, state, other)
    factor = row_factors(jnp.where(upper, logs, other_logs))
    id_rows = jnp.concatenate([rows[:ids], other_rows[:ids]], axis=0)
    if ids_o:
        ids_o[0][...] = id_rows
    sent = id_rows[:1] if ids_o else id_rows
    pay_o[...] = pack_state(early * factor + late, logs + other_logs, sent)
    if bit == 0:
        prefix_o[...] = jnp.where(upper, other, 0.0)
        logs_o[...] = jnp.where(upper, other_logs, 0.0)
    else:
        prefix, prefix_logs = before[0][...], before[1][...]
        prefix_o[...] = jnp.where(upper, prefix + row_factors(prefix_logs) * other, prefix)
        logs_o[...] = jnp.where(upper, prefix_logs + other_logs, prefix_logs)


def local_kernel(first, emb, key, val, crow, ccol, weight, query_o, intra_o):
    n, width = query_o.shape
    heads = ccol.shape[1] // 2
    ones, lanes = same_head(), head_spread(heads, first // 64, width // 64)
    mask_a, mask_b = half_masks()
    causal = iota((CHUNK, CHUNK), 0) >= iota((CHUNK, CHUNK), 1)

    def queries(i):
        query = dot(emb[chunk(i), :], weight[:, first : first + width])
        unit = lax.rsqrt(head_means(query, ones) + 1e-06) * 0.125
        query = query * unit
        decayed = query * spread(jnp.exp(ccol[chunk(i), :]), lanes)
        query_o[chunk(i), :] = decayed.astype(bf16)
        return query.astype(bf16)

    def scores(i, p, b, query):
        cut = pair_cut(p)
        wide = slice(first + p * LANES, first + (p + 1) * LANES)
        return dot(query[:, cut] * (mask_b if b else mask_a), key[wide, chunk(i)])

    units = [(i, p, b) for i in range(n // CHUNK) for p in range(width // LANES) for b in (0, 1)]
    query = {0: queries(0)}
    ready = scores(*units[0], query[0])
    held = None
    for u, (i, p, b) in enumerate(units):
        current = ready
        if u + 1 < len(units):
            j = units[u + 1][0]
            if j not in query:
                query[j] = queries(j)
            ready = scores(*units[u + 1], query[j])
        h = first // 64 + 2 * p + b
        gap = ccol[chunk(i), h : h + 1] - crow[i, h : h + 1, :]
        weights = jnp.where(causal, current * jnp.exp(gap), 0.0).astype(bf16)
        wide = slice(first + p * LANES, first + (p + 1) * LANES)
        part = dot(weights, val[chunk(i), wide] * (mask_b if b else mask_a))
        if b == 0:
            held = part
        else:
            intra_o[chunk(i), pair_cut(p)] = held + part


def candidate_kernel(
    order, owned, id_rows, stored, own, peer, query_w, pair_w, val_w_o, *quarters
):
    half, width = own.shape
    ids = id_rows[...]
    ids = (ids * float(LANES) + pltpu.roll(ids, LANES // 2, 1)).astype(i32)
    step = LANES // owned
    dp = lax.axis_index("dp")
    for start in range(0, len(order), 2 * step):
        tiles = []
        for first in (start, start + step):
            tile = None
            for k in range(step):
                j = order[first + k]
                slots = stored_slots(ids[j : j + 1], stored[...])
                if k:
                    moved = pltpu.roll(slots, k * owned, 1)
                    slots = jnp.where(iota((1, LANES), 1) >= k * owned, moved, tile)
                tile = slots
            tiles.append(tile)
        slots = jnp.concatenate(tiles, axis=1)
        found = picked_rows(slots, dp * half, own) + picked_rows(slots, (1 - dp) * half, peer)
        query = jnp.transpose(dot(found.astype(bf16), query_w[...])).astype(bf16)
        for k in (0, 1):
            quarters[start // step + k][...] = query[:, pair_cut(k)]
    val_w_o[...] = jnp.transpose(pair_w[:, width:].astype(f32)).astype(bf16)


def attend(alive_count, scale, query, key, val, buffers, emit):
    n, width = key.shape
    blocks = range(0, n, KEYS)
    pairs = width // LANES
    ones = jnp.ones((16, KEYS), bf16)

    def weights_of(p):
        rows = query[pair_cut(p), :]
        zero = jnp.zeros((64, LANES), bf16)
        top = jnp.concatenate([rows[:64], zero], axis=1)
        return jnp.concatenate([top, jnp.concatenate([zero, rows[64:]], axis=1)], axis=0)

    def store(p, block, weights, peak):
        values = dot(key[block : block + KEYS, pair_cut(p)], weights)
        values = jnp.where(iota((KEYS, 1), 0) < alive_count - block, values, DEAD)
        buffers[p % 2][block : block + KEYS, :] = values
        top = jnp.max(values.reshape(KEYS // 8, 8, 2 * LANES), axis=0)
        return top if peak is None else jnp.maximum(peak, top)

    peak, weights = None, weights_of(0)
    for block in blocks:
        peak = store(0, block, weights, peak)
    for p in range(pairs):
        factor = [
            jnp.broadcast_to(scale[0:1, h : h + 1], (1, LANES)) for h in (2 * p, 2 * p + 1)
        ]
        factor = jnp.concatenate(factor, axis=1) * LOG2E
        peak = jnp.max(peak, axis=0, keepdims=True)
        following = sums = None
        more = p + 1 < pairs
        if more:
            weights = weights_of(p + 1)
        for block in blocks:
            if more:
                following = store(p + 1, block, weights, following)
            gap = buffers[p % 2][block : block + KEYS, :] - peak
            probs = jnp.exp2(gap * factor).astype(bf16)
            side = jnp.concatenate([val[pair_cut(p), block : block + KEYS], ones], axis=0)
            part = dot(side, probs)
            sums = part if sums is None else sums + part
        total = sums[LANES : LANES + 1]
        logs = live(alive_count, peak * factor + jnp.log2(total))
        for b in (0, 1):
            cut = pair_cut(b)
            mean = sums[b * 64 : (b + 1) * 64, cut] / total[:, cut]
            emit(2 * p + b, mean, logs[:, cut])
        peak = following


def finish_kernel(
    bit, here, scale, emb, query_a, query_b, intra_a, intra_b, enter, ctl, got, prefix, prefix_logs,
    out_w, pair_w, val_w, cand_q, hist_o, key_o, val_o, pay_o,
    shown, sem, *buffers,
):
    n, width = emb.shape
    pairs = width // LANES
    ones = same_head()
    upper = (lax.axis_index("seq") >> bit) & 1 == 1
    state = unpack_state(got[...], pairs)[0]
    before, before_logs = prefix[...], prefix_logs[...]
    entering = jnp.where(upper, before + row_factors(before_logs) * state, before)
    lane = iota((1, 2 * LANES), 1) // 64
    chunks = n // CHUNK
    gone = [jnp.zeros((pairs, LANES), f32)]
    for i in range(chunks - 1):
        gone.append(gone[-1] + ctl[i * pairs : (i + 1) * pairs, :])

    def normed(i):
        states = enter[i] + row_factors(gone[i]) * entering
        parts = []
        for p in range(0, pairs, 2):
            wide = jnp.concatenate(
                [states[p * 64 : (p + 1) * 64], states[(p + 1) * 64 : (p + 2) * 64]], axis=1
            )
            matrix = jnp.concatenate([jnp.where(lane == k, wide, 0.0) for k in range(4)], axis=0)
            query, intra = (query_a, intra_a) if p < pairs // 2 else (query_b, intra_b)
            c = (p % (pairs // 2)) * LANES
            cut = slice(c, c + 2 * LANES)
            parts.append(dot(query[chunk(i), cut], matrix.astype(bf16)) + intra[chunk(i), cut])
        mixed = jnp.concatenate(parts, axis=1)
        return (mixed * lax.rsqrt(head_means(mixed, ones) + 1e-05)).astype(bf16)

    alive_count = here[0:1, 0:1]
    copies = [
        pltpu.make_async_copy(shown.at[chunk(i), :], hist_o.at[chunk(i), :], sem.at[i])
        for i in range(chunks)
    ]
    ready = normed(0)
    for i in range(chunks):
        current = ready
        if i + 1 < chunks:
            ready = normed(i + 1)
        hidden_sum = emb[chunk(i), :].astype(f32) + dot(current, out_w[...])
        alive = iota((CHUNK, 1), 0) < alive_count - i * CHUNK
        shown[chunk(i), :] = jnp.where(alive, hidden_sum, 0.0)
        copies[i].start()
        hidden = hidden_sum.astype(bf16)
        key_o[chunk(i), :] = dot(hidden, pair_w[:, :width]).astype(bf16)
        val_o[:, chunk(i)] = contract(val_w[...], hidden, 1, 1).astype(bf16)
    send_part(alive_count, scale, cand_q, key_o, val_o, pay_o, buffers)
    for copy in copies:
        copy.wait()


def send_part(alive_count, scale, query, key, val, pay_o, buffers):
    log_rows = []

    def emit(h, mean, logs):
        pay_o[h * 64 : (h + 1) * 64, :] = mean.astype(bf16)
        log_rows.append(logs)

    attend(alive_count, scale, query, key, val, buffers, emit)
    pay_o[val.shape[0] :, :] = pack_logs(jnp.concatenate(log_rows, axis=0))


def send_kernel(here, scale, query, key, val, pay_o, *buffers):
    send_part(here[0:1, 0:1], scale, query, key, val, pay_o, buffers)


def live(alive_count, logs):
    return jnp.where(jnp.broadcast_to(alive_count, logs.shape) > 0, logs, DEAD)


def pack_logs(logs):
    heads, cols = logs.shape
    return jnp.concatenate(
        [*thirds(logs), jnp.zeros((log_pad(heads) - 3 * heads, cols), f32)], axis=0
    ).astype(bf16)


def log_pad(heads):
    return -(-3 * heads // 16) * 16


def unpack_logs(rows, heads):
    rows = rows.astype(f32)
    return rows[:heads] + rows[heads : 2 * heads] + rows[2 * heads : 3 * heads]


def keep_kernel(here, scale, query, key, val, mean_o, logs_o, *buffers):
    def emit(h, mean, logs):
        mean_o[h * 64 : (h + 1) * 64, :] = mean
        logs_o[h : h + 1, :] = logs

    attend(here[0:1, 0:1], scale, query, key, val, buffers, emit)


def over_heads(rows):
    return jnp.concatenate(
        [jnp.broadcast_to(rows[h : h + 1], (64, rows.shape[1])) for h in range(rows.shape[0])],
        axis=0,
    )


def merge(parts):
    peak = parts[0][1]
    for _, logs in parts[1:]:
        peak = jnp.maximum(peak, logs)
    shares = [jnp.exp2(logs - peak) for _, logs in parts]
    total = sum(shares[1:], shares[0])
    mean = None
    for (value, _), share in zip(parts, shares):
        term = value * over_heads(share / total)
        mean = term if mean is None else mean + term
    return mean, peak + jnp.log2(total)


def received(got, heads):
    value = got[...].astype(f32)
    if value.shape[0] < heads * 64:
        value = jnp.concatenate([value, pltpu.roll(value, LANES // 2, 1)], axis=0)
    return value[: heads * 64], unpack_logs(value[heads * 64 :], heads)


def fold_kernel(mean, logs, *refs):
    gots, (mean_o, logs_o, pay_o) = refs[:-3], refs[-3:]
    heads, keep = logs_o.shape
    parts = [(mean[...], logs[...])] + [received(got, heads) for got in gots]
    new_mean, new_logs = merge(parts)
    mean_o[...] = new_mean[:, :keep]
    logs_o[...] = new_logs[:, :keep]
    whole = jnp.concatenate([new_mean, pack_logs(new_logs).astype(f32)], axis=0)
    if 2 * keep == LANES:
        half = whole.shape[0] // 2
        top = pltpu.roll(whole[:half], keep, 1)
        pay_o[...] = jnp.where(first_half((1, LANES)), top, whole[half:]).astype(bf16)
    else:
        pay_o[...] = whole[:, keep:].astype(bf16)


def last_kernel(mean, logs, got, out_w, cand_o):
    heads, cols = logs.shape
    other_mean, other_logs = received(got, heads)
    parts = [(mean[...], logs[...]), (other_mean[:, :cols], other_logs[:, :cols])]
    attended = merge(parts)[0].astype(bf16)
    cand_o[...] = contract(attended, out_w[...], 0, 0)


def shape(dims, dtype):
    return jax.ShapeDtypeStruct(dims, dtype)


VMEM = pl.BlockSpec(memory_space=pltpu.VMEM)
SMEM = pl.BlockSpec(memory_space=pltpu.SMEM)
ANY = pl.BlockSpec(memory_space=pl.ANY)
HBM = pl.BlockSpec(memory_space=pltpu.HBM)


def call(kernel, name, operands, outs, scratch=(), after=(), flops=0, space=VMEM, spaces=None, scalars=()):
    count = len(scalars) + len(operands)
    if space is HBM:
        operands = [pltpu.with_memory_space_constraint(value, pltpu.HBM) for value in operands]

    def body(*refs):
        kernel(*refs[:count], *refs[count + len(after) :])

    return pl.pallas_call(
        body,
        name=name,
        in_specs=[SMEM] * len(scalars) + [space] * len(operands) + [ANY] * len(after),
        out_specs=spaces or [VMEM] * len(outs),
        out_shape=outs,
        scratch_shapes=list(scratch),
        compiler_params=pltpu.CompilerParams(vmem_limit_bytes=VMEM_LIMIT),
        cost_estimate=pl.CostEstimate(flops=flops, transcendentals=0, bytes_accessed=0),
    )(*scalars, *operands, *after)


def reversed_bits(value, bits):
    return sum(((value >> b) & 1) << (bits - 1 - b) for b in range(bits))


def shards(
    history_item_index,
    log_head_retention,
    user_history_length,
    candidate_item_index,
    item_stored_row,
    item_embedding_table,
    head_score_scale,
    history_query_key_value_weight,
    history_output_weight,
    candidate_key_value_weight,
    candidate_query_weight,
    candidate_output_weight,
):
    users, n = history_item_index.shape
    heads = log_head_retention.shape[1]
    half, width = item_embedding_table.shape
    owned = candidate_item_index.shape[1]
    seq = lax.axis_size("seq")
    bits = seq.bit_length() - 1
    cands = owned * seq
    assert users == 1 and lax.axis_size("dp") == 2 and seq == 1 << bits and bits > 2
    assert width == heads * 64 and heads % 4 == 0 and LANES % owned == 0 and owned <= 64
    assert cands == 4 * LANES
    pairs = heads // 2
    rows = pairs * 64

    def swap(value, mask):
        return lax.ppermute(value, "seq", [(j, j ^ mask) for j in range(seq)])

    peer = lax.ppermute(item_embedding_table, "dp", [(0, 1), (1, 0)])
    far_ids = swap(candidate_item_index, seq // 2)
    scale = head_score_scale.reshape(1, heads)
    stored = item_stored_row.reshape(-1, LANES)
    ids = jnp.concatenate([candidate_item_index, far_ids], axis=0)
    ids = jnp.pad(ids, ((0, 0), (0, 64 - owned)))
    id_rows = jnp.concatenate([ids // LANES, ids % LANES], axis=1).astype(f32)
    decay = log_head_retention.reshape(heads, n)

    part, slot, crow, ccol, ctl, key_w = call(
        own_rows_kernel, "own_rows",
        [
            history_item_index, stored, decay, item_embedding_table,
            history_query_key_value_weight,
        ],
        [
            shape((n, width), bf16), shape((1, n), f32), shape((n // CHUNK, heads, CHUNK), f32),
            shape((n, 2 * heads), f32), shape((n // CHUNK * pairs, LANES), f32),
            shape((width, width), bf16),
        ],
        [
            pltpu.VMEM((1, n), i32), pltpu.VMEM(stored.shape, i32), pltpu.VMEM((heads, n), f32),
            pltpu.VMEM((half, width), bf16), pltpu.VMEM((width, width), bf16),
            pltpu.SemaphoreType.DMA((6,)),
        ],
        space=HBM,
        flops=2 * n * half * width,
    )
    emb, key, val, enter, pay, here = call(
        summary_kernel, "summary",
        [part, peer, slot, crow, ctl, id_rows, key_w, history_query_key_value_weight],
        [
            shape((n, width), bf16), shape((width, n), bf16), shape((n, width), bf16),
            shape((n // CHUNK, rows, LANES), f32), shape((state_rows(pairs, 2), LANES), bf16),
            shape((8, LANES), i32),
        ],
        scalars=[user_history_length],
        flops=2 * n * half * width,
    )

    def local(first, name, after):
        return call(
            lambda *refs: local_kernel(first, *refs), name,
            [emb, key, val, crow, ccol, history_query_key_value_weight],
            [shape((n, width // 2), bf16), shape((n, width // 2), f32)],
            after=after, flops=2 * n * half * width // 2,
        )

    early = [local(0, "local_a", [])]
    prefix = logs = None
    for bit in range(bits - 1):
        got = swap(pay, 1 << bit)
        if bit == 1:
            early.append(local(width // 2, "local_b", [prefix]))
        count = 2 << bit
        final = bit == bits - 2
        pay, prefix, logs, *every = call(
            lambda *refs, bit=bit, count=count: join_kernel(bit, count, pairs, *refs), "join",
            [pay, got] + ([prefix, logs] if bit else []),
            [
                shape((state_rows(pairs, 1 if final else 2 * count), LANES), bf16),
                shape((rows, LANES), f32), shape((pairs, LANES), f32),
            ] + [shape((2 * count, LANES), f32)] * final,
            after=[early[-1][1]],
        )
    got = swap(pay, 1 << (bits - 1))
    order = [t + 4 * reversed_bits(k, bits - 2) for t in range(4) for k in range(seq // 4)]
    order = [2 * (j % (seq // 2)) + j // (seq // 2) for j in order]
    work = cands * 2 * half * width
    val_w, *quarters = call(
        lambda *refs: candidate_kernel(order, owned, *refs), "candidates",
        [
            every[0], stored, item_embedding_table, peer, candidate_query_weight,
            candidate_key_value_weight,
        ],
        [shape((width, width), bf16)] + [shape((width, LANES), bf16)] * 4, flops=2 * work,
    )
    (query_a, intra_a), (query_b, intra_b) = early
    buffers = [pltpu.VMEM((n, 2 * LANES), f32)] * 2
    message = width + log_pad(heads)
    hist, key_two, val_two, pay = call(
        lambda *refs: finish_kernel(bits - 1, *refs), "finish",
        [
            here, scale, emb, query_a, query_b, intra_a, intra_b, enter, ctl, got, prefix, logs,
            history_output_weight, candidate_key_value_weight, val_w, quarters[3],
        ],
        [
            shape((n, width), f32), shape((n, width), bf16), shape((width, n), bf16),
            shape((message, LANES), bf16),
        ],
        [pltpu.VMEM((n, width), f32), pltpu.SemaphoreType.DMA((n // CHUNK,))] + buffers,
        spaces=[ANY, VMEM, VMEM, VMEM],
        flops=2 * n * half * width,
    )
    gots = [swap(pay, 3)]
    for t in (2, 1):
        (pay,) = call(
            send_kernel, "send", [here, scale, quarters[t], key_two, val_two],
            [shape((message, LANES), bf16)], buffers, after=[pay], flops=8 * work,
        )
        gots.append(swap(pay, t))
    mean, logs = call(
        keep_kernel, "keep", [here, scale, quarters[0], key_two, val_two],
        [shape((width, LANES), f32), shape((heads, LANES), f32)], buffers, after=[pay], flops=8 * work,
    )
    cols = LANES
    for bit in range(2, bits):
        cols //= 2
        packed = 2 * cols == LANES
        mean, logs, pay = call(
            fold_kernel, "fold", [mean, logs, *gots],
            [
                shape((width, cols), f32), shape((heads, cols), f32),
                shape((message // 2, LANES) if packed else (message, cols), bf16),
            ],
        )
        if packed and bit < bits - 1:
            pay = jnp.concatenate([pay[:, :cols], pay[:, cols:]], axis=0)
        gots = [swap(pay, 1 << bit)]
    (cand_out,) = call(
        last_kernel, "last", [mean, logs, *gots, candidate_output_weight],
        [shape((owned, width), f32)],
    )
    return hist[None], cand_out[None]


def solution(mesh):
    in_specs = (
        P(("groups", "dp"), "seq"),
        P(("groups", "dp"), None, "seq"),
        P(("groups", "dp")),
        P(("groups", "dp"), "seq"),
        P(),
        P("dp", None),
        P(),
        P(),
        P(),
        P(),
        P(),
        P(),
    )
    out_specs = (P(("groups", "dp"), "seq", None), P(("groups", "dp"), "seq", None))
    return jax.shard_map(shards, mesh=mesh, in_specs=in_specs, out_specs=out_specs, check_vma=False)
```

```python
import math

import jax
import jax.numpy as jnp
from jax import lax
from jax.experimental import pallas as pl
from jax.experimental.pallas import tpu as pltpu
from jax.sharding import PartitionSpec as P

f32, bf16, i32 = jnp.float32, jnp.bfloat16, jnp.int32
CHUNK = 256
KEYS = 512
LANES = 128
LOG2E = math.log2(math.e)
DEAD = -1e30
VMEM_LIMIT = 40 << 20


def dot(a, b):
    return jnp.dot(a, b, preferred_element_type=f32)


def contract(a, b, left, right):
    return lax.dot_general(a, b, (((left,), (right,)), ((), ())), preferred_element_type=f32)


def iota(shape, axis):
    return lax.broadcasted_iota(i32, shape, axis)


def thirds(value):
    high = value.astype(bf16).astype(f32)
    rest = value - high
    mid = rest.astype(bf16).astype(f32)
    return high, mid, rest - mid


def first_half(shape):
    return iota(shape, len(shape) - 1) % LANES < LANES // 2


def half_masks():
    low = first_half((1, LANES))
    return jnp.where(low, 1.0, 0.0).astype(bf16), jnp.where(low, 0.0, 1.0).astype(bf16)


def same_head():
    dims = (2 * LANES, 2 * LANES)
    return jnp.where(iota(dims, 0) // 64 == iota(dims, 1) // 64, 1.0, 0.0).astype(bf16)


def head_means(value, ones):
    square = (value * value).astype(bf16)
    step = ones.shape[0]
    parts = [dot(square[:, c : c + step], ones) for c in range(0, value.shape[1], step)]
    return jnp.concatenate(parts, axis=1) * (1.0 / 64.0)


def head_spread(heads, first, count):
    dims = (2 * heads, 64 * count)
    return jnp.where(iota(dims, 1) // 64 + first == iota(dims, 0) % heads, 1.0, 0.0).astype(bf16)


def spread(value, matrix):
    heads = value.shape[1] // 2
    high = value.astype(bf16).astype(f32)
    both = jnp.where(iota(value.shape, 1) < heads, high, value - high)
    return dot(both.astype(bf16), matrix)


def stored_slots(ids, stored):
    groups = stored.shape[0]
    n = ids.shape[1]
    pick = jnp.where(iota((groups, n), 0) == ids // LANES, 1.0, 0.0).astype(bf16)
    high = contract((stored // 64).astype(f32).astype(bf16), pick, 0, 0)
    low = contract((stored % 64).astype(f32).astype(bf16), pick, 0, 0)
    rows = jnp.where(iota((LANES, n), 0) == ids % LANES, high * 64.0 + low, 0.0)
    return jnp.sum(rows, axis=0, keepdims=True)


def picked_rows(slots, first, table):
    count = table.shape[0]
    hot = jnp.where(iota((count, slots.shape[1]), 0) == slots.astype(i32) - first, 1.0, 0.0)
    return contract(hot.astype(bf16), table[...], 0, 0)


def chunk(i):
    return slice(i * CHUNK, (i + 1) * CHUNK)


def pair_cut(p):
    return slice(p * LANES, (p + 1) * LANES)


def own_rows_kernel(
    ids_in, stored_in, decay_in, own_in, weight_in, part_o, slot_o, crow_o, ccol_o, ctl_o, key_w_o,
    ids, stored, decay, own, key_w, sem,
):
    n, half, heads = ids.shape[1], own.shape[0], decay.shape[0]
    width = own.shape[1]
    middle = weight_in.at[:, width : 2 * width]
    copies = [
        pltpu.make_async_copy(source, target, sem.at[k])
        for k, (source, target) in enumerate(
            (
                (ids_in, ids), (stored_in, stored), (decay_in, decay),
                (own_in.at[: half // 2], own.at[: half // 2]),
                (own_in.at[half // 2 :], own.at[half // 2 :]), (middle, key_w),
            )
        )
    ]
    for copy in copies:
        copy.start()
    copies[0].wait()
    copies[1].wait()
    slots = stored_slots(ids[...], stored[...])
    slot_o[...] = slots
    copies[2].wait()
    upto = jnp.where(
        iota((CHUNK, CHUNK), 0) <= iota((CHUNK, CHUNK), 1), 1.0, 0.0
    ).astype(bf16)
    low = first_half((1, LANES))
    for i in range(n // CHUNK):
        pieces = jnp.concatenate(thirds(decay[:, chunk(i)]), axis=0)
        sums = dot(pieces.astype(bf16), upto)
        cum = sums[:heads] + sums[heads : 2 * heads] + sums[2 * heads :]
        crow_o[i] = cum
        ccol_o[chunk(i), :] = jnp.transpose(jnp.concatenate([cum, cum], axis=0))
        for p in range(heads // 2):
            r = i * (heads // 2) + p
            ctl_o[r : r + 1, :] = jnp.where(
                low, cum[2 * p : 2 * p + 1, CHUNK - 1 :], cum[2 * p + 1 : 2 * p + 2, CHUNK - 1 :]
            )
    first = lax.axis_index("dp") * half
    for k in range(2):
        copies[3 + k].wait()
        piece = own.at[k * half // 2 : (k + 1) * half // 2]
        for i in range(n // CHUNK):
            rows = picked_rows(slots[:, chunk(i)], first + k * half // 2, piece)
            if k:
                rows += part_o[chunk(i), :].astype(f32)
            part_o[chunk(i), :] = rows.astype(bf16)
    copies[5].wait()
    key_w_o[...] = jnp.transpose(key_w[...].astype(f32)).astype(bf16)


def summary_kernel(
    length, part, peer, slot, crow, ctl, id_rows, key_w, weight,
    emb_o, key_o, val_o, enter_o, pay_o, here_o,
):
    n, width = part.shape
    half, heads = peer.shape[0], crow.shape[1]
    pairs = heads // 2
    block = LANES // 2
    low = first_half((1, LANES))
    chunks = n // CHUNK
    here = length[0] - lax.axis_index("seq") * n
    here_o[...] = jnp.full(here_o.shape, here, i32)

    def project(i):
        other = picked_rows(slot[:, chunk(i)], (1 - lax.axis_index("dp")) * half, peer)
        emb = (part[chunk(i), :].astype(f32) + other).astype(bf16)
        emb_o[chunk(i), :] = emb
        return contract(key_w[...], emb, 1, 1), dot(emb, weight[:, 2 * width :])

    total = [jnp.zeros((block, LANES), f32)] * pairs
    ready = project(0)
    for i in range(chunks):
        key, val = ready
        if i + 1 < chunks:
            ready = project(i + 1)
        val = jnp.where(iota((CHUNK, 1), 0) < here - i * CHUNK, val, 0.0).astype(bf16)
        val_o[chunk(i), :] = val
        alive = iota((1, CHUNK), 1) < here - i * CHUNK
        cum = crow[i]
        tail = jnp.exp(cum[:, CHUNK - 1 :] - cum)
        for p in range(pairs):
            keyed = []
            for h in (2 * p, 2 * p + 1):
                rows = key[h * 64 : (h + 1) * 64]
                mean = jnp.sum(rows * rows, axis=0, keepdims=True) * (1.0 / 64.0)
                unit = jnp.where(alive, lax.rsqrt(mean + 1e-06) * 0.125, 0.0)
                normed = rows * unit
                key_o[h * 64 : (h + 1) * 64, chunk(i)] = normed.astype(bf16)
                keyed.append(normed * tail[h : h + 1])
            keyed = jnp.concatenate(keyed, axis=0).astype(bf16)
            both = dot(keyed, val[:, pair_cut(p)])
            fresh = jnp.where(low, both[:block], both[block:])
            enter_o[i, p * block : (p + 1) * block, :] = total[p]
            total[p] = total[p] * jnp.exp(ctl[i * pairs + p : i * pairs + p + 1, :]) + fresh
    logs = ctl[0:pairs, :]
    for i in range(1, chunks):
        logs = logs + ctl[i * pairs : (i + 1) * pairs, :]
    pay_o[...] = pack_state(jnp.concatenate(total, axis=0), logs, id_rows[...])


def state_rows(pairs, ids):
    return pairs * 64 + -(-(3 * pairs + ids) // 16) * 16


def pack_state(state, logs, id_rows):
    pairs, ids = logs.shape[0], id_rows.shape[0]
    pad = state_rows(pairs, ids) - state.shape[0] - 3 * pairs - ids
    parts = [state, *thirds(logs), id_rows] + [jnp.zeros((pad, LANES), f32)] * (pad > 0)
    return jnp.concatenate(parts, axis=0).astype(bf16)


def unpack_state(packed, pairs):
    whole = packed.astype(f32)
    rows = pairs * 64
    logs = whole[rows : rows + pairs]
    for k in (1, 2):
        logs = logs + whole[rows + k * pairs : rows + (k + 1) * pairs]
    return whole[:rows], logs, whole[rows + 3 * pairs :]


def row_factors(logs):
    factors = jnp.exp(logs)
    return jnp.concatenate(
        [jnp.broadcast_to(factors[p : p + 1], (64, LANES)) for p in range(logs.shape[0])], axis=0
    )


def join_kernel(bit, ids, pairs, mine, got, *refs):
    before = refs[: 2 if bit else 0]
    pay_o, prefix_o, logs_o, *ids_o = refs[len(before) :]
    upper = (lax.axis_index("seq") >> bit) & 1 == 1
    state, logs, rows = unpack_state(mine[...], pairs)
    other, other_logs, other_rows = unpack_state(got[...], pairs)
    early = jnp.where(upper, other, state)
    late = jnp.where(upper, state, other)
    factor = row_factors(jnp.where(upper, logs, other_logs))
    id_rows = jnp.concatenate([rows[:ids], other_rows[:ids]], axis=0)
    if ids_o:
        ids_o[0][...] = id_rows
    sent = id_rows[:1] if ids_o else id_rows
    pay_o[...] = pack_state(early * factor + late, logs + other_logs, sent)
    if bit == 0:
        prefix_o[...] = jnp.where(upper, other, 0.0)
        logs_o[...] = jnp.where(upper, other_logs, 0.0)
    else:
        prefix, prefix_logs = before[0][...], before[1][...]
        prefix_o[...] = jnp.where(upper, prefix + row_factors(prefix_logs) * other, prefix)
        logs_o[...] = jnp.where(upper, prefix_logs + other_logs, prefix_logs)


def local_kernel(first, emb, key, val, crow, ccol, weight, query_o, intra_o):
    n, width = query_o.shape
    heads = ccol.shape[1] // 2
    ones, lanes = same_head(), head_spread(heads, first // 64, width // 64)
    mask_a, mask_b = half_masks()
    causal = iota((CHUNK, CHUNK), 0) >= iota((CHUNK, CHUNK), 1)

    def queries(i):
        query = dot(emb[chunk(i), :], weight[:, first : first + width])
        unit = lax.rsqrt(head_means(query, ones) + 1e-06) * 0.125
        query = query * unit
        decayed = query * spread(jnp.exp(ccol[chunk(i), :]), lanes)
        query_o[chunk(i), :] = decayed.astype(bf16)
        return query.astype(bf16)

    def scores(i, p, b, query):
        cut = pair_cut(p)
        wide = slice(first + p * LANES, first + (p + 1) * LANES)
        return dot(query[:, cut] * (mask_b if b else mask_a), key[wide, chunk(i)])

    units = [(i, p, b) for i in range(n // CHUNK) for p in range(width // LANES) for b in (0, 1)]
    query = {0: queries(0)}
    ready = scores(*units[0], query[0])
    held = None
    for u, (i, p, b) in enumerate(units):
        current = ready
        if u + 1 < len(units):
            j = units[u + 1][0]
            if j not in query:
                query[j] = queries(j)
            ready = scores(*units[u + 1], query[j])
        h = first // 64 + 2 * p + b
        gap = ccol[chunk(i), h : h + 1] - crow[i, h : h + 1, :]
        weights = jnp.where(causal, current * jnp.exp(gap), 0.0).astype(bf16)
        wide = slice(first + p * LANES, first + (p + 1) * LANES)
        part = dot(weights, val[chunk(i), wide] * (mask_b if b else mask_a))
        if b == 0:
            held = part
        else:
            intra_o[chunk(i), pair_cut(p)] = held + part


def candidate_kernel(
    order, owned, id_rows, stored, own, peer, query_w, pair_w, val_w_o, *quarters
):
    half, width = own.shape
    ids = id_rows[...]
    ids = (ids * float(LANES) + pltpu.roll(ids, LANES // 2, 1)).astype(i32)
    step = LANES // owned
    dp = lax.axis_index("dp")
    for start in range(0, len(order), 2 * step):
        tiles = []
        for first in (start, start + step):
            tile = None
            for k in range(step):
                j = order[first + k]
                slots = stored_slots(ids[j : j + 1], stored[...])
                if k:
                    moved = pltpu.roll(slots, k * owned, 1)
                    slots = jnp.where(iota((1, LANES), 1) >= k * owned, moved, tile)
                tile = slots
            tiles.append(tile)
        slots = jnp.concatenate(tiles, axis=1)
        found = picked_rows(slots, dp * half, own) + picked_rows(slots, (1 - dp) * half, peer)
        query = jnp.transpose(dot(found.astype(bf16), query_w[...])).astype(bf16)
        for k in (0, 1):
            quarters[start // step + k][...] = query[:, pair_cut(k)]
    val_w_o[...] = jnp.transpose(pair_w[:, width:].astype(f32)).astype(bf16)


def attend(alive_count, scale, queries, key, val, buffers, emit):
    n, width = key.shape
    blocks = range(0, n, KEYS)
    ones = jnp.ones((16, KEYS), bf16)
    heads = width // 64
    if len(queries) == 1:
        units = [[(h, 0), (h + 1, 0)] for h in range(0, heads, 2)]
    else:
        units = [[(h, 0), (h, 1)] for h in range(heads)]

    def weights_of(unit):
        parts = []
        for h, k in unit:
            rows = queries[k][h * 64 : (h + 1) * 64, :]
            zero = jnp.zeros_like(rows)
            parts.append(jnp.concatenate([zero, rows] if h % 2 else [rows, zero], axis=0))
        return jnp.concatenate(parts, axis=1)

    def store(u, block, weights, peak):
        values = dot(key[block : block + KEYS, pair_cut(units[u][0][0] // 2)], weights)
        values = jnp.where(iota((KEYS, 1), 0) < alive_count - block, values, DEAD)
        buffers[u % 2][block : block + KEYS, :] = values
        top = jnp.max(values.reshape(KEYS // 8, 8, 2 * LANES), axis=0)
        return top if peak is None else jnp.maximum(peak, top)

    peak, weights = None, weights_of(units[0])
    for block in blocks:
        peak = store(0, block, weights, peak)
    for u, unit in enumerate(units):
        factor = [jnp.broadcast_to(scale[0:1, h : h + 1], (1, LANES)) for h, _ in unit]
        factor = jnp.concatenate(factor, axis=1) * LOG2E
        first = unit[0][0] * 64
        rows = (unit[-1][0] + 1) * 64 - first
        peak = jnp.max(peak, axis=0, keepdims=True)
        following = sums = None
        more = u + 1 < len(units)
        if more:
            weights = weights_of(units[u + 1])
        for block in blocks:
            if more:
                following = store(u + 1, block, weights, following)
            gap = buffers[u % 2][block : block + KEYS, :] - peak
            probs = jnp.exp2(gap * factor).astype(bf16)
            side = [val[first : first + rows, block : block + KEYS], ones]
            part = dot(jnp.concatenate(side, axis=0), probs)
            sums = part if sums is None else sums + part
        total = sums[rows : rows + 1]
        logs = live(alive_count, peak * factor + jnp.log2(total))
        for b, (h, k) in enumerate(unit):
            top = h * 64 - first
            mean = sums[top : top + 64, pair_cut(b)] / total[:, pair_cut(b)]
            emit(h, k, mean, logs[:, pair_cut(b)])
        peak = following


def finish_kernel(
    bit, here, scale, emb, query_a, query_b, intra_a, intra_b, enter, ctl, got, prefix, prefix_logs,
    out_w, pair_w, val_w, cand_a, cand_b,
    hist_o, key_o, val_o, pay_a, pay_b, shown, sem, *buffers,
):
    n, width = emb.shape
    pairs = width // LANES
    ones = same_head()
    upper = (lax.axis_index("seq") >> bit) & 1 == 1
    state = unpack_state(got[...], pairs)[0]
    before, before_logs = prefix[...], prefix_logs[...]
    entering = jnp.where(upper, before + row_factors(before_logs) * state, before)
    lane = iota((1, 2 * LANES), 1) // 64
    chunks = n // CHUNK
    gone = [jnp.zeros((pairs, LANES), f32)]
    for i in range(chunks - 1):
        gone.append(gone[-1] + ctl[i * pairs : (i + 1) * pairs, :])

    def normed(i):
        states = enter[i] + row_factors(gone[i]) * entering
        parts = []
        for p in range(0, pairs, 2):
            wide = jnp.concatenate(
                [states[p * 64 : (p + 1) * 64], states[(p + 1) * 64 : (p + 2) * 64]], axis=1
            )
            matrix = jnp.concatenate([jnp.where(lane == k, wide, 0.0) for k in range(4)], axis=0)
            query, intra = (query_a, intra_a) if p < pairs // 2 else (query_b, intra_b)
            c = (p % (pairs // 2)) * LANES
            cut = slice(c, c + 2 * LANES)
            parts.append(dot(query[chunk(i), cut], matrix.astype(bf16)) + intra[chunk(i), cut])
        mixed = jnp.concatenate(parts, axis=1)
        return (mixed * lax.rsqrt(head_means(mixed, ones) + 1e-05)).astype(bf16)

    alive_count = here[0:1, 0:1]
    copies = [
        pltpu.make_async_copy(shown.at[chunk(i), :], hist_o.at[chunk(i), :], sem.at[i])
        for i in range(chunks)
    ]
    ready = normed(0)
    for i in range(chunks):
        current = ready
        if i + 1 < chunks:
            ready = normed(i + 1)
        hidden_sum = emb[chunk(i), :].astype(f32) + dot(current, out_w[...])
        alive = iota((CHUNK, 1), 0) < alive_count - i * CHUNK
        shown[chunk(i), :] = jnp.where(alive, hidden_sum, 0.0)
        copies[i].start()
        hidden = hidden_sum.astype(bf16)
        key_o[chunk(i), :] = dot(hidden, pair_w[:, :width]).astype(bf16)
        val_o[:, chunk(i)] = contract(val_w[...], hidden, 1, 1).astype(bf16)
    send_part(alive_count, scale, (cand_a, cand_b), key_o, val_o, (pay_a, pay_b), buffers)
    for copy in copies:
        copy.wait()


def send_part(alive_count, scale, queries, key, val, pays, buffers):
    log_rows = [[] for _ in pays]

    def emit(h, k, mean, logs):
        pays[k][h * 64 : (h + 1) * 64, :] = mean.astype(bf16)
        log_rows[k].append(logs)

    attend(alive_count, scale, queries, key, val, buffers, emit)
    for pay, rows in zip(pays, log_rows):
        pay[val.shape[0] :, :] = pack_logs(jnp.concatenate(rows, axis=0))


def send_kernel(here, scale, query, key, val, pay_o, *buffers):
    send_part(here[0:1, 0:1], scale, (query,), key, val, (pay_o,), buffers)


def live(alive_count, logs):
    return jnp.where(jnp.broadcast_to(alive_count, logs.shape) > 0, logs, DEAD)


def pack_logs(logs):
    heads, cols = logs.shape
    return jnp.concatenate(
        [*thirds(logs), jnp.zeros((log_pad(heads) - 3 * heads, cols), f32)], axis=0
    ).astype(bf16)


def log_pad(heads):
    return -(-3 * heads // 16) * 16


def unpack_logs(rows, heads):
    rows = rows.astype(f32)
    return rows[:heads] + rows[heads : 2 * heads] + rows[2 * heads : 3 * heads]


def keep_kernel(here, scale, query, key, val, mean_o, logs_o, *buffers):
    def emit(h, k, mean, logs):
        mean_o[h * 64 : (h + 1) * 64, :] = mean
        logs_o[h : h + 1, :] = logs

    attend(here[0:1, 0:1], scale, (query,), key, val, buffers, emit)


def over_heads(rows):
    return jnp.concatenate(
        [jnp.broadcast_to(rows[h : h + 1], (64, rows.shape[1])) for h in range(rows.shape[0])],
        axis=0,
    )


def merge(parts):
    peak = parts[0][1]
    for _, logs in parts[1:]:
        peak = jnp.maximum(peak, logs)
    shares = [jnp.exp2(logs - peak) for _, logs in parts]
    total = sum(shares[1:], shares[0])
    mean = None
    for (value, _), share in zip(parts, shares):
        term = value * over_heads(share / total)
        mean = term if mean is None else mean + term
    return mean, peak + jnp.log2(total)


def received(got, heads):
    value = got[...].astype(f32)
    if value.shape[0] < heads * 64:
        value = jnp.concatenate([value, pltpu.roll(value, LANES // 2, 1)], axis=0)
    return value[: heads * 64], unpack_logs(value[heads * 64 :], heads)


def fold_kernel(mean, logs, *refs):
    gots, (mean_o, logs_o, pay_o) = refs[:-3], refs[-3:]
    heads, keep = logs_o.shape
    parts = [(mean[...], logs[...])] + [received(got, heads) for got in gots]
    new_mean, new_logs = merge(parts)
    mean_o[...] = new_mean[:, :keep]
    logs_o[...] = new_logs[:, :keep]
    whole = jnp.concatenate([new_mean, pack_logs(new_logs).astype(f32)], axis=0)
    if 2 * keep == LANES:
        half = whole.shape[0] // 2
        top = pltpu.roll(whole[:half], keep, 1)
        pay_o[...] = jnp.where(first_half((1, LANES)), top, whole[half:]).astype(bf16)
    else:
        pay_o[...] = whole[:, keep:].astype(bf16)


def last_kernel(mean, logs, got, out_w, cand_o):
    heads, cols = logs.shape
    other_mean, other_logs = received(got, heads)
    parts = [(mean[...], logs[...]), (other_mean[:, :cols], other_logs[:, :cols])]
    attended = merge(parts)[0].astype(bf16)
    cand_o[...] = contract(attended, out_w[...], 0, 0)


def shape(dims, dtype):
    return jax.ShapeDtypeStruct(dims, dtype)


VMEM = pl.BlockSpec(memory_space=pltpu.VMEM)
SMEM = pl.BlockSpec(memory_space=pltpu.SMEM)
ANY = pl.BlockSpec(memory_space=pl.ANY)
HBM = pl.BlockSpec(memory_space=pltpu.HBM)


def call(kernel, name, operands, outs, scratch=(), after=(), flops=0, space=VMEM, spaces=None, scalars=()):
    count = len(scalars) + len(operands)
    if space is HBM:
        operands = [pltpu.with_memory_space_constraint(value, pltpu.HBM) for value in operands]

    def body(*refs):
        kernel(*refs[:count], *refs[count + len(after) :])

    return pl.pallas_call(
        body,
        name=name,
        in_specs=[SMEM] * len(scalars) + [space] * len(operands) + [ANY] * len(after),
        out_specs=spaces or [VMEM] * len(outs),
        out_shape=outs,
        scratch_shapes=list(scratch),
        compiler_params=pltpu.CompilerParams(vmem_limit_bytes=VMEM_LIMIT),
        cost_estimate=pl.CostEstimate(flops=flops, transcendentals=0, bytes_accessed=0),
    )(*scalars, *operands, *after)


def reversed_bits(value, bits):
    return sum(((value >> b) & 1) << (bits - 1 - b) for b in range(bits))


def shards(
    history_item_index,
    log_head_retention,
    user_history_length,
    candidate_item_index,
    item_stored_row,
    item_embedding_table,
    head_score_scale,
    history_query_key_value_weight,
    history_output_weight,
    candidate_key_value_weight,
    candidate_query_weight,
    candidate_output_weight,
):
    users, n = history_item_index.shape
    heads = log_head_retention.shape[1]
    half, width = item_embedding_table.shape
    owned = candidate_item_index.shape[1]
    seq = lax.axis_size("seq")
    bits = seq.bit_length() - 1
    cands = owned * seq
    assert users == 1 and lax.axis_size("dp") == 2 and seq == 1 << bits and bits > 2
    assert width == heads * 64 and heads % 4 == 0 and LANES % owned == 0 and owned <= 64
    assert cands == 4 * LANES
    pairs = heads // 2
    rows = pairs * 64

    def swap(value, mask):
        return lax.ppermute(value, "seq", [(j, j ^ mask) for j in range(seq)])

    peer = lax.ppermute(item_embedding_table, "dp", [(0, 1), (1, 0)])
    far_ids = swap(candidate_item_index, seq // 2)
    scale = head_score_scale.reshape(1, heads)
    stored = item_stored_row.reshape(-1, LANES)
    ids = jnp.concatenate([candidate_item_index, far_ids], axis=0)
    ids = jnp.pad(ids, ((0, 0), (0, 64 - owned)))
    id_rows = jnp.concatenate([ids // LANES, ids % LANES], axis=1).astype(f32)
    decay = log_head_retention.reshape(heads, n)

    part, slot, crow, ccol, ctl, key_w = call(
        own_rows_kernel, "own_rows",
        [
            history_item_index, stored, decay, item_embedding_table,
            history_query_key_value_weight,
        ],
        [
            shape((n, width), bf16), shape((1, n), f32), shape((n // CHUNK, heads, CHUNK), f32),
            shape((n, 2 * heads), f32), shape((n // CHUNK * pairs, LANES), f32),
            shape((width, width), bf16),
        ],
        [
            pltpu.VMEM((1, n), i32), pltpu.VMEM(stored.shape, i32), pltpu.VMEM((heads, n), f32),
            pltpu.VMEM((half, width), bf16), pltpu.VMEM((width, width), bf16),
            pltpu.SemaphoreType.DMA((6,)),
        ],
        space=HBM,
        flops=2 * n * half * width,
    )
    emb, key, val, enter, pay, here = call(
        summary_kernel, "summary",
        [part, peer, slot, crow, ctl, id_rows, key_w, history_query_key_value_weight],
        [
            shape((n, width), bf16), shape((width, n), bf16), shape((n, width), bf16),
            shape((n // CHUNK, rows, LANES), f32), shape((state_rows(pairs, 2), LANES), bf16),
            shape((8, LANES), i32),
        ],
        scalars=[user_history_length],
        flops=2 * n * half * width,
    )

    def local(first, name, after):
        return call(
            lambda *refs: local_kernel(first, *refs), name,
            [emb, key, val, crow, ccol, history_query_key_value_weight],
            [shape((n, width // 2), bf16), shape((n, width // 2), f32)],
            after=after, flops=2 * n * half * width // 2,
        )

    early = [local(0, "local_a", [])]
    prefix = logs = None
    for bit in range(bits - 1):
        got = swap(pay, 1 << bit)
        if bit == 1:
            early.append(local(width // 2, "local_b", [prefix]))
        count = 2 << bit
        final = bit == bits - 2
        pay, prefix, logs, *every = call(
            lambda *refs, bit=bit, count=count: join_kernel(bit, count, pairs, *refs), "join",
            [pay, got] + ([prefix, logs] if bit else []),
            [
                shape((state_rows(pairs, 1 if final else 2 * count), LANES), bf16),
                shape((rows, LANES), f32), shape((pairs, LANES), f32),
            ] + [shape((2 * count, LANES), f32)] * final,
            after=[early[-1][1]],
        )
    got = swap(pay, 1 << (bits - 1))
    order = [t + 4 * reversed_bits(k, bits - 2) for t in range(4) for k in range(seq // 4)]
    order = [2 * (j % (seq // 2)) + j // (seq // 2) for j in order]
    work = cands * 2 * half * width
    val_w, *quarters = call(
        lambda *refs: candidate_kernel(order, owned, *refs), "candidates",
        [
            every[0], stored, item_embedding_table, peer, candidate_query_weight,
            candidate_key_value_weight,
        ],
        [shape((width, width), bf16)] + [shape((width, LANES), bf16)] * 4, flops=2 * work,
    )
    (query_a, intra_a), (query_b, intra_b) = early
    buffers = [pltpu.VMEM((n, 2 * LANES), f32)] * 2
    message = width + log_pad(heads)
    hist, key_two, val_two, pay, pay_b = call(
        lambda *refs: finish_kernel(bits - 1, *refs), "finish",
        [
            here, scale, emb, query_a, query_b, intra_a, intra_b, enter, ctl, got, prefix, logs,
            history_output_weight, candidate_key_value_weight, val_w, quarters[3], quarters[2],
        ],
        [
            shape((n, width), f32), shape((n, width), bf16), shape((width, n), bf16),
            shape((message, LANES), bf16), shape((message, LANES), bf16),
        ],
        [pltpu.VMEM((n, width), f32), pltpu.SemaphoreType.DMA((n // CHUNK,))] + buffers,
        spaces=[ANY, VMEM, VMEM, VMEM, VMEM],
        flops=2 * n * half * width,
    )
    gots = [swap(pay, 3), swap(pay_b, 2)]
    (pay,) = call(
        send_kernel, "send", [here, scale, quarters[1], key_two, val_two],
        [shape((message, LANES), bf16)], buffers, after=[pay, pay_b], flops=20 * work,
    )
    gots.append(swap(pay, 1))
    mean, logs = call(
        keep_kernel, "keep", [here, scale, quarters[0], key_two, val_two],
        [shape((width, LANES), f32), shape((heads, LANES), f32)], buffers, after=[pay], flops=8 * work,
    )
    cols = LANES
    for bit in range(2, bits):
        cols //= 2
        packed = 2 * cols == LANES
        mean, logs, pay = call(
            fold_kernel, "fold", [mean, logs, *gots],
            [
                shape((width, cols), f32), shape((heads, cols), f32),
                shape((message // 2, LANES) if packed else (message, cols), bf16),
            ],
        )
        if packed and bit < bits - 1:
            pay = jnp.concatenate([pay[:, :cols], pay[:, cols:]], axis=0)
        gots = [swap(pay, 1 << bit)]
    (cand_out,) = call(
        last_kernel, "last", [mean, logs, *gots, candidate_output_weight],
        [shape((owned, width), f32)],
    )
    return hist[None], cand_out[None]


def solution(mesh):
    in_specs = (
        P(("groups", "dp"), "seq"),
        P(("groups", "dp"), None, "seq"),
        P(("groups", "dp")),
        P(("groups", "dp"), "seq"),
        P(),
        P("dp", None),
        P(),
        P(),
        P(),
        P(),
        P(),
        P(),
    )
    out_specs = (P(("groups", "dp"), "seq", None), P(("groups", "dp"), "seq", None))
    return jax.shard_map(shards, mesh=mesh, in_specs=in_specs, out_specs=out_specs, check_vma=False)
```

```python
import math

import jax
import jax.numpy as jnp
from jax import lax
from jax.experimental import pallas as pl
from jax.experimental.pallas import tpu as pltpu
from jax.sharding import PartitionSpec as P

f32, bf16, i32 = jnp.float32, jnp.bfloat16, jnp.int32
CHUNK = 256
KEYS = 512
LANES = 128
LOG2E = math.log2(math.e)
DEAD = -1e30
VMEM_LIMIT = 40 << 20


def dot(a, b):
    return jnp.dot(a, b, preferred_element_type=f32)


def contract(a, b, left, right):
    return lax.dot_general(a, b, (((left,), (right,)), ((), ())), preferred_element_type=f32)


def iota(shape, axis):
    return lax.broadcasted_iota(i32, shape, axis)


def thirds(value):
    high = value.astype(bf16).astype(f32)
    rest = value - high
    mid = rest.astype(bf16).astype(f32)
    return high, mid, rest - mid


def first_half(shape):
    return iota(shape, len(shape) - 1) % LANES < LANES // 2


def half_masks():
    low = first_half((1, LANES))
    return jnp.where(low, 1.0, 0.0).astype(bf16), jnp.where(low, 0.0, 1.0).astype(bf16)


def same_head():
    dims = (2 * LANES, 2 * LANES)
    return jnp.where(iota(dims, 0) // 64 == iota(dims, 1) // 64, 1.0, 0.0).astype(bf16)


def head_means(value, ones):
    square = (value * value).astype(bf16)
    step = ones.shape[0]
    parts = [dot(square[:, c : c + step], ones) for c in range(0, value.shape[1], step)]
    return jnp.concatenate(parts, axis=1) * (1.0 / 64.0)


def head_spread(heads, first, count):
    dims = (2 * heads, 64 * count)
    return jnp.where(iota(dims, 1) // 64 + first == iota(dims, 0) % heads, 1.0, 0.0).astype(bf16)


def spread(value, matrix):
    heads = value.shape[1] // 2
    high = value.astype(bf16).astype(f32)
    both = jnp.where(iota(value.shape, 1) < heads, high, value - high)
    return dot(both.astype(bf16), matrix)


def stored_slots(ids, stored):
    groups = stored.shape[0]
    n = ids.shape[1]
    pick = jnp.where(iota((groups, n), 0) == ids // LANES, 1.0, 0.0).astype(bf16)
    high = contract((stored // 64).astype(f32).astype(bf16), pick, 0, 0)
    low = contract((stored % 64).astype(f32).astype(bf16), pick, 0, 0)
    rows = jnp.where(iota((LANES, n), 0) == ids % LANES, high * 64.0 + low, 0.0)
    return jnp.sum(rows, axis=0, keepdims=True)


def picked_rows(slots, first, table):
    count = table.shape[0]
    hot = jnp.where(iota((count, slots.shape[1]), 0) == slots.astype(i32) - first, 1.0, 0.0)
    return contract(hot.astype(bf16), table[...], 0, 0)


def chunk(i):
    return slice(i * CHUNK, (i + 1) * CHUNK)


def pair_cut(p):
    return slice(p * LANES, (p + 1) * LANES)


def own_rows_kernel(
    ids_in, stored_in, decay_in, own_in, weight_in, part_o, slot_o, crow_o, ccol_o, ctl_o, key_w_o,
    ids, stored, decay, own, key_w, sem,
):
    n, half, heads = ids.shape[1], own.shape[0], decay.shape[0]
    width = own.shape[1]
    middle = weight_in.at[:, width : 2 * width]
    copies = [
        pltpu.make_async_copy(source, target, sem.at[k])
        for k, (source, target) in enumerate(
            (
                (ids_in, ids), (stored_in, stored), (decay_in, decay),
                (middle, key_w), (own_in, own),
            )
        )
    ]
    for copy in copies:
        copy.start()
    copies[0].wait()
    copies[1].wait()
    slots = stored_slots(ids[...], stored[...])
    slot_o[...] = slots
    copies[2].wait()
    upto = jnp.where(
        iota((CHUNK, CHUNK), 0) <= iota((CHUNK, CHUNK), 1), 1.0, 0.0
    ).astype(bf16)
    low = first_half((1, LANES))
    for i in range(n // CHUNK):
        pieces = jnp.concatenate(thirds(decay[:, chunk(i)]), axis=0)
        sums = dot(pieces.astype(bf16), upto)
        cum = sums[:heads] + sums[heads : 2 * heads] + sums[2 * heads :]
        crow_o[i] = cum
        ccol_o[chunk(i), :] = jnp.transpose(jnp.concatenate([cum, cum], axis=0))
        for p in range(heads // 2):
            r = i * (heads // 2) + p
            ctl_o[r : r + 1, :] = jnp.where(
                low, cum[2 * p : 2 * p + 1, CHUNK - 1 :], cum[2 * p + 1 : 2 * p + 2, CHUNK - 1 :]
            )
    copies[3].wait()
    key_w_o[...] = jnp.transpose(key_w[...].astype(f32)).astype(bf16)
    first = lax.axis_index("dp") * half
    copies[4].wait()
    for i in range(n // CHUNK):
        part_o[chunk(i), :] = picked_rows(slots[:, chunk(i)], first, own).astype(bf16)


def summary_kernel(
    length, part, peer, slot, crow, ctl, id_rows, key_w, weight,
    emb_o, key_o, val_o, enter_o, pay_o, here_o,
):
    n, width = part.shape
    half, heads = peer.shape[0], crow.shape[1]
    pairs = heads // 2
    block = LANES // 2
    low = first_half((1, LANES))
    chunks = n // CHUNK
    here = length[0] - lax.axis_index("seq") * n
    here_o[...] = jnp.full(here_o.shape, here, i32)

    def project(i):
        other = picked_rows(slot[:, chunk(i)], (1 - lax.axis_index("dp")) * half, peer)
        emb = (part[chunk(i), :].astype(f32) + other).astype(bf16)
        emb_o[chunk(i), :] = emb
        return contract(key_w[...], emb, 1, 1), dot(emb, weight[:, 2 * width :])

    total = [jnp.zeros((block, LANES), f32)] * pairs
    ready = project(0)
    for i in range(chunks):
        key, val = ready
        if i + 1 < chunks:
            ready = project(i + 1)
        val = jnp.where(iota((CHUNK, 1), 0) < here - i * CHUNK, val, 0.0).astype(bf16)
        val_o[chunk(i), :] = val
        alive = iota((1, CHUNK), 1) < here - i * CHUNK
        cum = crow[i]
        tail = jnp.exp(cum[:, CHUNK - 1 :] - cum)
        for p in range(pairs):
            keyed = []
            for h in (2 * p, 2 * p + 1):
                rows = key[h * 64 : (h + 1) * 64]
                mean = jnp.sum(rows * rows, axis=0, keepdims=True) * (1.0 / 64.0)
                unit = jnp.where(alive, lax.rsqrt(mean + 1e-06) * 0.125, 0.0)
                normed = rows * unit
                key_o[h * 64 : (h + 1) * 64, chunk(i)] = normed.astype(bf16)
                keyed.append(normed * tail[h : h + 1])
            keyed = jnp.concatenate(keyed, axis=0).astype(bf16)
            both = dot(keyed, val[:, pair_cut(p)])
            fresh = jnp.where(low, both[:block], both[block:])
            enter_o[i, p * block : (p + 1) * block, :] = total[p]
            total[p] = total[p] * jnp.exp(ctl[i * pairs + p : i * pairs + p + 1, :]) + fresh
    logs = ctl[0:pairs, :]
    for i in range(1, chunks):
        logs = logs + ctl[i * pairs : (i + 1) * pairs, :]
    pay_o[...] = pack_state(jnp.concatenate(total, axis=0), logs, id_rows[...])


def state_rows(pairs, ids):
    return pairs * 64 + -(-(3 * pairs + ids) // 16) * 16


def pack_state(state, logs, id_rows):
    pairs, ids = logs.shape[0], id_rows.shape[0]
    pad = state_rows(pairs, ids) - state.shape[0] - 3 * pairs - ids
    parts = [state, *thirds(logs), id_rows] + [jnp.zeros((pad, LANES), f32)] * (pad > 0)
    return jnp.concatenate(parts, axis=0).astype(bf16)


def unpack_state(packed, pairs):
    whole = packed.astype(f32)
    rows = pairs * 64
    logs = whole[rows : rows + pairs]
    for k in (1, 2):
        logs = logs + whole[rows + k * pairs : rows + (k + 1) * pairs]
    return whole[:rows], logs, whole[rows + 3 * pairs :]


def row_factors(logs):
    factors = jnp.exp(logs)
    return jnp.concatenate(
        [jnp.broadcast_to(factors[p : p + 1], (64, LANES)) for p in range(logs.shape[0])], axis=0
    )


def join_kernel(bit, ids, pairs, mine, got, *refs):
    before = refs[: 2 if bit else 0]
    pay_o, prefix_o, logs_o, *ids_o = refs[len(before) :]
    upper = (lax.axis_index("seq") >> bit) & 1 == 1
    state, logs, rows = unpack_state(mine[...], pairs)
    other, other_logs, other_rows = unpack_state(got[...], pairs)
    early = jnp.where(upper, other, state)
    late = jnp.where(upper, state, other)
    factor = row_factors(jnp.where(upper, logs, other_logs))
    id_rows = jnp.concatenate([rows[:ids], other_rows[:ids]], axis=0)
    if ids_o:
        ids_o[0][...] = id_rows
    sent = id_rows[:1] if ids_o else id_rows
    pay_o[...] = pack_state(early * factor + late, logs + other_logs, sent)
    if bit == 0:
        prefix_o[...] = jnp.where(upper, other, 0.0)
        logs_o[...] = jnp.where(upper, other_logs, 0.0)
    else:
        prefix, prefix_logs = before[0][...], before[1][...]
        prefix_o[...] = jnp.where(upper, prefix + row_factors(prefix_logs) * other, prefix)
        logs_o[...] = jnp.where(upper, prefix_logs + other_logs, prefix_logs)


def local_kernel(first, emb, key, val, crow, ccol, weight, query_o, intra_o):
    n, width = query_o.shape
    heads = ccol.shape[1] // 2
    ones, lanes = same_head(), head_spread(heads, first // 64, width // 64)
    mask_a, mask_b = half_masks()
    causal = iota((CHUNK, CHUNK), 0) >= iota((CHUNK, CHUNK), 1)

    def queries(i):
        query = dot(emb[chunk(i), :], weight[:, first : first + width])
        unit = lax.rsqrt(head_means(query, ones) + 1e-06) * 0.125
        query = query * unit
        decayed = query * spread(jnp.exp(ccol[chunk(i), :]), lanes)
        query_o[chunk(i), :] = decayed.astype(bf16)
        return query.astype(bf16)

    def scores(i, p, b, query):
        cut = pair_cut(p)
        wide = slice(first + p * LANES, first + (p + 1) * LANES)
        return dot(query[:, cut] * (mask_b if b else mask_a), key[wide, chunk(i)])

    units = [(i, p, b) for i in range(n // CHUNK) for p in range(width // LANES) for b in (0, 1)]
    query = {0: queries(0)}
    ready = scores(*units[0], query[0])
    held = None
    for u, (i, p, b) in enumerate(units):
        current = ready
        if u + 1 < len(units):
            j = units[u + 1][0]
            if j not in query:
                query[j] = queries(j)
            ready = scores(*units[u + 1], query[j])
        h = first // 64 + 2 * p + b
        gap = ccol[chunk(i), h : h + 1] - crow[i, h : h + 1, :]
        weights = jnp.where(causal, current * jnp.exp(gap), 0.0).astype(bf16)
        wide = slice(first + p * LANES, first + (p + 1) * LANES)
        part = dot(weights, val[chunk(i), wide] * (mask_b if b else mask_a))
        if b == 0:
            held = part
        else:
            intra_o[chunk(i), pair_cut(p)] = held + part


def candidate_kernel(
    orders, owned, id_rows, stored, own, peer, query_w, pair_w, val_w_o, *quarters
):
    half, width = own.shape
    ids = id_rows[...]
    ids = (ids * float(LANES) + pltpu.roll(ids, LANES // 2, 1)).astype(i32)
    step = LANES // owned
    dp = lax.axis_index("dp")
    for start in range(0, len(orders[0]), 2 * step):
        tiles = []
        for first in (start, start + step):
            tile = None
            for k in range(step):
                one, two = (order[first + k] for order in orders)
                row = jnp.where(dp == 0, ids[one : one + 1], ids[two : two + 1])
                slots = stored_slots(row, stored[...])
                if k:
                    moved = pltpu.roll(slots, k * owned, 1)
                    slots = jnp.where(iota((1, LANES), 1) >= k * owned, moved, tile)
                tile = slots
            tiles.append(tile)
        slots = jnp.concatenate(tiles, axis=1)
        found = picked_rows(slots, dp * half, own) + picked_rows(slots, (1 - dp) * half, peer)
        query = jnp.transpose(dot(found.astype(bf16), query_w[...])).astype(bf16)
        for k in (0, 1):
            quarters[start // step + k][...] = query[:, pair_cut(k)]
    val_w_o[...] = jnp.transpose(pair_w[:, width:].astype(f32)).astype(bf16)


def attend(alive_count, scale, queries, key, val, buffers, emit):
    n, width = key.shape
    blocks = range(0, n, KEYS)
    ones = jnp.ones((16, KEYS), bf16)
    heads = width // 64
    if len(queries) == 1:
        units = [[(h, 0), (h + 1, 0)] for h in range(0, heads, 2)]
    else:
        units = [[(h, 0), (h, 1)] for h in range(heads)]

    def weights_of(unit):
        parts = []
        for h, k in unit:
            rows = queries[k][h * 64 : (h + 1) * 64, :]
            zero = jnp.zeros_like(rows)
            parts.append(jnp.concatenate([zero, rows] if h % 2 else [rows, zero], axis=0))
        return jnp.concatenate(parts, axis=1)

    def store(u, block, weights, peak):
        values = dot(key[block : block + KEYS, pair_cut(units[u][0][0] // 2)], weights)
        values = jnp.where(iota((KEYS, 1), 0) < alive_count - block, values, DEAD)
        buffers[u % 2][block : block + KEYS, :] = values
        top = jnp.max(values.reshape(KEYS // 8, 8, 2 * LANES), axis=0)
        return top if peak is None else jnp.maximum(peak, top)

    peak, weights = None, weights_of(units[0])
    for block in blocks:
        peak = store(0, block, weights, peak)
    for u, unit in enumerate(units):
        factor = [jnp.broadcast_to(scale[0:1, h : h + 1], (1, LANES)) for h, _ in unit]
        factor = jnp.concatenate(factor, axis=1) * LOG2E
        first = unit[0][0] * 64
        rows = (unit[-1][0] + 1) * 64 - first
        peak = jnp.max(peak, axis=0, keepdims=True)
        following = sums = None
        more = u + 1 < len(units)
        if more:
            weights = weights_of(units[u + 1])
        for block in blocks:
            if more:
                following = store(u + 1, block, weights, following)
            gap = buffers[u % 2][block : block + KEYS, :] - peak
            probs = jnp.exp2(gap * factor).astype(bf16)
            side = [val[first : first + rows, block : block + KEYS], ones]
            part = dot(jnp.concatenate(side, axis=0), probs)
            sums = part if sums is None else sums + part
        total = sums[rows : rows + 1]
        logs = live(alive_count, peak * factor + jnp.log2(total))
        for b, (h, k) in enumerate(unit):
            top = h * 64 - first
            mean = sums[top : top + 64, pair_cut(b)] / total[:, pair_cut(b)]
            emit(h, k, mean, logs[:, pair_cut(b)])
        peak = following


def finish_kernel(
    bit, here, scale, emb, query_a, query_b, intra_a, intra_b, enter, ctl, got, prefix, prefix_logs,
    out_w, pair_w, val_w, cand_a, cand_b,
    hist_o, key_o, val_o, pay_a, pay_b, shown, sem, *buffers,
):
    n, width = emb.shape
    pairs = width // LANES
    ones = same_head()
    upper = (lax.axis_index("seq") >> bit) & 1 == 1
    state = unpack_state(got[...], pairs)[0]
    before, before_logs = prefix[...], prefix_logs[...]
    entering = jnp.where(upper, before + row_factors(before_logs) * state, before)
    lane = iota((1, 2 * LANES), 1) // 64
    chunks = n // CHUNK
    gone = [jnp.zeros((pairs, LANES), f32)]
    for i in range(chunks - 1):
        gone.append(gone[-1] + ctl[i * pairs : (i + 1) * pairs, :])

    def normed(i):
        states = enter[i] + row_factors(gone[i]) * entering
        parts = []
        for p in range(0, pairs, 2):
            wide = jnp.concatenate(
                [states[p * 64 : (p + 1) * 64], states[(p + 1) * 64 : (p + 2) * 64]], axis=1
            )
            matrix = jnp.concatenate([jnp.where(lane == k, wide, 0.0) for k in range(4)], axis=0)
            query, intra = (query_a, intra_a) if p < pairs // 2 else (query_b, intra_b)
            c = (p % (pairs // 2)) * LANES
            cut = slice(c, c + 2 * LANES)
            parts.append(dot(query[chunk(i), cut], matrix.astype(bf16)) + intra[chunk(i), cut])
        mixed = jnp.concatenate(parts, axis=1)
        return (mixed * lax.rsqrt(head_means(mixed, ones) + 1e-05)).astype(bf16)

    alive_count = here[0:1, 0:1]
    copies = [
        pltpu.make_async_copy(shown.at[chunk(i), :], hist_o.at[chunk(i), :], sem.at[i])
        for i in range(chunks)
    ]
    ready = normed(0)
    for i in range(chunks):
        current = ready
        if i + 1 < chunks:
            ready = normed(i + 1)
        hidden_sum = emb[chunk(i), :].astype(f32) + dot(current, out_w[...])
        alive = iota((CHUNK, 1), 0) < alive_count - i * CHUNK
        shown[chunk(i), :] = jnp.where(alive, hidden_sum, 0.0)
        copies[i].start()
        hidden = hidden_sum.astype(bf16)
        key_o[chunk(i), :] = dot(hidden, pair_w[:, :width]).astype(bf16)
        val_o[:, chunk(i)] = contract(val_w[...], hidden, 1, 1).astype(bf16)
    send_part(alive_count, scale, (cand_a, cand_b), key_o, val_o, (pay_a, pay_b), buffers)
    for copy in copies:
        copy.wait()


def send_part(alive_count, scale, queries, key, val, pays, buffers):
    log_rows = [[] for _ in pays]

    def emit(h, k, mean, logs):
        pays[k][h * 64 : (h + 1) * 64, :] = mean.astype(bf16)
        log_rows[k].append(logs)

    attend(alive_count, scale, queries, key, val, buffers, emit)
    for pay, rows in zip(pays, log_rows):
        pay[val.shape[0] :, :] = pack_logs(jnp.concatenate(rows, axis=0))


def send_kernel(here, scale, query, key, val, pay_o, *buffers):
    send_part(here[0:1, 0:1], scale, (query,), key, val, (pay_o,), buffers)


def live(alive_count, logs):
    return jnp.where(jnp.broadcast_to(alive_count, logs.shape) > 0, logs, DEAD)


def pack_logs(logs):
    heads, cols = logs.shape
    return jnp.concatenate(
        [*thirds(logs), jnp.zeros((log_pad(heads) - 3 * heads, cols), f32)], axis=0
    ).astype(bf16)


def log_pad(heads):
    return -(-3 * heads // 16) * 16


def unpack_logs(rows, heads):
    rows = rows.astype(f32)
    return rows[:heads] + rows[heads : 2 * heads] + rows[2 * heads : 3 * heads]


def keep_kernel(here, scale, query, key, val, mean_o, logs_o, *buffers):
    def emit(h, k, mean, logs):
        mean_o[h * 64 : (h + 1) * 64, :] = mean
        logs_o[h : h + 1, :] = logs

    attend(here[0:1, 0:1], scale, (query,), key, val, buffers, emit)


def over_heads(rows):
    return jnp.concatenate(
        [jnp.broadcast_to(rows[h : h + 1], (64, rows.shape[1])) for h in range(rows.shape[0])],
        axis=0,
    )


def merge(parts):
    peak = parts[0][1]
    for _, logs in parts[1:]:
        peak = jnp.maximum(peak, logs)
    shares = [jnp.exp2(logs - peak) for _, logs in parts]
    total = sum(shares[1:], shares[0])
    mean = None
    for (value, _), share in zip(parts, shares):
        term = value * over_heads(share / total)
        mean = term if mean is None else mean + term
    return mean, peak + jnp.log2(total)


def received(got, heads):
    value = got[...].astype(f32)
    if value.shape[0] < heads * 64:
        value = jnp.concatenate([value, pltpu.roll(value, LANES // 2, 1)], axis=0)
    return value[: heads * 64], unpack_logs(value[heads * 64 :], heads)


def fold_kernel(mean, logs, *refs):
    gots, (mean_o, logs_o, pay_o) = refs[:-3], refs[-3:]
    heads, keep = logs_o.shape
    parts = [(mean[...], logs[...])] + [received(got, heads) for got in gots]
    new_mean, new_logs = merge(parts)
    mean_o[...] = new_mean[:, :keep]
    logs_o[...] = new_logs[:, :keep]
    whole = jnp.concatenate([new_mean, pack_logs(new_logs).astype(f32)], axis=0)
    if 2 * keep == LANES:
        half = whole.shape[0] // 2
        top = pltpu.roll(whole[:half], keep, 1)
        pay_o[...] = jnp.where(first_half((1, LANES)), top, whole[half:]).astype(bf16)
    else:
        pay_o[...] = whole[:, keep:].astype(bf16)


def last_kernel(mean, logs, got, out_w, cand_o):
    heads, cols = logs.shape
    other_mean, other_logs = received(got, heads)
    parts = [(mean[...], logs[...]), (other_mean[:, :cols], other_logs[:, :cols])]
    attended = merge(parts)[0].astype(bf16)
    cand_o[...] = contract(attended, out_w[...], 0, 0)


def shape(dims, dtype):
    return jax.ShapeDtypeStruct(dims, dtype)


VMEM = pl.BlockSpec(memory_space=pltpu.VMEM)
SMEM = pl.BlockSpec(memory_space=pltpu.SMEM)
ANY = pl.BlockSpec(memory_space=pl.ANY)
HBM = pl.BlockSpec(memory_space=pltpu.HBM)


def call(kernel, name, operands, outs, scratch=(), after=(), flops=0, space=VMEM, spaces=None, scalars=()):
    count = len(scalars) + len(operands)
    if space is HBM:
        operands = [pltpu.with_memory_space_constraint(value, pltpu.HBM) for value in operands]

    def body(*refs):
        kernel(*refs[:count], *refs[count + len(after) :])

    return pl.pallas_call(
        body,
        name=name,
        in_specs=[SMEM] * len(scalars) + [space] * len(operands) + [ANY] * len(after),
        out_specs=spaces or [VMEM] * len(outs),
        out_shape=outs,
        scratch_shapes=list(scratch),
        compiler_params=pltpu.CompilerParams(vmem_limit_bytes=VMEM_LIMIT),
        cost_estimate=pl.CostEstimate(flops=flops, transcendentals=0, bytes_accessed=0),
    )(*scalars, *operands, *after)


def reversed_bits(value, bits):
    return sum(((value >> b) & 1) << (bits - 1 - b) for b in range(bits))


def shards(
    history_item_index,
    log_head_retention,
    user_history_length,
    candidate_item_index,
    item_stored_row,
    item_embedding_table,
    head_score_scale,
    history_query_key_value_weight,
    history_output_weight,
    candidate_key_value_weight,
    candidate_query_weight,
    candidate_output_weight,
):
    users, n = history_item_index.shape
    heads = log_head_retention.shape[1]
    half, width = item_embedding_table.shape
    owned = candidate_item_index.shape[1]
    seq = lax.axis_size("seq")
    bits = seq.bit_length() - 1
    cands = owned * seq
    assert users == 1 and lax.axis_size("dp") == 2 and seq == 1 << bits and bits > 2
    assert width == heads * 64 and heads % 4 == 0 and LANES % owned == 0 and owned <= 64
    assert cands == 4 * LANES
    pairs = heads // 2
    rows = pairs * 64

    def swap(value, mask):
        return lax.ppermute(value, "seq", [(j, j ^ mask) for j in range(seq)])

    def swap_by_core(value, masks):
        pairs = [
            (2 * j + core, 2 * (j ^ mask) + core) for j in range(seq) for core, mask in enumerate(masks)
        ]
        return lax.ppermute(value, ("seq", "dp"), pairs)

    peer = lax.ppermute(item_embedding_table, "dp", [(0, 1), (1, 0)])
    far_ids = swap(candidate_item_index, seq // 2)
    scale = head_score_scale.reshape(1, heads)
    stored = item_stored_row.reshape(-1, LANES)
    ids = jnp.concatenate([candidate_item_index, far_ids], axis=0)
    ids = jnp.pad(ids, ((0, 0), (0, 64 - owned)))
    id_rows = jnp.concatenate([ids // LANES, ids % LANES], axis=1).astype(f32)
    decay = log_head_retention.reshape(heads, n)

    part, slot, crow, ccol, ctl, key_w = call(
        own_rows_kernel, "own_rows",
        [
            history_item_index, stored, decay, item_embedding_table,
            history_query_key_value_weight,
        ],
        [
            shape((n, width), bf16), shape((1, n), f32), shape((n // CHUNK, heads, CHUNK), f32),
            shape((n, 2 * heads), f32), shape((n // CHUNK * pairs, LANES), f32),
            shape((width, width), bf16),
        ],
        [
            pltpu.VMEM((1, n), i32), pltpu.VMEM(stored.shape, i32), pltpu.VMEM((heads, n), f32),
            pltpu.VMEM((half, width), bf16), pltpu.VMEM((width, width), bf16),
            pltpu.SemaphoreType.DMA((6,)),
        ],
        space=HBM,
        flops=2 * n * half * width,
    )
    emb, key, val, enter, pay, here = call(
        summary_kernel, "summary",
        [part, peer, slot, crow, ctl, id_rows, key_w, history_query_key_value_weight],
        [
            shape((n, width), bf16), shape((width, n), bf16), shape((n, width), bf16),
            shape((n // CHUNK, rows, LANES), f32), shape((state_rows(pairs, 2), LANES), bf16),
            shape((8, LANES), i32),
        ],
        scalars=[user_history_length],
        flops=2 * n * half * width,
    )

    def local(first, name, after):
        return call(
            lambda *refs: local_kernel(first, *refs), name,
            [emb, key, val, crow, ccol, history_query_key_value_weight],
            [shape((n, width // 2), bf16), shape((n, width // 2), f32)],
            after=after, flops=2 * n * half * width // 2,
        )

    early = [local(0, "local_a", [])]
    prefix = logs = None
    for bit in range(bits - 1):
        got = swap(pay, 1 << bit)
        if bit == 1:
            early.append(local(width // 2, "local_b", [prefix]))
        count = 2 << bit
        final = bit == bits - 2
        pay, prefix, logs, *every = call(
            lambda *refs, bit=bit, count=count: join_kernel(bit, count, pairs, *refs), "join",
            [pay, got] + ([prefix, logs] if bit else []),
            [
                shape((state_rows(pairs, 1 if final else 2 * count), LANES), bf16),
                shape((rows, LANES), f32), shape((pairs, LANES), f32),
            ] + [shape((2 * count, LANES), f32)] * final,
            after=[early[-1][1]],
        )
    got = swap(pay, 1 << (bits - 1))
    orders = []
    for turn in ((0, 1, 2, 3), (0, 2, 1, 3)):
        order = [t + 4 * reversed_bits(k, bits - 2) for t in turn for k in range(seq // 4)]
        orders.append([2 * (j % (seq // 2)) + j // (seq // 2) for j in order])
    work = cands * 2 * half * width
    val_w, *quarters = call(
        lambda *refs: candidate_kernel(orders, owned, *refs), "candidates",
        [
            every[0], stored, item_embedding_table, peer, candidate_query_weight,
            candidate_key_value_weight,
        ],
        [shape((width, width), bf16)] + [shape((width, LANES), bf16)] * 4, flops=2 * work,
    )
    (query_a, intra_a), (query_b, intra_b) = early
    buffers = [pltpu.VMEM((n, 2 * LANES), f32)] * 2
    message = width + log_pad(heads)
    hist, key_two, val_two, pay, pay_b = call(
        lambda *refs: finish_kernel(bits - 1, *refs), "finish",
        [
            here, scale, emb, query_a, query_b, intra_a, intra_b, enter, ctl, got, prefix, logs,
            history_output_weight, candidate_key_value_weight, val_w, quarters[3], quarters[2],
        ],
        [
            shape((n, width), f32), shape((n, width), bf16), shape((width, n), bf16),
            shape((message, LANES), bf16), shape((message, LANES), bf16),
        ],
        [pltpu.VMEM((n, width), f32), pltpu.SemaphoreType.DMA((n // CHUNK,))] + buffers,
        spaces=[ANY, VMEM, VMEM, VMEM, VMEM],
        flops=2 * n * half * width,
    )
    gots = [swap(pay, 3), swap_by_core(pay_b, (2, 1))]
    (pay,) = call(
        send_kernel, "send", [here, scale, quarters[1], key_two, val_two],
        [shape((message, LANES), bf16)], buffers, after=[pay, pay_b], flops=20 * work,
    )
    gots.append(swap_by_core(pay, (1, 2)))
    mean, logs = call(
        keep_kernel, "keep", [here, scale, quarters[0], key_two, val_two],
        [shape((width, LANES), f32), shape((heads, LANES), f32)], buffers, after=[pay], flops=8 * work,
    )
    cols = LANES
    for bit in range(2, bits):
        cols //= 2
        packed = 2 * cols == LANES
        mean, logs, pay = call(
            fold_kernel, "fold", [mean, logs, *gots],
            [
                shape((width, cols), f32), shape((heads, cols), f32),
                shape((message // 2, LANES) if packed else (message, cols), bf16),
            ],
        )
        if packed and bit < bits - 1:
            pay = jnp.concatenate([pay[:, :cols], pay[:, cols:]], axis=0)
        gots = [swap(pay, 1 << bit)]
    (cand_out,) = call(
        last_kernel, "last", [mean, logs, *gots, candidate_output_weight],
        [shape((owned, width), f32)],
    )
    return hist[None], cand_out[None]


def solution(mesh):
    in_specs = (
        P(("groups", "dp"), "seq"),
        P(("groups", "dp"), None, "seq"),
        P(("groups", "dp")),
        P(("groups", "dp"), "seq"),
        P(),
        P("dp", None),
        P(),
        P(),
        P(),
        P(),
        P(),
        P(),
    )
    out_specs = (P(("groups", "dp"), "seq", None), P(("groups", "dp"), "seq", None))
    return jax.shard_map(shards, mesh=mesh, in_specs=in_specs, out_specs=out_specs, check_vma=False)
```

```python
import math

import jax
import jax.numpy as jnp
from jax import lax
from jax.experimental import pallas as pl
from jax.experimental.pallas import tpu as pltpu
from jax.sharding import PartitionSpec as P

f32, bf16, i32 = jnp.float32, jnp.bfloat16, jnp.int32
CHUNK = 256
KEYS = 512
LANES = 128
LOG2E = math.log2(math.e)
DEAD = -1e30
VMEM_LIMIT = 40 << 20


def dot(a, b):
    return jnp.dot(a, b, preferred_element_type=f32)


def contract(a, b, left, right):
    return lax.dot_general(a, b, (((left,), (right,)), ((), ())), preferred_element_type=f32)


def iota(shape, axis):
    return lax.broadcasted_iota(i32, shape, axis)


def thirds(value):
    high = value.astype(bf16).astype(f32)
    rest = value - high
    mid = rest.astype(bf16).astype(f32)
    return high, mid, rest - mid


def first_half(shape):
    return iota(shape, len(shape) - 1) % LANES < LANES // 2


def half_masks():
    low = first_half((1, LANES))
    return jnp.where(low, 1.0, 0.0).astype(bf16), jnp.where(low, 0.0, 1.0).astype(bf16)


def same_head():
    dims = (2 * LANES, 2 * LANES)
    return jnp.where(iota(dims, 0) // 64 == iota(dims, 1) // 64, 1.0, 0.0).astype(bf16)


def head_means(value, ones):
    square = (value * value).astype(bf16)
    step = ones.shape[0]
    parts = [dot(square[:, c : c + step], ones) for c in range(0, value.shape[1], step)]
    return jnp.concatenate(parts, axis=1) * (1.0 / 64.0)


def head_spread(heads, first, count):
    dims = (2 * heads, 64 * count)
    return jnp.where(iota(dims, 1) // 64 + first == iota(dims, 0) % heads, 1.0, 0.0).astype(bf16)


def spread(value, matrix):
    heads = value.shape[1] // 2
    high = value.astype(bf16).astype(f32)
    both = jnp.where(iota(value.shape, 1) < heads, high, value - high)
    return dot(both.astype(bf16), matrix)


def stored_slots(ids, stored):
    groups = stored.shape[0]
    n = ids.shape[1]
    pick = jnp.where(iota((groups, n), 0) == ids // LANES, 1.0, 0.0).astype(bf16)
    high = contract((stored // 64).astype(f32).astype(bf16), pick, 0, 0)
    low = contract((stored % 64).astype(f32).astype(bf16), pick, 0, 0)
    rows = jnp.where(iota((LANES, n), 0) == ids % LANES, high * 64.0 + low, 0.0)
    return jnp.sum(rows, axis=0, keepdims=True)


def picked_rows(slots, first, table):
    count = table.shape[0]
    hot = jnp.where(iota((count, slots.shape[1]), 0) == slots.astype(i32) - first, 1.0, 0.0)
    return contract(hot.astype(bf16), table[...], 0, 0)


def chunk(i):
    return slice(i * CHUNK, (i + 1) * CHUNK)


def pair_cut(p):
    return slice(p * LANES, (p + 1) * LANES)


def own_rows_kernel(
    ids_in, stored_in, decay_in, own_in, weight_in, part_o, slot_o, crow_o, ccol_o, ctl_o, key_w_o,
    ids, stored, decay, own, key_w, sem,
):
    n, half, heads = ids.shape[1], own.shape[0], decay.shape[0]
    width = own.shape[1]
    middle = weight_in.at[:, width : 2 * width]
    copies = [
        pltpu.make_async_copy(source, target, sem.at[k])
        for k, (source, target) in enumerate(
            (
                (ids_in, ids), (stored_in, stored), (decay_in, decay),
                (middle, key_w), (own_in, own),
            )
        )
    ]
    for copy in copies:
        copy.start()
    copies[0].wait()
    copies[1].wait()
    slots = stored_slots(ids[...], stored[...])
    slot_o[...] = slots
    copies[2].wait()
    upto = jnp.where(
        iota((CHUNK, CHUNK), 0) <= iota((CHUNK, CHUNK), 1), 1.0, 0.0
    ).astype(bf16)
    low = first_half((1, LANES))
    for i in range(n // CHUNK):
        pieces = jnp.concatenate(thirds(decay[:, chunk(i)]), axis=0)
        sums = dot(pieces.astype(bf16), upto)
        cum = sums[:heads] + sums[heads : 2 * heads] + sums[2 * heads :]
        crow_o[i] = cum
        ccol_o[chunk(i), :] = jnp.transpose(jnp.concatenate([cum, cum], axis=0))
        for p in range(heads // 2):
            r = i * (heads // 2) + p
            ctl_o[r : r + 1, :] = jnp.where(
                low, cum[2 * p : 2 * p + 1, CHUNK - 1 :], cum[2 * p + 1 : 2 * p + 2, CHUNK - 1 :]
            )
    copies[3].wait()
    key_w_o[...] = jnp.transpose(key_w[...].astype(f32)).astype(bf16)
    first = lax.axis_index("dp") * half
    copies[4].wait()
    for i in range(n // CHUNK):
        part_o[chunk(i), :] = picked_rows(slots[:, chunk(i)], first, own).astype(bf16)


def summary_kernel(
    length, part, peer, slot, crow, ctl, id_rows, key_w, weight,
    emb_o, key_o, val_o, enter_o, pay_o, here_o,
):
    n, width = part.shape
    half, heads = peer.shape[0], crow.shape[1]
    pairs = heads // 2
    block = LANES // 2
    low = first_half((1, LANES))
    chunks = n // CHUNK
    here = length[0] - lax.axis_index("seq") * n
    here_o[...] = jnp.full(here_o.shape, here, i32)

    def project(i):
        other = picked_rows(slot[:, chunk(i)], (1 - lax.axis_index("dp")) * half, peer)
        emb = (part[chunk(i), :].astype(f32) + other).astype(bf16)
        emb_o[chunk(i), :] = emb
        return contract(key_w[...], emb, 1, 1), dot(emb, weight[:, 2 * width :])

    total = [jnp.zeros((block, LANES), f32)] * pairs
    ready = project(0)
    for i in range(chunks):
        key, val = ready
        if i + 1 < chunks:
            ready = project(i + 1)
        val = jnp.where(iota((CHUNK, 1), 0) < here - i * CHUNK, val, 0.0).astype(bf16)
        val_o[chunk(i), :] = val
        alive = iota((1, CHUNK), 1) < here - i * CHUNK
        cum = crow[i]
        tail = jnp.exp(cum[:, CHUNK - 1 :] - cum)
        for p in range(pairs):
            keyed = []
            for h in (2 * p, 2 * p + 1):
                rows = key[h * 64 : (h + 1) * 64]
                mean = jnp.sum(rows * rows, axis=0, keepdims=True) * (1.0 / 64.0)
                unit = jnp.where(alive, lax.rsqrt(mean + 1e-06) * 0.125, 0.0)
                normed = rows * unit
                key_o[h * 64 : (h + 1) * 64, chunk(i)] = normed.astype(bf16)
                keyed.append(normed * tail[h : h + 1])
            keyed = jnp.concatenate(keyed, axis=0).astype(bf16)
            both = dot(keyed, val[:, pair_cut(p)])
            fresh = jnp.where(low, both[:block], both[block:])
            enter_o[i, p * block : (p + 1) * block, :] = total[p]
            total[p] = total[p] * jnp.exp(ctl[i * pairs + p : i * pairs + p + 1, :]) + fresh
    logs = ctl[0:pairs, :]
    for i in range(1, chunks):
        logs = logs + ctl[i * pairs : (i + 1) * pairs, :]
    pay_o[...] = pack_state(jnp.concatenate(total, axis=0), logs, id_rows[...])


def state_rows(pairs, ids):
    return pairs * 64 + -(-(3 * pairs + ids) // 16) * 16


def pack_state(state, logs, id_rows):
    pairs, ids = logs.shape[0], id_rows.shape[0]
    pad = state_rows(pairs, ids) - state.shape[0] - 3 * pairs - ids
    parts = [state, *thirds(logs), id_rows] + [jnp.zeros((pad, LANES), f32)] * (pad > 0)
    return jnp.concatenate(parts, axis=0).astype(bf16)


def unpack_state(packed, pairs):
    whole = packed.astype(f32)
    rows = pairs * 64
    logs = whole[rows : rows + pairs]
    for k in (1, 2):
        logs = logs + whole[rows + k * pairs : rows + (k + 1) * pairs]
    return whole[:rows], logs, whole[rows + 3 * pairs :]


def row_factors(logs):
    factors = jnp.exp(logs)
    return jnp.concatenate(
        [jnp.broadcast_to(factors[p : p + 1], (64, LANES)) for p in range(logs.shape[0])], axis=0
    )


def join_kernel(bit, ids, pairs, mine, got, *refs):
    before = refs[: 2 if bit else 0]
    pay_o, prefix_o, logs_o, *ids_o = refs[len(before) :]
    upper = (lax.axis_index("seq") >> bit) & 1 == 1
    state, logs, rows = unpack_state(mine[...], pairs)
    other, other_logs, other_rows = unpack_state(got[...], pairs)
    early = jnp.where(upper, other, state)
    late = jnp.where(upper, state, other)
    factor = row_factors(jnp.where(upper, logs, other_logs))
    id_rows = jnp.concatenate([rows[:ids], other_rows[:ids]], axis=0)
    if ids_o:
        ids_o[0][...] = id_rows
    sent = id_rows[:1] if ids_o else id_rows
    pay_o[...] = pack_state(early * factor + late, logs + other_logs, sent)
    if bit == 0:
        prefix_o[...] = jnp.where(upper, other, 0.0)
        logs_o[...] = jnp.where(upper, other_logs, 0.0)
    else:
        prefix, prefix_logs = before[0][...], before[1][...]
        prefix_o[...] = jnp.where(upper, prefix + row_factors(prefix_logs) * other, prefix)
        logs_o[...] = jnp.where(upper, prefix_logs + other_logs, prefix_logs)


def local_kernel(first, emb, key, val, crow, ccol, weight, query_o, intra_o):
    n, width = query_o.shape
    heads = ccol.shape[1] // 2
    ones, lanes = same_head(), head_spread(heads, first // 64, width // 64)
    mask_a, mask_b = half_masks()
    causal = iota((CHUNK, CHUNK), 0) >= iota((CHUNK, CHUNK), 1)

    def queries(i):
        query = dot(emb[chunk(i), :], weight[:, first : first + width])
        unit = lax.rsqrt(head_means(query, ones) + 1e-06) * 0.125
        query = query * unit
        decayed = query * spread(jnp.exp(ccol[chunk(i), :]), lanes)
        query_o[chunk(i), :] = decayed.astype(bf16)
        return query.astype(bf16)

    def scores(i, p, b, query):
        cut = pair_cut(p)
        wide = slice(first + p * LANES, first + (p + 1) * LANES)
        return dot(query[:, cut] * (mask_b if b else mask_a), key[wide, chunk(i)])

    units = [(i, p, b) for i in range(n // CHUNK) for p in range(width // LANES) for b in (0, 1)]
    query = {0: queries(0)}
    ready = scores(*units[0], query[0])
    held = None
    for u, (i, p, b) in enumerate(units):
        current = ready
        if u + 1 < len(units):
            j = units[u + 1][0]
            if j not in query:
                query[j] = queries(j)
            ready = scores(*units[u + 1], query[j])
        h = first // 64 + 2 * p + b
        gap = ccol[chunk(i), h : h + 1] - crow[i, h : h + 1, :]
        weights = jnp.where(causal, current * jnp.exp(gap), 0.0).astype(bf16)
        wide = slice(first + p * LANES, first + (p + 1) * LANES)
        part = dot(weights, val[chunk(i), wide] * (mask_b if b else mask_a))
        if b == 0:
            held = part
        else:
            intra_o[chunk(i), pair_cut(p)] = held + part


def candidate_kernel(
    orders, owned, id_rows, stored, own, peer, query_w, pair_w, val_w_o, *quarters
):
    half, width = own.shape
    ids = id_rows[...]
    ids = (ids * float(LANES) + pltpu.roll(ids, LANES // 2, 1)).astype(i32)
    step = LANES // owned
    dp = lax.axis_index("dp")
    for start in range(0, len(orders[0]), 2 * step):
        tiles = []
        for first in (start, start + step):
            tile = None
            for k in range(step):
                one, two = (order[first + k] for order in orders)
                row = jnp.where(dp == 0, ids[one : one + 1], ids[two : two + 1])
                slots = stored_slots(row, stored[...])
                if k:
                    moved = pltpu.roll(slots, k * owned, 1)
                    slots = jnp.where(iota((1, LANES), 1) >= k * owned, moved, tile)
                tile = slots
            tiles.append(tile)
        slots = jnp.concatenate(tiles, axis=1)
        found = picked_rows(slots, dp * half, own) + picked_rows(slots, (1 - dp) * half, peer)
        query = jnp.transpose(dot(found.astype(bf16), query_w[...])).astype(bf16)
        for k in (0, 1):
            quarters[start // step + k][...] = query[:, pair_cut(k)]
    val_w_o[...] = jnp.transpose(pair_w[:, width:].astype(f32)).astype(bf16)


def attend(alive_count, scale, queries, key, val, buffers, emit):
    n, width = key.shape
    blocks = range(0, n, KEYS)
    ones = jnp.ones((16, KEYS), bf16)
    heads = width // 64
    if len(queries) == 1:
        units = [[(h, 0), (h + 1, 0)] for h in range(0, heads, 2)]
    else:
        units = [[(h, 0), (h, 1)] for h in range(heads)]

    def weights_of(unit):
        parts = []
        for h, k in unit:
            rows = queries[k][h * 64 : (h + 1) * 64, :]
            zero = jnp.zeros_like(rows)
            parts.append(jnp.concatenate([zero, rows] if h % 2 else [rows, zero], axis=0))
        return jnp.concatenate(parts, axis=1)

    def store(u, block, weights, peak):
        values = dot(key[block : block + KEYS, pair_cut(units[u][0][0] // 2)], weights)
        values = jnp.where(iota((KEYS, 1), 0) < alive_count - block, values, DEAD)
        buffers[u % 2][block : block + KEYS, :] = values
        top = jnp.max(values.reshape(KEYS // 8, 8, 2 * LANES), axis=0)
        return top if peak is None else jnp.maximum(peak, top)

    peak, weights = None, weights_of(units[0])
    for block in blocks:
        peak = store(0, block, weights, peak)
    for u, unit in enumerate(units):
        factor = [jnp.broadcast_to(scale[0:1, h : h + 1], (1, LANES)) for h, _ in unit]
        factor = jnp.concatenate(factor, axis=1) * LOG2E
        first = unit[0][0] * 64
        rows = (unit[-1][0] + 1) * 64 - first
        peak = jnp.max(peak, axis=0, keepdims=True)
        following = sums = None
        more = u + 1 < len(units)
        if more:
            weights = weights_of(units[u + 1])
        for block in blocks:
            if more:
                following = store(u + 1, block, weights, following)
            gap = buffers[u % 2][block : block + KEYS, :] - peak
            probs = jnp.exp2(gap * factor).astype(bf16)
            side = [val[first : first + rows, block : block + KEYS], ones]
            part = dot(jnp.concatenate(side, axis=0), probs)
            sums = part if sums is None else sums + part
        total = sums[rows : rows + 1]
        logs = live(alive_count, peak * factor + jnp.log2(total))
        for b, (h, k) in enumerate(unit):
            top = h * 64 - first
            mean = sums[top : top + 64, pair_cut(b)] / total[:, pair_cut(b)]
            emit(h, k, mean, logs[:, pair_cut(b)])
        peak = following


def finish_kernel(
    bit, here, scale, emb, query_a, query_b, intra_a, intra_b, enter, ctl, got, prefix, prefix_logs,
    out_w, pair_w, val_w, cand_a, cand_b,
    hist_o, key_o, val_o, pay_a, pay_b, shown, sem, *buffers,
):
    n, width = emb.shape
    pairs = width // LANES
    ones = same_head()
    upper = (lax.axis_index("seq") >> bit) & 1 == 1
    state = unpack_state(got[...], pairs)[0]
    before, before_logs = prefix[...], prefix_logs[...]
    entering = jnp.where(upper, before + row_factors(before_logs) * state, before)
    lane = iota((1, 2 * LANES), 1) // 64
    chunks = n // CHUNK
    gone = [jnp.zeros((pairs, LANES), f32)]
    for i in range(chunks - 1):
        gone.append(gone[-1] + ctl[i * pairs : (i + 1) * pairs, :])

    def normed(i):
        states = enter[i] + row_factors(gone[i]) * entering
        parts = []
        for p in range(0, pairs, 2):
            wide = jnp.concatenate(
                [states[p * 64 : (p + 1) * 64], states[(p + 1) * 64 : (p + 2) * 64]], axis=1
            )
            matrix = jnp.concatenate([jnp.where(lane == k, wide, 0.0) for k in range(4)], axis=0)
            query, intra = (query_a, intra_a) if p < pairs // 2 else (query_b, intra_b)
            c = (p % (pairs // 2)) * LANES
            cut = slice(c, c + 2 * LANES)
            parts.append(dot(query[chunk(i), cut], matrix.astype(bf16)) + intra[chunk(i), cut])
        mixed = jnp.concatenate(parts, axis=1)
        return (mixed * lax.rsqrt(head_means(mixed, ones) + 1e-05)).astype(bf16)

    alive_count = here[0:1, 0:1]
    copies = [
        pltpu.make_async_copy(shown.at[chunk(i), :], hist_o.at[chunk(i), :], sem.at[i])
        for i in range(chunks)
    ]
    ready = normed(0)
    for i in range(chunks):
        current = ready
        if i + 1 < chunks:
            ready = normed(i + 1)
        hidden_sum = emb[chunk(i), :].astype(f32) + dot(current, out_w[...])
        alive = iota((CHUNK, 1), 0) < alive_count - i * CHUNK
        shown[chunk(i), :] = jnp.where(alive, hidden_sum, 0.0)
        copies[i].start()
        hidden = hidden_sum.astype(bf16)
        key_o[chunk(i), :] = dot(hidden, pair_w[:, :width]).astype(bf16)
        val_o[:, chunk(i)] = contract(val_w[...], hidden, 1, 1).astype(bf16)
    send_part(alive_count, scale, (cand_a, cand_b), key_o, val_o, (pay_a, pay_b), buffers)
    for copy in copies:
        copy.wait()


def send_part(alive_count, scale, queries, key, val, pays, buffers):
    log_rows = [[] for _ in pays]

    def emit(h, k, mean, logs):
        pays[k][h * 64 : (h + 1) * 64, :] = mean.astype(bf16)
        log_rows[k].append(logs)

    attend(alive_count, scale, queries, key, val, buffers, emit)
    for pay, rows in zip(pays, log_rows):
        pay[val.shape[0] :, :] = pack_logs(jnp.concatenate(rows, axis=0))


def send_kernel(here, scale, query, key, val, pay_o, *buffers):
    send_part(here[0:1, 0:1], scale, (query,), key, val, (pay_o,), buffers)


def live(alive_count, logs):
    return jnp.where(jnp.broadcast_to(alive_count, logs.shape) > 0, logs, DEAD)


def pack_logs(logs):
    heads, cols = logs.shape
    return jnp.concatenate(
        [*thirds(logs), jnp.zeros((log_pad(heads) - 3 * heads, cols), f32)], axis=0
    ).astype(bf16)


def log_pad(heads):
    return -(-3 * heads // 16) * 16


def unpack_logs(rows, heads):
    rows = rows.astype(f32)
    return rows[:heads] + rows[heads : 2 * heads] + rows[2 * heads : 3 * heads]


def keep_kernel(here, scale, query, key, val, mean_o, logs_o, *buffers):
    def emit(h, k, mean, logs):
        mean_o[h * 64 : (h + 1) * 64, :] = mean
        logs_o[h : h + 1, :] = logs

    attend(here[0:1, 0:1], scale, (query,), key, val, buffers, emit)


def over_heads(rows):
    return jnp.concatenate(
        [jnp.broadcast_to(rows[h : h + 1], (64, rows.shape[1])) for h in range(rows.shape[0])],
        axis=0,
    )


def merge(parts):
    peak = parts[0][1]
    for _, logs in parts[1:]:
        peak = jnp.maximum(peak, logs)
    shares = [jnp.exp2(logs - peak) for _, logs in parts]
    total = sum(shares[1:], shares[0])
    mean = None
    for (value, _), share in zip(parts, shares):
        term = value * over_heads(share / total)
        mean = term if mean is None else mean + term
    return mean, peak + jnp.log2(total)


def received(got, heads):
    value = got[...].astype(f32)
    if value.shape[0] < heads * 64:
        value = jnp.concatenate([value, pltpu.roll(value, LANES // 2, 1)], axis=0)
    return value[: heads * 64], unpack_logs(value[heads * 64 :], heads)


def fold_kernel(mean, logs, *refs):
    gots, (mean_o, logs_o, pay_o) = refs[:-3], refs[-3:]
    heads, keep = logs_o.shape
    parts = [(mean[...], logs[...])] + [received(got, heads) for got in gots]
    new_mean, new_logs = merge(parts)
    mean_o[...] = new_mean[:, :keep]
    logs_o[...] = new_logs[:, :keep]
    whole = jnp.concatenate([new_mean, pack_logs(new_logs).astype(f32)], axis=0)
    if 2 * keep == LANES:
        half = whole.shape[0] // 2
        top = pltpu.roll(whole[:half], keep, 1)
        pay_o[...] = jnp.where(first_half((1, LANES)), top, whole[half:]).astype(bf16)
    else:
        pay_o[...] = whole[:, keep:].astype(bf16)


def last_kernel(mean, logs, got, out_w, cand_o):
    heads, cols = logs.shape
    other_mean, other_logs = received(got, heads)
    parts = [(mean[...], logs[...]), (other_mean[:, :cols], other_logs[:, :cols])]
    attended = merge(parts)[0].astype(bf16)
    cand_o[...] = contract(attended, out_w[...], 0, 0)


def shape(dims, dtype):
    return jax.ShapeDtypeStruct(dims, dtype)


VMEM = pl.BlockSpec(memory_space=pltpu.VMEM)
SMEM = pl.BlockSpec(memory_space=pltpu.SMEM)
ANY = pl.BlockSpec(memory_space=pl.ANY)
HBM = pl.BlockSpec(memory_space=pltpu.HBM)


def call(kernel, name, operands, outs, scratch=(), after=(), flops=0, space=VMEM, spaces=None, scalars=()):
    count = len(scalars) + len(operands)
    if space is HBM:
        operands = [pltpu.with_memory_space_constraint(value, pltpu.HBM) for value in operands]

    def body(*refs):
        kernel(*refs[:count], *refs[count + len(after) :])

    return pl.pallas_call(
        body,
        name=name,
        in_specs=[SMEM] * len(scalars) + [space] * len(operands) + [ANY] * len(after),
        out_specs=spaces or [VMEM] * len(outs),
        out_shape=outs,
        scratch_shapes=list(scratch),
        compiler_params=pltpu.CompilerParams(vmem_limit_bytes=VMEM_LIMIT),
        cost_estimate=pl.CostEstimate(flops=flops, transcendentals=0, bytes_accessed=0),
    )(*scalars, *operands, *after)


def reversed_bits(value, bits):
    return sum(((value >> b) & 1) << (bits - 1 - b) for b in range(bits))


def shards(
    history_item_index,
    log_head_retention,
    user_history_length,
    candidate_item_index,
    item_stored_row,
    item_embedding_table,
    head_score_scale,
    history_query_key_value_weight,
    history_output_weight,
    candidate_key_value_weight,
    candidate_query_weight,
    candidate_output_weight,
):
    users, n = history_item_index.shape
    heads = log_head_retention.shape[1]
    half, width = item_embedding_table.shape
    owned = candidate_item_index.shape[1]
    seq = lax.axis_size("seq")
    bits = seq.bit_length() - 1
    cands = owned * seq
    assert users == 1 and lax.axis_size("dp") == 2 and seq == 1 << bits and bits > 2
    assert width == heads * 64 and heads % 4 == 0 and LANES % owned == 0 and owned <= 64
    assert cands == 4 * LANES
    pairs = heads // 2
    rows = pairs * 64

    def swap(value, mask):
        return lax.ppermute(value, "seq", [(j, j ^ mask) for j in range(seq)])

    def swap_by_core(value, masks):
        pairs = [
            (2 * j + core, 2 * (j ^ mask) + core) for j in range(seq) for core, mask in enumerate(masks)
        ]
        return lax.ppermute(value, ("seq", "dp"), pairs)

    peer = lax.ppermute(item_embedding_table, "dp", [(0, 1), (1, 0)])
    far_ids = swap(candidate_item_index, seq // 2)
    scale = head_score_scale.reshape(1, heads)
    stored = item_stored_row.reshape(-1, LANES)
    ids = jnp.concatenate([candidate_item_index, far_ids], axis=0)
    ids = jnp.pad(ids, ((0, 0), (0, 64 - owned)))
    id_rows = jnp.concatenate([ids // LANES, ids % LANES], axis=1).astype(f32)
    decay = log_head_retention.reshape(heads, n)

    part, slot, crow, ccol, ctl, key_w = call(
        own_rows_kernel, "own_rows",
        [
            history_item_index, stored, decay, item_embedding_table,
            history_query_key_value_weight,
        ],
        [
            shape((n, width), bf16), shape((1, n), f32), shape((n // CHUNK, heads, CHUNK), f32),
            shape((n, 2 * heads), f32), shape((n // CHUNK * pairs, LANES), f32),
            shape((width, width), bf16),
        ],
        [
            pltpu.VMEM((1, n), i32), pltpu.VMEM(stored.shape, i32), pltpu.VMEM((heads, n), f32),
            pltpu.VMEM((half, width), bf16), pltpu.VMEM((width, width), bf16),
            pltpu.SemaphoreType.DMA((6,)),
        ],
        space=HBM,
        flops=2 * n * half * width,
    )
    emb, key, val, enter, pay, here = call(
        summary_kernel, "summary",
        [part, peer, slot, crow, ctl, id_rows, key_w, history_query_key_value_weight],
        [
            shape((n, width), bf16), shape((width, n), bf16), shape((n, width), bf16),
            shape((n // CHUNK, rows, LANES), f32), shape((state_rows(pairs, 2), LANES), bf16),
            shape((8, LANES), i32),
        ],
        scalars=[user_history_length],
        flops=2 * n * half * width,
    )

    def local(first, name, after):
        return call(
            lambda *refs: local_kernel(first, *refs), name,
            [emb, key, val, crow, ccol, history_query_key_value_weight],
            [shape((n, width // 2), bf16), shape((n, width // 2), f32)],
            after=after, flops=2 * n * half * width // 2,
        )

    early = [local(0, "local_a", [])]
    prefix = logs = None
    for bit in range(bits - 1):
        got = swap(pay, 1 << bit)
        if bit == 1:
            early.append(local(width // 2, "local_b", [prefix]))
        count = 2 << bit
        final = bit == bits - 2
        pay, prefix, logs, *every = call(
            lambda *refs, bit=bit, count=count: join_kernel(bit, count, pairs, *refs), "join",
            [pay, got] + ([prefix, logs] if bit else []),
            [
                shape((state_rows(pairs, 1 if final else 2 * count), LANES), bf16),
                shape((rows, LANES), f32), shape((pairs, LANES), f32),
            ] + [shape((2 * count, LANES), f32)] * final,
            after=[early[-1][1]],
        )
    got = swap(pay, 1 << (bits - 1))
    orders = []
    for turn in ((0, 1, 2, 3), (0, 2, 1, 3)):
        order = [t + 4 * reversed_bits(k, bits - 2) for t in turn for k in range(seq // 4)]
        orders.append([2 * (j % (seq // 2)) + j // (seq // 2) for j in order])
    work = cands * 2 * half * width
    val_w, *quarters = call(
        lambda *refs: candidate_kernel(orders, owned, *refs), "candidates",
        [
            every[0], stored, item_embedding_table, peer, candidate_query_weight,
            candidate_key_value_weight,
        ],
        [shape((width, width), bf16)] + [shape((width, LANES), bf16)] * 4, flops=2 * work,
    )
    (query_a, intra_a), (query_b, intra_b) = early
    buffers = [pltpu.VMEM((n, 2 * LANES), f32)] * 2
    message = width + log_pad(heads)
    hist, key_two, val_two, pay, pay_b = call(
        lambda *refs: finish_kernel(bits - 1, *refs), "finish",
        [
            here, scale, emb, query_a, query_b, intra_a, intra_b, enter, ctl, got, prefix, logs,
            history_output_weight, candidate_key_value_weight, val_w, quarters[3], quarters[2],
        ],
        [
            shape((n, width), f32), shape((n, width), bf16), shape((width, n), bf16),
            shape((message, LANES), bf16), shape((message, LANES), bf16),
        ],
        [pltpu.VMEM((n, width), f32), pltpu.SemaphoreType.DMA((n // CHUNK,))] + buffers,
        spaces=[ANY, VMEM, VMEM, VMEM, VMEM],
        flops=2 * n * half * width,
    )
    gots = [swap(pay, 3), swap_by_core(pay_b, (2, 1))]
    (pay,) = call(
        send_kernel, "send", [here, scale, quarters[1], key_two, val_two],
        [shape((message, LANES), bf16)], buffers, after=[pay], flops=8 * work,
    )
    gots.append(swap_by_core(pay, (1, 2)))
    mean, logs = call(
        keep_kernel, "keep", [here, scale, quarters[0], key_two, val_two],
        [shape((width, LANES), f32), shape((heads, LANES), f32)], buffers, after=[pay], flops=8 * work,
    )
    cols = LANES
    for bit in range(2, bits):
        cols //= 2
        packed = 2 * cols == LANES
        mean, logs, pay = call(
            fold_kernel, "fold", [mean, logs, *gots],
            [
                shape((width, cols), f32), shape((heads, cols), f32),
                shape((message // 2, LANES) if packed else (message, cols), bf16),
            ],
        )
        if packed and bit < bits - 1:
            pay = jnp.concatenate([pay[:, :cols], pay[:, cols:]], axis=0)
        gots = [swap(pay, 1 << bit)]
    (cand_out,) = call(
        last_kernel, "last", [mean, logs, *gots, candidate_output_weight],
        [shape((owned, width), f32)],
    )
    return hist[None], cand_out[None]


def solution(mesh):
    in_specs = (
        P(("groups", "dp"), "seq"),
        P(("groups", "dp"), None, "seq"),
        P(("groups", "dp")),
        P(("groups", "dp"), "seq"),
        P(),
        P("dp", None),
        P(),
        P(),
        P(),
        P(),
        P(),
        P(),
    )
    out_specs = (P(("groups", "dp"), "seq", None), P(("groups", "dp"), "seq", None))
    return jax.shard_map(shards, mesh=mesh, in_specs=in_specs, out_specs=out_specs, check_vma=False)
```

```python
import math

import jax
import jax.numpy as jnp
from jax import lax
from jax.experimental import pallas as pl
from jax.experimental.pallas import tpu as pltpu
from jax.sharding import PartitionSpec as P

f32, bf16, i32 = jnp.float32, jnp.bfloat16, jnp.int32
CHUNK = 256
KEYS = 512
LANES = 128
LOG2E = math.log2(math.e)
DEAD = -1e30
VMEM_LIMIT = 40 << 20


def dot(a, b):
    return jnp.dot(a, b, preferred_element_type=f32)


def contract(a, b, left, right):
    return lax.dot_general(a, b, (((left,), (right,)), ((), ())), preferred_element_type=f32)


def iota(shape, axis):
    return lax.broadcasted_iota(i32, shape, axis)


def thirds(value):
    high = value.astype(bf16).astype(f32)
    rest = value - high
    mid = rest.astype(bf16).astype(f32)
    return high, mid, rest - mid


def first_half(shape):
    return iota(shape, len(shape) - 1) % LANES < LANES // 2


def half_masks():
    low = first_half((1, LANES))
    return jnp.where(low, 1.0, 0.0).astype(bf16), jnp.where(low, 0.0, 1.0).astype(bf16)


def same_head():
    dims = (2 * LANES, 2 * LANES)
    return jnp.where(iota(dims, 0) // 64 == iota(dims, 1) // 64, 1.0, 0.0).astype(bf16)


def head_means(value, ones):
    square = (value * value).astype(bf16)
    step = ones.shape[0]
    parts = [dot(square[:, c : c + step], ones) for c in range(0, value.shape[1], step)]
    return jnp.concatenate(parts, axis=1) * (1.0 / 64.0)


def head_spread(heads, first, count):
    dims = (2 * heads, 64 * count)
    return jnp.where(iota(dims, 1) // 64 + first == iota(dims, 0) % heads, 1.0, 0.0).astype(bf16)


def spread(value, matrix):
    heads = value.shape[1] // 2
    high = value.astype(bf16).astype(f32)
    both = jnp.where(iota(value.shape, 1) < heads, high, value - high)
    return dot(both.astype(bf16), matrix)


def stored_slots(ids, stored):
    groups = stored.shape[0]
    n = ids.shape[1]
    pick = jnp.where(iota((groups, n), 0) == ids // LANES, 1.0, 0.0).astype(bf16)
    high = contract((stored // 64).astype(f32).astype(bf16), pick, 0, 0)
    low = contract((stored % 64).astype(f32).astype(bf16), pick, 0, 0)
    rows = jnp.where(iota((LANES, n), 0) == ids % LANES, high * 64.0 + low, 0.0)
    return jnp.sum(rows, axis=0, keepdims=True)


def picked_rows(slots, first, table):
    count = table.shape[0]
    hot = jnp.where(iota((count, slots.shape[1]), 0) == slots.astype(i32) - first, 1.0, 0.0)
    return contract(hot.astype(bf16), table[...], 0, 0)


def chunk(i):
    return slice(i * CHUNK, (i + 1) * CHUNK)


def pair_cut(p):
    return slice(p * LANES, (p + 1) * LANES)


def own_rows_kernel(
    ids_in, stored_in, decay_in, own_in, weight_in, part_o, slot_o, crow_o, ccol_o, ctl_o, key_w_o,
    ids, stored, decay, own, key_w, sem,
):
    n, half, heads = ids.shape[1], own.shape[0], decay.shape[0]
    width = own.shape[1]
    middle = weight_in.at[:, width : 2 * width]
    copies = [
        pltpu.make_async_copy(source, target, sem.at[k])
        for k, (source, target) in enumerate(
            (
                (ids_in, ids), (stored_in, stored), (decay_in, decay),
                (middle, key_w), (own_in, own),
            )
        )
    ]
    for copy in copies:
        copy.start()
    copies[0].wait()
    copies[1].wait()
    slots = stored_slots(ids[...], stored[...])
    slot_o[...] = slots
    copies[2].wait()
    upto = jnp.where(
        iota((CHUNK, CHUNK), 0) <= iota((CHUNK, CHUNK), 1), 1.0, 0.0
    ).astype(bf16)
    low = first_half((1, LANES))
    for i in range(n // CHUNK):
        pieces = jnp.concatenate(thirds(decay[:, chunk(i)]), axis=0)
        sums = dot(pieces.astype(bf16), upto)
        cum = sums[:heads] + sums[heads : 2 * heads] + sums[2 * heads :]
        crow_o[i] = cum
        ccol_o[chunk(i), :] = jnp.transpose(jnp.concatenate([cum, cum], axis=0))
        for p in range(heads // 2):
            r = i * (heads // 2) + p
            ctl_o[r : r + 1, :] = jnp.where(
                low, cum[2 * p : 2 * p + 1, CHUNK - 1 :], cum[2 * p + 1 : 2 * p + 2, CHUNK - 1 :]
            )
    copies[3].wait()
    key_w_o[...] = jnp.transpose(key_w[...].astype(f32)).astype(bf16)
    first = lax.axis_index("dp") * half
    copies[4].wait()
    for i in range(n // CHUNK):
        part_o[chunk(i), :] = picked_rows(slots[:, chunk(i)], first, own).astype(bf16)


def summary_kernel(
    length, part, peer, slot, crow, ctl, id_rows, key_w, weight,
    emb_o, key_o, val_o, enter_o, pay_o, here_o,
):
    n, width = part.shape
    half, heads = peer.shape[0], crow.shape[1]
    pairs = heads // 2
    block = LANES // 2
    low = first_half((1, LANES))
    chunks = n // CHUNK
    here = length[0] - lax.axis_index("seq") * n
    here_o[...] = jnp.full(here_o.shape, here, i32)

    def project(i):
        other = picked_rows(slot[:, chunk(i)], (1 - lax.axis_index("dp")) * half, peer)
        emb = (part[chunk(i), :].astype(f32) + other).astype(bf16)
        emb_o[chunk(i), :] = emb
        return contract(key_w[...], emb, 1, 1), dot(emb, weight[:, 2 * width :])

    total = [jnp.zeros((block, LANES), f32)] * pairs
    ready = project(0)
    for i in range(chunks):
        key, val = ready
        if i + 1 < chunks:
            ready = project(i + 1)
        val = jnp.where(iota((CHUNK, 1), 0) < here - i * CHUNK, val, 0.0).astype(bf16)
        val_o[chunk(i), :] = val
        alive = iota((1, CHUNK), 1) < here - i * CHUNK
        cum = crow[i]
        tail = jnp.exp(cum[:, CHUNK - 1 :] - cum)
        for p in range(pairs):
            keyed = []
            for h in (2 * p, 2 * p + 1):
                rows = key[h * 64 : (h + 1) * 64]
                mean = jnp.sum(rows * rows, axis=0, keepdims=True) * (1.0 / 64.0)
                unit = jnp.where(alive, lax.rsqrt(mean + 1e-06) * 0.125, 0.0)
                normed = rows * unit
                key_o[h * 64 : (h + 1) * 64, chunk(i)] = normed.astype(bf16)
                keyed.append(normed * tail[h : h + 1])
            keyed = jnp.concatenate(keyed, axis=0).astype(bf16)
            both = dot(keyed, val[:, pair_cut(p)])
            fresh = jnp.where(low, both[:block], both[block:])
            enter_o[i, p * block : (p + 1) * block, :] = total[p]
            total[p] = total[p] * jnp.exp(ctl[i * pairs + p : i * pairs + p + 1, :]) + fresh
    logs = ctl[0:pairs, :]
    for i in range(1, chunks):
        logs = logs + ctl[i * pairs : (i + 1) * pairs, :]
    pay_o[...] = pack_state(jnp.concatenate(total, axis=0), logs, id_rows[...])


def state_rows(pairs, ids):
    return pairs * 64 + -(-(3 * pairs + ids) // 16) * 16


def pack_state(state, logs, id_rows):
    pairs, ids = logs.shape[0], id_rows.shape[0]
    pad = state_rows(pairs, ids) - state.shape[0] - 3 * pairs - ids
    parts = [state, *thirds(logs), id_rows] + [jnp.zeros((pad, LANES), f32)] * (pad > 0)
    return jnp.concatenate(parts, axis=0).astype(bf16)


def unpack_state(packed, pairs):
    whole = packed.astype(f32)
    rows = pairs * 64
    logs = whole[rows : rows + pairs]
    for k in (1, 2):
        logs = logs + whole[rows + k * pairs : rows + (k + 1) * pairs]
    return whole[:rows], logs, whole[rows + 3 * pairs :]


def row_factors(logs):
    factors = jnp.exp(logs)
    return jnp.concatenate(
        [jnp.broadcast_to(factors[p : p + 1], (64, LANES)) for p in range(logs.shape[0])], axis=0
    )


def join_kernel(bit, ids, pairs, mine, got, *refs):
    before = refs[: 2 if bit else 0]
    pay_o, prefix_o, logs_o, *ids_o = refs[len(before) :]
    upper = (lax.axis_index("seq") >> bit) & 1 == 1
    state, logs, rows = unpack_state(mine[...], pairs)
    other, other_logs, other_rows = unpack_state(got[...], pairs)
    early = jnp.where(upper, other, state)
    late = jnp.where(upper, state, other)
    factor = row_factors(jnp.where(upper, logs, other_logs))
    id_rows = jnp.concatenate([rows[:ids], other_rows[:ids]], axis=0)
    if ids_o:
        ids_o[0][...] = id_rows
    sent = id_rows[:1] if ids_o else id_rows
    pay_o[...] = pack_state(early * factor + late, logs + other_logs, sent)
    if bit == 0:
        prefix_o[...] = jnp.where(upper, other, 0.0)
        logs_o[...] = jnp.where(upper, other_logs, 0.0)
    else:
        prefix, prefix_logs = before[0][...], before[1][...]
        prefix_o[...] = jnp.where(upper, prefix + row_factors(prefix_logs) * other, prefix)
        logs_o[...] = jnp.where(upper, prefix_logs + other_logs, prefix_logs)


def local_kernel(first, emb, key, val, crow, ccol, weight, *refs):
    if len(refs) > 2:
        pair_w, *refs, val_w_o = refs
        val_w_o[...] = jnp.transpose(pair_w[:, val_w_o.shape[1] :].astype(f32)).astype(bf16)
    query_o, intra_o = refs
    n, width = query_o.shape
    heads = ccol.shape[1] // 2
    ones, lanes = same_head(), head_spread(heads, first // 64, width // 64)
    mask_a, mask_b = half_masks()
    causal = iota((CHUNK, CHUNK), 0) >= iota((CHUNK, CHUNK), 1)

    def queries(i):
        query = dot(emb[chunk(i), :], weight[:, first : first + width])
        unit = lax.rsqrt(head_means(query, ones) + 1e-06) * 0.125
        query = query * unit
        decayed = query * spread(jnp.exp(ccol[chunk(i), :]), lanes)
        query_o[chunk(i), :] = decayed.astype(bf16)
        return query.astype(bf16)

    def scores(i, p, b, query):
        cut = pair_cut(p)
        wide = slice(first + p * LANES, first + (p + 1) * LANES)
        return dot(query[:, cut] * (mask_b if b else mask_a), key[wide, chunk(i)])

    units = [(i, p, b) for i in range(n // CHUNK) for p in range(width // LANES) for b in (0, 1)]
    query = {0: queries(0)}
    ready = scores(*units[0], query[0])
    held = None
    for u, (i, p, b) in enumerate(units):
        current = ready
        if u + 1 < len(units):
            j = units[u + 1][0]
            if j not in query:
                query[j] = queries(j)
            ready = scores(*units[u + 1], query[j])
        h = first // 64 + 2 * p + b
        gap = ccol[chunk(i), h : h + 1] - crow[i, h : h + 1, :]
        weights = jnp.where(causal, current * jnp.exp(gap), 0.0).astype(bf16)
        wide = slice(first + p * LANES, first + (p + 1) * LANES)
        part = dot(weights, val[chunk(i), wide] * (mask_b if b else mask_a))
        if b == 0:
            held = part
        else:
            intra_o[chunk(i), pair_cut(p)] = held + part


def candidate_kernel(
    orders, owned, id_rows, stored, own, peer, query_w, *quarters
):
    half, width = own.shape
    ids = id_rows[...]
    ids = (ids * float(LANES) + pltpu.roll(ids, LANES // 2, 1)).astype(i32)
    step = LANES // owned
    dp = lax.axis_index("dp")
    for start in range(0, len(orders[0]), 2 * step):
        tiles = []
        for first in (start, start + step):
            tile = None
            for k in range(step):
                one, two = (order[first + k] for order in orders)
                row = jnp.where(dp == 0, ids[one : one + 1], ids[two : two + 1])
                slots = stored_slots(row, stored[...])
                if k:
                    moved = pltpu.roll(slots, k * owned, 1)
                    slots = jnp.where(iota((1, LANES), 1) >= k * owned, moved, tile)
                tile = slots
            tiles.append(tile)
        slots = jnp.concatenate(tiles, axis=1)
        found = picked_rows(slots, dp * half, own) + picked_rows(slots, (1 - dp) * half, peer)
        query = jnp.transpose(dot(found.astype(bf16), query_w[...])).astype(bf16)
        for k in (0, 1):
            quarters[start // step + k][...] = query[:, pair_cut(k)]


def attend(alive_count, scale, queries, key, val, buffers, emit):
    n, width = key.shape
    blocks = range(0, n, KEYS)
    ones = jnp.ones((16, KEYS), bf16)
    heads = width // 64
    if len(queries) == 1:
        units = [[(h, 0), (h + 1, 0)] for h in range(0, heads, 2)]
    else:
        units = [[(h, 0), (h, 1)] for h in range(heads)]

    def weights_of(unit):
        parts = []
        for h, k in unit:
            rows = queries[k][h * 64 : (h + 1) * 64, :]
            zero = jnp.zeros_like(rows)
            parts.append(jnp.concatenate([zero, rows] if h % 2 else [rows, zero], axis=0))
        return jnp.concatenate(parts, axis=1)

    def store(u, block, weights, peak):
        values = dot(key[block : block + KEYS, pair_cut(units[u][0][0] // 2)], weights)
        values = jnp.where(iota((KEYS, 1), 0) < alive_count - block, values, DEAD)
        buffers[u % 2][block : block + KEYS, :] = values
        top = jnp.max(values.reshape(KEYS // 8, 8, 2 * LANES), axis=0)
        return top if peak is None else jnp.maximum(peak, top)

    peak, weights = None, weights_of(units[0])
    for block in blocks:
        peak = store(0, block, weights, peak)
    for u, unit in enumerate(units):
        factor = [jnp.broadcast_to(scale[0:1, h : h + 1], (1, LANES)) for h, _ in unit]
        factor = jnp.concatenate(factor, axis=1) * LOG2E
        first = unit[0][0] * 64
        rows = (unit[-1][0] + 1) * 64 - first
        peak = jnp.max(peak, axis=0, keepdims=True)
        following = sums = None
        more = u + 1 < len(units)
        if more:
            weights = weights_of(units[u + 1])
        for block in blocks:
            if more:
                following = store(u + 1, block, weights, following)
            gap = buffers[u % 2][block : block + KEYS, :] - peak
            probs = jnp.exp2(gap * factor).astype(bf16)
            side = [val[first : first + rows, block : block + KEYS], ones]
            part = dot(jnp.concatenate(side, axis=0), probs)
            sums = part if sums is None else sums + part
        total = sums[rows : rows + 1]
        logs = live(alive_count, peak * factor + jnp.log2(total))
        for b, (h, k) in enumerate(unit):
            top = h * 64 - first
            mean = sums[top : top + 64, pair_cut(b)] / total[:, pair_cut(b)]
            emit(h, k, mean, logs[:, pair_cut(b)])
        peak = following


def finish_kernel(
    bit, here, scale, emb, query_a, query_b, intra_a, intra_b, enter, ctl, got, prefix, prefix_logs,
    out_w, pair_w, val_w, cand_a, cand_b,
    hist_o, key_o, val_o, pay_a, pay_b, shown, sem, *buffers,
):
    n, width = emb.shape
    pairs = width // LANES
    ones = same_head()
    upper = (lax.axis_index("seq") >> bit) & 1 == 1
    state = unpack_state(got[...], pairs)[0]
    before, before_logs = prefix[...], prefix_logs[...]
    entering = jnp.where(upper, before + row_factors(before_logs) * state, before)
    lane = iota((1, 2 * LANES), 1) // 64
    chunks = n // CHUNK
    gone = [jnp.zeros((pairs, LANES), f32)]
    for i in range(chunks - 1):
        gone.append(gone[-1] + ctl[i * pairs : (i + 1) * pairs, :])

    def normed(i):
        states = enter[i] + row_factors(gone[i]) * entering
        parts = []
        for p in range(0, pairs, 2):
            wide = jnp.concatenate(
                [states[p * 64 : (p + 1) * 64], states[(p + 1) * 64 : (p + 2) * 64]], axis=1
            )
            matrix = jnp.concatenate([jnp.where(lane == k, wide, 0.0) for k in range(4)], axis=0)
            query, intra = (query_a, intra_a) if p < pairs // 2 else (query_b, intra_b)
            c = (p % (pairs // 2)) * LANES
            cut = slice(c, c + 2 * LANES)
            parts.append(dot(query[chunk(i), cut], matrix.astype(bf16)) + intra[chunk(i), cut])
        mixed = jnp.concatenate(parts, axis=1)
        return (mixed * lax.rsqrt(head_means(mixed, ones) + 1e-05)).astype(bf16)

    alive_count = here[0:1, 0:1]
    copies = [
        pltpu.make_async_copy(shown.at[chunk(i), :], hist_o.at[chunk(i), :], sem.at[i])
        for i in range(chunks)
    ]
    ready = normed(0)
    for i in range(chunks):
        current = ready
        if i + 1 < chunks:
            ready = normed(i + 1)
        hidden_sum = emb[chunk(i), :].astype(f32) + dot(current, out_w[...])
        alive = iota((CHUNK, 1), 0) < alive_count - i * CHUNK
        shown[chunk(i), :] = jnp.where(alive, hidden_sum, 0.0)
        copies[i].start()
        hidden = hidden_sum.astype(bf16)
        key_o[chunk(i), :] = dot(hidden, pair_w[:, :width]).astype(bf16)
        val_o[:, chunk(i)] = contract(val_w[...], hidden, 1, 1).astype(bf16)
    send_part(alive_count, scale, (cand_a, cand_b), key_o, val_o, (pay_a, pay_b), buffers)
    for copy in copies:
        copy.wait()


def send_part(alive_count, scale, queries, key, val, pays, buffers):
    log_rows = [[] for _ in pays]

    def emit(h, k, mean, logs):
        pays[k][h * 64 : (h + 1) * 64, :] = mean.astype(bf16)
        log_rows[k].append(logs)

    attend(alive_count, scale, queries, key, val, buffers, emit)
    for pay, rows in zip(pays, log_rows):
        pay[val.shape[0] :, :] = pack_logs(jnp.concatenate(rows, axis=0))


def send_kernel(here, scale, query, key, val, pay_o, *buffers):
    send_part(here[0:1, 0:1], scale, (query,), key, val, (pay_o,), buffers)


def live(alive_count, logs):
    return jnp.where(jnp.broadcast_to(alive_count, logs.shape) > 0, logs, DEAD)


def pack_logs(logs):
    heads, cols = logs.shape
    return jnp.concatenate(
        [*thirds(logs), jnp.zeros((log_pad(heads) - 3 * heads, cols), f32)], axis=0
    ).astype(bf16)


def log_pad(heads):
    return -(-3 * heads // 16) * 16


def unpack_logs(rows, heads):
    rows = rows.astype(f32)
    return rows[:heads] + rows[heads : 2 * heads] + rows[2 * heads : 3 * heads]


def keep_kernel(here, scale, query, key, val, mean_o, logs_o, *buffers):
    def emit(h, k, mean, logs):
        mean_o[h * 64 : (h + 1) * 64, :] = mean
        logs_o[h : h + 1, :] = logs

    attend(here[0:1, 0:1], scale, (query,), key, val, buffers, emit)


def over_heads(rows):
    return jnp.concatenate(
        [jnp.broadcast_to(rows[h : h + 1], (64, rows.shape[1])) for h in range(rows.shape[0])],
        axis=0,
    )


def merge(parts):
    peak = parts[0][1]
    for _, logs in parts[1:]:
        peak = jnp.maximum(peak, logs)
    shares = [jnp.exp2(logs - peak) for _, logs in parts]
    total = sum(shares[1:], shares[0])
    mean = None
    for (value, _), share in zip(parts, shares):
        term = value * over_heads(share / total)
        mean = term if mean is None else mean + term
    return mean, peak + jnp.log2(total)


def received(got, heads):
    value = got[...].astype(f32)
    if value.shape[0] < heads * 64:
        value = jnp.concatenate([value, pltpu.roll(value, LANES // 2, 1)], axis=0)
    return value[: heads * 64], unpack_logs(value[heads * 64 :], heads)


def fold_kernel(mean, logs, *refs):
    gots, (mean_o, logs_o, pay_o) = refs[:-3], refs[-3:]
    heads, keep = logs_o.shape
    parts = [(mean[...], logs[...])] + [received(got, heads) for got in gots]
    new_mean, new_logs = merge(parts)
    mean_o[...] = new_mean[:, :keep]
    logs_o[...] = new_logs[:, :keep]
    whole = jnp.concatenate([new_mean, pack_logs(new_logs).astype(f32)], axis=0)
    if 2 * keep == LANES:
        half = whole.shape[0] // 2
        top = pltpu.roll(whole[:half], keep, 1)
        pay_o[...] = jnp.where(first_half((1, LANES)), top, whole[half:]).astype(bf16)
    else:
        pay_o[...] = whole[:, keep:].astype(bf16)


def last_kernel(mean, logs, got, out_w, cand_o):
    heads, cols = logs.shape
    other_mean, other_logs = received(got, heads)
    parts = [(mean[...], logs[...]), (other_mean[:, :cols], other_logs[:, :cols])]
    attended = merge(parts)[0].astype(bf16)
    cand_o[...] = contract(attended, out_w[...], 0, 0)


def shape(dims, dtype):
    return jax.ShapeDtypeStruct(dims, dtype)


VMEM = pl.BlockSpec(memory_space=pltpu.VMEM)
SMEM = pl.BlockSpec(memory_space=pltpu.SMEM)
ANY = pl.BlockSpec(memory_space=pl.ANY)
HBM = pl.BlockSpec(memory_space=pltpu.HBM)


def call(kernel, name, operands, outs, scratch=(), after=(), flops=0, space=VMEM, spaces=None, scalars=()):
    count = len(scalars) + len(operands)
    if space is HBM:
        operands = [pltpu.with_memory_space_constraint(value, pltpu.HBM) for value in operands]

    def body(*refs):
        kernel(*refs[:count], *refs[count + len(after) :])

    return pl.pallas_call(
        body,
        name=name,
        in_specs=[SMEM] * len(scalars) + [space] * len(operands) + [ANY] * len(after),
        out_specs=spaces or [VMEM] * len(outs),
        out_shape=outs,
        scratch_shapes=list(scratch),
        compiler_params=pltpu.CompilerParams(vmem_limit_bytes=VMEM_LIMIT),
        cost_estimate=pl.CostEstimate(flops=flops, transcendentals=0, bytes_accessed=0),
    )(*scalars, *operands, *after)


def reversed_bits(value, bits):
    return sum(((value >> b) & 1) << (bits - 1 - b) for b in range(bits))


def shards(
    history_item_index,
    log_head_retention,
    user_history_length,
    candidate_item_index,
    item_stored_row,
    item_embedding_table,
    head_score_scale,
    history_query_key_value_weight,
    history_output_weight,
    candidate_key_value_weight,
    candidate_query_weight,
    candidate_output_weight,
):
    users, n = history_item_index.shape
    heads = log_head_retention.shape[1]
    half, width = item_embedding_table.shape
    owned = candidate_item_index.shape[1]
    seq = lax.axis_size("seq")
    bits = seq.bit_length() - 1
    cands = owned * seq
    assert users == 1 and lax.axis_size("dp") == 2 and seq == 1 << bits and bits > 2
    assert width == heads * 64 and heads % 4 == 0 and LANES % owned == 0 and owned <= 64
    assert cands == 4 * LANES
    pairs = heads // 2
    rows = pairs * 64

    def swap(value, mask):
        return lax.ppermute(value, "seq", [(j, j ^ mask) for j in range(seq)])

    def swap_by_core(value, masks):
        pairs = [
            (2 * j + core, 2 * (j ^ mask) + core) for j in range(seq) for core, mask in enumerate(masks)
        ]
        return lax.ppermute(value, ("seq", "dp"), pairs)

    peer = lax.ppermute(item_embedding_table, "dp", [(0, 1), (1, 0)])
    far_ids = swap(candidate_item_index, seq // 2)
    scale = head_score_scale.reshape(1, heads)
    stored = item_stored_row.reshape(-1, LANES)
    ids = jnp.concatenate([candidate_item_index, far_ids], axis=0)
    ids = jnp.pad(ids, ((0, 0), (0, 64 - owned)))
    id_rows = jnp.concatenate([ids // LANES, ids % LANES], axis=1).astype(f32)
    decay = log_head_retention.reshape(heads, n)

    part, slot, crow, ccol, ctl, key_w = call(
        own_rows_kernel, "own_rows",
        [
            history_item_index, stored, decay, item_embedding_table,
            history_query_key_value_weight,
        ],
        [
            shape((n, width), bf16), shape((1, n), f32), shape((n // CHUNK, heads, CHUNK), f32),
            shape((n, 2 * heads), f32), shape((n // CHUNK * pairs, LANES), f32),
            shape((width, width), bf16),
        ],
        [
            pltpu.VMEM((1, n), i32), pltpu.VMEM(stored.shape, i32), pltpu.VMEM((heads, n), f32),
            pltpu.VMEM((half, width), bf16), pltpu.VMEM((width, width), bf16),
            pltpu.SemaphoreType.DMA((6,)),
        ],
        space=HBM,
        flops=2 * n * half * width,
    )
    emb, key, val, enter, pay, here = call(
        summary_kernel, "summary",
        [part, peer, slot, crow, ctl, id_rows, key_w, history_query_key_value_weight],
        [
            shape((n, width), bf16), shape((width, n), bf16), shape((n, width), bf16),
            shape((n // CHUNK, rows, LANES), f32), shape((state_rows(pairs, 2), LANES), bf16),
            shape((8, LANES), i32),
        ],
        scalars=[user_history_length],
        flops=2 * n * half * width,
    )

    def local(first, name, after, more=()):
        return call(
            lambda *refs: local_kernel(first, *refs), name,
            [emb, key, val, crow, ccol, history_query_key_value_weight, *more],
            [shape((n, width // 2), bf16), shape((n, width // 2), f32)]
            + [shape((width, width), bf16)] * len(more),
            after=after, flops=2 * n * half * width // 2,
        )

    early = [local(0, "local_a", [])]
    prefix = logs = None
    for bit in range(bits - 1):
        got = swap(pay, 1 << bit)
        if bit == 1:
            early.append(local(width // 2, "local_b", [prefix], [candidate_key_value_weight]))
        count = 2 << bit
        final = bit == bits - 2
        pay, prefix, logs, *every = call(
            lambda *refs, bit=bit, count=count: join_kernel(bit, count, pairs, *refs), "join",
            [pay, got] + ([prefix, logs] if bit else []),
            [
                shape((state_rows(pairs, 1 if final else 2 * count), LANES), bf16),
                shape((rows, LANES), f32), shape((pairs, LANES), f32),
            ] + [shape((2 * count, LANES), f32)] * final,
            after=[early[-1][1]],
        )
    got = swap(pay, 1 << (bits - 1))
    orders = []
    for turn in ((0, 1, 2, 3), (0, 2, 1, 3)):
        order = [t + 4 * reversed_bits(k, bits - 2) for t in turn for k in range(seq // 4)]
        orders.append([2 * (j % (seq // 2)) + j // (seq // 2) for j in order])
    work = cands * 2 * half * width
    quarters = call(
        lambda *refs: candidate_kernel(orders, owned, *refs), "candidates",
        [
            every[0], stored, item_embedding_table, peer, candidate_query_weight,
        ],
        [shape((width, LANES), bf16)] * 4, flops=2 * work,
    )
    (query_a, intra_a), (query_b, intra_b, val_w) = early
    buffers = [pltpu.VMEM((n, 2 * LANES), f32)] * 2
    message = width + log_pad(heads)
    hist, key_two, val_two, pay, pay_b = call(
        lambda *refs: finish_kernel(bits - 1, *refs), "finish",
        [
            here, scale, emb, query_a, query_b, intra_a, intra_b, enter, ctl, got, prefix, logs,
            history_output_weight, candidate_key_value_weight, val_w, quarters[3], quarters[2],
        ],
        [
            shape((n, width), f32), shape((n, width), bf16), shape((width, n), bf16),
            shape((message, LANES), bf16), shape((message, LANES), bf16),
        ],
        [pltpu.VMEM((n, width), f32), pltpu.SemaphoreType.DMA((n // CHUNK,))] + buffers,
        spaces=[ANY, VMEM, VMEM, VMEM, VMEM],
        flops=2 * n * half * width,
    )
    gots = [swap(pay, 3), swap_by_core(pay_b, (2, 1))]
    (pay,) = call(
        send_kernel, "send", [here, scale, quarters[1], key_two, val_two],
        [shape((message, LANES), bf16)], buffers, after=[pay, pay_b], flops=20 * work,
    )
    gots.append(swap_by_core(pay, (1, 2)))
    mean, logs = call(
        keep_kernel, "keep", [here, scale, quarters[0], key_two, val_two],
        [shape((width, LANES), f32), shape((heads, LANES), f32)], buffers, after=[pay], flops=8 * work,
    )
    cols = LANES
    for bit in range(2, bits):
        cols //= 2
        packed = 2 * cols == LANES
        mean, logs, pay = call(
            fold_kernel, "fold", [mean, logs, *gots],
            [
                shape((width, cols), f32), shape((heads, cols), f32),
                shape((message // 2, LANES) if packed else (message, cols), bf16),
            ],
        )
        if packed and bit < bits - 1:
            pay = jnp.concatenate([pay[:, :cols], pay[:, cols:]], axis=0)
        gots = [swap(pay, 1 << bit)]
    (cand_out,) = call(
        last_kernel, "last", [mean, logs, *gots, candidate_output_weight],
        [shape((owned, width), f32)],
    )
    return hist[None], cand_out[None]


def solution(mesh):
    in_specs = (
        P(("groups", "dp"), "seq"),
        P(("groups", "dp"), None, "seq"),
        P(("groups", "dp")),
        P(("groups", "dp"), "seq"),
        P(),
        P("dp", None),
        P(),
        P(),
        P(),
        P(),
        P(),
        P(),
    )
    out_specs = (P(("groups", "dp"), "seq", None), P(("groups", "dp"), "seq", None))
    return jax.shard_map(shards, mesh=mesh, in_specs=in_specs, out_specs=out_specs, check_vma=False)
```

```python
import math

import jax
import jax.numpy as jnp
from jax import lax
from jax.experimental import pallas as pl
from jax.experimental.pallas import tpu as pltpu
from jax.sharding import PartitionSpec as P

f32, bf16, i32 = jnp.float32, jnp.bfloat16, jnp.int32
CHUNK = 256
KEYS = 512
LANES = 128
LOG2E = math.log2(math.e)
DEAD = -1e30
VMEM_LIMIT = 40 << 20


def dot(a, b):
    return jnp.dot(a, b, preferred_element_type=f32)


def contract(a, b, left, right):
    return lax.dot_general(a, b, (((left,), (right,)), ((), ())), preferred_element_type=f32)


def iota(shape, axis):
    return lax.broadcasted_iota(i32, shape, axis)


def thirds(value):
    high = value.astype(bf16).astype(f32)
    rest = value - high
    mid = rest.astype(bf16).astype(f32)
    return high, mid, rest - mid


def first_half(shape):
    return iota(shape, len(shape) - 1) % LANES < LANES // 2


def half_masks():
    low = first_half((1, LANES))
    return jnp.where(low, 1.0, 0.0).astype(bf16), jnp.where(low, 0.0, 1.0).astype(bf16)


def same_head():
    dims = (2 * LANES, 2 * LANES)
    return jnp.where(iota(dims, 0) // 64 == iota(dims, 1) // 64, 1.0, 0.0).astype(bf16)


def head_means(value, ones):
    square = (value * value).astype(bf16)
    step = ones.shape[0]
    parts = [dot(square[:, c : c + step], ones) for c in range(0, value.shape[1], step)]
    return jnp.concatenate(parts, axis=1) * (1.0 / 64.0)


def head_spread(heads, first, count):
    dims = (2 * heads, 64 * count)
    return jnp.where(iota(dims, 1) // 64 + first == iota(dims, 0) % heads, 1.0, 0.0).astype(bf16)


def spread(value, matrix):
    heads = value.shape[1] // 2
    high = value.astype(bf16).astype(f32)
    both = jnp.where(iota(value.shape, 1) < heads, high, value - high)
    return dot(both.astype(bf16), matrix)


def stored_slots(ids, stored):
    groups = stored.shape[0]
    n = ids.shape[1]
    pick = jnp.where(iota((groups, n), 0) == ids // LANES, 1.0, 0.0).astype(bf16)
    high = contract((stored // 64).astype(f32).astype(bf16), pick, 0, 0)
    low = contract((stored % 64).astype(f32).astype(bf16), pick, 0, 0)
    rows = jnp.where(iota((LANES, n), 0) == ids % LANES, high * 64.0 + low, 0.0)
    return jnp.sum(rows, axis=0, keepdims=True)


def picked_rows(slots, first, table):
    count = table.shape[0]
    hot = jnp.where(iota((count, slots.shape[1]), 0) == slots.astype(i32) - first, 1.0, 0.0)
    return contract(hot.astype(bf16), table[...], 0, 0)


def chunk(i):
    return slice(i * CHUNK, (i + 1) * CHUNK)


def pair_cut(p):
    return slice(p * LANES, (p + 1) * LANES)


def own_rows_kernel(
    ids_in, stored_in, decay_in, own_in, weight_in, part_o, slot_o, crow_o, ccol_o, ctl_o, key_w_o,
    ids, stored, decay, own, key_w, sem,
):
    n, half, heads = ids.shape[1], own.shape[0], decay.shape[0]
    width = own.shape[1]
    middle = weight_in.at[:, width : 2 * width]
    copies = [
        pltpu.make_async_copy(source, target, sem.at[k])
        for k, (source, target) in enumerate(
            (
                (ids_in, ids), (stored_in, stored), (decay_in, decay),
                (middle, key_w), (own_in, own),
            )
        )
    ]
    for copy in copies:
        copy.start()
    copies[0].wait()
    copies[1].wait()
    slots = stored_slots(ids[...], stored[...])
    slot_o[...] = slots
    copies[2].wait()
    upto = jnp.where(
        iota((CHUNK, CHUNK), 0) <= iota((CHUNK, CHUNK), 1), 1.0, 0.0
    ).astype(bf16)
    low = first_half((1, LANES))
    for i in range(n // CHUNK):
        pieces = jnp.concatenate(thirds(decay[:, chunk(i)]), axis=0)
        sums = dot(pieces.astype(bf16), upto)
        cum = sums[:heads] + sums[heads : 2 * heads] + sums[2 * heads :]
        crow_o[i] = cum
        ccol_o[chunk(i), :] = jnp.transpose(jnp.concatenate([cum, cum], axis=0))
        for p in range(heads // 2):
            r = i * (heads // 2) + p
            ctl_o[r : r + 1, :] = jnp.where(
                low, cum[2 * p : 2 * p + 1, CHUNK - 1 :], cum[2 * p + 1 : 2 * p + 2, CHUNK - 1 :]
            )
    copies[3].wait()
    key_w_o[...] = jnp.transpose(key_w[...].astype(f32)).astype(bf16)
    first = lax.axis_index("dp") * half
    copies[4].wait()
    for i in range(n // CHUNK):
        part_o[chunk(i), :] = picked_rows(slots[:, chunk(i)], first, own).astype(bf16)


def summary_kernel(
    length, part, peer, slot, crow, ctl, id_rows, key_w, weight,
    emb_o, key_o, val_o, enter_o, pay_o, here_o,
):
    n, width = part.shape
    half, heads = peer.shape[0], crow.shape[1]
    pairs = heads // 2
    block = LANES // 2
    low = first_half((1, LANES))
    chunks = n // CHUNK
    here = length[0] - lax.axis_index("seq") * n
    here_o[...] = jnp.full(here_o.shape, here, i32)

    def project(i):
        other = picked_rows(slot[:, chunk(i)], (1 - lax.axis_index("dp")) * half, peer)
        emb = (part[chunk(i), :].astype(f32) + other).astype(bf16)
        emb_o[chunk(i), :] = emb
        return contract(key_w[...], emb, 1, 1), dot(emb, weight[:, 2 * width :])

    total = [jnp.zeros((block, LANES), f32)] * pairs
    ready = project(0)
    for i in range(chunks):
        key, val = ready
        if i + 1 < chunks:
            ready = project(i + 1)
        val = jnp.where(iota((CHUNK, 1), 0) < here - i * CHUNK, val, 0.0).astype(bf16)
        val_o[chunk(i), :] = val
        alive = iota((1, CHUNK), 1) < here - i * CHUNK
        cum = crow[i]
        tail = jnp.exp(cum[:, CHUNK - 1 :] - cum)
        for p in range(pairs):
            keyed = []
            for h in (2 * p, 2 * p + 1):
                rows = key[h * 64 : (h + 1) * 64]
                mean = jnp.sum(rows * rows, axis=0, keepdims=True) * (1.0 / 64.0)
                unit = jnp.where(alive, lax.rsqrt(mean + 1e-06) * 0.125, 0.0)
                normed = rows * unit
                key_o[h * 64 : (h + 1) * 64, chunk(i)] = normed.astype(bf16)
                keyed.append(normed * tail[h : h + 1])
            keyed = jnp.concatenate(keyed, axis=0).astype(bf16)
            both = dot(keyed, val[:, pair_cut(p)])
            fresh = jnp.where(low, both[:block], both[block:])
            enter_o[i, p * block : (p + 1) * block, :] = total[p]
            total[p] = total[p] * jnp.exp(ctl[i * pairs + p : i * pairs + p + 1, :]) + fresh
    logs = ctl[0:pairs, :]
    for i in range(1, chunks):
        logs = logs + ctl[i * pairs : (i + 1) * pairs, :]
    pay_o[...] = pack_state(jnp.concatenate(total, axis=0), logs, id_rows[...])


def state_rows(pairs, ids):
    return pairs * 64 + -(-(3 * pairs + ids) // 16) * 16


def pack_state(state, logs, id_rows):
    pairs, ids = logs.shape[0], id_rows.shape[0]
    pad = state_rows(pairs, ids) - state.shape[0] - 3 * pairs - ids
    parts = [state, *thirds(logs), id_rows] + [jnp.zeros((pad, LANES), f32)] * (pad > 0)
    return jnp.concatenate(parts, axis=0).astype(bf16)


def unpack_state(packed, pairs):
    whole = packed.astype(f32)
    rows = pairs * 64
    logs = whole[rows : rows + pairs]
    for k in (1, 2):
        logs = logs + whole[rows + k * pairs : rows + (k + 1) * pairs]
    return whole[:rows], logs, whole[rows + 3 * pairs :]


def row_factors(logs):
    factors = jnp.exp(logs)
    return jnp.concatenate(
        [jnp.broadcast_to(factors[p : p + 1], (64, LANES)) for p in range(logs.shape[0])], axis=0
    )


def join_kernel(bit, ids, pairs, mine, got, *refs):
    before = refs[: 2 if bit else 0]
    pay_o, prefix_o, logs_o, *ids_o = refs[len(before) :]
    upper = (lax.axis_index("seq") >> bit) & 1 == 1
    state, logs, rows = unpack_state(mine[...], pairs)
    other, other_logs, other_rows = unpack_state(got[...], pairs)
    early = jnp.where(upper, other, state)
    late = jnp.where(upper, state, other)
    factor = row_factors(jnp.where(upper, logs, other_logs))
    id_rows = jnp.concatenate([rows[:ids], other_rows[:ids]], axis=0)
    if ids_o:
        ids_o[0][...] = id_rows
    sent = id_rows[:1] if ids_o else id_rows
    pay_o[...] = pack_state(early * factor + late, logs + other_logs, sent)
    if bit == 0:
        prefix_o[...] = jnp.where(upper, other, 0.0)
        logs_o[...] = jnp.where(upper, other_logs, 0.0)
    else:
        prefix, prefix_logs = before[0][...], before[1][...]
        prefix_o[...] = jnp.where(upper, prefix + row_factors(prefix_logs) * other, prefix)
        logs_o[...] = jnp.where(upper, prefix_logs + other_logs, prefix_logs)


def local_kernel(first, emb, key, val, crow, ccol, weight, *refs):
    if len(refs) > 2:
        pair_w, *refs, val_w_o = refs
        val_w_o[...] = jnp.transpose(pair_w[:, val_w_o.shape[1] :].astype(f32)).astype(bf16)
    query_o, intra_o = refs
    n, width = query_o.shape
    heads = ccol.shape[1] // 2
    ones, lanes = same_head(), head_spread(heads, first // 64, width // 64)
    mask_a, mask_b = half_masks()
    causal = iota((CHUNK, CHUNK), 0) >= iota((CHUNK, CHUNK), 1)

    def queries(i):
        query = dot(emb[chunk(i), :], weight[:, first : first + width])
        unit = lax.rsqrt(head_means(query, ones) + 1e-06) * 0.125
        query = query * unit
        decayed = query * spread(jnp.exp(ccol[chunk(i), :]), lanes)
        query_o[chunk(i), :] = decayed.astype(bf16)
        return query.astype(bf16)

    def scores(i, p, b, query):
        cut = pair_cut(p)
        wide = slice(first + p * LANES, first + (p + 1) * LANES)
        return dot(query[:, cut] * (mask_b if b else mask_a), key[wide, chunk(i)])

    units = [(i, p, b) for i in range(n // CHUNK) for p in range(width // LANES) for b in (0, 1)]
    query = {0: queries(0)}
    ready = scores(*units[0], query[0])
    held = None
    for u, (i, p, b) in enumerate(units):
        current = ready
        if u + 1 < len(units):
            j = units[u + 1][0]
            if j not in query:
                query[j] = queries(j)
            ready = scores(*units[u + 1], query[j])
        h = first // 64 + 2 * p + b
        gap = ccol[chunk(i), h : h + 1] - crow[i, h : h + 1, :]
        weights = jnp.where(causal, current * jnp.exp(gap), 0.0).astype(bf16)
        wide = slice(first + p * LANES, first + (p + 1) * LANES)
        part = dot(weights, val[chunk(i), wide] * (mask_b if b else mask_a))
        if b == 0:
            held = part
        else:
            intra_o[chunk(i), pair_cut(p)] = held + part


def candidate_kernel(
    orders, owned, id_rows, stored, own, peer, query_w, *quarters
):
    half, width = own.shape
    ids = id_rows[...]
    ids = (ids * float(LANES) + pltpu.roll(ids, LANES // 2, 1)).astype(i32)
    step = LANES // owned
    dp = lax.axis_index("dp")
    for start in range(0, len(orders[0]), 2 * step):
        tiles = []
        for first in (start, start + step):
            tile = None
            for k in range(step):
                one, two = (order[first + k] for order in orders)
                row = jnp.where(dp == 0, ids[one : one + 1], ids[two : two + 1])
                slots = stored_slots(row, stored[...])
                if k:
                    moved = pltpu.roll(slots, k * owned, 1)
                    slots = jnp.where(iota((1, LANES), 1) >= k * owned, moved, tile)
                tile = slots
            tiles.append(tile)
        slots = jnp.concatenate(tiles, axis=1)
        found = picked_rows(slots, dp * half, own) + picked_rows(slots, (1 - dp) * half, peer)
        query = jnp.transpose(dot(found.astype(bf16), query_w[...])).astype(bf16)
        for k in (0, 1):
            quarters[start // step + k][...] = query[:, pair_cut(k)]


def attend(alive_count, scale, queries, key, val, buffers, emit):
    n, width = key.shape
    keys = KEYS // 2 if len(queries) == 1 else KEYS
    blocks = range(0, n, keys)
    ones = jnp.ones((16, keys), bf16)
    heads = width // 64
    if len(queries) == 1:
        units = [[(h, 0), (h + 1, 0)] for h in range(0, heads, 2)]
    else:
        units = [[(h, 0), (h, 1)] for h in range(heads)]

    def weights_of(unit):
        parts = []
        for h, k in unit:
            rows = queries[k][h * 64 : (h + 1) * 64, :]
            zero = jnp.zeros_like(rows)
            parts.append(jnp.concatenate([zero, rows] if h % 2 else [rows, zero], axis=0))
        return jnp.concatenate(parts, axis=1)

    def store(u, block, weights, peak):
        values = dot(key[block : block + keys, pair_cut(units[u][0][0] // 2)], weights)
        values = jnp.where(iota((keys, 1), 0) < alive_count - block, values, DEAD)
        buffers[u % 2][block : block + keys, :] = values
        top = jnp.max(values.reshape(keys // 8, 8, 2 * LANES), axis=0)
        return top if peak is None else jnp.maximum(peak, top)

    peak, weights = None, weights_of(units[0])
    for block in blocks:
        peak = store(0, block, weights, peak)
    for u, unit in enumerate(units):
        factor = [jnp.broadcast_to(scale[0:1, h : h + 1], (1, LANES)) for h, _ in unit]
        factor = jnp.concatenate(factor, axis=1) * LOG2E
        first = unit[0][0] * 64
        rows = (unit[-1][0] + 1) * 64 - first
        peak = jnp.max(peak, axis=0, keepdims=True)
        following = sums = None
        more = u + 1 < len(units)
        if more:
            weights = weights_of(units[u + 1])
        for block in blocks:
            if more:
                following = store(u + 1, block, weights, following)
            gap = buffers[u % 2][block : block + keys, :] - peak
            probs = jnp.exp2(gap * factor).astype(bf16)
            side = [val[first : first + rows, block : block + keys], ones]
            part = dot(jnp.concatenate(side, axis=0), probs)
            sums = part if sums is None else sums + part
        total = sums[rows : rows + 1]
        logs = live(alive_count, peak * factor + jnp.log2(total))
        for b, (h, k) in enumerate(unit):
            top = h * 64 - first
            mean = sums[top : top + 64, pair_cut(b)] / total[:, pair_cut(b)]
            emit(h, k, mean, logs[:, pair_cut(b)])
        peak = following


def finish_kernel(
    bit, here, scale, emb, query_a, query_b, intra_a, intra_b, enter, ctl, got, prefix, prefix_logs,
    out_w, pair_w, val_w, cand_a, cand_b,
    hist_o, key_o, val_o, pay_a, pay_b, shown, sem, *buffers,
):
    n, width = emb.shape
    pairs = width // LANES
    ones = same_head()
    upper = (lax.axis_index("seq") >> bit) & 1 == 1
    state = unpack_state(got[...], pairs)[0]
    before, before_logs = prefix[...], prefix_logs[...]
    entering = jnp.where(upper, before + row_factors(before_logs) * state, before)
    lane = iota((1, 2 * LANES), 1) // 64
    chunks = n // CHUNK
    gone = [jnp.zeros((pairs, LANES), f32)]
    for i in range(chunks - 1):
        gone.append(gone[-1] + ctl[i * pairs : (i + 1) * pairs, :])

    def normed(i):
        states = enter[i] + row_factors(gone[i]) * entering
        parts = []
        for p in range(0, pairs, 2):
            wide = jnp.concatenate(
                [states[p * 64 : (p + 1) * 64], states[(p + 1) * 64 : (p + 2) * 64]], axis=1
            )
            matrix = jnp.concatenate([jnp.where(lane == k, wide, 0.0) for k in range(4)], axis=0)
            query, intra = (query_a, intra_a) if p < pairs // 2 else (query_b, intra_b)
            c = (p % (pairs // 2)) * LANES
            cut = slice(c, c + 2 * LANES)
            parts.append(dot(query[chunk(i), cut], matrix.astype(bf16)) + intra[chunk(i), cut])
        mixed = jnp.concatenate(parts, axis=1)
        return (mixed * lax.rsqrt(head_means(mixed, ones) + 1e-05)).astype(bf16)

    alive_count = here[0:1, 0:1]
    copies = [
        pltpu.make_async_copy(shown.at[chunk(i), :], hist_o.at[chunk(i), :], sem.at[i])
        for i in range(chunks)
    ]
    ready = normed(0)
    for i in range(chunks):
        current = ready
        if i + 1 < chunks:
            ready = normed(i + 1)
        hidden_sum = emb[chunk(i), :].astype(f32) + dot(current, out_w[...])
        alive = iota((CHUNK, 1), 0) < alive_count - i * CHUNK
        shown[chunk(i), :] = jnp.where(alive, hidden_sum, 0.0)
        copies[i].start()
        hidden = hidden_sum.astype(bf16)
        key_o[chunk(i), :] = dot(hidden, pair_w[:, :width]).astype(bf16)
        val_o[:, chunk(i)] = contract(val_w[...], hidden, 1, 1).astype(bf16)
    send_part(alive_count, scale, (cand_a, cand_b), key_o, val_o, (pay_a, pay_b), buffers)
    for copy in copies:
        copy.wait()


def send_part(alive_count, scale, queries, key, val, pays, buffers):
    log_rows = [[] for _ in pays]

    def emit(h, k, mean, logs):
        pays[k][h * 64 : (h + 1) * 64, :] = mean.astype(bf16)
        log_rows[k].append(logs)

    attend(alive_count, scale, queries, key, val, buffers, emit)
    for pay, rows in zip(pays, log_rows):
        pay[val.shape[0] :, :] = pack_logs(jnp.concatenate(rows, axis=0))


def send_kernel(here, scale, query, key, val, pay_o, *buffers):
    send_part(here[0:1, 0:1], scale, (query,), key, val, (pay_o,), buffers)


def live(alive_count, logs):
    return jnp.where(jnp.broadcast_to(alive_count, logs.shape) > 0, logs, DEAD)


def pack_logs(logs):
    heads, cols = logs.shape
    return jnp.concatenate(
        [*thirds(logs), jnp.zeros((log_pad(heads) - 3 * heads, cols), f32)], axis=0
    ).astype(bf16)


def log_pad(heads):
    return -(-3 * heads // 16) * 16


def unpack_logs(rows, heads):
    rows = rows.astype(f32)
    return rows[:heads] + rows[heads : 2 * heads] + rows[2 * heads : 3 * heads]


def keep_kernel(here, scale, query, key, val, mean_o, logs_o, *buffers):
    def emit(h, k, mean, logs):
        mean_o[h * 64 : (h + 1) * 64, :] = mean
        logs_o[h : h + 1, :] = logs

    attend(here[0:1, 0:1], scale, (query,), key, val, buffers, emit)


def over_heads(rows):
    return jnp.concatenate(
        [jnp.broadcast_to(rows[h : h + 1], (64, rows.shape[1])) for h in range(rows.shape[0])],
        axis=0,
    )


def merge(parts):
    peak = parts[0][1]
    for _, logs in parts[1:]:
        peak = jnp.maximum(peak, logs)
    shares = [jnp.exp2(logs - peak) for _, logs in parts]
    total = sum(shares[1:], shares[0])
    mean = None
    for (value, _), share in zip(parts, shares):
        term = value * over_heads(share / total)
        mean = term if mean is None else mean + term
    return mean, peak + jnp.log2(total)


def received(got, heads):
    value = got[...].astype(f32)
    if value.shape[0] < heads * 64:
        value = jnp.concatenate([value, pltpu.roll(value, LANES // 2, 1)], axis=0)
    return value[: heads * 64], unpack_logs(value[heads * 64 :], heads)


def fold_kernel(mean, logs, *refs):
    gots, (mean_o, logs_o, pay_o) = refs[:-3], refs[-3:]
    heads, keep = logs_o.shape
    parts = [(mean[...], logs[...])] + [received(got, heads) for got in gots]
    new_mean, new_logs = merge(parts)
    mean_o[...] = new_mean[:, :keep]
    logs_o[...] = new_logs[:, :keep]
    whole = jnp.concatenate([new_mean, pack_logs(new_logs).astype(f32)], axis=0)
    if 2 * keep == LANES:
        half = whole.shape[0] // 2
        top = pltpu.roll(whole[:half], keep, 1)
        pay_o[...] = jnp.where(first_half((1, LANES)), top, whole[half:]).astype(bf16)
    else:
        pay_o[...] = whole[:, keep:].astype(bf16)


def last_kernel(mean, logs, got, out_w, cand_o):
    heads, cols = logs.shape
    other_mean, other_logs = received(got, heads)
    parts = [(mean[...], logs[...]), (other_mean[:, :cols], other_logs[:, :cols])]
    attended = merge(parts)[0].astype(bf16)
    cand_o[...] = contract(attended, out_w[...], 0, 0)


def shape(dims, dtype):
    return jax.ShapeDtypeStruct(dims, dtype)


VMEM = pl.BlockSpec(memory_space=pltpu.VMEM)
SMEM = pl.BlockSpec(memory_space=pltpu.SMEM)
ANY = pl.BlockSpec(memory_space=pl.ANY)
HBM = pl.BlockSpec(memory_space=pltpu.HBM)


def call(kernel, name, operands, outs, scratch=(), after=(), flops=0, space=VMEM, spaces=None, scalars=()):
    count = len(scalars) + len(operands)
    if space is HBM:
        operands = [pltpu.with_memory_space_constraint(value, pltpu.HBM) for value in operands]

    def body(*refs):
        kernel(*refs[:count], *refs[count + len(after) :])

    return pl.pallas_call(
        body,
        name=name,
        in_specs=[SMEM] * len(scalars) + [space] * len(operands) + [ANY] * len(after),
        out_specs=spaces or [VMEM] * len(outs),
        out_shape=outs,
        scratch_shapes=list(scratch),
        compiler_params=pltpu.CompilerParams(vmem_limit_bytes=VMEM_LIMIT),
        cost_estimate=pl.CostEstimate(flops=flops, transcendentals=0, bytes_accessed=0),
    )(*scalars, *operands, *after)


def reversed_bits(value, bits):
    return sum(((value >> b) & 1) << (bits - 1 - b) for b in range(bits))


def shards(
    history_item_index,
    log_head_retention,
    user_history_length,
    candidate_item_index,
    item_stored_row,
    item_embedding_table,
    head_score_scale,
    history_query_key_value_weight,
    history_output_weight,
    candidate_key_value_weight,
    candidate_query_weight,
    candidate_output_weight,
):
    users, n = history_item_index.shape
    heads = log_head_retention.shape[1]
    half, width = item_embedding_table.shape
    owned = candidate_item_index.shape[1]
    seq = lax.axis_size("seq")
    bits = seq.bit_length() - 1
    cands = owned * seq
    assert users == 1 and lax.axis_size("dp") == 2 and seq == 1 << bits and bits > 2
    assert width == heads * 64 and heads % 4 == 0 and LANES % owned == 0 and owned <= 64
    assert cands == 4 * LANES
    pairs = heads // 2
    rows = pairs * 64

    def swap(value, mask):
        return lax.ppermute(value, "seq", [(j, j ^ mask) for j in range(seq)])

    def swap_by_core(value, masks):
        pairs = [
            (2 * j + core, 2 * (j ^ mask) + core) for j in range(seq) for core, mask in enumerate(masks)
        ]
        return lax.ppermute(value, ("seq", "dp"), pairs)

    peer = lax.ppermute(item_embedding_table, "dp", [(0, 1), (1, 0)])
    far_ids = swap(candidate_item_index, seq // 2)
    scale = head_score_scale.reshape(1, heads)
    stored = item_stored_row.reshape(-1, LANES)
    ids = jnp.concatenate([candidate_item_index, far_ids], axis=0)
    ids = jnp.pad(ids, ((0, 0), (0, 64 - owned)))
    id_rows = jnp.concatenate([ids // LANES, ids % LANES], axis=1).astype(f32)
    decay = log_head_retention.reshape(heads, n)

    part, slot, crow, ccol, ctl, key_w = call(
        own_rows_kernel, "own_rows",
        [
            history_item_index, stored, decay, item_embedding_table,
            history_query_key_value_weight,
        ],
        [
            shape((n, width), bf16), shape((1, n), f32), shape((n // CHUNK, heads, CHUNK), f32),
            shape((n, 2 * heads), f32), shape((n // CHUNK * pairs, LANES), f32),
            shape((width, width), bf16),
        ],
        [
            pltpu.VMEM((1, n), i32), pltpu.VMEM(stored.shape, i32), pltpu.VMEM((heads, n), f32),
            pltpu.VMEM((half, width), bf16), pltpu.VMEM((width, width), bf16),
            pltpu.SemaphoreType.DMA((6,)),
        ],
        space=HBM,
        flops=2 * n * half * width,
    )
    emb, key, val, enter, pay, here = call(
        summary_kernel, "summary",
        [part, peer, slot, crow, ctl, id_rows, key_w, history_query_key_value_weight],
        [
            shape((n, width), bf16), shape((width, n), bf16), shape((n, width), bf16),
            shape((n // CHUNK, rows, LANES), f32), shape((state_rows(pairs, 2), LANES), bf16),
            shape((8, LANES), i32),
        ],
        scalars=[user_history_length],
        flops=2 * n * half * width,
    )

    def local(first, name, after, more=()):
        return call(
            lambda *refs: local_kernel(first, *refs), name,
            [emb, key, val, crow, ccol, history_query_key_value_weight, *more],
            [shape((n, width // 2), bf16), shape((n, width // 2), f32)]
            + [shape((width, width), bf16)] * len(more),
            after=after, flops=2 * n * half * width // 2,
        )

    early = [local(0, "local_a", [])]
    prefix = logs = None
    for bit in range(bits - 1):
        got = swap(pay, 1 << bit)
        if bit == 1:
            early.append(local(width // 2, "local_b", [prefix], [candidate_key_value_weight]))
        count = 2 << bit
        final = bit == bits - 2
        pay, prefix, logs, *every = call(
            lambda *refs, bit=bit, count=count: join_kernel(bit, count, pairs, *refs), "join",
            [pay, got] + ([prefix, logs] if bit else []),
            [
                shape((state_rows(pairs, 1 if final else 2 * count), LANES), bf16),
                shape((rows, LANES), f32), shape((pairs, LANES), f32),
            ] + [shape((2 * count, LANES), f32)] * final,
            after=[early[-1][1]],
        )
    got = swap(pay, 1 << (bits - 1))
    orders = []
    for turn in ((0, 1, 2, 3), (0, 2, 1, 3)):
        order = [t + 4 * reversed_bits(k, bits - 2) for t in turn for k in range(seq // 4)]
        orders.append([2 * (j % (seq // 2)) + j // (seq // 2) for j in order])
    work = cands * 2 * half * width
    quarters = call(
        lambda *refs: candidate_kernel(orders, owned, *refs), "candidates",
        [
            every[0], stored, item_embedding_table, peer, candidate_query_weight,
        ],
        [shape((width, LANES), bf16)] * 4, flops=2 * work,
    )
    (query_a, intra_a), (query_b, intra_b, val_w) = early
    buffers = [pltpu.VMEM((n, 2 * LANES), f32)] * 2
    message = width + log_pad(heads)
    hist, key_two, val_two, pay, pay_b = call(
        lambda *refs: finish_kernel(bits - 1, *refs), "finish",
        [
            here, scale, emb, query_a, query_b, intra_a, intra_b, enter, ctl, got, prefix, logs,
            history_output_weight, candidate_key_value_weight, val_w, quarters[3], quarters[2],
        ],
        [
            shape((n, width), f32), shape((n, width), bf16), shape((width, n), bf16),
            shape((message, LANES), bf16), shape((message, LANES), bf16),
        ],
        [pltpu.VMEM((n, width), f32), pltpu.SemaphoreType.DMA((n // CHUNK,))] + buffers,
        spaces=[ANY, VMEM, VMEM, VMEM, VMEM],
        flops=2 * n * half * width,
    )
    gots = [swap(pay, 3), swap_by_core(pay_b, (2, 1))]
    (pay,) = call(
        send_kernel, "send", [here, scale, quarters[1], key_two, val_two],
        [shape((message, LANES), bf16)], buffers, after=[pay, pay_b], flops=20 * work,
    )
    gots.append(swap_by_core(pay, (1, 2)))
    mean, logs = call(
        keep_kernel, "keep", [here, scale, quarters[0], key_two, val_two],
        [shape((width, LANES), f32), shape((heads, LANES), f32)], buffers, after=[pay], flops=8 * work,
    )
    cols = LANES
    for bit in range(2, bits):
        cols //= 2
        packed = 2 * cols == LANES
        mean, logs, pay = call(
            fold_kernel, "fold", [mean, logs, *gots],
            [
                shape((width, cols), f32), shape((heads, cols), f32),
                shape((message // 2, LANES) if packed else (message, cols), bf16),
            ],
        )
        if packed and bit < bits - 1:
            pay = jnp.concatenate([pay[:, :cols], pay[:, cols:]], axis=0)
        gots = [swap(pay, 1 << bit)]
    (cand_out,) = call(
        last_kernel, "last", [mean, logs, *gots, candidate_output_weight],
        [shape((owned, width), f32)],
    )
    return hist[None], cand_out[None]


def solution(mesh):
    in_specs = (
        P(("groups", "dp"), "seq"),
        P(("groups", "dp"), None, "seq"),
        P(("groups", "dp")),
        P(("groups", "dp"), "seq"),
        P(),
        P("dp", None),
        P(),
        P(),
        P(),
        P(),
        P(),
        P(),
    )
    out_specs = (P(("groups", "dp"), "seq", None), P(("groups", "dp"), "seq", None))
    return jax.shard_map(shards, mesh=mesh, in_specs=in_specs, out_specs=out_specs, check_vma=False)
```
